32 devices in a mesh: blk: 8 (over z, x), head: 4 (over y, core).
Axes of the slice: x: 2, y: 2, z: 4, core: 2. Of those that a mesh axis runs over, the one named last changes fastest.
Arguments:
- tokens: bfloat16 [1, 4096, 2048], P(None, ('blk', 'head')), may hold values from -6 to 6
- attention_norm: bfloat16 [2048], P(('blk', 'head')), may hold values from 0.5 to 1.5
- query_weight: bfloat16 [2048, 2048], P(('blk', 'head')), may hold values from -0.125 to 0.125
- key_projection: bfloat16 [2048, 1024], P(('blk', 'head')), may hold values from -0.125 to 0.125
- value_projection: bfloat16 [2048, 1024], P(('blk', 'head')), may hold values from -0.125 to 0.125
- query_norm: bfloat16 [128], P(('blk', 'head')), may hold values from 0.5 to 1.5
- key_norm: bfloat16 [128], P(('blk', 'head')), may hold values from 0.5 to 1.5
- output_weight: bfloat16 [2048, 2048], P(('blk', 'head')), may hold values from -2 to 2
- feedforward_norm: bfloat16 [2048], P(('blk', 'head')), may hold values from 0.5 to 1.5
- gate_weight: bfloat16 [2048, 6144], P(('blk', 'head')), may hold values from -0.125 to 0.125
- up_weight: bfloat16 [2048, 6144], P(('blk', 'head')), may hold values from -0.125 to 0.125
- down_weight: bfloat16 [6144, 2048], P(('blk', 'head')), may hold values from -0.078125 to 0.078125
- stretch_order: int32 [1, 16], replicated, may hold values from 0 to 15, each once within a row
- out_cotangent: bfloat16 [1, 4096, 2048], P(None, ('blk', 'head')), may hold values from -6 to 6
Outputs:
- layer_out: bfloat16 [1, 4096, 2048], P(None, ('blk', 'head'))
- tokens_gradient: bfloat16 [1, 4096, 2048], P(None, ('blk', 'head'))
- attention_norm_gradient: float32 [2048], P(('blk', 'head'))
- query_weight_gradient: float32 [2048, 2048], P(('blk', 'head'))
- key_weight_gradient: float32 [2048, 1024], P(('blk', 'head'))
- value_weight_gradient: float32 [2048, 1024], P(('blk', 'head'))
- query_norm_gradient: float32 [128], P(('blk', 'head'))
- key_norm_gradient: float32 [128], P(('blk', 'head'))
- output_weight_gradient: float32 [2048, 2048], P(('blk', 'head'))
- feedforward_norm_gradient: float32 [2048], P(('blk', 'head'))
- gate_weight_gradient: float32 [2048, 6144], P(('blk', 'head'))
- up_weight_gradient: float32 [2048, 6144], P(('blk', 'head'))
- down_weight_gradient: float32 [6144, 2048], P(('blk', 'head'))
The draws below stay inside these ranges and needn't reach their ends.
Inputs may be any that keep to these rules, and one draw needn't show every extreme that they name: Each row is an order of the 16 stretches of a sequence: stored slot j holds positions stretch_order[b, j] * 256 to stretch_order[b, j] * 256 + 255.
All inputs are finite; a program needn't handle non-finite values.
Results may differ from the reference program's by a relative error of at most 0.025.
Values may be sent and summed in bfloat16 or wider, within the bound.
No kernel may reach another device: no remote copies, remote signals or barrier semaphores. Data moves between devices by JAX's collectives and lax.ppermute only.
A program may use at most 384 MiB of HBM per device.

```python
import math
import jax
import jax.numpy as jnp
from jax import lax

MODEL_WIDTH = 2048
QUERY_HEADS = 16
KEY_VALUE_HEADS = 8
HEAD_SIZE = 128
FF = 6144
SEQUENCE_COUNT = 1
SEQUENCE_LENGTH = 4096
STRETCH = 256
NCHUNK = 16


def block_levels(stream_key, shape, split, smallest, top_value):
    def one(position, parts):
        steps = jax.random.uniform(jax.random.fold_in(jax.random.fold_in(stream_key, 6), position), (parts,), jnp.float32, smallest / len(split), top_value / len(split))
        return jnp.repeat(jnp.exp(steps), shape[position] // parts).reshape((-1,) + (1,) * (len(shape) - position - 1))

    loudness = one(*split[0])
    for cut in split[1:]:
        loudness = loudness * one(*cut)
    return loudness


def scatter_about(key, extent, width, limit, pieces=(), kind=jnp.bfloat16):
    array = width * jax.random.normal(key, extent, jnp.float32)
    if pieces:
        array = array * block_levels(key, extent, pieces, -0.22, 0.18)
    return jnp.clip(array, -limit, limit).astype(kind)


def setup_inputs(seed: int = 0) -> dict:
    splits = jax.random.split(jax.random.key(seed), 15)
    tokens = scatter_about(splits[0], (SEQUENCE_COUNT, SEQUENCE_LENGTH, MODEL_WIDTH), 1.0, 6.0, ((1, 32),))
    attention_norm = jnp.clip(1.0 + 0.1 * jax.random.normal(splits[1], (MODEL_WIDTH,), jnp.float32), 0.5, 1.5).astype(jnp.bfloat16)
    query_weight = scatter_about(splits[2], (MODEL_WIDTH, QUERY_HEADS * HEAD_SIZE), MODEL_WIDTH ** -0.5, 0.125, ((0, 32),))
    key_projection = scatter_about(splits[3], (MODEL_WIDTH, KEY_VALUE_HEADS * HEAD_SIZE), MODEL_WIDTH ** -0.5, 0.125, ((0, 32),))
    value_projection = scatter_about(splits[4], (MODEL_WIDTH, KEY_VALUE_HEADS * HEAD_SIZE), MODEL_WIDTH ** -0.5, 0.125, ((0, 32),))
    query_norm = jnp.clip(1.0 + 0.1 * jax.random.normal(splits[5], (HEAD_SIZE,), jnp.float32), 0.5, 1.5).astype(jnp.bfloat16)
    key_norm = jnp.clip(1.0 + 0.1 * jax.random.normal(splits[6], (HEAD_SIZE,), jnp.float32), 0.5, 1.5).astype(jnp.bfloat16)
    output_weight = scatter_about(splits[7], (QUERY_HEADS * HEAD_SIZE, MODEL_WIDTH), (HEAD_SIZE // 16) ** -0.5, 2.0, ((0, 32),))
    feedforward_norm = jnp.clip(1.0 + 0.1 * jax.random.normal(splits[8], (MODEL_WIDTH,), jnp.float32), 0.5, 1.5).astype(jnp.bfloat16)
    gate_weight = scatter_about(splits[9], (MODEL_WIDTH, FF), MODEL_WIDTH ** -0.5, 0.125, ((0, 32),))
    up_weight = scatter_about(splits[10], (MODEL_WIDTH, FF), MODEL_WIDTH ** -0.5, 0.125, ((0, 32),))
    down_weight = scatter_about(splits[11], (FF, MODEL_WIDTH), FF ** -0.5, 0.078125, ((0, 32),))
    stretch_order = jax.vmap(lambda own: jax.random.permutation(own, NCHUNK))(jax.random.split(splits[12], SEQUENCE_COUNT)).reshape((SEQUENCE_COUNT, NCHUNK)).astype(jnp.int32)
    out_cotangent = scatter_about(splits[13], (SEQUENCE_COUNT, SEQUENCE_LENGTH, MODEL_WIDTH), 1.0, 6.0, ((1, 32),))
    return {"tokens": tokens, "attention_norm": attention_norm, "query_weight": query_weight, "key_projection": key_projection, "value_projection": value_projection, "query_norm": query_norm, "key_norm": key_norm, "output_weight": output_weight, "feedforward_norm": feedforward_norm, "gate_weight": gate_weight, "up_weight": up_weight, "down_weight": down_weight, "stretch_order": stretch_order, "out_cotangent": out_cotangent}


EPS = 1e-06
NEG = -1e+30
ROPE_BASE = 1000000.0

@jax.custom_vjp
def low(v):
    return lax.optimization_barrier(v.astype(jnp.bfloat16)).astype(jnp.float32)

@jax.custom_vjp
def lower_backward(v):
    return v

def low_keep(v):
    return (low(v), None)

def low_pass(kept, grad):
    return (grad,)

def back_keep(v):
    return (v, None)

def back_low(kept, grad):
    return (low(grad),)
low.defvjp(low_keep, low_pass)
lower_backward.defvjp(back_keep, back_low)

def both_rounded(inputs):
    return low(lower_backward(inputs))

def norm_rows(inputs, norm_gain):
    return inputs * lax.rsqrt(lax.optimization_barrier(jnp.mean(inputs * inputs, axis=-1, keepdims=True)) + EPS) * norm_gain

def rotary(inputs, phases):
    half_width = inputs.shape[-1] // 2
    cosine = jnp.cos(phases)
    sine_term = jnp.sin(phases)
    first_half = inputs[..., :half_width]
    second_half = inputs[..., half_width:]
    return jnp.concatenate([first_half * cosine - second_half * sine_term, second_half * cosine + first_half * sine_term], axis=-1)

def angles(positions, head_width):
    half_width = head_width // 2
    frequency = jnp.exp(jnp.arange(half_width, dtype=jnp.float32) * (-2.0 * math.log(ROPE_BASE) / head_width))
    return positions.astype(jnp.float32)[..., None, None] * frequency

def token_positions(stretch_order, first_row, row_count, stretch_rows):
    row_index = first_row + jnp.arange(row_count, dtype=jnp.int32)
    slot_index = row_index // stretch_rows
    matches = slot_index[:, None] == jnp.arange(stretch_order.shape[1], dtype=jnp.int32)[None, :]
    picked = lax.optimization_barrier(jnp.sum(jnp.where(matches[None], stretch_order[:, None, :], 0), axis=-1))
    return picked * stretch_rows + row_index % stretch_rows

def apply_projection(inputs, matrix):
    return jnp.einsum('btd,de->bte', inputs, matrix, precision=lax.Precision.HIGHEST)

def attention(query_rows, keys, value_rows, positions):
    rows_per_block = min(512, SEQUENCE_LENGTH)
    heads_per_group = QUERY_HEADS // KEY_VALUE_HEADS
    score_scale = 1.0 / math.sqrt(HEAD_SIZE)
    count_of_blocks = SEQUENCE_LENGTH // rows_per_block
    blocks_of_query = query_rows.reshape(SEQUENCE_COUNT, count_of_blocks, rows_per_block, KEY_VALUE_HEADS, heads_per_group, HEAD_SIZE)
    position_blocks = positions.reshape(SEQUENCE_COUNT, count_of_blocks, rows_per_block)

    def one_block(operands):
        query_block, query_pos = operands
        scores = jnp.einsum('bqkgd,bckd->bkgqc', query_block, keys, precision=lax.Precision.HIGHEST) * score_scale
        scores = lower_backward(scores)
        allowed = positions[:, None, None, None, :] <= query_pos[:, None, None, :, None]
        scores = jnp.where(allowed, scores, NEG)
        probs = low(jax.nn.softmax(scores, axis=-1))
        return jnp.einsum('bkgqc,bckd->bqkgd', probs, value_rows, precision=lax.Precision.HIGHEST)
    results = lax.map(jax.checkpoint(one_block), (jnp.moveaxis(blocks_of_query, 1, 0), jnp.moveaxis(position_blocks, 1, 0)))
    return jnp.moveaxis(results, 0, 1).reshape(SEQUENCE_COUNT, SEQUENCE_LENGTH, QUERY_HEADS * HEAD_SIZE)

def layer(tokens, attention_norm, query_weight, key_projection, value_projection, query_norm, key_norm, output_weight, feedforward_norm, gate_weight, up_weight, down_weight, positions):
    phases = angles(positions, HEAD_SIZE)
    first_normed = low(norm_rows(tokens, attention_norm))
    query_raw = lower_backward(apply_projection(first_normed, query_weight)).reshape(SEQUENCE_COUNT, SEQUENCE_LENGTH, QUERY_HEADS, HEAD_SIZE)
    key_unnormed = lower_backward(apply_projection(first_normed, key_projection)).reshape(SEQUENCE_COUNT, SEQUENCE_LENGTH, KEY_VALUE_HEADS, HEAD_SIZE)
    value_rows = both_rounded(apply_projection(first_normed, value_projection)).reshape(SEQUENCE_COUNT, SEQUENCE_LENGTH, KEY_VALUE_HEADS, HEAD_SIZE)
    query_rows = both_rounded(rotary(norm_rows(query_raw, query_norm), phases))
    keys = both_rounded(rotary(norm_rows(key_unnormed, key_norm), phases))
    attended = both_rounded(attention(query_rows, keys, value_rows, positions))
    branch = lower_backward(apply_projection(attended, output_weight))
    resid = tokens + branch
    normed_two = low(norm_rows(resid, feedforward_norm))
    gate = lower_backward(apply_projection(normed_two, gate_weight))
    up_proj = lower_backward(apply_projection(normed_two, up_weight))
    hidden = low(jax.nn.silu(gate) * up_proj)
    return resid + lower_backward(apply_projection(hidden, down_weight))

def reference(tokens, attention_norm, query_weight, key_projection, value_projection, query_norm, key_norm, output_weight, feedforward_norm, gate_weight, up_weight, down_weight, stretch_order, out_cotangent):
    positions = token_positions(stretch_order, 0, SEQUENCE_LENGTH, STRETCH)
    params = tuple((item.astype(jnp.float32) for item in (tokens, attention_norm, query_weight, key_projection, value_projection, query_norm, key_norm, output_weight, feedforward_norm, gate_weight, up_weight, down_weight)))

    def forward(*inputs):
        return layer(*inputs, positions)
    result, pullback = jax.vjp(forward, *params)
    grads = pullback(out_cotangent.astype(jnp.float32))
    return (result.astype(jnp.bfloat16), grads[0].astype(jnp.bfloat16), grads[1], grads[2], grads[3], grads[4], grads[5], grads[6], grads[7], grads[8], grads[9], grads[10], grads[11])
```

```python
import math

import jax
import jax.numpy as jnp
from jax import lax
from jax.experimental import pallas as pl
from jax.experimental.pallas import tpu as pltpu
from jax.sharding import PartitionSpec as P

QUERY_HEADS = 16
KEY_VALUE_HEADS = 8
HEAD_SIZE = 128


EPS = 1e-06
NEG = -1e30
ROPE_BASE = 1000000.0


def passed_along(value, axis, by):
    count = lax.axis_size(axis)
    return lax.ppermute(value, axis, [(i, (i + by) % count) for i in range(count)])


def norm_rows(inputs, norm_gain):
    return inputs * lax.rsqrt(jnp.mean(inputs * inputs, axis=-1, keepdims=True) + EPS) * norm_gain


def rotary(inputs, phases):
    half_width = inputs.shape[-1] // 2
    cosine = jnp.cos(phases)
    sine_term = jnp.sin(phases)
    first_half = inputs[..., :half_width]
    second_half = inputs[..., half_width:]
    return jnp.concatenate(
        [
            first_half * cosine - second_half * sine_term,
            second_half * cosine + first_half * sine_term,
        ],
        axis=-1,
    )


def angles(positions, head_width):
    half_width = head_width // 2
    frequency = jnp.exp(
        jnp.arange(half_width, dtype=jnp.float32) * (-2.0 * math.log(ROPE_BASE) / head_width)
    )
    return positions.astype(jnp.float32)[..., None, None] * frequency


def token_positions(stretch_order, first_row, row_count, stretch_rows):
    row_index = first_row + jnp.arange(row_count, dtype=jnp.int32)
    slot_index = row_index // stretch_rows
    matches = slot_index[:, None] == jnp.arange(stretch_order.shape[1], dtype=jnp.int32)[None, :]
    picked = jnp.sum(jnp.where(matches[None], stretch_order[:, None, :], 0), axis=-1)
    return picked * stretch_rows + row_index % stretch_rows


def per_device_by_tokens(
    tokens,
    attention_norm,
    query_weight,
    key_projection,
    value_projection,
    query_norm,
    key_norm,
    output_weight,
    feedforward_norm,
    gate_weight,
    up_weight,
    down_weight,
    stretch_order,
    out_cotangent,
):
    count_of_heads = lax.axis_size("head")
    span_count = lax.axis_size("blk")
    span_index = lax.axis_index("blk")
    head_index = lax.axis_index("head")
    sequence_total = tokens.shape[0]
    local_rows = tokens.shape[1]
    group_rows = local_rows * count_of_heads
    stretch_rows = group_rows // 2
    heads_shared = KEY_VALUE_HEADS // count_of_heads
    heads_per_group = QUERY_HEADS // KEY_VALUE_HEADS
    score_scale = 1.0 / math.sqrt(HEAD_SIZE)
    gain_one, query_matrix, key_matrix, value_matrix, query_gain, key_gain, output_matrix = (
        lax.all_gather(attention_norm, ("blk", "head"), axis=0, tiled=True),
        lax.all_gather(query_weight, ("blk", "head"), axis=0, tiled=True),
        lax.all_gather(key_projection, ("blk", "head"), axis=0, tiled=True),
        lax.all_gather(value_projection, ("blk", "head"), axis=0, tiled=True),
        lax.all_gather(query_norm, ("blk", "head"), axis=0, tiled=True),
        lax.all_gather(key_norm, ("blk", "head"), axis=0, tiled=True),
        lax.all_gather(output_weight, ("blk", "head"), axis=0, tiled=True),
    )
    gain_two, gate_matrix, up_matrix, down_matrix = (
        lax.all_gather(feedforward_norm, ("blk", "head"), axis=0, tiled=True),
        lax.all_gather(gate_weight, ("blk", "head"), axis=0, tiled=True),
        lax.all_gather(up_weight, ("blk", "head"), axis=0, tiled=True),
        lax.all_gather(down_weight, ("blk", "head"), axis=0, tiled=True),
    )
    gain_one = gain_one.astype(jnp.float32)
    gain_two = gain_two.astype(jnp.float32)
    query_gain = query_gain.astype(jnp.float32)
    key_gain = key_gain.astype(jnp.float32)
    own_first = (span_index * count_of_heads + head_index) * local_rows
    own_pos = token_positions(stretch_order, own_first, local_rows, stretch_rows)
    group_pos = token_positions(stretch_order, span_index * group_rows, group_rows, stretch_rows)
    phases = angles(own_pos, HEAD_SIZE)
    tokens_wide = tokens.astype(jnp.float32)
    first_normed, norm_one_back = jax.vjp(norm_rows, tokens_wide, gain_one)
    first_normed = first_normed.astype(jnp.bfloat16)
    query_raw = jnp.einsum(
        "btd,de->bte", first_normed, query_matrix, preferred_element_type=jnp.float32
    ).reshape(sequence_total, local_rows, QUERY_HEADS, HEAD_SIZE)
    key_unnormed = jnp.einsum(
        "btd,de->bte", first_normed, key_matrix, preferred_element_type=jnp.float32
    ).reshape(sequence_total, local_rows, KEY_VALUE_HEADS, HEAD_SIZE)
    value_tokens = (
        jnp.einsum("btd,de->bte", first_normed, value_matrix, preferred_element_type=jnp.float32)
        .astype(jnp.bfloat16)
        .reshape(sequence_total, local_rows, KEY_VALUE_HEADS, HEAD_SIZE)
    )

    def heads_local(query_in, key_in, query_scale, key_scale):
        return (
            rotary(norm_rows(query_in, query_scale), phases),
            rotary(norm_rows(key_in, key_scale), phases),
        )

    (query_tokens, key_tokens), heads_back = jax.vjp(
        heads_local, query_raw, key_unnormed, query_gain, key_gain
    )
    query_tokens = query_tokens.astype(jnp.bfloat16)
    key_tokens = key_tokens.astype(jnp.bfloat16)
    query_group, key_group, value_group = (
        lax.all_to_all(query_tokens, "head", split_axis=2, concat_axis=1, tiled=True),
        lax.all_to_all(key_tokens, "head", split_axis=2, concat_axis=1, tiled=True),
        lax.all_to_all(value_tokens, "head", split_axis=2, concat_axis=1, tiled=True),
    )
    query_five = query_group.reshape(
        sequence_total, group_rows, heads_shared, heads_per_group, HEAD_SIZE
    )

    def block_update(carry, key_block, value_block, key_pos):
        run_max, run_sum, run_total = carry
        scores = (
            jnp.einsum(
                "bqkgd,bckd->bkgqc", query_five, key_block, preferred_element_type=jnp.float32
            )
            * score_scale
        )
        allowed = key_pos[:, None, None, None, :] <= group_pos[:, None, None, :, None]
        scores = jnp.where(allowed, scores, NEG)
        new_max = jnp.maximum(run_max, jnp.max(scores, axis=-1))
        exponent = jnp.where(allowed, jnp.exp(scores - new_max[..., None]), 0.0)
        factor = jnp.exp(run_max - new_max)
        new_sum = run_sum * factor + jnp.sum(exponent, axis=-1)
        new_total = run_total * factor[..., None] + jnp.einsum(
            "bkgqc,bckd->bkgqd",
            exponent.astype(jnp.bfloat16),
            value_block,
            preferred_element_type=jnp.float32,
        )
        return (new_max, new_sum, new_total)

    def fold_update(carry, key_block, value_block, key_pos):
        result = block_update(carry, key_block, value_block, key_pos)
        return result

    stat_shape = (sequence_total, heads_shared, heads_per_group, group_rows)
    start_state = (
        jnp.full(stat_shape, NEG, jnp.float32),
        jnp.zeros(stat_shape, jnp.float32),
        jnp.zeros(stat_shape + (HEAD_SIZE,), jnp.float32),
    )
    key_piece = lax.all_gather(key_group, "blk", axis=1, tiled=True)
    value_piece = lax.all_gather(value_group, "blk", axis=1, tiled=True)
    piece_rows = key_piece.shape[1]
    block_len = math.gcd(group_rows, piece_rows)

    def inner(block_number, carry_in):
        offset = block_number * block_len
        key_block = lax.dynamic_slice_in_dim(key_piece, offset, block_len, 1)
        value_block = lax.dynamic_slice_in_dim(value_piece, offset, block_len, 1)
        key_pos = token_positions(stretch_order, offset, block_len, stretch_rows)
        return fold_update(carry_in, key_block, value_block, key_pos)

    run_max, run_sum, run_total = lax.fori_loop(0, piece_rows // block_len, inner, start_state)
    log_total = run_max + jnp.log(run_sum)
    attended_five = run_total / run_sum[..., None]
    attended_group = (
        jnp.transpose(attended_five, (0, 3, 1, 2, 4))
        .reshape(sequence_total, group_rows, heads_shared * heads_per_group, HEAD_SIZE)
        .astype(jnp.bfloat16)
    )
    attended_tokens = lax.all_to_all(
        attended_group, "head", split_axis=1, concat_axis=2, tiled=True
    ).reshape(sequence_total, local_rows, QUERY_HEADS * HEAD_SIZE)
    branch = jnp.einsum(
        "bte,ed->btd", attended_tokens, output_matrix, preferred_element_type=jnp.float32
    )
    resid = tokens_wide + branch
    normed_two, norm_two_back = jax.vjp(norm_rows, resid, gain_two)
    normed_two = normed_two.astype(jnp.bfloat16)
    gate = jnp.einsum("btd,df->btf", normed_two, gate_matrix, preferred_element_type=jnp.float32)
    up_proj = jnp.einsum("btd,df->btf", normed_two, up_matrix, preferred_element_type=jnp.float32)

    def swish_product(gate_in, up_in):
        return jax.nn.silu(gate_in) * up_in

    hidden, swish_back = jax.vjp(swish_product, gate, up_proj)
    hidden = hidden.astype(jnp.bfloat16)
    layer_out = (
        resid + jnp.einsum("btf,fd->btd", hidden, down_matrix, preferred_element_type=jnp.float32)
    ).astype(jnp.bfloat16)
    gain_again, gate_matrix, up_matrix, down_matrix = (
        lax.all_gather(feedforward_norm, ("blk", "head"), axis=0, tiled=True),
        lax.all_gather(gate_weight, ("blk", "head"), axis=0, tiled=True),
        lax.all_gather(up_weight, ("blk", "head"), axis=0, tiled=True),
        lax.all_gather(down_weight, ("blk", "head"), axis=0, tiled=True),
    )
    down_gradient = jnp.einsum(
        "btf,btd->fd", hidden, out_cotangent, preferred_element_type=jnp.float32
    )
    hidden_gradient = jnp.einsum(
        "btd,fd->btf", out_cotangent, down_matrix, preferred_element_type=jnp.float32
    )
    gate_gradient, up_gradient = swish_back(hidden_gradient)
    gate_gradient = gate_gradient.astype(jnp.bfloat16)
    up_gradient = up_gradient.astype(jnp.bfloat16)
    gate_matrix_gradient = jnp.einsum(
        "btd,btf->df", normed_two, gate_gradient, preferred_element_type=jnp.float32
    )
    up_matrix_gradient = jnp.einsum(
        "btd,btf->df", normed_two, up_gradient, preferred_element_type=jnp.float32
    )
    normed_two_gradient = jnp.einsum(
        "btf,df->btd", gate_gradient, gate_matrix, preferred_element_type=jnp.float32
    ) + jnp.einsum("btf,df->btd", up_gradient, up_matrix, preferred_element_type=jnp.float32)
    resid_part, gain_two_gradient = norm_two_back(normed_two_gradient)
    resid_gradient = out_cotangent.astype(jnp.float32) + resid_part
    feedforward_sums = (
        lax.psum_scatter(gain_two_gradient, ("blk", "head"), scatter_dimension=0, tiled=True),
        lax.psum_scatter(gate_matrix_gradient, ("blk", "head"), scatter_dimension=0, tiled=True),
        lax.psum_scatter(up_matrix_gradient, ("blk", "head"), scatter_dimension=0, tiled=True),
        lax.psum_scatter(down_gradient, ("blk", "head"), scatter_dimension=0, tiled=True),
    )
    gain_again, query_matrix, key_matrix, value_matrix, query_again, key_again, output_matrix = (
        lax.all_gather(attention_norm, ("blk", "head"), axis=0, tiled=True),
        lax.all_gather(query_weight, ("blk", "head"), axis=0, tiled=True),
        lax.all_gather(key_projection, ("blk", "head"), axis=0, tiled=True),
        lax.all_gather(value_projection, ("blk", "head"), axis=0, tiled=True),
        lax.all_gather(query_norm, ("blk", "head"), axis=0, tiled=True),
        lax.all_gather(key_norm, ("blk", "head"), axis=0, tiled=True),
        lax.all_gather(output_weight, ("blk", "head"), axis=0, tiled=True),
    )
    branch_gradient = resid_gradient.astype(jnp.bfloat16)
    output_matrix_gradient = jnp.einsum(
        "bte,btd->ed", attended_tokens, branch_gradient, preferred_element_type=jnp.float32
    )
    attended_gradient = (
        jnp.einsum(
            "btd,ed->bte", branch_gradient, output_matrix, preferred_element_type=jnp.float32
        )
        .astype(jnp.bfloat16)
        .reshape(sequence_total, local_rows, QUERY_HEADS, HEAD_SIZE)
    )
    attended_grad_group = lax.all_to_all(
        attended_gradient, "head", split_axis=2, concat_axis=1, tiled=True
    ).reshape(sequence_total, group_rows, heads_shared, heads_per_group, HEAD_SIZE)
    delta = jnp.sum(
        jnp.transpose(attended_grad_group.astype(jnp.float32), (0, 2, 3, 1, 4)) * attended_five,
        axis=-1,
    )

    def block_grads(sums_in, key_current, value_current, key_pos):
        key_sum, value_sum, query_sum = sums_in
        scores = (
            jnp.einsum(
                "bqkgd,bckd->bkgqc", query_five, key_current, preferred_element_type=jnp.float32
            )
            * score_scale
        )
        allowed = key_pos[:, None, None, None, :] <= group_pos[:, None, None, :, None]
        weights = jnp.where(allowed, jnp.exp(scores - log_total[..., None]), 0.0)
        probs = weights.astype(jnp.bfloat16)
        value_sum = value_sum + jnp.einsum(
            "bkgqc,bqkgd->bckd", probs, attended_grad_group, preferred_element_type=jnp.float32
        )
        probs_gradient = jnp.einsum(
            "bqkgd,bckd->bkgqc",
            attended_grad_group,
            value_current,
            preferred_element_type=jnp.float32,
        )
        scores_gradient = (weights * (probs_gradient - delta[..., None])).astype(jnp.bfloat16)
        query_sum = (
            query_sum
            + jnp.einsum(
                "bkgqc,bckd->bqkgd",
                scores_gradient,
                key_current,
                preferred_element_type=jnp.float32,
            )
            * score_scale
        )
        key_sum = (
            key_sum
            + jnp.einsum(
                "bkgqc,bqkgd->bckd", scores_gradient, query_five, preferred_element_type=jnp.float32
            )
            * score_scale
        )
        return (key_sum, value_sum, query_sum)

    def pass_step(step_index, carry):
        key_current, value_current, key_sum, value_sum, query_sum = carry
        anchor = (span_index - step_index) % span_count
        key_pos = token_positions(stretch_order, anchor * group_rows, group_rows, stretch_rows)
        key_sum, value_sum, query_sum = block_grads(
            (key_sum, value_sum, query_sum), key_current, value_current, key_pos
        )
        key_current, value_current = passed_along((key_current, value_current), "blk", 1)
        key_sum, value_sum = (
            passed_along(key_sum.astype(jnp.bfloat16), "blk", 1).astype(key_sum.dtype),
            passed_along(value_sum.astype(jnp.bfloat16), "blk", 1).astype(value_sum.dtype),
        )
        return (key_current, value_current, key_sum, value_sum, query_sum)

    kv_zeros = jnp.zeros((sequence_total, group_rows, heads_shared, HEAD_SIZE), jnp.float32)
    query_zeros = jnp.zeros(
        (sequence_total, group_rows, heads_shared, heads_per_group, HEAD_SIZE), jnp.float32
    )
    final_state = lax.fori_loop(
        0, span_count, pass_step, (key_group, value_group, kv_zeros, kv_zeros, query_zeros)
    )
    key_grad_group = final_state[2].astype(jnp.bfloat16)
    value_grad_group = final_state[3].astype(jnp.bfloat16)
    query_grad_group = (
        final_state[4]
        .astype(jnp.bfloat16)
        .reshape(sequence_total, group_rows, heads_shared * heads_per_group, HEAD_SIZE)
    )
    query_grad_tokens, key_grad_tokens, value_gradient_tokens = (
        lax.all_to_all(query_grad_group, "head", split_axis=1, concat_axis=2, tiled=True),
        lax.all_to_all(key_grad_group, "head", split_axis=1, concat_axis=2, tiled=True),
        lax.all_to_all(value_grad_group, "head", split_axis=1, concat_axis=2, tiled=True),
    )
    query_raw_gradient, key_unnormed_gradient, query_gain_gradient, key_gain_gradient = heads_back(
        (query_grad_tokens.astype(jnp.float32), key_grad_tokens.astype(jnp.float32))
    )
    query_raw_gradient = query_raw_gradient.astype(jnp.bfloat16).reshape(
        sequence_total, local_rows, QUERY_HEADS * HEAD_SIZE
    )
    key_unnormed_gradient = key_unnormed_gradient.astype(jnp.bfloat16).reshape(
        sequence_total, local_rows, KEY_VALUE_HEADS * HEAD_SIZE
    )
    value_unnormed_gradient = value_gradient_tokens.reshape(
        sequence_total, local_rows, KEY_VALUE_HEADS * HEAD_SIZE
    )
    query_matrix_gradient = jnp.einsum(
        "btd,bte->de", first_normed, query_raw_gradient, preferred_element_type=jnp.float32
    )
    key_matrix_gradient = jnp.einsum(
        "btd,bte->de", first_normed, key_unnormed_gradient, preferred_element_type=jnp.float32
    )
    value_matrix_gradient = jnp.einsum(
        "btd,bte->de", first_normed, value_unnormed_gradient, preferred_element_type=jnp.float32
    )
    normed_one_gradient = jnp.einsum(
        "bte,de->btd", query_raw_gradient, query_matrix, preferred_element_type=jnp.float32
    )
    normed_one_gradient = normed_one_gradient + jnp.einsum(
        "bte,de->btd", key_unnormed_gradient, key_matrix, preferred_element_type=jnp.float32
    )
    normed_one_gradient = normed_one_gradient + jnp.einsum(
        "bte,de->btd", value_unnormed_gradient, value_matrix, preferred_element_type=jnp.float32
    )
    token_part, gain_one_gradient = norm_one_back(normed_one_gradient)
    tokens_gradient = (resid_gradient + token_part).astype(jnp.bfloat16)
    attention_sums = (
        lax.psum_scatter(gain_one_gradient, ("blk", "head"), scatter_dimension=0, tiled=True),
        lax.psum_scatter(query_matrix_gradient, ("blk", "head"), scatter_dimension=0, tiled=True),
        lax.psum_scatter(key_matrix_gradient, ("blk", "head"), scatter_dimension=0, tiled=True),
        lax.psum_scatter(value_matrix_gradient, ("blk", "head"), scatter_dimension=0, tiled=True),
        lax.psum_scatter(query_gain_gradient, ("blk", "head"), scatter_dimension=0, tiled=True),
        lax.psum_scatter(key_gain_gradient, ("blk", "head"), scatter_dimension=0, tiled=True),
        lax.psum_scatter(output_matrix_gradient, ("blk", "head"), scatter_dimension=0, tiled=True),
    )
    return (
        layer_out,
        tokens_gradient,
        attention_sums[0],
        attention_sums[1],
        attention_sums[2],
        attention_sums[3],
        attention_sums[4],
        attention_sums[5],
        attention_sums[6],
        feedforward_sums[0],
        feedforward_sums[1],
        feedforward_sums[2],
        feedforward_sums[3],
    )


LOG2E = math.log2(math.e)
STRIP = 128
CHUNK = 512
ALONG = (((1,), (1,)), ((), ()))
DOWN = (((0,), (0,)), ((), ()))


def two_heads(block):
    return jnp.concatenate([block[:, :HEAD_SIZE], block[:, HEAD_SIZE:]], axis=0)


def side_by_side(rows):
    half = rows.shape[0] // 2
    return jnp.concatenate([rows[:half], rows[half:]], axis=1)


def attend_kernel(place_ref, order_ref, q_ref, kv_ref, out_ref, lse_ref, keys, values):
    step = pl.program_id(0)

    @pl.when(step == 0)
    def _():
        values[:, HEAD_SIZE:] = jnp.ones((values.shape[0], HEAD_SIZE), jnp.bfloat16)

        def sort(index, carry):
            source = pl.multiple_of(order_ref[index] * STRIP, STRIP)
            target = pl.multiple_of(index * STRIP, STRIP)
            keys[pl.ds(target, STRIP), :] = kv_ref[pl.ds(source, STRIP), :HEAD_SIZE]
            values[pl.ds(target, STRIP), :HEAD_SIZE] = kv_ref[pl.ds(source, STRIP), HEAD_SIZE:]
            return carry

        lax.fori_loop(0, kv_ref.shape[0] // STRIP, sort, 0)

    place = place_ref[step]
    queries = two_heads(q_ref[...])
    last = place // (CHUNK // STRIP)

    def part(index, total, masked):
        first = pl.multiple_of(index * CHUNK, CHUNK)
        scores = lax.dot_general(
            queries, keys[pl.ds(first, CHUNK), :], ALONG, preferred_element_type=jnp.float32
        )
        weights = jnp.exp2(scores)
        if masked:
            row = lax.broadcasted_iota(jnp.int32, scores.shape, 0) % STRIP
            column = lax.broadcasted_iota(jnp.int32, scores.shape, 1)
            weights = jnp.where(column - row <= place * STRIP - first, weights, 0.0)
        return total + jnp.dot(
            weights.astype(jnp.bfloat16),
            values[pl.ds(first, CHUNK), :],
            preferred_element_type=jnp.float32,
        )

    total = jnp.zeros((2 * STRIP, 2 * HEAD_SIZE), jnp.float32)
    total = lax.fori_loop(0, last, lambda index, t: part(index, t, False), total)
    total = part(last, total, True)
    norm = total[:, HEAD_SIZE:]
    out_ref[...] = side_by_side(total[:, :HEAD_SIZE] / norm).astype(jnp.bfloat16)
    lse_ref[0] = jnp.transpose(jnp.log2(norm))[:8]


def attend(place, order, queries, kv):
    rows, width = queries.shape
    steps = rows // STRIP
    whole = pl.BlockSpec(kv.shape, lambda i, *_: (0, 0))
    strip = pl.BlockSpec((STRIP, width), lambda i, *_: (i, 0))
    flops = 4 * rows * 2 * kv.shape[0] * HEAD_SIZE // 2
    return pl.pallas_call(
        attend_kernel,
        grid_spec=pltpu.PrefetchScalarGridSpec(
            num_scalar_prefetch=2,
            grid=(steps,),
            in_specs=[strip, whole],
            out_specs=[strip, pl.BlockSpec((1, 8, 2 * STRIP), lambda i, *_: (i, 0, 0))],
            scratch_shapes=[
                pltpu.VMEM((kv.shape[0], HEAD_SIZE), jnp.bfloat16),
                pltpu.VMEM((kv.shape[0], 2 * HEAD_SIZE), jnp.bfloat16),
            ],
        ),
        out_shape=[
            jax.ShapeDtypeStruct((rows, width), jnp.bfloat16),
            jax.ShapeDtypeStruct((steps, 8, 2 * STRIP), jnp.float32),
        ],
        cost_estimate=pl.CostEstimate(
            flops=flops, bytes_accessed=kv.size * 2 + queries.size * 4, transcendentals=rows * kv.shape[0]
        ),
        name="attend",
    )(place, order, queries, kv)


def attend_back_kernel(
    place_ref, order_ref, q_ref, grad_ref, out_ref, lse_ref, kv_ref, dq_ref, dkv_ref,
    keys, values, key_sums, value_sums,
):
    step = pl.program_id(0)
    strips = kv_ref.shape[0] // STRIP

    @pl.when(step == 0)
    def _():
        key_sums[...] = jnp.zeros_like(key_sums)
        value_sums[...] = jnp.zeros_like(value_sums)

        def sort(index, carry):
            source = pl.multiple_of(order_ref[index] * STRIP, STRIP)
            target = pl.multiple_of(index * STRIP, STRIP)
            keys[pl.ds(target, STRIP), :] = kv_ref[pl.ds(source, STRIP), :HEAD_SIZE]
            values[pl.ds(target, STRIP), :] = kv_ref[pl.ds(source, STRIP), HEAD_SIZE:]
            return carry

        lax.fori_loop(0, strips, sort, 0)

    place = place_ref[step]
    queries = two_heads(q_ref[...])
    grads = two_heads(grad_ref[...])
    product = grads.astype(jnp.float32) * two_heads(out_ref[...]).astype(jnp.float32)
    delta = jnp.sum(jnp.transpose(product), axis=0, keepdims=True)
    lse = lse_ref[0, :1]
    last = place // (CHUNK // STRIP)

    def part(index, total, masked):
        first = pl.multiple_of(index * CHUNK, CHUNK)
        here = pl.ds(first, CHUNK)
        key_rows = keys[here, :]
        scores = lax.dot_general(key_rows, queries, ALONG, preferred_element_type=jnp.float32)
        weights = jnp.exp2(scores - lse)
        if masked:
            row = lax.broadcasted_iota(jnp.int32, scores.shape, 0)
            column = lax.broadcasted_iota(jnp.int32, scores.shape, 1) % STRIP
            weights = jnp.where(row - column <= place * STRIP - first, weights, 0.0)
        slopes = lax.dot_general(
            values[here, :], grads, ALONG, preferred_element_type=jnp.float32
        )
        score_grads = (weights * (slopes - delta)).astype(jnp.bfloat16)
        value_sums[here, :] += jnp.dot(
            weights.astype(jnp.bfloat16), grads, preferred_element_type=jnp.float32
        )
        key_sums[here, :] += jnp.dot(score_grads, queries, preferred_element_type=jnp.float32)
        return total + lax.dot_general(
            score_grads, key_rows, DOWN, preferred_element_type=jnp.float32
        )

    total = jnp.zeros((2 * STRIP, HEAD_SIZE), jnp.float32)
    total = lax.fori_loop(0, last, lambda index, t: part(index, t, False), total)
    total = part(last, total, True)
    dq_ref[...] = side_by_side(total * (1.0 / math.sqrt(HEAD_SIZE))).astype(jnp.bfloat16)

    @pl.when(step == pl.num_programs(0) - 1)
    def _():
        def spread(index, carry):
            target = pl.multiple_of(order_ref[index] * STRIP, STRIP)
            source = pl.multiple_of(index * STRIP, STRIP)
            dkv_ref[pl.ds(target, STRIP), :HEAD_SIZE] = (
                key_sums[pl.ds(source, STRIP), :] * (1.0 / LOG2E)
            ).astype(jnp.bfloat16)
            dkv_ref[pl.ds(target, STRIP), HEAD_SIZE:] = value_sums[
                pl.ds(source, STRIP), :
            ].astype(jnp.bfloat16)
            return carry

        lax.fori_loop(0, strips, spread, 0)


def attend_back(place, order, queries, grads, attended, lse, kv):
    rows, width = queries.shape
    steps = rows // STRIP
    total = kv.shape[0]
    whole = pl.BlockSpec(kv.shape, lambda i, *_: (0, 0))
    strip = pl.BlockSpec((STRIP, width), lambda i, *_: (i, 0))
    return pl.pallas_call(
        attend_back_kernel,
        grid_spec=pltpu.PrefetchScalarGridSpec(
            num_scalar_prefetch=2,
            grid=(steps,),
            in_specs=[
                strip, strip, strip, pl.BlockSpec((1, 8, 2 * STRIP), lambda i, *_: (i, 0, 0)), whole,
            ],
            out_specs=[strip, whole],
            scratch_shapes=[
                pltpu.VMEM((total, HEAD_SIZE), jnp.bfloat16),
                pltpu.VMEM((total, HEAD_SIZE), jnp.bfloat16),
                pltpu.VMEM((total, HEAD_SIZE), jnp.float32),
                pltpu.VMEM((total, HEAD_SIZE), jnp.float32),
            ],
        ),
        out_shape=[
            jax.ShapeDtypeStruct((rows, width), jnp.bfloat16),
            jax.ShapeDtypeStruct(kv.shape, jnp.bfloat16),
        ],
        cost_estimate=pl.CostEstimate(
            flops=10 * rows * 2 * total * HEAD_SIZE // 2,
            bytes_accessed=kv.size * 4 + queries.size * 8,
            transcendentals=rows * total,
        ),
        name="attend_back",
    )(place, order, queries, grads, attended, lse, kv)


def matmul(left, right, dims=(((1,), (0,)), ((), ()))):
    return lax.dot_general(left, right, dims, preferred_element_type=jnp.float32)


def gather_blk(rows):
    return lax.all_gather(rows, "blk", axis=0, tiled=True)


def scatter_blk(rows):
    return lax.psum_scatter(rows, "blk", scatter_dimension=0, tiled=True)


def exchange_blk(pieces):
    return lax.all_to_all(pieces, "blk", split_axis=0, concat_axis=0, tiled=True)


def gather_head(rows):
    return lax.all_gather(rows, "head", axis=0, tiled=True)


def scatter_head(rows):
    return lax.psum_scatter(rows, "head", scatter_dimension=0, tiled=True)


def inverse_rms(rows):
    return lax.rsqrt(jnp.mean(rows * rows, axis=-1, keepdims=True) + EPS)


def per_device(
    tokens,
    attention_norm,
    query_weight,
    key_projection,
    value_projection,
    query_norm,
    key_norm,
    output_weight,
    feedforward_norm,
    gate_weight,
    up_weight,
    down_weight,
    stretch_order,
    out_cotangent,
):
    blk_count = lax.axis_size("blk")
    head_count = lax.axis_size("head")
    head_index = lax.axis_index("head")
    narrow, wide = jnp.bfloat16, jnp.float32
    tokens, out_cotangent = tokens[0], out_cotangent[0]
    local_rows, model_width = tokens.shape
    group_rows = local_rows * blk_count
    weight_rows = query_weight.shape[0]
    ff_local = gate_weight.shape[1] // blk_count
    group_heads = QUERY_HEADS // blk_count
    query_cols = group_heads * HEAD_SIZE
    attn_cols = query_cols + 2 * HEAD_SIZE
    strip_count = blk_count * head_count
    halves = strip_count // stretch_order.shape[1]

    def by_head(rows):
        shape = (rows.shape[0], blk_count, head_count, weight_rows)
        return rows.reshape(shape).transpose(0, 2, 1, 3).reshape(rows.shape)

    def by_blk(rows):
        shape = (rows.shape[0], head_count, blk_count, weight_rows)
        return rows.reshape(shape).transpose(0, 2, 1, 3).reshape(rows.shape)

    attn_pieces = jnp.concatenate(
        [
            query_weight.reshape(weight_rows, blk_count, query_cols),
            key_projection.reshape(weight_rows, blk_count, HEAD_SIZE),
            value_projection.reshape(weight_rows, blk_count, HEAD_SIZE),
        ],
        axis=2,
    ).transpose(1, 0, 2)
    small = query_norm.shape[0]
    gains = jnp.concatenate([attention_norm, feedforward_norm, query_norm, key_norm])
    gains = jnp.pad(gains, (0, attn_cols - gains.shape[0]))[None, None, :]
    gains = jnp.pad(gains, ((0, 0), (0, 15), (0, 0)))
    attn_pieces = jnp.concatenate(
        [attn_pieces, jnp.broadcast_to(gains, (blk_count, 16, attn_cols))], axis=1
    )
    attn_all = gather_head(exchange_blk(attn_pieces)).reshape(
        head_count, blk_count, weight_rows + 16, attn_cols
    )
    attn_matrix = attn_all[:, :, :weight_rows].reshape(model_width, attn_cols)
    gain_rows = attn_all[:, :, weight_rows]
    gain_one = gain_rows[:, :, :weight_rows].reshape(1, model_width).astype(wide)
    gain_two_rows = gain_rows[:, :, weight_rows : 2 * weight_rows].astype(wide)
    gain_two = gain_two_rows.transpose(1, 0, 2).reshape(1, model_width)
    gain_one_natural = by_blk(gain_one)
    at = 2 * weight_rows
    query_gain = gain_rows[:, :, at : at + small].transpose(1, 0, 2).reshape(HEAD_SIZE)
    key_gain = gain_rows[:, :, at + small : at + 2 * small].transpose(1, 0, 2).reshape(HEAD_SIZE)
    query_gain, key_gain = query_gain.astype(wide), key_gain.astype(wide)

    ff_pieces = jnp.concatenate(
        [
            gate_weight.reshape(weight_rows, blk_count, ff_local),
            up_weight.reshape(weight_rows, blk_count, ff_local),
        ],
        axis=2,
    ).transpose(1, 0, 2)
    ff_matrix = gather_head(exchange_blk(ff_pieces)).reshape(model_width, 2 * ff_local)
    down_matrix = gather_head(down_weight)
    output_matrix = lax.all_gather(output_weight, ("blk", "head"), axis=0, tiled=True)

    strip_blk = jnp.arange(strip_count, dtype=jnp.int32) % blk_count
    strip_head = jnp.arange(strip_count, dtype=jnp.int32) // blk_count
    strip = strip_blk * head_count + strip_head
    slots = jnp.arange(stretch_order.shape[1], dtype=jnp.int32)
    held = jnp.sum(
        jnp.where((strip // halves)[:, None] == slots[None, :], stretch_order, 0), axis=1
    )
    strip_place = held * halves + strip % halves
    ranks = jnp.arange(strip_count, dtype=jnp.int32)
    order = jnp.sum(
        jnp.where(strip_place[None, :] == ranks[:, None], ranks[None, :], 0), axis=1
    ).astype(jnp.int32)
    place = jnp.sum(
        jnp.where(
            jnp.arange(head_count, dtype=jnp.int32)[:, None] == head_index,
            strip_place.reshape(head_count, blk_count),
            0,
        ),
        axis=0,
    ).astype(jnp.int32)
    positions = (
        place[:, None] * local_rows + jnp.arange(local_rows, dtype=jnp.int32)[None, :]
    ).reshape(group_rows)
    phases = angles(positions, HEAD_SIZE)

    tokens_wide = tokens.astype(wide)
    group_tokens = gather_blk(by_head(tokens)).astype(wide)
    first_normed = (group_tokens * inverse_rms(group_tokens) * gain_one).astype(narrow)
    attn_raw = matmul(first_normed, attn_matrix)
    query_raw = attn_raw[:, :query_cols].reshape(group_rows, group_heads, HEAD_SIZE)
    key_raw = attn_raw[:, query_cols : query_cols + HEAD_SIZE].reshape(group_rows, 1, HEAD_SIZE)
    value_rows = attn_raw[:, query_cols + HEAD_SIZE :].astype(narrow)

    def heads_local(query_in, key_in, query_scale, key_scale):
        return (
            rotary(norm_rows(query_in, query_scale), phases),
            rotary(norm_rows(key_in, key_scale), phases),
        )

    (query_rows, key_rows), heads_back = jax.vjp(
        heads_local, query_raw, key_raw, query_gain, key_gain
    )
    query_rows = (query_rows * (LOG2E / math.sqrt(HEAD_SIZE))).astype(narrow)
    query_rows = query_rows.reshape(group_rows, query_cols)
    kv = jnp.concatenate([key_rows.reshape(group_rows, HEAD_SIZE).astype(narrow), value_rows], 1)
    kv = gather_head(kv)
    attended_heads, lse = attend(place, order, query_rows, kv)
    attended = (
        exchange_blk(attended_heads.reshape(blk_count, local_rows, query_cols))
        .transpose(1, 0, 2)
        .reshape(local_rows, QUERY_HEADS * HEAD_SIZE)
    )

    resid = tokens_wide + matmul(attended, output_matrix)
    rho_two = inverse_rms(resid)
    unit_two = resid * rho_two
    second_normed = gather_blk(by_head((unit_two * gain_two).astype(narrow)))
    group_cotangent = gather_blk(out_cotangent)
    ff_raw = matmul(second_normed, ff_matrix)
    gate, up_proj = ff_raw[:, :ff_local], ff_raw[:, ff_local:]
    sigma = jax.nn.sigmoid(gate)
    swish = gate * sigma
    hidden = (swish * up_proj).astype(narrow)
    out_part = scatter_blk(matmul(hidden, down_matrix).astype(narrow))
    layer_out = (resid + out_part.astype(wide)).astype(narrow)

    hidden_gradient = matmul(group_cotangent, down_matrix, ALONG)
    gate_gradient = hidden_gradient * up_proj * (sigma * (1.0 + gate * (1.0 - sigma)))
    ff_gradient = jnp.concatenate([gate_gradient, hidden_gradient * swish], 1).astype(narrow)
    second_gradient = matmul(ff_gradient, ff_matrix, ALONG).astype(narrow)
    second_gradient = by_blk(scatter_blk(second_gradient)).astype(wide)
    down_gradient = scatter_head(matmul(hidden, group_cotangent, DOWN).astype(narrow))
    ff_matrix_gradient = scatter_head(matmul(second_normed, ff_gradient, DOWN).astype(narrow))
    ff_matrix_gradient = exchange_blk(
        ff_matrix_gradient.reshape(blk_count, weight_rows, 2 * ff_local)
    ).astype(wide)
    gate_weight_gradient = (
        ff_matrix_gradient[:, :, :ff_local].transpose(1, 0, 2).reshape(gate_weight.shape)
    )
    up_weight_gradient = (
        ff_matrix_gradient[:, :, ff_local:].transpose(1, 0, 2).reshape(up_weight.shape)
    )
    feedforward_norm_gradient = (
        jnp.sum(gate_weight_gradient * gate_weight.astype(wide), axis=1)
        + jnp.sum(up_weight_gradient * up_weight.astype(wide), axis=1)
    ) / feedforward_norm.astype(wide)
    scaled = gain_two * second_gradient
    resid_gradient = out_cotangent.astype(wide) + rho_two * (
        scaled - unit_two * jnp.mean(unit_two * scaled, axis=-1, keepdims=True)
    )

    branch_gradient = resid_gradient.astype(narrow)
    attended_gradient = (
        matmul(branch_gradient, output_matrix, ALONG)
        .astype(narrow)
        .reshape(local_rows, blk_count, query_cols)
        .transpose(1, 0, 2)
    )
    attended_gradient = exchange_blk(attended_gradient).reshape(group_rows, query_cols)
    output_weight_gradient = lax.psum_scatter(
        matmul(attended, branch_gradient, DOWN).astype(narrow),
        ("blk", "head"),
        scatter_dimension=0,
        tiled=True,
    ).astype(wide)
    query_grads, kv_grads = attend_back(
        place, order, query_rows, attended_gradient, attended_heads, lse, kv
    )
    kv_grads = scatter_head(kv_grads)
    query_raw_gradient, key_raw_gradient, query_gain_part, key_gain_part = heads_back(
        (
            query_grads.reshape(group_rows, group_heads, HEAD_SIZE).astype(wide),
            kv_grads[:, :HEAD_SIZE].reshape(group_rows, 1, HEAD_SIZE).astype(wide),
        )
    )
    attn_gradient = jnp.concatenate(
        [
            query_raw_gradient.reshape(group_rows, query_cols).astype(narrow),
            key_raw_gradient.reshape(group_rows, HEAD_SIZE).astype(narrow),
            kv_grads[:, HEAD_SIZE:],
        ],
        axis=1,
    )
    first_gradient = scatter_blk(matmul(attn_gradient, attn_matrix, ALONG).astype(narrow))
    first_gradient = by_blk(first_gradient).astype(wide)
    attn_matrix_gradient = (
        matmul(first_normed, attn_gradient, DOWN)
        .astype(narrow)
        .reshape(head_count, blk_count, weight_rows, attn_cols)
    )
    gain_parts = jnp.stack(
        [
            query_gain_part.reshape(blk_count, head_count, small),
            key_gain_part.reshape(blk_count, head_count, small),
        ],
        axis=2,
    ).transpose(1, 0, 2, 3)
    gain_parts = gain_parts.reshape(head_count, blk_count, 1, 2 * small).astype(narrow)
    gain_parts = jnp.pad(gain_parts, ((0, 0), (0, 0), (0, 15), (0, attn_cols - 2 * small)))
    attn_matrix_gradient = jnp.concatenate([attn_matrix_gradient, gain_parts], axis=2)
    attn_matrix_gradient = exchange_blk(
        scatter_head(
            attn_matrix_gradient.reshape(head_count * blk_count, weight_rows + 16, attn_cols)
        )
    ).astype(wide)
    attn_rows = attn_matrix_gradient[:, :weight_rows]
    query_weight_gradient = (
        attn_rows[:, :, :query_cols].transpose(1, 0, 2).reshape(query_weight.shape)
    )
    key_weight_gradient = (
        attn_rows[:, :, query_cols : query_cols + HEAD_SIZE]
        .transpose(1, 0, 2)
        .reshape(key_projection.shape)
    )
    value_weight_gradient = (
        attn_rows[:, :, query_cols + HEAD_SIZE :].transpose(1, 0, 2).reshape(value_projection.shape)
    )
    gain_sums = jnp.sum(attn_matrix_gradient[:, weight_rows], axis=0)
    attention_norm_gradient = (
        jnp.sum(query_weight_gradient * query_weight.astype(wide), axis=1)
        + jnp.sum(key_weight_gradient * key_projection.astype(wide), axis=1)
        + jnp.sum(value_weight_gradient * value_projection.astype(wide), axis=1)
    ) / attention_norm.astype(wide)
    rho_one = inverse_rms(tokens_wide)
    unit_one = tokens_wide * rho_one
    scaled = gain_one_natural * first_gradient
    tokens_gradient = resid_gradient + rho_one * (
        scaled - unit_one * jnp.mean(unit_one * scaled, axis=-1, keepdims=True)
    )
    return (
        layer_out[None],
        tokens_gradient.astype(narrow)[None],
        attention_norm_gradient,
        query_weight_gradient,
        key_weight_gradient,
        value_weight_gradient,
        gain_sums[:small],
        gain_sums[small : 2 * small],
        output_weight_gradient,
        feedforward_norm_gradient,
        gate_weight_gradient,
        up_weight_gradient,
        down_gradient.astype(wide),
    )


def solution(mesh):
    placed = (
        P(None, ("blk", "head"), None),
        P(("blk", "head")),
        P(("blk", "head"), None),
        P(("blk", "head"), None),
        P(("blk", "head"), None),
        P(("blk", "head")),
        P(("blk", "head")),
        P(("blk", "head"), None),
        P(("blk", "head")),
        P(("blk", "head"), None),
        P(("blk", "head"), None),
        P(("blk", "head"), None),
        P(),
        P(None, ("blk", "head"), None),
    )
    fits = mesh.shape["blk"] == KEY_VALUE_HEADS and mesh.shape["head"] == 4
    return jax.shard_map(
        per_device if fits else per_device_by_tokens,
        mesh=mesh,
        in_specs=placed,
        out_specs=(
            P(None, ("blk", "head"), None),
            P(None, ("blk", "head"), None),
            P(("blk", "head")),
            P(("blk", "head"), None),
            P(("blk", "head"), None),
            P(("blk", "head"), None),
            P(("blk", "head")),
            P(("blk", "head")),
            P(("blk", "head"), None),
            P(("blk", "head")),
            P(("blk", "head"), None),
            P(("blk", "head"), None),
            P(("blk", "head"), None),
        ),
        check_vma=False,
    )
```

```python
import math

import jax
import jax.numpy as jnp
from jax import lax
from jax.experimental import pallas as pl
from jax.experimental.pallas import tpu as pltpu
from jax.sharding import PartitionSpec as P

QUERY_HEADS = 16
KEY_VALUE_HEADS = 8
HEAD_SIZE = 128


EPS = 1e-06
NEG = -1e30
ROPE_BASE = 1000000.0


def passed_along(value, axis, by):
    count = lax.axis_size(axis)
    return lax.ppermute(value, axis, [(i, (i + by) % count) for i in range(count)])


def norm_rows(inputs, norm_gain):
    return inputs * lax.rsqrt(jnp.mean(inputs * inputs, axis=-1, keepdims=True) + EPS) * norm_gain


def rotary(inputs, phases):
    half_width = inputs.shape[-1] // 2
    cosine = jnp.cos(phases)
    sine_term = jnp.sin(phases)
    first_half = inputs[..., :half_width]
    second_half = inputs[..., half_width:]
    return jnp.concatenate(
        [
            first_half * cosine - second_half * sine_term,
            second_half * cosine + first_half * sine_term,
        ],
        axis=-1,
    )


def angles(positions, head_width):
    half_width = head_width // 2
    frequency = jnp.exp(
        jnp.arange(half_width, dtype=jnp.float32) * (-2.0 * math.log(ROPE_BASE) / head_width)
    )
    return positions.astype(jnp.float32)[..., None, None] * frequency


def token_positions(stretch_order, first_row, row_count, stretch_rows):
    row_index = first_row + jnp.arange(row_count, dtype=jnp.int32)
    slot_index = row_index // stretch_rows
    matches = slot_index[:, None] == jnp.arange(stretch_order.shape[1], dtype=jnp.int32)[None, :]
    picked = jnp.sum(jnp.where(matches[None], stretch_order[:, None, :], 0), axis=-1)
    return picked * stretch_rows + row_index % stretch_rows


def per_device_by_tokens(
    tokens,
    attention_norm,
    query_weight,
    key_projection,
    value_projection,
    query_norm,
    key_norm,
    output_weight,
    feedforward_norm,
    gate_weight,
    up_weight,
    down_weight,
    stretch_order,
    out_cotangent,
):
    count_of_heads = lax.axis_size("head")
    span_count = lax.axis_size("blk")
    span_index = lax.axis_index("blk")
    head_index = lax.axis_index("head")
    sequence_total = tokens.shape[0]
    local_rows = tokens.shape[1]
    group_rows = local_rows * count_of_heads
    stretch_rows = group_rows // 2
    heads_shared = KEY_VALUE_HEADS // count_of_heads
    heads_per_group = QUERY_HEADS // KEY_VALUE_HEADS
    score_scale = 1.0 / math.sqrt(HEAD_SIZE)
    gain_one, query_matrix, key_matrix, value_matrix, query_gain, key_gain, output_matrix = (
        lax.all_gather(attention_norm, ("blk", "head"), axis=0, tiled=True),
        lax.all_gather(query_weight, ("blk", "head"), axis=0, tiled=True),
        lax.all_gather(key_projection, ("blk", "head"), axis=0, tiled=True),
        lax.all_gather(value_projection, ("blk", "head"), axis=0, tiled=True),
        lax.all_gather(query_norm, ("blk", "head"), axis=0, tiled=True),
        lax.all_gather(key_norm, ("blk", "head"), axis=0, tiled=True),
        lax.all_gather(output_weight, ("blk", "head"), axis=0, tiled=True),
    )
    gain_two, gate_matrix, up_matrix, down_matrix = (
        lax.all_gather(feedforward_norm, ("blk", "head"), axis=0, tiled=True),
        lax.all_gather(gate_weight, ("blk", "head"), axis=0, tiled=True),
        lax.all_gather(up_weight, ("blk", "head"), axis=0, tiled=True),
        lax.all_gather(down_weight, ("blk", "head"), axis=0, tiled=True),
    )
    gain_one = gain_one.astype(jnp.float32)
    gain_two = gain_two.astype(jnp.float32)
    query_gain = query_gain.astype(jnp.float32)
    key_gain = key_gain.astype(jnp.float32)
    own_first = (span_index * count_of_heads + head_index) * local_rows
    own_pos = token_positions(stretch_order, own_first, local_rows, stretch_rows)
    group_pos = token_positions(stretch_order, span_index * group_rows, group_rows, stretch_rows)
    phases = angles(own_pos, HEAD_SIZE)
    tokens_wide = tokens.astype(jnp.float32)
    first_normed, norm_one_back = jax.vjp(norm_rows, tokens_wide, gain_one)
    first_normed = first_normed.astype(jnp.bfloat16)
    query_raw = jnp.einsum(
        "btd,de->bte", first_normed, query_matrix, preferred_element_type=jnp.float32
    ).reshape(sequence_total, local_rows, QUERY_HEADS, HEAD_SIZE)
    key_unnormed = jnp.einsum(
        "btd,de->bte", first_normed, key_matrix, preferred_element_type=jnp.float32
    ).reshape(sequence_total, local_rows, KEY_VALUE_HEADS, HEAD_SIZE)
    value_tokens = (
        jnp.einsum("btd,de->bte", first_normed, value_matrix, preferred_element_type=jnp.float32)
        .astype(jnp.bfloat16)
        .reshape(sequence_total, local_rows, KEY_VALUE_HEADS, HEAD_SIZE)
    )

    def heads_local(query_in, key_in, query_scale, key_scale):
        return (
            rotary(norm_rows(query_in, query_scale), phases),
            rotary(norm_rows(key_in, key_scale), phases),
        )

    (query_tokens, key_tokens), heads_back = jax.vjp(
        heads_local, query_raw, key_unnormed, query_gain, key_gain
    )
    query_tokens = query_tokens.astype(jnp.bfloat16)
    key_tokens = key_tokens.astype(jnp.bfloat16)
    query_group, key_group, value_group = (
        lax.all_to_all(query_tokens, "head", split_axis=2, concat_axis=1, tiled=True),
        lax.all_to_all(key_tokens, "head", split_axis=2, concat_axis=1, tiled=True),
        lax.all_to_all(value_tokens, "head", split_axis=2, concat_axis=1, tiled=True),
    )
    query_five = query_group.reshape(
        sequence_total, group_rows, heads_shared, heads_per_group, HEAD_SIZE
    )

    def block_update(carry, key_block, value_block, key_pos):
        run_max, run_sum, run_total = carry
        scores = (
            jnp.einsum(
                "bqkgd,bckd->bkgqc", query_five, key_block, preferred_element_type=jnp.float32
            )
            * score_scale
        )
        allowed = key_pos[:, None, None, None, :] <= group_pos[:, None, None, :, None]
        scores = jnp.where(allowed, scores, NEG)
        new_max = jnp.maximum(run_max, jnp.max(scores, axis=-1))
        exponent = jnp.where(allowed, jnp.exp(scores - new_max[..., None]), 0.0)
        factor = jnp.exp(run_max - new_max)
        new_sum = run_sum * factor + jnp.sum(exponent, axis=-1)
        new_total = run_total * factor[..., None] + jnp.einsum(
            "bkgqc,bckd->bkgqd",
            exponent.astype(jnp.bfloat16),
            value_block,
            preferred_element_type=jnp.float32,
        )
        return (new_max, new_sum, new_total)

    def fold_update(carry, key_block, value_block, key_pos):
        result = block_update(carry, key_block, value_block, key_pos)
        return result

    stat_shape = (sequence_total, heads_shared, heads_per_group, group_rows)
    start_state = (
        jnp.full(stat_shape, NEG, jnp.float32),
        jnp.zeros(stat_shape, jnp.float32),
        jnp.zeros(stat_shape + (HEAD_SIZE,), jnp.float32),
    )
    key_piece = lax.all_gather(key_group, "blk", axis=1, tiled=True)
    value_piece = lax.all_gather(value_group, "blk", axis=1, tiled=True)
    piece_rows = key_piece.shape[1]
    block_len = math.gcd(group_rows, piece_rows)

    def inner(block_number, carry_in):
        offset = block_number * block_len
        key_block = lax.dynamic_slice_in_dim(key_piece, offset, block_len, 1)
        value_block = lax.dynamic_slice_in_dim(value_piece, offset, block_len, 1)
        key_pos = token_positions(stretch_order, offset, block_len, stretch_rows)
        return fold_update(carry_in, key_block, value_block, key_pos)

    run_max, run_sum, run_total = lax.fori_loop(0, piece_rows // block_len, inner, start_state)
    log_total = run_max + jnp.log(run_sum)
    attended_five = run_total / run_sum[..., None]
    attended_group = (
        jnp.transpose(attended_five, (0, 3, 1, 2, 4))
        .reshape(sequence_total, group_rows, heads_shared * heads_per_group, HEAD_SIZE)
        .astype(jnp.bfloat16)
    )
    attended_tokens = lax.all_to_all(
        attended_group, "head", split_axis=1, concat_axis=2, tiled=True
    ).reshape(sequence_total, local_rows, QUERY_HEADS * HEAD_SIZE)
    branch = jnp.einsum(
        "bte,ed->btd", attended_tokens, output_matrix, preferred_element_type=jnp.float32
    )
    resid = tokens_wide + branch
    normed_two, norm_two_back = jax.vjp(norm_rows, resid, gain_two)
    normed_two = normed_two.astype(jnp.bfloat16)
    gate = jnp.einsum("btd,df->btf", normed_two, gate_matrix, preferred_element_type=jnp.float32)
    up_proj = jnp.einsum("btd,df->btf", normed_two, up_matrix, preferred_element_type=jnp.float32)

    def swish_product(gate_in, up_in):
        return jax.nn.silu(gate_in) * up_in

    hidden, swish_back = jax.vjp(swish_product, gate, up_proj)
    hidden = hidden.astype(jnp.bfloat16)
    layer_out = (
        resid + jnp.einsum("btf,fd->btd", hidden, down_matrix, preferred_element_type=jnp.float32)
    ).astype(jnp.bfloat16)
    gain_again, gate_matrix, up_matrix, down_matrix = (
        lax.all_gather(feedforward_norm, ("blk", "head"), axis=0, tiled=True),
        lax.all_gather(gate_weight, ("blk", "head"), axis=0, tiled=True),
        lax.all_gather(up_weight, ("blk", "head"), axis=0, tiled=True),
        lax.all_gather(down_weight, ("blk", "head"), axis=0, tiled=True),
    )
    down_gradient = jnp.einsum(
        "btf,btd->fd", hidden, out_cotangent, preferred_element_type=jnp.float32
    )
    hidden_gradient = jnp.einsum(
        "btd,fd->btf", out_cotangent, down_matrix, preferred_element_type=jnp.float32
    )
    gate_gradient, up_gradient = swish_back(hidden_gradient)
    gate_gradient = gate_gradient.astype(jnp.bfloat16)
    up_gradient = up_gradient.astype(jnp.bfloat16)
    gate_matrix_gradient = jnp.einsum(
        "btd,btf->df", normed_two, gate_gradient, preferred_element_type=jnp.float32
    )
    up_matrix_gradient = jnp.einsum(
        "btd,btf->df", normed_two, up_gradient, preferred_element_type=jnp.float32
    )
    normed_two_gradient = jnp.einsum(
        "btf,df->btd", gate_gradient, gate_matrix, preferred_element_type=jnp.float32
    ) + jnp.einsum("btf,df->btd", up_gradient, up_matrix, preferred_element_type=jnp.float32)
    resid_part, gain_two_gradient = norm_two_back(normed_two_gradient)
    resid_gradient = out_cotangent.astype(jnp.float32) + resid_part
    feedforward_sums = (
        lax.psum_scatter(gain_two_gradient, ("blk", "head"), scatter_dimension=0, tiled=True),
        lax.psum_scatter(gate_matrix_gradient, ("blk", "head"), scatter_dimension=0, tiled=True),
        lax.psum_scatter(up_matrix_gradient, ("blk", "head"), scatter_dimension=0, tiled=True),
        lax.psum_scatter(down_gradient, ("blk", "head"), scatter_dimension=0, tiled=True),
    )
    gain_again, query_matrix, key_matrix, value_matrix, query_again, key_again, output_matrix = (
        lax.all_gather(attention_norm, ("blk", "head"), axis=0, tiled=True),
        lax.all_gather(query_weight, ("blk", "head"), axis=0, tiled=True),
        lax.all_gather(key_projection, ("blk", "head"), axis=0, tiled=True),
        lax.all_gather(value_projection, ("blk", "head"), axis=0, tiled=True),
        lax.all_gather(query_norm, ("blk", "head"), axis=0, tiled=True),
        lax.all_gather(key_norm, ("blk", "head"), axis=0, tiled=True),
        lax.all_gather(output_weight, ("blk", "head"), axis=0, tiled=True),
    )
    branch_gradient = resid_gradient.astype(jnp.bfloat16)
    output_matrix_gradient = jnp.einsum(
        "bte,btd->ed", attended_tokens, branch_gradient, preferred_element_type=jnp.float32
    )
    attended_gradient = (
        jnp.einsum(
            "btd,ed->bte", branch_gradient, output_matrix, preferred_element_type=jnp.float32
        )
        .astype(jnp.bfloat16)
        .reshape(sequence_total, local_rows, QUERY_HEADS, HEAD_SIZE)
    )
    attended_grad_group = lax.all_to_all(
        attended_gradient, "head", split_axis=2, concat_axis=1, tiled=True
    ).reshape(sequence_total, group_rows, heads_shared, heads_per_group, HEAD_SIZE)
    delta = jnp.sum(
        jnp.transpose(attended_grad_group.astype(jnp.float32), (0, 2, 3, 1, 4)) * attended_five,
        axis=-1,
    )

    def block_grads(sums_in, key_current, value_current, key_pos):
        key_sum, value_sum, query_sum = sums_in
        scores = (
            jnp.einsum(
                "bqkgd,bckd->bkgqc", query_five, key_current, preferred_element_type=jnp.float32
            )
            * score_scale
        )
        allowed = key_pos[:, None, None, None, :] <= group_pos[:, None, None, :, None]
        weights = jnp.where(allowed, jnp.exp(scores - log_total[..., None]), 0.0)
        probs = weights.astype(jnp.bfloat16)
        value_sum = value_sum + jnp.einsum(
            "bkgqc,bqkgd->bckd", probs, attended_grad_group, preferred_element_type=jnp.float32
        )
        probs_gradient = jnp.einsum(
            "bqkgd,bckd->bkgqc",
            attended_grad_group,
            value_current,
            preferred_element_type=jnp.float32,
        )
        scores_gradient = (weights * (probs_gradient - delta[..., None])).astype(jnp.bfloat16)
        query_sum = (
            query_sum
            + jnp.einsum(
                "bkgqc,bckd->bqkgd",
                scores_gradient,
                key_current,
                preferred_element_type=jnp.float32,
            )
            * score_scale
        )
        key_sum = (
            key_sum
            + jnp.einsum(
                "bkgqc,bqkgd->bckd", scores_gradient, query_five, preferred_element_type=jnp.float32
            )
            * score_scale
        )
        return (key_sum, value_sum, query_sum)

    def pass_step(step_index, carry):
        key_current, value_current, key_sum, value_sum, query_sum = carry
        anchor = (span_index - step_index) % span_count
        key_pos = token_positions(stretch_order, anchor * group_rows, group_rows, stretch_rows)
        key_sum, value_sum, query_sum = block_grads(
            (key_sum, value_sum, query_sum), key_current, value_current, key_pos
        )
        key_current, value_current = passed_along((key_current, value_current), "blk", 1)
        key_sum, value_sum = (
            passed_along(key_sum.astype(jnp.bfloat16), "blk", 1).astype(key_sum.dtype),
            passed_along(value_sum.astype(jnp.bfloat16), "blk", 1).astype(value_sum.dtype),
        )
        return (key_current, value_current, key_sum, value_sum, query_sum)

    kv_zeros = jnp.zeros((sequence_total, group_rows, heads_shared, HEAD_SIZE), jnp.float32)
    query_zeros = jnp.zeros(
        (sequence_total, group_rows, heads_shared, heads_per_group, HEAD_SIZE), jnp.float32
    )
    final_state = lax.fori_loop(
        0, span_count, pass_step, (key_group, value_group, kv_zeros, kv_zeros, query_zeros)
    )
    key_grad_group = final_state[2].astype(jnp.bfloat16)
    value_grad_group = final_state[3].astype(jnp.bfloat16)
    query_grad_group = (
        final_state[4]
        .astype(jnp.bfloat16)
        .reshape(sequence_total, group_rows, heads_shared * heads_per_group, HEAD_SIZE)
    )
    query_grad_tokens, key_grad_tokens, value_gradient_tokens = (
        lax.all_to_all(query_grad_group, "head", split_axis=1, concat_axis=2, tiled=True),
        lax.all_to_all(key_grad_group, "head", split_axis=1, concat_axis=2, tiled=True),
        lax.all_to_all(value_grad_group, "head", split_axis=1, concat_axis=2, tiled=True),
    )
    query_raw_gradient, key_unnormed_gradient, query_gain_gradient, key_gain_gradient = heads_back(
        (query_grad_tokens.astype(jnp.float32), key_grad_tokens.astype(jnp.float32))
    )
    query_raw_gradient = query_raw_gradient.astype(jnp.bfloat16).reshape(
        sequence_total, local_rows, QUERY_HEADS * HEAD_SIZE
    )
    key_unnormed_gradient = key_unnormed_gradient.astype(jnp.bfloat16).reshape(
        sequence_total, local_rows, KEY_VALUE_HEADS * HEAD_SIZE
    )
    value_unnormed_gradient = value_gradient_tokens.reshape(
        sequence_total, local_rows, KEY_VALUE_HEADS * HEAD_SIZE
    )
    query_matrix_gradient = jnp.einsum(
        "btd,bte->de", first_normed, query_raw_gradient, preferred_element_type=jnp.float32
    )
    key_matrix_gradient = jnp.einsum(
        "btd,bte->de", first_normed, key_unnormed_gradient, preferred_element_type=jnp.float32
    )
    value_matrix_gradient = jnp.einsum(
        "btd,bte->de", first_normed, value_unnormed_gradient, preferred_element_type=jnp.float32
    )
    normed_one_gradient = jnp.einsum(
        "bte,de->btd", query_raw_gradient, query_matrix, preferred_element_type=jnp.float32
    )
    normed_one_gradient = normed_one_gradient + jnp.einsum(
        "bte,de->btd", key_unnormed_gradient, key_matrix, preferred_element_type=jnp.float32
    )
    normed_one_gradient = normed_one_gradient + jnp.einsum(
        "bte,de->btd", value_unnormed_gradient, value_matrix, preferred_element_type=jnp.float32
    )
    token_part, gain_one_gradient = norm_one_back(normed_one_gradient)
    tokens_gradient = (resid_gradient + token_part).astype(jnp.bfloat16)
    attention_sums = (
        lax.psum_scatter(gain_one_gradient, ("blk", "head"), scatter_dimension=0, tiled=True),
        lax.psum_scatter(query_matrix_gradient, ("blk", "head"), scatter_dimension=0, tiled=True),
        lax.psum_scatter(key_matrix_gradient, ("blk", "head"), scatter_dimension=0, tiled=True),
        lax.psum_scatter(value_matrix_gradient, ("blk", "head"), scatter_dimension=0, tiled=True),
        lax.psum_scatter(query_gain_gradient, ("blk", "head"), scatter_dimension=0, tiled=True),
        lax.psum_scatter(key_gain_gradient, ("blk", "head"), scatter_dimension=0, tiled=True),
        lax.psum_scatter(output_matrix_gradient, ("blk", "head"), scatter_dimension=0, tiled=True),
    )
    return (
        layer_out,
        tokens_gradient,
        attention_sums[0],
        attention_sums[1],
        attention_sums[2],
        attention_sums[3],
        attention_sums[4],
        attention_sums[5],
        attention_sums[6],
        feedforward_sums[0],
        feedforward_sums[1],
        feedforward_sums[2],
        feedforward_sums[3],
    )


LOG2E = math.log2(math.e)
STRIP = 128
CHUNK = 512
ALONG = (((1,), (1,)), ((), ()))
DOWN = (((0,), (0,)), ((), ()))


def two_heads(block):
    return jnp.concatenate([block[:, :HEAD_SIZE], block[:, HEAD_SIZE:]], axis=0)


def side_by_side(rows):
    half = rows.shape[0] // 2
    return jnp.concatenate([rows[:half], rows[half:]], axis=1)


def attend_kernel(place_ref, order_ref, q_ref, kv_ref, out_ref, lse_ref, keys, values):
    step = pl.program_id(0)

    @pl.when(step == 0)
    def _():
        values[:, HEAD_SIZE:] = jnp.ones((values.shape[0], HEAD_SIZE), jnp.bfloat16)

        def sort(index, carry):
            source = pl.multiple_of(order_ref[index] * STRIP, STRIP)
            target = pl.multiple_of(index * STRIP, STRIP)
            keys[pl.ds(target, STRIP), :] = kv_ref[pl.ds(source, STRIP), :HEAD_SIZE]
            values[pl.ds(target, STRIP), :HEAD_SIZE] = kv_ref[pl.ds(source, STRIP), HEAD_SIZE:]
            return carry

        lax.fori_loop(0, kv_ref.shape[0] // STRIP, sort, 0)

    place = place_ref[step]
    queries = two_heads(q_ref[...])
    last = place // (CHUNK // STRIP)

    def part(index, total, masked):
        first = pl.multiple_of(index * CHUNK, CHUNK)
        scores = lax.dot_general(
            queries, keys[pl.ds(first, CHUNK), :], ALONG, preferred_element_type=jnp.float32
        )
        weights = jnp.exp2(scores)
        if masked:
            row = lax.broadcasted_iota(jnp.int32, scores.shape, 0) % STRIP
            column = lax.broadcasted_iota(jnp.int32, scores.shape, 1)
            weights = jnp.where(column - row <= place * STRIP - first, weights, 0.0)
        return total + jnp.dot(
            weights.astype(jnp.bfloat16),
            values[pl.ds(first, CHUNK), :],
            preferred_element_type=jnp.float32,
        )

    total = jnp.zeros((2 * STRIP, 2 * HEAD_SIZE), jnp.float32)
    total = lax.fori_loop(0, last, lambda index, t: part(index, t, False), total)
    total = part(last, total, True)
    norm = total[:, HEAD_SIZE:]
    out_ref[...] = side_by_side(total[:, :HEAD_SIZE] / norm).astype(jnp.bfloat16)
    lse_ref[0] = jnp.transpose(jnp.log2(norm))[:8]


def attend(place, order, queries, kv):
    rows, width = queries.shape
    steps = rows // STRIP
    whole = pl.BlockSpec(kv.shape, lambda i, *_: (0, 0))
    strip = pl.BlockSpec((STRIP, width), lambda i, *_: (i, 0))
    flops = 4 * rows * 2 * kv.shape[0] * HEAD_SIZE // 2
    return pl.pallas_call(
        attend_kernel,
        grid_spec=pltpu.PrefetchScalarGridSpec(
            num_scalar_prefetch=2,
            grid=(steps,),
            in_specs=[strip, whole],
            out_specs=[strip, pl.BlockSpec((1, 8, 2 * STRIP), lambda i, *_: (i, 0, 0))],
            scratch_shapes=[
                pltpu.VMEM((kv.shape[0], HEAD_SIZE), jnp.bfloat16),
                pltpu.VMEM((kv.shape[0], 2 * HEAD_SIZE), jnp.bfloat16),
            ],
        ),
        out_shape=[
            jax.ShapeDtypeStruct((rows, width), jnp.bfloat16),
            jax.ShapeDtypeStruct((steps, 8, 2 * STRIP), jnp.float32),
        ],
        cost_estimate=pl.CostEstimate(
            flops=flops, bytes_accessed=kv.size * 2 + queries.size * 4, transcendentals=rows * kv.shape[0]
        ),
        name="attend",
    )(place, order, queries, kv)


def attend_back_kernel(
    place_ref, order_ref, q_ref, grad_ref, out_ref, lse_ref, kv_ref, dq_ref, dkv_ref,
    keys, values, key_sums, value_sums,
):
    step = pl.program_id(0)
    strips = kv_ref.shape[0] // STRIP

    @pl.when(step == 0)
    def _():
        key_sums[...] = jnp.zeros_like(key_sums)
        value_sums[...] = jnp.zeros_like(value_sums)

        def sort(index, carry):
            source = pl.multiple_of(order_ref[index] * STRIP, STRIP)
            target = pl.multiple_of(index * STRIP, STRIP)
            keys[pl.ds(target, STRIP), :] = kv_ref[pl.ds(source, STRIP), :HEAD_SIZE]
            values[pl.ds(target, STRIP), :] = kv_ref[pl.ds(source, STRIP), HEAD_SIZE:]
            return carry

        lax.fori_loop(0, strips, sort, 0)

    place = place_ref[step]
    queries = two_heads(q_ref[...])
    grads = two_heads(grad_ref[...])
    product = grads.astype(jnp.float32) * two_heads(out_ref[...]).astype(jnp.float32)
    delta = jnp.sum(jnp.transpose(product), axis=0, keepdims=True)
    lse = lse_ref[0, :1]
    last = place // (CHUNK // STRIP)

    def part(index, total, masked):
        first = pl.multiple_of(index * CHUNK, CHUNK)
        here = pl.ds(first, CHUNK)
        key_rows = keys[here, :]
        scores = lax.dot_general(key_rows, queries, ALONG, preferred_element_type=jnp.float32)
        weights = jnp.exp2(scores - lse)
        if masked:
            row = lax.broadcasted_iota(jnp.int32, scores.shape, 0)
            column = lax.broadcasted_iota(jnp.int32, scores.shape, 1) % STRIP
            weights = jnp.where(row - column <= place * STRIP - first, weights, 0.0)
        slopes = lax.dot_general(
            values[here, :], grads, ALONG, preferred_element_type=jnp.float32
        )
        score_grads = (weights * (slopes - delta)).astype(jnp.bfloat16)
        value_sums[here, :] += jnp.dot(
            weights.astype(jnp.bfloat16), grads, preferred_element_type=jnp.float32
        )
        key_sums[here, :] += jnp.dot(score_grads, queries, preferred_element_type=jnp.float32)
        return total + lax.dot_general(
            score_grads, key_rows, DOWN, preferred_element_type=jnp.float32
        )

    total = jnp.zeros((2 * STRIP, HEAD_SIZE), jnp.float32)
    total = lax.fori_loop(0, last, lambda index, t: part(index, t, False), total)
    total = part(last, total, True)
    dq_ref[...] = side_by_side(total * (1.0 / math.sqrt(HEAD_SIZE))).astype(jnp.bfloat16)

    @pl.when(step == pl.num_programs(0) - 1)
    def _():
        def spread(index, carry):
            target = pl.multiple_of(order_ref[index] * STRIP, STRIP)
            source = pl.multiple_of(index * STRIP, STRIP)
            dkv_ref[pl.ds(target, STRIP), :HEAD_SIZE] = (
                key_sums[pl.ds(source, STRIP), :] * (1.0 / LOG2E)
            ).astype(jnp.bfloat16)
            dkv_ref[pl.ds(target, STRIP), HEAD_SIZE:] = value_sums[
                pl.ds(source, STRIP), :
            ].astype(jnp.bfloat16)
            return carry

        lax.fori_loop(0, strips, spread, 0)


def attend_back(place, order, queries, grads, attended, lse, kv):
    rows, width = queries.shape
    steps = rows // STRIP
    total = kv.shape[0]
    whole = pl.BlockSpec(kv.shape, lambda i, *_: (0, 0))
    strip = pl.BlockSpec((STRIP, width), lambda i, *_: (i, 0))
    return pl.pallas_call(
        attend_back_kernel,
        grid_spec=pltpu.PrefetchScalarGridSpec(
            num_scalar_prefetch=2,
            grid=(steps,),
            in_specs=[
                strip, strip, strip, pl.BlockSpec((1, 8, 2 * STRIP), lambda i, *_: (i, 0, 0)), whole,
            ],
            out_specs=[strip, whole],
            scratch_shapes=[
                pltpu.VMEM((total, HEAD_SIZE), jnp.bfloat16),
                pltpu.VMEM((total, HEAD_SIZE), jnp.bfloat16),
                pltpu.VMEM((total, HEAD_SIZE), jnp.float32),
                pltpu.VMEM((total, HEAD_SIZE), jnp.float32),
            ],
        ),
        out_shape=[
            jax.ShapeDtypeStruct((rows, width), jnp.bfloat16),
            jax.ShapeDtypeStruct(kv.shape, jnp.bfloat16),
        ],
        cost_estimate=pl.CostEstimate(
            flops=10 * rows * 2 * total * HEAD_SIZE // 2,
            bytes_accessed=kv.size * 4 + queries.size * 8,
            transcendentals=rows * total,
        ),
        name="attend_back",
    )(place, order, queries, grads, attended, lse, kv)


def matmul(left, right, dims=(((1,), (0,)), ((), ()))):
    return lax.dot_general(left, right, dims, preferred_element_type=jnp.float32)


RING = (0, 2, 4, 6, 7, 5, 3, 1)
STRIPS = (0, 1, 7, 2, 6, 3, 5, 4)
GROUPS = ((0, 3), (3, 5), (5, 7), (7, 8))


def hop(value, by):
    count = len(RING)
    return lax.ppermute(value, "blk", [(RING[i], RING[(i + by) % count]) for i in range(count)])


def cross(value, by):
    return lax.ppermute(value, "head", [(i, i ^ by) for i in range(4)])


def add(left, right):
    return (left.astype(jnp.float32) + right.astype(jnp.float32)).astype(left.dtype)


def ring_gather(own):
    half = own.shape[0] // 2
    got = {0: own}
    for step in (1, 2, 3):
        got[step] = hop(got[step - 1], -1)
        got[8 - step] = hop(got[(9 - step) % 8], 1)
    got[4] = jnp.concatenate([hop(got[3][:half], -1), hop(got[5][half:], 1)], axis=0)
    return [got[s] for s in STRIPS]


def ring_scatter(parts):
    part = dict(zip(STRIPS, parts))
    half = part[0].shape[0] // 2
    up = hop(part[4][:half], 1)
    down = hop(part[4][half:], -1)
    up = hop(jnp.concatenate([add(part[3][:half], up), part[3][half:]], axis=0), 1)
    down = hop(jnp.concatenate([part[5][:half], add(part[5][half:], down)], axis=0), -1)
    up, down = hop(add(part[2], up), 1), hop(add(part[6], down), -1)
    up, down = hop(add(part[1], up), 1), hop(add(part[7], down), -1)
    wide = jnp.float32
    return part[0].astype(wide) + up.astype(wide) + down.astype(wide)


def grouped(strips):
    return [
        jnp.concatenate(strips[a:b], axis=0) if b - a > 1 else strips[a] for a, b in GROUPS
    ]


def split_groups(groups, rows):
    return [
        group[i * rows : (i + 1) * rows]
        for group in groups
        for i in range(group.shape[0] // rows)
    ]


def swap_slices(pieces, place, blk_index):
    ring = jnp.asarray(RING, jnp.int32)
    own = lax.dynamic_index_in_dim(pieces, blk_index, 0)
    out = lax.dynamic_update_slice_in_dim(jnp.zeros_like(pieces), own, blk_index, 0)
    for by in (4, 1, 7, 2, 6, 3, 5):
        target = ring[(place + by) % 8]
        source = ring[(place - by) % 8]
        moved = hop(lax.dynamic_index_in_dim(pieces, target, 0), by)
        out = lax.dynamic_update_slice_in_dim(out, moved, source, 0)
    return out


def gather_head(rows):
    return lax.all_gather(rows, "head", axis=0, tiled=True)


def scatter_head(rows):
    return lax.psum_scatter(rows, "head", scatter_dimension=0, tiled=True)


def inverse_rms(rows):
    return lax.rsqrt(jnp.mean(rows * rows, axis=-1, keepdims=True) + EPS)


def turn(rows, cosine, sine):
    half = HEAD_SIZE // 2
    first, second = rows[:, :half], rows[:, half:]
    return jnp.concatenate(
        [first * cosine - second * sine, second * cosine + first * sine], axis=1
    )


def head_back(grads, raw, gain, cosine, sine):
    rho = inverse_rms(raw)
    unit = raw * rho
    turned = turn(grads.astype(jnp.float32), cosine, -sine)
    gain_part = jnp.sum(turned * unit, axis=0)
    scaled = turned * gain
    return rho * (scaled - unit * jnp.mean(unit * scaled, axis=-1, keepdims=True)), gain_part


def after(value, *earlier):
    return lax.optimization_barrier((value, *earlier))[0]


def per_device(
    tokens,
    attention_norm,
    query_weight,
    key_projection,
    value_projection,
    query_norm,
    key_norm,
    output_weight,
    feedforward_norm,
    gate_weight,
    up_weight,
    down_weight,
    stretch_order,
    out_cotangent,
):
    blk_count = lax.axis_size("blk")
    head_count = lax.axis_size("head")
    head_index = lax.axis_index("head")
    blk_index = lax.axis_index("blk")
    narrow, wide = jnp.bfloat16, jnp.float32
    tokens, out_cotangent = tokens[0], out_cotangent[0]
    local_rows, model_width = tokens.shape
    group_rows = local_rows * blk_count
    weight_rows = query_weight.shape[0]
    ff_local = gate_weight.shape[1] // blk_count
    group_heads = QUERY_HEADS // blk_count
    query_cols = group_heads * HEAD_SIZE
    attn_cols = query_cols + 2 * HEAD_SIZE
    strip_count = blk_count * head_count
    halves = strip_count // stretch_order.shape[1]
    ring_place = jnp.where(blk_index % 2 == 0, blk_index // 2, 7 - blk_index // 2)

    def pieces_of(*weights):
        return jnp.concatenate(
            [w.reshape(weight_rows, blk_count, w.shape[1] // blk_count) for w in weights], axis=2
        ).transpose(1, 0, 2)

    def natural(pieces, rows):
        return pieces.reshape(head_count, blk_count, rows, -1).transpose(1, 0, 2, 3)

    small = query_norm.shape[0]
    gains = jnp.concatenate([attention_norm, feedforward_norm, query_norm, key_norm])
    gains = jnp.pad(gains, (0, attn_cols - gains.shape[0]))[None, None, :]
    gains = jnp.pad(gains, ((0, 0), (0, 15), (0, 0)))
    attn_pieces = jnp.concatenate(
        [
            pieces_of(query_weight, key_projection, value_projection),
            jnp.broadcast_to(gains, (blk_count, 16, attn_cols)),
        ],
        axis=1,
    )
    token_strips = ring_gather(tokens)
    attn_all = natural(
        gather_head(swap_slices(attn_pieces, ring_place, blk_index)), weight_rows + 16
    )
    attn_matrix = attn_all[:, :, :weight_rows].reshape(model_width, attn_cols)
    gain_rows = attn_all[:, :, weight_rows]
    gain_one = gain_rows[:, :, :weight_rows].reshape(1, model_width).astype(wide)
    gain_two = (
        gain_rows[:, :, weight_rows : 2 * weight_rows].reshape(1, model_width).astype(wide)
    )
    at = 2 * weight_rows
    query_gain = gain_rows[:, :, at : at + small].reshape(1, HEAD_SIZE).astype(wide)
    key_gain = gain_rows[:, :, at + small : at + 2 * small].reshape(1, HEAD_SIZE).astype(wide)

    output_rows = gather_head(output_weight)
    ff_pieces = after(pieces_of(gate_weight, up_weight), token_strips[-1])
    ff_matrix = natural(
        gather_head(swap_slices(ff_pieces, ring_place, blk_index)), weight_rows
    ).reshape(model_width, 2 * ff_local)
    down_matrix = gather_head(down_weight)
    cotangent_strips = ring_gather(after(out_cotangent, token_strips[-1]))

    numbers = jnp.arange(strip_count, dtype=jnp.int32)
    on = jnp.asarray(STRIPS, jnp.int32)
    ring_spot = (ring_place + on) % blk_count
    strip_blk = jnp.where(ring_spot < 4, 2 * ring_spot, 15 - 2 * ring_spot)
    strip_head = head_index ^ jnp.arange(head_count, dtype=jnp.int32)
    strip = (strip_blk[None, :] * head_count + strip_head[:, None]).reshape(strip_count)
    slots = jnp.arange(stretch_order.shape[1], dtype=jnp.int32)
    held = jnp.sum(
        jnp.where((strip // halves)[:, None] == slots[None, :], stretch_order, 0), axis=1
    )
    strip_place = held * halves + strip % halves
    order = jnp.sum(
        jnp.where(strip_place[None, :] == numbers[:, None], numbers[None, :], 0), axis=1
    ).astype(jnp.int32)
    place = strip_place[:blk_count].astype(jnp.int32)
    positions = (
        place[:, None] * local_rows + jnp.arange(local_rows, dtype=jnp.int32)[None, :]
    ).reshape(group_rows)
    phases = angles(positions, HEAD_SIZE)[:, 0, :]
    cosine, sine = jnp.cos(phases), jnp.sin(phases)

    tokens_wide = tokens.astype(wide)
    raw_groups, normed_groups, query_groups, kv_groups = [], [], [], []
    for (first, last), rows in zip(GROUPS, grouped(token_strips)):
        here = slice(first * local_rows, last * local_rows)
        rows = rows.astype(wide)
        normed = (rows * inverse_rms(rows) * gain_one).astype(narrow)
        raw = matmul(normed, attn_matrix)
        heads = []
        for h in range(group_heads + 1):
            part = raw[:, h * HEAD_SIZE : (h + 1) * HEAD_SIZE]
            gain = query_gain if h < group_heads else key_gain
            part = turn(part * inverse_rms(part) * gain, cosine[here], sine[here])
            if h < group_heads:
                part = part * (LOG2E / math.sqrt(HEAD_SIZE))
            heads.append(part.astype(narrow))
        raw_groups.append(raw)
        normed_groups.append(normed)
        query_groups.append(jnp.concatenate(heads[:group_heads], axis=1))
        kv_groups.append(
            jnp.concatenate(
                [heads[group_heads], raw[:, query_cols + HEAD_SIZE :].astype(narrow)], axis=1
            )
        )
    first_normed = jnp.concatenate(normed_groups, axis=0)
    attn_raw = jnp.concatenate(raw_groups, axis=0)
    query_rows = jnp.concatenate(query_groups, axis=0)
    kv_own = jnp.concatenate(kv_groups, axis=0)
    kv_far = cross(kv_own, 2)
    kv = jnp.concatenate([kv_own, cross(kv_own, 1), kv_far, cross(kv_far, 1)], axis=0)
    attended, lse = attend(place, order, query_rows, kv)

    def by_groups(rows):
        return [rows[a * local_rows : b * local_rows] for a, b in GROUPS]

    branch_parts = [
        matmul(rows, output_rows).astype(narrow) for rows in reversed(by_groups(attended))
    ]
    branch = ring_scatter(split_groups(branch_parts[::-1], local_rows))
    resid = tokens_wide + branch
    rho_two = inverse_rms(resid)
    unit_two = resid * rho_two
    second_strips = ring_gather((unit_two * gain_two).astype(narrow))

    hidden_groups, ff_gradient_groups, second_parts = [], [], []
    second_groups = grouped(second_strips)
    cotangent_groups = grouped(cotangent_strips)
    for rows, grads in zip(second_groups, cotangent_groups):
        ff_raw = matmul(rows, ff_matrix)
        gate, up_proj = ff_raw[:, :ff_local], ff_raw[:, ff_local:]
        sigma = jax.nn.sigmoid(gate)
        swish = gate * sigma
        hidden_groups.append((swish * up_proj).astype(narrow))
        hidden_gradient = matmul(grads, down_matrix, ALONG)
        gate_gradient = hidden_gradient * up_proj * (sigma * (1.0 + gate * (1.0 - sigma)))
        ff_gradient_groups.append(
            jnp.concatenate([gate_gradient, hidden_gradient * swish], 1).astype(narrow)
        )
    for rows in reversed(ff_gradient_groups):
        second_parts.append(matmul(rows, ff_matrix, ALONG).astype(narrow))
    second_gradient = ring_scatter(split_groups(second_parts[::-1], local_rows))
    scaled = gain_two * second_gradient
    resid_gradient = out_cotangent.astype(wide) + rho_two * (
        scaled - unit_two * jnp.mean(unit_two * scaled, axis=-1, keepdims=True)
    )
    branch_gradient = resid_gradient.astype(narrow)
    branch_strips = ring_gather(branch_gradient)

    out_parts = [matmul(rows, down_matrix).astype(narrow) for rows in reversed(hidden_groups)]
    out_parts = split_groups(out_parts[::-1], local_rows)
    out_part = ring_scatter(out_parts[:-1] + [after(out_parts[-1], branch_strips[-1])])
    layer_out = (resid + out_part).astype(narrow)

    second_normed = jnp.concatenate(second_groups, axis=0)
    group_cotangent = jnp.concatenate(cotangent_groups, axis=0)
    hidden = jnp.concatenate(hidden_groups, axis=0)
    ff_gradient = jnp.concatenate(ff_gradient_groups, axis=0)

    def by_head(grads, rows):
        shape = (blk_count, head_count, rows, grads.shape[-1])
        return grads.reshape(shape).transpose(1, 0, 2, 3).reshape(-1, rows, grads.shape[-1])

    down_gradient = scatter_head(matmul(hidden, group_cotangent, DOWN).astype(narrow))
    ff_matrix_gradient = scatter_head(
        by_head(matmul(second_normed, ff_gradient, DOWN).astype(narrow), weight_rows)
    )
    ff_matrix_gradient = swap_slices(ff_matrix_gradient, ring_place, blk_index).astype(wide)
    gate_weight_gradient = (
        ff_matrix_gradient[:, :, :ff_local].transpose(1, 0, 2).reshape(gate_weight.shape)
    )
    up_weight_gradient = (
        ff_matrix_gradient[:, :, ff_local:].transpose(1, 0, 2).reshape(up_weight.shape)
    )
    feedforward_norm_gradient = (
        jnp.sum(gate_weight_gradient * gate_weight.astype(wide), axis=1)
        + jnp.sum(up_weight_gradient * up_weight.astype(wide), axis=1)
    ) / feedforward_norm.astype(wide)

    branch_groups = grouped(branch_strips)
    attended_gradient = jnp.concatenate(
        [matmul(rows, output_rows, ALONG).astype(narrow) for rows in branch_groups], axis=0
    )
    output_weight_gradient = scatter_head(
        matmul(attended, jnp.concatenate(branch_groups, axis=0), DOWN).astype(narrow)
    ).astype(wide)
    query_grads, kv_grads = attend_back(
        place, order, query_rows, attended_gradient, attended, lse, kv
    )
    kv_near = [kv_grads[j * group_rows : (j + 1) * group_rows] for j in range(head_count)]
    kv_sent = cross(jnp.concatenate([kv_near[1], kv_near[3]], axis=0), 1)
    kv_grads = add(
        add(kv_near[0], kv_sent[:group_rows]), cross(add(kv_near[2], kv_sent[group_rows:]), 2)
    )
    attn_gradient, gain_parts = [], []
    for h in range(group_heads + 1):
        cols = slice(h * HEAD_SIZE, (h + 1) * HEAD_SIZE)
        grads = query_grads[:, cols] if h < group_heads else kv_grads[:, :HEAD_SIZE]
        gain = query_gain if h < group_heads else key_gain
        raw_gradient, gain_part = head_back(grads, attn_raw[:, cols], gain, cosine, sine)
        attn_gradient.append(raw_gradient.astype(narrow))
        gain_parts.append(gain_part)
    attn_gradient = jnp.concatenate(attn_gradient + [kv_grads[:, HEAD_SIZE:]], axis=1)
    first_parts = [
        matmul(rows, attn_matrix, ALONG).astype(narrow)
        for rows in reversed(by_groups(attn_gradient))
    ]
    first_gradient = ring_scatter(split_groups(first_parts[::-1], local_rows))
    attn_matrix_gradient = by_head(
        matmul(first_normed, attn_gradient, DOWN).astype(narrow), weight_rows
    )
    gain_parts = jnp.stack(
        [
            sum(gain_parts[:group_heads]).reshape(blk_count, head_count, small),
            gain_parts[group_heads].reshape(blk_count, head_count, small),
        ],
        axis=2,
    ).transpose(1, 0, 2, 3)
    gain_parts = gain_parts.reshape(strip_count, 1, 2 * small).astype(narrow)
    gain_parts = jnp.pad(gain_parts, ((0, 0), (0, 15), (0, attn_cols - 2 * small)))
    attn_matrix_gradient = swap_slices(
        scatter_head(jnp.concatenate([attn_matrix_gradient, gain_parts], axis=1)),
        ring_place,
        blk_index,
    ).astype(wide)
    attn_rows = attn_matrix_gradient[:, :weight_rows]
    query_weight_gradient = (
        attn_rows[:, :, :query_cols].transpose(1, 0, 2).reshape(query_weight.shape)
    )
    key_weight_gradient = (
        attn_rows[:, :, query_cols : query_cols + HEAD_SIZE]
        .transpose(1, 0, 2)
        .reshape(key_projection.shape)
    )
    value_weight_gradient = (
        attn_rows[:, :, query_cols + HEAD_SIZE :].transpose(1, 0, 2).reshape(value_projection.shape)
    )
    gain_sums = jnp.sum(attn_matrix_gradient[:, weight_rows], axis=0)
    attention_norm_gradient = (
        jnp.sum(query_weight_gradient * query_weight.astype(wide), axis=1)
        + jnp.sum(key_weight_gradient * key_projection.astype(wide), axis=1)
        + jnp.sum(value_weight_gradient * value_projection.astype(wide), axis=1)
    ) / attention_norm.astype(wide)
    rho_one = inverse_rms(tokens_wide)
    unit_one = tokens_wide * rho_one
    scaled = gain_one * first_gradient
    tokens_gradient = resid_gradient + rho_one * (
        scaled - unit_one * jnp.mean(unit_one * scaled, axis=-1, keepdims=True)
    )
    return (
        layer_out[None],
        tokens_gradient.astype(narrow)[None],
        attention_norm_gradient,
        query_weight_gradient,
        key_weight_gradient,
        value_weight_gradient,
        gain_sums[:small],
        gain_sums[small : 2 * small],
        output_weight_gradient,
        feedforward_norm_gradient,
        gate_weight_gradient,
        up_weight_gradient,
        down_gradient.astype(wide),
    )


def solution(mesh):
    placed = (
        P(None, ("blk", "head"), None),
        P(("blk", "head")),
        P(("blk", "head"), None),
        P(("blk", "head"), None),
        P(("blk", "head"), None),
        P(("blk", "head")),
        P(("blk", "head")),
        P(("blk", "head"), None),
        P(("blk", "head")),
        P(("blk", "head"), None),
        P(("blk", "head"), None),
        P(("blk", "head"), None),
        P(),
        P(None, ("blk", "head"), None),
    )
    fits = mesh.shape["blk"] == KEY_VALUE_HEADS and mesh.shape["head"] == 4
    return jax.shard_map(
        per_device if fits else per_device_by_tokens,
        mesh=mesh,
        in_specs=placed,
        out_specs=(
            P(None, ("blk", "head"), None),
            P(None, ("blk", "head"), None),
            P(("blk", "head")),
            P(("blk", "head"), None),
            P(("blk", "head"), None),
            P(("blk", "head"), None),
            P(("blk", "head")),
            P(("blk", "head")),
            P(("blk", "head"), None),
            P(("blk", "head")),
            P(("blk", "head"), None),
            P(("blk", "head"), None),
            P(("blk", "head"), None),
        ),
        check_vma=False,
    )
```

```python
import math

import jax
import jax.numpy as jnp
from jax import lax
from jax.experimental import pallas as pl
from jax.experimental.pallas import tpu as pltpu
from jax.sharding import PartitionSpec as P

QUERY_HEADS = 16
KEY_VALUE_HEADS = 8
HEAD_SIZE = 128


EPS = 1e-06
NEG = -1e30
ROPE_BASE = 1000000.0


def passed_along(value, axis, by):
    count = lax.axis_size(axis)
    return lax.ppermute(value, axis, [(i, (i + by) % count) for i in range(count)])


def norm_rows(inputs, norm_gain):
    return inputs * lax.rsqrt(jnp.mean(inputs * inputs, axis=-1, keepdims=True) + EPS) * norm_gain


def rotary(inputs, phases):
    half_width = inputs.shape[-1] // 2
    cosine = jnp.cos(phases)
    sine_term = jnp.sin(phases)
    first_half = inputs[..., :half_width]
    second_half = inputs[..., half_width:]
    return jnp.concatenate(
        [
            first_half * cosine - second_half * sine_term,
            second_half * cosine + first_half * sine_term,
        ],
        axis=-1,
    )


def angles(positions, head_width):
    half_width = head_width // 2
    frequency = jnp.exp(
        jnp.arange(half_width, dtype=jnp.float32) * (-2.0 * math.log(ROPE_BASE) / head_width)
    )
    return positions.astype(jnp.float32)[..., None, None] * frequency


def token_positions(stretch_order, first_row, row_count, stretch_rows):
    row_index = first_row + jnp.arange(row_count, dtype=jnp.int32)
    slot_index = row_index // stretch_rows
    matches = slot_index[:, None] == jnp.arange(stretch_order.shape[1], dtype=jnp.int32)[None, :]
    picked = jnp.sum(jnp.where(matches[None], stretch_order[:, None, :], 0), axis=-1)
    return picked * stretch_rows + row_index % stretch_rows


def per_device_by_tokens(
    tokens,
    attention_norm,
    query_weight,
    key_projection,
    value_projection,
    query_norm,
    key_norm,
    output_weight,
    feedforward_norm,
    gate_weight,
    up_weight,
    down_weight,
    stretch_order,
    out_cotangent,
):
    count_of_heads = lax.axis_size("head")
    span_count = lax.axis_size("blk")
    span_index = lax.axis_index("blk")
    head_index = lax.axis_index("head")
    sequence_total = tokens.shape[0]
    local_rows = tokens.shape[1]
    group_rows = local_rows * count_of_heads
    stretch_rows = group_rows // 2
    heads_shared = KEY_VALUE_HEADS // count_of_heads
    heads_per_group = QUERY_HEADS // KEY_VALUE_HEADS
    score_scale = 1.0 / math.sqrt(HEAD_SIZE)
    gain_one, query_matrix, key_matrix, value_matrix, query_gain, key_gain, output_matrix = (
        lax.all_gather(attention_norm, ("blk", "head"), axis=0, tiled=True),
        lax.all_gather(query_weight, ("blk", "head"), axis=0, tiled=True),
        lax.all_gather(key_projection, ("blk", "head"), axis=0, tiled=True),
        lax.all_gather(value_projection, ("blk", "head"), axis=0, tiled=True),
        lax.all_gather(query_norm, ("blk", "head"), axis=0, tiled=True),
        lax.all_gather(key_norm, ("blk", "head"), axis=0, tiled=True),
        lax.all_gather(output_weight, ("blk", "head"), axis=0, tiled=True),
    )
    gain_two, gate_matrix, up_matrix, down_matrix = (
        lax.all_gather(feedforward_norm, ("blk", "head"), axis=0, tiled=True),
        lax.all_gather(gate_weight, ("blk", "head"), axis=0, tiled=True),
        lax.all_gather(up_weight, ("blk", "head"), axis=0, tiled=True),
        lax.all_gather(down_weight, ("blk", "head"), axis=0, tiled=True),
    )
    gain_one = gain_one.astype(jnp.float32)
    gain_two = gain_two.astype(jnp.float32)
    query_gain = query_gain.astype(jnp.float32)
    key_gain = key_gain.astype(jnp.float32)
    own_first = (span_index * count_of_heads + head_index) * local_rows
    own_pos = token_positions(stretch_order, own_first, local_rows, stretch_rows)
    group_pos = token_positions(stretch_order, span_index * group_rows, group_rows, stretch_rows)
    phases = angles(own_pos, HEAD_SIZE)
    tokens_wide = tokens.astype(jnp.float32)
    first_normed, norm_one_back = jax.vjp(norm_rows, tokens_wide, gain_one)
    first_normed = first_normed.astype(jnp.bfloat16)
    query_raw = jnp.einsum(
        "btd,de->bte", first_normed, query_matrix, preferred_element_type=jnp.float32
    ).reshape(sequence_total, local_rows, QUERY_HEADS, HEAD_SIZE)
    key_unnormed = jnp.einsum(
        "btd,de->bte", first_normed, key_matrix, preferred_element_type=jnp.float32
    ).reshape(sequence_total, local_rows, KEY_VALUE_HEADS, HEAD_SIZE)
    value_tokens = (
        jnp.einsum("btd,de->bte", first_normed, value_matrix, preferred_element_type=jnp.float32)
        .astype(jnp.bfloat16)
        .reshape(sequence_total, local_rows, KEY_VALUE_HEADS, HEAD_SIZE)
    )

    def heads_local(query_in, key_in, query_scale, key_scale):
        return (
            rotary(norm_rows(query_in, query_scale), phases),
            rotary(norm_rows(key_in, key_scale), phases),
        )

    (query_tokens, key_tokens), heads_back = jax.vjp(
        heads_local, query_raw, key_unnormed, query_gain, key_gain
    )
    query_tokens = query_tokens.astype(jnp.bfloat16)
    key_tokens = key_tokens.astype(jnp.bfloat16)
    query_group, key_group, value_group = (
        lax.all_to_all(query_tokens, "head", split_axis=2, concat_axis=1, tiled=True),
        lax.all_to_all(key_tokens, "head", split_axis=2, concat_axis=1, tiled=True),
        lax.all_to_all(value_tokens, "head", split_axis=2, concat_axis=1, tiled=True),
    )
    query_five = query_group.reshape(
        sequence_total, group_rows, heads_shared, heads_per_group, HEAD_SIZE
    )

    def block_update(carry, key_block, value_block, key_pos):
        run_max, run_sum, run_total = carry
        scores = (
            jnp.einsum(
                "bqkgd,bckd->bkgqc", query_five, key_block, preferred_element_type=jnp.float32
            )
            * score_scale
        )
        allowed = key_pos[:, None, None, None, :] <= group_pos[:, None, None, :, None]
        scores = jnp.where(allowed, scores, NEG)
        new_max = jnp.maximum(run_max, jnp.max(scores, axis=-1))
        exponent = jnp.where(allowed, jnp.exp(scores - new_max[..., None]), 0.0)
        factor = jnp.exp(run_max - new_max)
        new_sum = run_sum * factor + jnp.sum(exponent, axis=-1)
        new_total = run_total * factor[..., None] + jnp.einsum(
            "bkgqc,bckd->bkgqd",
            exponent.astype(jnp.bfloat16),
            value_block,
            preferred_element_type=jnp.float32,
        )
        return (new_max, new_sum, new_total)

    def fold_update(carry, key_block, value_block, key_pos):
        result = block_update(carry, key_block, value_block, key_pos)
        return result

    stat_shape = (sequence_total, heads_shared, heads_per_group, group_rows)
    start_state = (
        jnp.full(stat_shape, NEG, jnp.float32),
        jnp.zeros(stat_shape, jnp.float32),
        jnp.zeros(stat_shape + (HEAD_SIZE,), jnp.float32),
    )
    key_piece = lax.all_gather(key_group, "blk", axis=1, tiled=True)
    value_piece = lax.all_gather(value_group, "blk", axis=1, tiled=True)
    piece_rows = key_piece.shape[1]
    block_len = math.gcd(group_rows, piece_rows)

    def inner(block_number, carry_in):
        offset = block_number * block_len
        key_block = lax.dynamic_slice_in_dim(key_piece, offset, block_len, 1)
        value_block = lax.dynamic_slice_in_dim(value_piece, offset, block_len, 1)
        key_pos = token_positions(stretch_order, offset, block_len, stretch_rows)
        return fold_update(carry_in, key_block, value_block, key_pos)

    run_max, run_sum, run_total = lax.fori_loop(0, piece_rows // block_len, inner, start_state)
    log_total = run_max + jnp.log(run_sum)
    attended_five = run_total / run_sum[..., None]
    attended_group = (
        jnp.transpose(attended_five, (0, 3, 1, 2, 4))
        .reshape(sequence_total, group_rows, heads_shared * heads_per_group, HEAD_SIZE)
        .astype(jnp.bfloat16)
    )
    attended_tokens = lax.all_to_all(
        attended_group, "head", split_axis=1, concat_axis=2, tiled=True
    ).reshape(sequence_total, local_rows, QUERY_HEADS * HEAD_SIZE)
    branch = jnp.einsum(
        "bte,ed->btd", attended_tokens, output_matrix, preferred_element_type=jnp.float32
    )
    resid = tokens_wide + branch
    normed_two, norm_two_back = jax.vjp(norm_rows, resid, gain_two)
    normed_two = normed_two.astype(jnp.bfloat16)
    gate = jnp.einsum("btd,df->btf", normed_two, gate_matrix, preferred_element_type=jnp.float32)
    up_proj = jnp.einsum("btd,df->btf", normed_two, up_matrix, preferred_element_type=jnp.float32)

    def swish_product(gate_in, up_in):
        return jax.nn.silu(gate_in) * up_in

    hidden, swish_back = jax.vjp(swish_product, gate, up_proj)
    hidden = hidden.astype(jnp.bfloat16)
    layer_out = (
        resid + jnp.einsum("btf,fd->btd", hidden, down_matrix, preferred_element_type=jnp.float32)
    ).astype(jnp.bfloat16)
    gain_again, gate_matrix, up_matrix, down_matrix = (
        lax.all_gather(feedforward_norm, ("blk", "head"), axis=0, tiled=True),
        lax.all_gather(gate_weight, ("blk", "head"), axis=0, tiled=True),
        lax.all_gather(up_weight, ("blk", "head"), axis=0, tiled=True),
        lax.all_gather(down_weight, ("blk", "head"), axis=0, tiled=True),
    )
    down_gradient = jnp.einsum(
        "btf,btd->fd", hidden, out_cotangent, preferred_element_type=jnp.float32
    )
    hidden_gradient = jnp.einsum(
        "btd,fd->btf", out_cotangent, down_matrix, preferred_element_type=jnp.float32
    )
    gate_gradient, up_gradient = swish_back(hidden_gradient)
    gate_gradient = gate_gradient.astype(jnp.bfloat16)
    up_gradient = up_gradient.astype(jnp.bfloat16)
    gate_matrix_gradient = jnp.einsum(
        "btd,btf->df", normed_two, gate_gradient, preferred_element_type=jnp.float32
    )
    up_matrix_gradient = jnp.einsum(
        "btd,btf->df", normed_two, up_gradient, preferred_element_type=jnp.float32
    )
    normed_two_gradient = jnp.einsum(
        "btf,df->btd", gate_gradient, gate_matrix, preferred_element_type=jnp.float32
    ) + jnp.einsum("btf,df->btd", up_gradient, up_matrix, preferred_element_type=jnp.float32)
    resid_part, gain_two_gradient = norm_two_back(normed_two_gradient)
    resid_gradient = out_cotangent.astype(jnp.float32) + resid_part
    feedforward_sums = (
        lax.psum_scatter(gain_two_gradient, ("blk", "head"), scatter_dimension=0, tiled=True),
        lax.psum_scatter(gate_matrix_gradient, ("blk", "head"), scatter_dimension=0, tiled=True),
        lax.psum_scatter(up_matrix_gradient, ("blk", "head"), scatter_dimension=0, tiled=True),
        lax.psum_scatter(down_gradient, ("blk", "head"), scatter_dimension=0, tiled=True),
    )
    gain_again, query_matrix, key_matrix, value_matrix, query_again, key_again, output_matrix = (
        lax.all_gather(attention_norm, ("blk", "head"), axis=0, tiled=True),
        lax.all_gather(query_weight, ("blk", "head"), axis=0, tiled=True),
        lax.all_gather(key_projection, ("blk", "head"), axis=0, tiled=True),
        lax.all_gather(value_projection, ("blk", "head"), axis=0, tiled=True),
        lax.all_gather(query_norm, ("blk", "head"), axis=0, tiled=True),
        lax.all_gather(key_norm, ("blk", "head"), axis=0, tiled=True),
        lax.all_gather(output_weight, ("blk", "head"), axis=0, tiled=True),
    )
    branch_gradient = resid_gradient.astype(jnp.bfloat16)
    output_matrix_gradient = jnp.einsum(
        "bte,btd->ed", attended_tokens, branch_gradient, preferred_element_type=jnp.float32
    )
    attended_gradient = (
        jnp.einsum(
            "btd,ed->bte", branch_gradient, output_matrix, preferred_element_type=jnp.float32
        )
        .astype(jnp.bfloat16)
        .reshape(sequence_total, local_rows, QUERY_HEADS, HEAD_SIZE)
    )
    attended_grad_group = lax.all_to_all(
        attended_gradient, "head", split_axis=2, concat_axis=1, tiled=True
    ).reshape(sequence_total, group_rows, heads_shared, heads_per_group, HEAD_SIZE)
    delta = jnp.sum(
        jnp.transpose(attended_grad_group.astype(jnp.float32), (0, 2, 3, 1, 4)) * attended_five,
        axis=-1,
    )

    def block_grads(sums_in, key_current, value_current, key_pos):
        key_sum, value_sum, query_sum = sums_in
        scores = (
            jnp.einsum(
                "bqkgd,bckd->bkgqc", query_five, key_current, preferred_element_type=jnp.float32
            )
            * score_scale
        )
        allowed = key_pos[:, None, None, None, :] <= group_pos[:, None, None, :, None]
        weights = jnp.where(allowed, jnp.exp(scores - log_total[..., None]), 0.0)
        probs = weights.astype(jnp.bfloat16)
        value_sum = value_sum + jnp.einsum(
            "bkgqc,bqkgd->bckd", probs, attended_grad_group, preferred_element_type=jnp.float32
        )
        probs_gradient = jnp.einsum(
            "bqkgd,bckd->bkgqc",
            attended_grad_group,
            value_current,
            preferred_element_type=jnp.float32,
        )
        scores_gradient = (weights * (probs_gradient - delta[..., None])).astype(jnp.bfloat16)
        query_sum = (
            query_sum
            + jnp.einsum(
                "bkgqc,bckd->bqkgd",
                scores_gradient,
                key_current,
                preferred_element_type=jnp.float32,
            )
            * score_scale
        )
        key_sum = (
            key_sum
            + jnp.einsum(
                "bkgqc,bqkgd->bckd", scores_gradient, query_five, preferred_element_type=jnp.float32
            )
            * score_scale
        )
        return (key_sum, value_sum, query_sum)

    def pass_step(step_index, carry):
        key_current, value_current, key_sum, value_sum, query_sum = carry
        anchor = (span_index - step_index) % span_count
        key_pos = token_positions(stretch_order, anchor * group_rows, group_rows, stretch_rows)
        key_sum, value_sum, query_sum = block_grads(
            (key_sum, value_sum, query_sum), key_current, value_current, key_pos
        )
        key_current, value_current = passed_along((key_current, value_current), "blk", 1)
        key_sum, value_sum = (
            passed_along(key_sum.astype(jnp.bfloat16), "blk", 1).astype(key_sum.dtype),
            passed_along(value_sum.astype(jnp.bfloat16), "blk", 1).astype(value_sum.dtype),
        )
        return (key_current, value_current, key_sum, value_sum, query_sum)

    kv_zeros = jnp.zeros((sequence_total, group_rows, heads_shared, HEAD_SIZE), jnp.float32)
    query_zeros = jnp.zeros(
        (sequence_total, group_rows, heads_shared, heads_per_group, HEAD_SIZE), jnp.float32
    )
    final_state = lax.fori_loop(
        0, span_count, pass_step, (key_group, value_group, kv_zeros, kv_zeros, query_zeros)
    )
    key_grad_group = final_state[2].astype(jnp.bfloat16)
    value_grad_group = final_state[3].astype(jnp.bfloat16)
    query_grad_group = (
        final_state[4]
        .astype(jnp.bfloat16)
        .reshape(sequence_total, group_rows, heads_shared * heads_per_group, HEAD_SIZE)
    )
    query_grad_tokens, key_grad_tokens, value_gradient_tokens = (
        lax.all_to_all(query_grad_group, "head", split_axis=1, concat_axis=2, tiled=True),
        lax.all_to_all(key_grad_group, "head", split_axis=1, concat_axis=2, tiled=True),
        lax.all_to_all(value_grad_group, "head", split_axis=1, concat_axis=2, tiled=True),
    )
    query_raw_gradient, key_unnormed_gradient, query_gain_gradient, key_gain_gradient = heads_back(
        (query_grad_tokens.astype(jnp.float32), key_grad_tokens.astype(jnp.float32))
    )
    query_raw_gradient = query_raw_gradient.astype(jnp.bfloat16).reshape(
        sequence_total, local_rows, QUERY_HEADS * HEAD_SIZE
    )
    key_unnormed_gradient = key_unnormed_gradient.astype(jnp.bfloat16).reshape(
        sequence_total, local_rows, KEY_VALUE_HEADS * HEAD_SIZE
    )
    value_unnormed_gradient = value_gradient_tokens.reshape(
        sequence_total, local_rows, KEY_VALUE_HEADS * HEAD_SIZE
    )
    query_matrix_gradient = jnp.einsum(
        "btd,bte->de", first_normed, query_raw_gradient, preferred_element_type=jnp.float32
    )
    key_matrix_gradient = jnp.einsum(
        "btd,bte->de", first_normed, key_unnormed_gradient, preferred_element_type=jnp.float32
    )
    value_matrix_gradient = jnp.einsum(
        "btd,bte->de", first_normed, value_unnormed_gradient, preferred_element_type=jnp.float32
    )
    normed_one_gradient = jnp.einsum(
        "bte,de->btd", query_raw_gradient, query_matrix, preferred_element_type=jnp.float32
    )
    normed_one_gradient = normed_one_gradient + jnp.einsum(
        "bte,de->btd", key_unnormed_gradient, key_matrix, preferred_element_type=jnp.float32
    )
    normed_one_gradient = normed_one_gradient + jnp.einsum(
        "bte,de->btd", value_unnormed_gradient, value_matrix, preferred_element_type=jnp.float32
    )
    token_part, gain_one_gradient = norm_one_back(normed_one_gradient)
    tokens_gradient = (resid_gradient + token_part).astype(jnp.bfloat16)
    attention_sums = (
        lax.psum_scatter(gain_one_gradient, ("blk", "head"), scatter_dimension=0, tiled=True),
        lax.psum_scatter(query_matrix_gradient, ("blk", "head"), scatter_dimension=0, tiled=True),
        lax.psum_scatter(key_matrix_gradient, ("blk", "head"), scatter_dimension=0, tiled=True),
        lax.psum_scatter(value_matrix_gradient, ("blk", "head"), scatter_dimension=0, tiled=True),
        lax.psum_scatter(query_gain_gradient, ("blk", "head"), scatter_dimension=0, tiled=True),
        lax.psum_scatter(key_gain_gradient, ("blk", "head"), scatter_dimension=0, tiled=True),
        lax.psum_scatter(output_matrix_gradient, ("blk", "head"), scatter_dimension=0, tiled=True),
    )
    return (
        layer_out,
        tokens_gradient,
        attention_sums[0],
        attention_sums[1],
        attention_sums[2],
        attention_sums[3],
        attention_sums[4],
        attention_sums[5],
        attention_sums[6],
        feedforward_sums[0],
        feedforward_sums[1],
        feedforward_sums[2],
        feedforward_sums[3],
    )


LOG2E = math.log2(math.e)
STRIP = 128
CHUNK = 512
ALONG = (((1,), (1,)), ((), ()))
DOWN = (((0,), (0,)), ((), ()))


def two_heads(block):
    return jnp.concatenate([block[:, :HEAD_SIZE], block[:, HEAD_SIZE:]], axis=0)


def side_by_side(rows):
    half = rows.shape[0] // 2
    return jnp.concatenate([rows[:half], rows[half:]], axis=1)


def attend_kernel(place_ref, order_ref, q_ref, kv_ref, out_ref, lse_ref, keys, values):
    step = pl.program_id(0)

    @pl.when(step == 0)
    def _():
        values[:, HEAD_SIZE:] = jnp.ones((values.shape[0], HEAD_SIZE), jnp.bfloat16)

        def sort(index, carry):
            source = pl.multiple_of(order_ref[index] * STRIP, STRIP)
            target = pl.multiple_of(index * STRIP, STRIP)
            keys[pl.ds(target, STRIP), :] = kv_ref[pl.ds(source, STRIP), :HEAD_SIZE]
            values[pl.ds(target, STRIP), :HEAD_SIZE] = kv_ref[pl.ds(source, STRIP), HEAD_SIZE:]
            return carry

        lax.fori_loop(0, kv_ref.shape[0] // STRIP, sort, 0)

    place = place_ref[step]
    queries = two_heads(q_ref[...])
    last = place // (CHUNK // STRIP)

    def part(index, total, masked):
        first = pl.multiple_of(index * CHUNK, CHUNK)
        scores = lax.dot_general(
            queries, keys[pl.ds(first, CHUNK), :], ALONG, preferred_element_type=jnp.float32
        )
        weights = jnp.exp2(scores)
        if masked:
            row = lax.broadcasted_iota(jnp.int32, scores.shape, 0) % STRIP
            column = lax.broadcasted_iota(jnp.int32, scores.shape, 1)
            weights = jnp.where(column - row <= place * STRIP - first, weights, 0.0)
        return total + jnp.dot(
            weights.astype(jnp.bfloat16),
            values[pl.ds(first, CHUNK), :],
            preferred_element_type=jnp.float32,
        )

    total = jnp.zeros((2 * STRIP, 2 * HEAD_SIZE), jnp.float32)
    total = lax.fori_loop(0, last, lambda index, t: part(index, t, False), total)
    total = part(last, total, True)
    norm = total[:, HEAD_SIZE:]
    out_ref[...] = side_by_side(total[:, :HEAD_SIZE] / norm).astype(jnp.bfloat16)
    lse_ref[0] = jnp.transpose(jnp.log2(norm))[:8]


def attend(place, order, queries, kv):
    rows, width = queries.shape
    steps = rows // STRIP
    whole = pl.BlockSpec(kv.shape, lambda i, *_: (0, 0))
    strip = pl.BlockSpec((STRIP, width), lambda i, *_: (i, 0))
    flops = 4 * rows * 2 * kv.shape[0] * HEAD_SIZE // 2
    return pl.pallas_call(
        attend_kernel,
        grid_spec=pltpu.PrefetchScalarGridSpec(
            num_scalar_prefetch=2,
            grid=(steps,),
            in_specs=[strip, whole],
            out_specs=[strip, pl.BlockSpec((1, 8, 2 * STRIP), lambda i, *_: (i, 0, 0))],
            scratch_shapes=[
                pltpu.VMEM((kv.shape[0], HEAD_SIZE), jnp.bfloat16),
                pltpu.VMEM((kv.shape[0], 2 * HEAD_SIZE), jnp.bfloat16),
            ],
        ),
        out_shape=[
            jax.ShapeDtypeStruct((rows, width), jnp.bfloat16),
            jax.ShapeDtypeStruct((steps, 8, 2 * STRIP), jnp.float32),
        ],
        cost_estimate=pl.CostEstimate(
            flops=flops, bytes_accessed=kv.size * 2 + queries.size * 4, transcendentals=rows * kv.shape[0]
        ),
        name="attend",
    )(place, order, queries, kv)


def attend_back_kernel(
    place_ref, order_ref, q_ref, grad_ref, out_ref, lse_ref, kv_ref, dq_ref, dkv_ref,
    keys, values, key_sums, value_sums,
):
    step = pl.program_id(0)
    strips = kv_ref.shape[0] // STRIP

    @pl.when(step == 0)
    def _():
        key_sums[...] = jnp.zeros_like(key_sums)
        value_sums[...] = jnp.zeros_like(value_sums)

        def sort(index, carry):
            source = pl.multiple_of(order_ref[index] * STRIP, STRIP)
            target = pl.multiple_of(index * STRIP, STRIP)
            keys[pl.ds(target, STRIP), :] = kv_ref[pl.ds(source, STRIP), :HEAD_SIZE]
            values[pl.ds(target, STRIP), :] = kv_ref[pl.ds(source, STRIP), HEAD_SIZE:]
            return carry

        lax.fori_loop(0, strips, sort, 0)

    place = place_ref[step]
    queries = two_heads(q_ref[...])
    grads = two_heads(grad_ref[...])
    product = grads.astype(jnp.float32) * two_heads(out_ref[...]).astype(jnp.float32)
    delta = jnp.sum(jnp.transpose(product), axis=0, keepdims=True)
    lse = lse_ref[0, :1]
    last = place // (CHUNK // STRIP)

    def part(index, total, masked):
        first = pl.multiple_of(index * CHUNK, CHUNK)
        here = pl.ds(first, CHUNK)
        key_rows = keys[here, :]
        scores = lax.dot_general(key_rows, queries, ALONG, preferred_element_type=jnp.float32)
        weights = jnp.exp2(scores - lse)
        if masked:
            row = lax.broadcasted_iota(jnp.int32, scores.shape, 0)
            column = lax.broadcasted_iota(jnp.int32, scores.shape, 1) % STRIP
            weights = jnp.where(row - column <= place * STRIP - first, weights, 0.0)
        slopes = lax.dot_general(
            values[here, :], grads, ALONG, preferred_element_type=jnp.float32
        )
        score_grads = (weights * (slopes - delta)).astype(jnp.bfloat16)
        value_sums[here, :] += jnp.dot(
            weights.astype(jnp.bfloat16), grads, preferred_element_type=jnp.float32
        )
        key_sums[here, :] += jnp.dot(score_grads, queries, preferred_element_type=jnp.float32)
        return total + lax.dot_general(
            score_grads, key_rows, DOWN, preferred_element_type=jnp.float32
        )

    total = jnp.zeros((2 * STRIP, HEAD_SIZE), jnp.float32)
    total = lax.fori_loop(0, last, lambda index, t: part(index, t, False), total)
    total = part(last, total, True)
    dq_ref[...] = side_by_side(total * (1.0 / math.sqrt(HEAD_SIZE))).astype(jnp.bfloat16)

    @pl.when(step == pl.num_programs(0) - 1)
    def _():
        def spread(index, carry):
            target = pl.multiple_of(order_ref[index] * STRIP, STRIP)
            source = pl.multiple_of(index * STRIP, STRIP)
            dkv_ref[pl.ds(target, STRIP), :HEAD_SIZE] = (
                key_sums[pl.ds(source, STRIP), :] * (1.0 / LOG2E)
            ).astype(jnp.bfloat16)
            dkv_ref[pl.ds(target, STRIP), HEAD_SIZE:] = value_sums[
                pl.ds(source, STRIP), :
            ].astype(jnp.bfloat16)
            return carry

        lax.fori_loop(0, strips, spread, 0)


def attend_back(place, order, queries, grads, attended, lse, kv):
    rows, width = queries.shape
    steps = rows // STRIP
    total = kv.shape[0]
    whole = pl.BlockSpec(kv.shape, lambda i, *_: (0, 0))
    strip = pl.BlockSpec((STRIP, width), lambda i, *_: (i, 0))
    return pl.pallas_call(
        attend_back_kernel,
        grid_spec=pltpu.PrefetchScalarGridSpec(
            num_scalar_prefetch=2,
            grid=(steps,),
            in_specs=[
                strip, strip, strip, pl.BlockSpec((1, 8, 2 * STRIP), lambda i, *_: (i, 0, 0)), whole,
            ],
            out_specs=[strip, whole],
            scratch_shapes=[
                pltpu.VMEM((total, HEAD_SIZE), jnp.bfloat16),
                pltpu.VMEM((total, HEAD_SIZE), jnp.bfloat16),
                pltpu.VMEM((total, HEAD_SIZE), jnp.float32),
                pltpu.VMEM((total, HEAD_SIZE), jnp.float32),
            ],
        ),
        out_shape=[
            jax.ShapeDtypeStruct((rows, width), jnp.bfloat16),
            jax.ShapeDtypeStruct(kv.shape, jnp.bfloat16),
        ],
        cost_estimate=pl.CostEstimate(
            flops=10 * rows * 2 * total * HEAD_SIZE // 2,
            bytes_accessed=kv.size * 4 + queries.size * 8,
            transcendentals=rows * total,
        ),
        name="attend_back",
    )(place, order, queries, grads, attended, lse, kv)


def matmul(left, right, dims=(((1,), (0,)), ((), ()))):
    return lax.dot_general(left, right, dims, preferred_element_type=jnp.float32)


RING = (0, 2, 4, 6, 7, 5, 3, 1)
STRIPS = (0, 1, 7, 2, 6, 3, 5, 4)
GROUPS = ((0, 3), (3, 5), (5, 7), (7, 8))


def hop(value, by):
    count = len(RING)
    return lax.ppermute(value, "blk", [(RING[i], RING[(i + by) % count]) for i in range(count)])


def cross(value, by):
    return lax.ppermute(value, "head", [(i, i ^ by) for i in range(4)])


def add(left, right):
    return (left.astype(jnp.float32) + right.astype(jnp.float32)).astype(left.dtype)


def tied(values, extra):
    if not extra:
        return values
    return lax.optimization_barrier((*values, *extra))[: len(values)]


def no_fill(step, got):
    return ()


def ring_gather(own, fill=no_fill):
    half = own.shape[0] // 2
    got = {0: own}
    left = right = own
    for step in (1, 2, 3):
        got[step], got[8 - step] = left, right = hop(left, -1), hop(right, 1)
        left, right = tied((left, right), fill(step, got))
    got[4] = jnp.concatenate([hop(left[:half], -1), hop(right[half:], 1)], axis=0)
    fill(4, got)
    return [got[s] for s in STRIPS]


def ring_scatter(part, fill=no_fill):
    half = part[0].shape[0] // 2
    up, down = hop(part[4][:half], 1), hop(part[4][half:], -1)
    up = jnp.concatenate([add(part[3][:half], up), part[3][half:]], axis=0)
    down = jnp.concatenate([part[5][:half], add(part[5][half:], down)], axis=0)
    for step in (2, 1):
        up, down = tied((up, down), fill(3 - step, None))
        up, down = add(part[step], hop(up, 1)), add(part[8 - step], hop(down, -1))
    up, down = tied((up, down), fill(3, None))
    up, down = hop(up, 1), hop(down, -1)
    wide = jnp.float32
    return part[0].astype(wide) + up.astype(wide) + down.astype(wide)


def ring_swap(pieces, rows, fill=no_fill):
    cut = 4 * rows + rows // 2
    right, left = pieces[rows:cut], pieces[cut:]
    from_left, from_right = [], []
    for step in (1, 2, 3, 4):
        right, left = hop(right, 1), hop(left, -1)
        if step < 4:
            from_left.append(right[:rows])
            from_right.append(left[-rows:])
            right, left = tied((right[rows:], left[:-rows]), fill(step, None))
    return jnp.concatenate(
        [pieces[:rows], *from_right, right, left, *reversed(from_left)], axis=0
    )


def gather_cross(own):
    far = cross(own, 2)
    return own, cross(own, 1), far, cross(far, 1)


def scatter_cross(pieces):
    half = pieces.shape[0] // 2
    kept = add(pieces[:half], cross(pieces[half:], 1))
    return add(kept[: half // 2], cross(kept[half // 2 :], 2))


def slice_attn_kernel(at_ref, q_ref, k_ref, v_ref, gain_ref, out_ref):
    rows, cols = q_ref.shape
    out_ref[:rows, :cols] = q_ref[...]
    out_ref[:rows, cols : cols + HEAD_SIZE] = k_ref[...]
    out_ref[:rows, cols + HEAD_SIZE :] = v_ref[...]
    out_ref[rows:, :] = gain_ref[...]


def slice_attn(at, query, key, value, gains):
    count = at.shape[0]
    rows, pad = query.shape[0], gains.shape[0]
    widths = [w.shape[1] // count for w in (query, key, value)]
    specs = [pl.BlockSpec((rows, w), lambda i, at: (0, at[i])) for w in widths]
    return pl.pallas_call(
        slice_attn_kernel,
        grid_spec=pltpu.PrefetchScalarGridSpec(
            num_scalar_prefetch=1,
            grid=(count,),
            in_specs=specs + [pl.BlockSpec(gains.shape, lambda i, at: (0, 0))],
            out_specs=pl.BlockSpec((rows + pad, sum(widths)), lambda i, at: (i, 0)),
        ),
        out_shape=jax.ShapeDtypeStruct((count * (rows + pad), sum(widths)), jnp.bfloat16),
        name="slice_attn",
    )(at, query, key, value, gains)


def slice_ff_kernel(at_ref, gate_ref, up_ref, out_ref):
    cols = gate_ref.shape[1]
    out_ref[:, :cols] = gate_ref[...]
    out_ref[:, cols:] = up_ref[...]


def slice_ff(at, gate, up):
    count = at.shape[0]
    rows, cols = gate.shape[0], gate.shape[1] // count
    spec = pl.BlockSpec((rows, cols), lambda i, at: (0, at[i]))
    return pl.pallas_call(
        slice_ff_kernel,
        grid_spec=pltpu.PrefetchScalarGridSpec(
            num_scalar_prefetch=1,
            grid=(count,),
            in_specs=[spec, spec],
            out_specs=pl.BlockSpec((rows, 2 * cols), lambda i, at: (i, 0)),
        ),
        out_shape=jax.ShapeDtypeStruct((count * rows, 2 * cols), jnp.bfloat16),
        name="slice_ff",
    )(at, gate, up)


def assemble_kernel(at_ref, *refs, rows):
    inputs, outputs = refs[:4], refs[4:]
    own = at_ref[8]
    for j, piece in enumerate(inputs):
        outputs[0][0, own ^ j] = piece[:rows]
        if len(outputs) > 1:
            outputs[1][0, own ^ j] = piece[rows:]


def assemble(at, pieces, rows):
    count = at.shape[0] - 1
    total, cols = pieces[0].shape
    each = total // count
    parts = [rows] if each == rows else [rows, each - rows]
    return pl.pallas_call(
        lambda *refs: assemble_kernel(*refs, rows=rows),
        grid_spec=pltpu.PrefetchScalarGridSpec(
            num_scalar_prefetch=1,
            grid=(count,),
            in_specs=[pl.BlockSpec((each, cols), lambda i, at: (i, 0))] * 4,
            out_specs=[
                pl.BlockSpec((1, 4, part, cols), lambda i, at: (at[i], 0, 0, 0)) for part in parts
            ],
        ),
        out_shape=[
            jax.ShapeDtypeStruct((count, 4, part, cols), jnp.bfloat16) for part in parts
        ],
        name="assemble",
    )(at, *pieces)


def weight_grads_kernel(at_ref, left_ref, right_ref, *refs, rows):
    out_ref, held = refs[-2:]
    own = at_ref[8]
    sums = lax.dot_general(left_ref[...], right_ref[...], DOWN, preferred_element_type=jnp.float32)
    held[...] = sums.astype(jnp.bfloat16).reshape(held.shape)
    for k, j in enumerate((0, 2, 1, 3)):
        out_ref[k, 0, :rows] = held[own ^ j]
        if len(refs) > 2:
            out_ref[k, 0, rows:] = refs[0][0, own ^ j]


def weight_grads(at, left, right, rows, extra=None):
    count = at.shape[0] - 1
    tokens, cols = right.shape
    each = rows if extra is None else rows + extra.shape[2]
    in_specs = [
        pl.BlockSpec((tokens, 4 * rows), lambda i, at: (0, at[i])),
        pl.BlockSpec((tokens, cols), lambda i, at: (0, 0)),
    ]
    operands = [left, right]
    if extra is not None:
        in_specs.append(pl.BlockSpec((1, *extra.shape[1:]), lambda i, at: (at[i], 0, 0, 0)))
        operands.append(extra)
    out = pl.pallas_call(
        lambda *refs: weight_grads_kernel(*refs, rows=rows),
        grid_spec=pltpu.PrefetchScalarGridSpec(
            num_scalar_prefetch=1,
            grid=(count,),
            in_specs=in_specs,
            out_specs=pl.BlockSpec((4, 1, each, cols), lambda i, at: (0, i, 0, 0)),
            scratch_shapes=[pltpu.VMEM((4, rows, cols), jnp.bfloat16)],
        ),
        out_shape=jax.ShapeDtypeStruct((4, count, each, cols), jnp.bfloat16),
        cost_estimate=pl.CostEstimate(
            flops=2 * left.size * cols,
            bytes_accessed=2 * (left.size + right.size + left.shape[1] * cols),
            transcendentals=0,
        ),
        name="weight_grads",
    )(at, *operands)
    return out.reshape(4 * count * each, cols)


def lane_sums(block):
    return sum(block[:, i : i + 128] for i in range(0, block.shape[1], 128))


def widen_kernel(at_ref, piece_ref, *refs, count):
    weights, grads, sums_ref = refs[:count], refs[count : 2 * count], refs[2 * count]
    rows = weights[0].shape[0]

    @pl.when(pl.program_id(0) == 0)
    def _():
        for ref in refs[2 * count :]:
            ref[...] = jnp.zeros_like(ref)

    first = 0
    for weight, grad in zip(weights, grads):
        cols = weight.shape[1]
        block = piece_ref[:rows, first : first + cols].astype(jnp.float32)
        grad[...] = block
        sums_ref[...] += lane_sums(block * weight[...].astype(jnp.float32))
        first += cols
    if len(refs) > 2 * count + 1:
        refs[-1][...] += piece_ref[rows:, :].astype(jnp.float32)


def widen(at, pieces, *weights):
    count = at.shape[0]
    rows = weights[0].shape[0]
    each, cols = pieces.shape[0] // count, pieces.shape[1]
    specs = [
        pl.BlockSpec((rows, w.shape[1] // count), lambda i, at: (0, at[i])) for w in weights
    ]
    shapes = [w.shape for w in weights] + [(rows, 128)]
    out_specs = specs + [pl.BlockSpec((rows, 128), lambda i, at: (0, 0))]
    if each > rows:
        shapes.append((each - rows, cols))
        out_specs.append(pl.BlockSpec(shapes[-1], lambda i, at: (0, 0)))
    return pl.pallas_call(
        lambda *refs: widen_kernel(*refs, count=len(weights)),
        grid_spec=pltpu.PrefetchScalarGridSpec(
            num_scalar_prefetch=1,
            grid=(count,),
            in_specs=[pl.BlockSpec((each, cols), lambda i, at: (i, 0))] + specs,
            out_specs=out_specs,
        ),
        out_shape=[jax.ShapeDtypeStruct(shape, jnp.float32) for shape in shapes],
        name="widen",
    )(at, pieces, *weights)


def grouped(strips):
    return [
        jnp.concatenate(strips[a:b], axis=0) if b - a > 1 else strips[a] for a, b in GROUPS
    ]


def split_groups(groups, rows):
    return [
        group[i * rows : (i + 1) * rows]
        for group in groups
        for i in range(group.shape[0] // rows)
    ]


def gather_head(rows):
    return lax.all_gather(rows, "head", axis=0, tiled=True)


def scatter_head(rows):
    return lax.psum_scatter(rows, "head", scatter_dimension=0, tiled=True)


def inverse_rms(rows):
    return lax.rsqrt(jnp.mean(rows * rows, axis=-1, keepdims=True) + EPS)


def turn(rows, cosine, sine):
    half = HEAD_SIZE // 2
    first, second = rows[:, :half], rows[:, half:]
    return jnp.concatenate(
        [first * cosine - second * sine, second * cosine + first * sine], axis=1
    )


def head_back(grads, raw, gain, cosine, sine):
    rho = inverse_rms(raw)
    unit = raw * rho
    turned = turn(grads.astype(jnp.float32), cosine, -sine)
    gain_part = jnp.sum(turned * unit, axis=0)
    scaled = turned * gain
    return rho * (scaled - unit * jnp.mean(unit * scaled, axis=-1, keepdims=True)), gain_part


def per_device(
    tokens,
    attention_norm,
    query_weight,
    key_projection,
    value_projection,
    query_norm,
    key_norm,
    output_weight,
    feedforward_norm,
    gate_weight,
    up_weight,
    down_weight,
    stretch_order,
    out_cotangent,
):
    blk_count = lax.axis_size("blk")
    head_count = lax.axis_size("head")
    head_index = lax.axis_index("head")
    blk_index = lax.axis_index("blk")
    narrow, wide = jnp.bfloat16, jnp.float32
    tokens, out_cotangent = tokens[0], out_cotangent[0]
    local_rows, model_width = tokens.shape
    group_rows = local_rows * blk_count
    weight_rows = query_weight.shape[0]
    ff_local = gate_weight.shape[1] // blk_count
    group_heads = QUERY_HEADS // blk_count
    query_cols = group_heads * HEAD_SIZE
    attn_cols = query_cols + 2 * HEAD_SIZE
    strip_count = blk_count * head_count
    halves = strip_count // stretch_order.shape[1]
    ring_place = jnp.where(blk_index % 2 == 0, blk_index // 2, 7 - blk_index // 2)

    on = jnp.arange(blk_count, dtype=jnp.int32)
    spot = (ring_place + on) % blk_count
    at = jnp.where(spot < 4, 2 * spot, 15 - 2 * spot).astype(jnp.int32)
    at_own = jnp.concatenate([at, head_index[None].astype(jnp.int32)])
    small = query_norm.shape[0]
    gains = jnp.concatenate([attention_norm, feedforward_norm, query_norm, key_norm])
    gains = jnp.pad(gains[None, :], ((0, 15), (0, attn_cols - gains.shape[0])))
    attn_pieces = slice_attn(at, query_weight, key_projection, value_projection, gains)
    attn_pieces = ring_swap(attn_pieces, weight_rows + 16)
    token_strips = ring_gather(tokens)
    attn_matrix, gain_rows = assemble(at_own, gather_cross(attn_pieces), weight_rows)
    attn_matrix = attn_matrix.reshape(model_width, attn_cols)
    gain_rows = gain_rows[:, :, 0].astype(wide)
    gain_one = gain_rows[:, :, :weight_rows].reshape(1, model_width)
    gain_two = gain_rows[:, :, weight_rows : 2 * weight_rows].reshape(1, model_width)
    first = 2 * weight_rows
    query_gain = gain_rows[:, :, first : first + small].reshape(1, HEAD_SIZE)
    key_gain = gain_rows[:, :, first + small : first + 2 * small].reshape(1, HEAD_SIZE)
    output_rows = gather_head(output_weight)
    down_matrix = gather_head(down_weight)

    numbers = jnp.arange(strip_count, dtype=jnp.int32)
    ring_spot = (ring_place + jnp.asarray(STRIPS, jnp.int32)) % blk_count
    strip_blk = jnp.where(ring_spot < 4, 2 * ring_spot, 15 - 2 * ring_spot)
    strip_head = head_index ^ jnp.asarray((0, 2, 1, 3), jnp.int32)
    strip = (strip_blk[None, :] * head_count + strip_head[:, None]).reshape(strip_count)
    slots = jnp.arange(stretch_order.shape[1], dtype=jnp.int32)
    held = jnp.sum(
        jnp.where((strip // halves)[:, None] == slots[None, :], stretch_order, 0), axis=1
    )
    strip_place = held * halves + strip % halves
    order = jnp.sum(
        jnp.where(strip_place[None, :] == numbers[:, None], numbers[None, :], 0), axis=1
    ).astype(jnp.int32)
    place = strip_place[:blk_count].astype(jnp.int32)
    positions = (
        place[:, None] * local_rows + jnp.arange(local_rows, dtype=jnp.int32)[None, :]
    ).reshape(group_rows)
    phases = angles(positions, HEAD_SIZE)[:, 0, :]
    cosine, sine = jnp.cos(phases), jnp.sin(phases)

    tokens_wide = tokens.astype(wide)
    raw_groups, normed_groups, query_groups, kv_groups = [], [], [], []
    for (first, last), rows in zip(GROUPS, grouped(token_strips)):
        here = slice(first * local_rows, last * local_rows)
        rows = rows.astype(wide)
        normed = (rows * inverse_rms(rows) * gain_one).astype(narrow)
        raw = matmul(normed, attn_matrix)
        heads = []
        for h in range(group_heads + 1):
            part = raw[:, h * HEAD_SIZE : (h + 1) * HEAD_SIZE]
            gain = query_gain if h < group_heads else key_gain
            part = turn(part * inverse_rms(part) * gain, cosine[here], sine[here])
            if h < group_heads:
                part = part * (LOG2E / math.sqrt(HEAD_SIZE))
            heads.append(part.astype(narrow))
        raw_groups.append(raw)
        normed_groups.append(normed)
        query_groups.append(jnp.concatenate(heads[:group_heads], axis=1))
        kv_groups.append(
            jnp.concatenate(
                [heads[group_heads], raw[:, query_cols + HEAD_SIZE :].astype(narrow)], axis=1
            )
        )
    first_normed = jnp.concatenate(normed_groups, axis=0)
    attn_raw = jnp.concatenate(raw_groups, axis=0)
    query_rows = jnp.concatenate(query_groups, axis=0)
    kv_own = jnp.concatenate(kv_groups, axis=0)
    own, near, far, both = gather_cross(kv_own)
    kv = jnp.concatenate([own, far, near, both], axis=0)
    attended, lse = attend(place, order, query_rows, kv)

    ties = {1: (query_rows, kv_own), 2: (kv,), 3: (attended,)}
    ff_pieces, cotangent = tied(
        (slice_ff(at, gate_weight, up_weight), out_cotangent), (token_strips[-1],)
    )
    ff_pieces = ring_swap(ff_pieces, weight_rows, lambda step, got: ties[step])
    cotangent_strips = ring_gather(cotangent, lambda step, got: ties.get(step, ()))
    ff_matrix = assemble(at_own, gather_cross(ff_pieces), weight_rows)[0].reshape(
        model_width, 2 * ff_local
    )

    def by_groups(rows):
        return [rows[a * local_rows : b * local_rows] for a, b in GROUPS]

    def by_strips(groups):
        return dict(zip(STRIPS, split_groups(groups, local_rows)))

    def group_of(got, index):
        first, last = GROUPS[index]
        return jnp.concatenate([got[s] for s in STRIPS[first:last]], axis=0)

    cotangent_groups = grouped(cotangent_strips)
    branch_parts = [matmul(rows, output_rows).astype(narrow) for rows in by_groups(attended)]
    branch = ring_scatter(by_strips(branch_parts))
    resid = tokens_wide + branch
    rho_two = inverse_rms(resid)
    unit_two = resid * rho_two
    hidden_grads = [matmul(rows, down_matrix, ALONG) for rows in cotangent_groups]

    second_groups, hidden_groups, ff_gradient_groups = [], [], []

    def feed_forward(step, got):
        if step == 1:
            return ()
        rows = group_of(got, step - 2)
        ff_raw = matmul(rows, ff_matrix)
        gate, up_proj = ff_raw[:, :ff_local], ff_raw[:, ff_local:]
        sigma = jax.nn.sigmoid(gate)
        swish = gate * sigma
        hidden_gradient = hidden_grads[step - 2]
        gate_gradient = hidden_gradient * up_proj * (sigma * (1.0 + gate * (1.0 - sigma)))
        second_groups.append(rows)
        hidden_groups.append((swish * up_proj).astype(narrow))
        ff_gradient_groups.append(
            jnp.concatenate([gate_gradient, hidden_gradient * swish], 1).astype(narrow)
        )
        return hidden_groups[-1], ff_gradient_groups[-1]

    second_strips = ring_gather((unit_two * gain_two).astype(narrow), feed_forward)
    feed_forward(5, dict(zip(STRIPS, second_strips)))
    second_normed = jnp.concatenate(second_groups, axis=0)
    group_cotangent = jnp.concatenate(cotangent_groups, axis=0)
    hidden = jnp.concatenate(hidden_groups, axis=0)
    ff_gradient = jnp.concatenate(ff_gradient_groups, axis=0)
    ff_matrix_gradient = weight_grads(at_own, second_normed, ff_gradient, weight_rows)
    down_gradient = matmul(hidden, group_cotangent, DOWN).astype(narrow)
    out_parts = [matmul(rows, down_matrix).astype(narrow) for rows in hidden_groups]
    second_parts = [
        matmul(rows, ff_matrix, ALONG).astype(narrow) for rows in ff_gradient_groups
    ]
    fillers = {1: (ff_matrix_gradient,), 2: (down_gradient,), 3: tuple(out_parts)}
    second_gradient = ring_scatter(by_strips(second_parts), lambda step, got: fillers[step])
    down_gradient = scatter_head(down_gradient)
    ff_matrix_gradient = scatter_cross(ff_matrix_gradient)
    scaled = gain_two * second_gradient
    resid_gradient = out_cotangent.astype(wide) + rho_two * (
        scaled - unit_two * jnp.mean(unit_two * scaled, axis=-1, keepdims=True)
    )
    branch_gradient = resid_gradient.astype(narrow)
    branch_strips = ring_gather(branch_gradient)

    branch_groups = grouped(branch_strips)
    attended_gradient = jnp.concatenate(
        [matmul(rows, output_rows, ALONG).astype(narrow) for rows in branch_groups], axis=0
    )
    output_weight_gradient = scatter_head(
        matmul(attended, jnp.concatenate(branch_groups, axis=0), DOWN).astype(narrow)
    ).astype(wide)
    query_grads, kv_grads = attend_back(
        place, order, query_rows, attended_gradient, attended, lse, kv
    )
    kv_sums = scatter_cross(kv_grads)

    ties = {1: (query_grads,), 2: (kv_sums,), 3: ()}
    out_strips = by_strips(out_parts)
    out_strips[4], ff_matrix_gradient = tied(
        (out_strips[4], ff_matrix_gradient), (branch_strips[-1],)
    )
    out_part = ring_scatter(out_strips, lambda step, got: ties[step])
    layer_out = (resid + out_part).astype(narrow)
    ff_matrix_gradient = ring_swap(
        ff_matrix_gradient, weight_rows, lambda step, got: ties[step]
    )
    gate_weight_gradient, up_weight_gradient, norm_sums = widen(
        at, ff_matrix_gradient, gate_weight, up_weight
    )
    feedforward_norm_gradient = jnp.sum(norm_sums, axis=1) / feedforward_norm.astype(wide)

    attn_gradient, gain_parts = [], []
    for h in range(group_heads + 1):
        cols = slice(h * HEAD_SIZE, (h + 1) * HEAD_SIZE)
        grads = query_grads[:, cols] if h < group_heads else kv_sums[:, :HEAD_SIZE]
        gain = query_gain if h < group_heads else key_gain
        raw_gradient, gain_part = head_back(grads, attn_raw[:, cols], gain, cosine, sine)
        attn_gradient.append(raw_gradient.astype(narrow))
        gain_parts.append(gain_part)
    attn_gradient = jnp.concatenate(attn_gradient + [kv_sums[:, HEAD_SIZE:]], axis=1)
    first_parts = [
        matmul(rows, attn_matrix, ALONG).astype(narrow) for rows in by_groups(attn_gradient)
    ]
    gain_parts = jnp.stack(
        [
            sum(gain_parts[:group_heads]).reshape(blk_count, head_count, small),
            gain_parts[group_heads].reshape(blk_count, head_count, small),
        ],
        axis=2,
    ).reshape(blk_count, head_count, 1, 2 * small)
    gain_parts = jnp.pad(
        gain_parts.astype(narrow), ((0, 0), (0, 0), (0, 15), (0, attn_cols - 2 * small))
    )
    attn_matrix_gradient = weight_grads(
        at_own, first_normed, attn_gradient, weight_rows, gain_parts
    )
    first_gradient = ring_scatter(
        by_strips(first_parts),
        lambda step, got: (attn_matrix_gradient,) if step == 1 else (),
    )
    attn_matrix_gradient = ring_swap(scatter_cross(attn_matrix_gradient), weight_rows + 16)
    (
        query_weight_gradient,
        key_weight_gradient,
        value_weight_gradient,
        norm_sums,
        gain_sums,
    ) = widen(at, attn_matrix_gradient, query_weight, key_projection, value_projection)
    gain_sums = gain_sums[0]
    attention_norm_gradient = jnp.sum(norm_sums, axis=1) / attention_norm.astype(wide)
    rho_one = inverse_rms(tokens_wide)
    unit_one = tokens_wide * rho_one
    scaled = gain_one * first_gradient
    tokens_gradient = resid_gradient + rho_one * (
        scaled - unit_one * jnp.mean(unit_one * scaled, axis=-1, keepdims=True)
    )
    return (
        layer_out[None],
        tokens_gradient.astype(narrow)[None],
        attention_norm_gradient,
        query_weight_gradient,
        key_weight_gradient,
        value_weight_gradient,
        gain_sums[:small],
        gain_sums[small : 2 * small],
        output_weight_gradient,
        feedforward_norm_gradient,
        gate_weight_gradient,
        up_weight_gradient,
        down_gradient.astype(wide),
    )


def solution(mesh):
    placed = (
        P(None, ("blk", "head"), None),
        P(("blk", "head")),
        P(("blk", "head"), None),
        P(("blk", "head"), None),
        P(("blk", "head"), None),
        P(("blk", "head")),
        P(("blk", "head")),
        P(("blk", "head"), None),
        P(("blk", "head")),
        P(("blk", "head"), None),
        P(("blk", "head"), None),
        P(("blk", "head"), None),
        P(),
        P(None, ("blk", "head"), None),
    )
    fits = mesh.shape["blk"] == KEY_VALUE_HEADS and mesh.shape["head"] == 4
    return jax.shard_map(
        per_device if fits else per_device_by_tokens,
        mesh=mesh,
        in_specs=placed,
        out_specs=(
            P(None, ("blk", "head"), None),
            P(None, ("blk", "head"), None),
            P(("blk", "head")),
            P(("blk", "head"), None),
            P(("blk", "head"), None),
            P(("blk", "head"), None),
            P(("blk", "head")),
            P(("blk", "head")),
            P(("blk", "head"), None),
            P(("blk", "head")),
            P(("blk", "head"), None),
            P(("blk", "head"), None),
            P(("blk", "head"), None),
        ),
        check_vma=False,
    )
```

```python
import math

import jax
import jax.numpy as jnp
from jax import lax
from jax.experimental import pallas as pl
from jax.experimental.pallas import tpu as pltpu
from jax.sharding import PartitionSpec as P

QUERY_HEADS = 16
KEY_VALUE_HEADS = 8
HEAD_SIZE = 128


EPS = 1e-06
NEG = -1e30
ROPE_BASE = 1000000.0


def passed_along(value, axis, by):
    count = lax.axis_size(axis)
    return lax.ppermute(value, axis, [(i, (i + by) % count) for i in range(count)])


def norm_rows(inputs, norm_gain):
    return inputs * lax.rsqrt(jnp.mean(inputs * inputs, axis=-1, keepdims=True) + EPS) * norm_gain


def rotary(inputs, phases):
    half_width = inputs.shape[-1] // 2
    cosine = jnp.cos(phases)
    sine_term = jnp.sin(phases)
    first_half = inputs[..., :half_width]
    second_half = inputs[..., half_width:]
    return jnp.concatenate(
        [
            first_half * cosine - second_half * sine_term,
            second_half * cosine + first_half * sine_term,
        ],
        axis=-1,
    )


def angles(positions, head_width):
    half_width = head_width // 2
    frequency = jnp.exp(
        jnp.arange(half_width, dtype=jnp.float32) * (-2.0 * math.log(ROPE_BASE) / head_width)
    )
    return positions.astype(jnp.float32)[..., None, None] * frequency


def token_positions(stretch_order, first_row, row_count, stretch_rows):
    row_index = first_row + jnp.arange(row_count, dtype=jnp.int32)
    slot_index = row_index // stretch_rows
    matches = slot_index[:, None] == jnp.arange(stretch_order.shape[1], dtype=jnp.int32)[None, :]
    picked = jnp.sum(jnp.where(matches[None], stretch_order[:, None, :], 0), axis=-1)
    return picked * stretch_rows + row_index % stretch_rows


def per_device_by_tokens(
    tokens,
    attention_norm,
    query_weight,
    key_projection,
    value_projection,
    query_norm,
    key_norm,
    output_weight,
    feedforward_norm,
    gate_weight,
    up_weight,
    down_weight,
    stretch_order,
    out_cotangent,
):
    count_of_heads = lax.axis_size("head")
    span_count = lax.axis_size("blk")
    span_index = lax.axis_index("blk")
    head_index = lax.axis_index("head")
    sequence_total = tokens.shape[0]
    local_rows = tokens.shape[1]
    group_rows = local_rows * count_of_heads
    stretch_rows = group_rows // 2
    heads_shared = KEY_VALUE_HEADS // count_of_heads
    heads_per_group = QUERY_HEADS // KEY_VALUE_HEADS
    score_scale = 1.0 / math.sqrt(HEAD_SIZE)
    gain_one, query_matrix, key_matrix, value_matrix, query_gain, key_gain, output_matrix = (
        lax.all_gather(attention_norm, ("blk", "head"), axis=0, tiled=True),
        lax.all_gather(query_weight, ("blk", "head"), axis=0, tiled=True),
        lax.all_gather(key_projection, ("blk", "head"), axis=0, tiled=True),
        lax.all_gather(value_projection, ("blk", "head"), axis=0, tiled=True),
        lax.all_gather(query_norm, ("blk", "head"), axis=0, tiled=True),
        lax.all_gather(key_norm, ("blk", "head"), axis=0, tiled=True),
        lax.all_gather(output_weight, ("blk", "head"), axis=0, tiled=True),
    )
    gain_two, gate_matrix, up_matrix, down_matrix = (
        lax.all_gather(feedforward_norm, ("blk", "head"), axis=0, tiled=True),
        lax.all_gather(gate_weight, ("blk", "head"), axis=0, tiled=True),
        lax.all_gather(up_weight, ("blk", "head"), axis=0, tiled=True),
        lax.all_gather(down_weight, ("blk", "head"), axis=0, tiled=True),
    )
    gain_one = gain_one.astype(jnp.float32)
    gain_two = gain_two.astype(jnp.float32)
    query_gain = query_gain.astype(jnp.float32)
    key_gain = key_gain.astype(jnp.float32)
    own_first = (span_index * count_of_heads + head_index) * local_rows
    own_pos = token_positions(stretch_order, own_first, local_rows, stretch_rows)
    group_pos = token_positions(stretch_order, span_index * group_rows, group_rows, stretch_rows)
    phases = angles(own_pos, HEAD_SIZE)
    tokens_wide = tokens.astype(jnp.float32)
    first_normed, norm_one_back = jax.vjp(norm_rows, tokens_wide, gain_one)
    first_normed = first_normed.astype(jnp.bfloat16)
    query_raw = jnp.einsum(
        "btd,de->bte", first_normed, query_matrix, preferred_element_type=jnp.float32
    ).reshape(sequence_total, local_rows, QUERY_HEADS, HEAD_SIZE)
    key_unnormed = jnp.einsum(
        "btd,de->bte", first_normed, key_matrix, preferred_element_type=jnp.float32
    ).reshape(sequence_total, local_rows, KEY_VALUE_HEADS, HEAD_SIZE)
    value_tokens = (
        jnp.einsum("btd,de->bte", first_normed, value_matrix, preferred_element_type=jnp.float32)
        .astype(jnp.bfloat16)
        .reshape(sequence_total, local_rows, KEY_VALUE_HEADS, HEAD_SIZE)
    )

    def heads_local(query_in, key_in, query_scale, key_scale):
        return (
            rotary(norm_rows(query_in, query_scale), phases),
            rotary(norm_rows(key_in, key_scale), phases),
        )

    (query_tokens, key_tokens), heads_back = jax.vjp(
        heads_local, query_raw, key_unnormed, query_gain, key_gain
    )
    query_tokens = query_tokens.astype(jnp.bfloat16)
    key_tokens = key_tokens.astype(jnp.bfloat16)
    query_group, key_group, value_group = (
        lax.all_to_all(query_tokens, "head", split_axis=2, concat_axis=1, tiled=True),
        lax.all_to_all(key_tokens, "head", split_axis=2, concat_axis=1, tiled=True),
        lax.all_to_all(value_tokens, "head", split_axis=2, concat_axis=1, tiled=True),
    )
    query_five = query_group.reshape(
        sequence_total, group_rows, heads_shared, heads_per_group, HEAD_SIZE
    )

    def block_update(carry, key_block, value_block, key_pos):
        run_max, run_sum, run_total = carry
        scores = (
            jnp.einsum(
                "bqkgd,bckd->bkgqc", query_five, key_block, preferred_element_type=jnp.float32
            )
            * score_scale
        )
        allowed = key_pos[:, None, None, None, :] <= group_pos[:, None, None, :, None]
        scores = jnp.where(allowed, scores, NEG)
        new_max = jnp.maximum(run_max, jnp.max(scores, axis=-1))
        exponent = jnp.where(allowed, jnp.exp(scores - new_max[..., None]), 0.0)
        factor = jnp.exp(run_max - new_max)
        new_sum = run_sum * factor + jnp.sum(exponent, axis=-1)
        new_total = run_total * factor[..., None] + jnp.einsum(
            "bkgqc,bckd->bkgqd",
            exponent.astype(jnp.bfloat16),
            value_block,
            preferred_element_type=jnp.float32,
        )
        return (new_max, new_sum, new_total)

    def fold_update(carry, key_block, value_block, key_pos):
        result = block_update(carry, key_block, value_block, key_pos)
        return result

    stat_shape = (sequence_total, heads_shared, heads_per_group, group_rows)
    start_state = (
        jnp.full(stat_shape, NEG, jnp.float32),
        jnp.zeros(stat_shape, jnp.float32),
        jnp.zeros(stat_shape + (HEAD_SIZE,), jnp.float32),
    )
    key_piece = lax.all_gather(key_group, "blk", axis=1, tiled=True)
    value_piece = lax.all_gather(value_group, "blk", axis=1, tiled=True)
    piece_rows = key_piece.shape[1]
    block_len = math.gcd(group_rows, piece_rows)

    def inner(block_number, carry_in):
        offset = block_number * block_len
        key_block = lax.dynamic_slice_in_dim(key_piece, offset, block_len, 1)
        value_block = lax.dynamic_slice_in_dim(value_piece, offset, block_len, 1)
        key_pos = token_positions(stretch_order, offset, block_len, stretch_rows)
        return fold_update(carry_in, key_block, value_block, key_pos)

    run_max, run_sum, run_total = lax.fori_loop(0, piece_rows // block_len, inner, start_state)
    log_total = run_max + jnp.log(run_sum)
    attended_five = run_total / run_sum[..., None]
    attended_group = (
        jnp.transpose(attended_five, (0, 3, 1, 2, 4))
        .reshape(sequence_total, group_rows, heads_shared * heads_per_group, HEAD_SIZE)
        .astype(jnp.bfloat16)
    )
    attended_tokens = lax.all_to_all(
        attended_group, "head", split_axis=1, concat_axis=2, tiled=True
    ).reshape(sequence_total, local_rows, QUERY_HEADS * HEAD_SIZE)
    branch = jnp.einsum(
        "bte,ed->btd", attended_tokens, output_matrix, preferred_element_type=jnp.float32
    )
    resid = tokens_wide + branch
    normed_two, norm_two_back = jax.vjp(norm_rows, resid, gain_two)
    normed_two = normed_two.astype(jnp.bfloat16)
    gate = jnp.einsum("btd,df->btf", normed_two, gate_matrix, preferred_element_type=jnp.float32)
    up_proj = jnp.einsum("btd,df->btf", normed_two, up_matrix, preferred_element_type=jnp.float32)

    def swish_product(gate_in, up_in):
        return jax.nn.silu(gate_in) * up_in

    hidden, swish_back = jax.vjp(swish_product, gate, up_proj)
    hidden = hidden.astype(jnp.bfloat16)
    layer_out = (
        resid + jnp.einsum("btf,fd->btd", hidden, down_matrix, preferred_element_type=jnp.float32)
    ).astype(jnp.bfloat16)
    gain_again, gate_matrix, up_matrix, down_matrix = (
        lax.all_gather(feedforward_norm, ("blk", "head"), axis=0, tiled=True),
        lax.all_gather(gate_weight, ("blk", "head"), axis=0, tiled=True),
        lax.all_gather(up_weight, ("blk", "head"), axis=0, tiled=True),
        lax.all_gather(down_weight, ("blk", "head"), axis=0, tiled=True),
    )
    down_gradient = jnp.einsum(
        "btf,btd->fd", hidden, out_cotangent, preferred_element_type=jnp.float32
    )
    hidden_gradient = jnp.einsum(
        "btd,fd->btf", out_cotangent, down_matrix, preferred_element_type=jnp.float32
    )
    gate_gradient, up_gradient = swish_back(hidden_gradient)
    gate_gradient = gate_gradient.astype(jnp.bfloat16)
    up_gradient = up_gradient.astype(jnp.bfloat16)
    gate_matrix_gradient = jnp.einsum(
        "btd,btf->df", normed_two, gate_gradient, preferred_element_type=jnp.float32
    )
    up_matrix_gradient = jnp.einsum(
        "btd,btf->df", normed_two, up_gradient, preferred_element_type=jnp.float32
    )
    normed_two_gradient = jnp.einsum(
        "btf,df->btd", gate_gradient, gate_matrix, preferred_element_type=jnp.float32
    ) + jnp.einsum("btf,df->btd", up_gradient, up_matrix, preferred_element_type=jnp.float32)
    resid_part, gain_two_gradient = norm_two_back(normed_two_gradient)
    resid_gradient = out_cotangent.astype(jnp.float32) + resid_part
    feedforward_sums = (
        lax.psum_scatter(gain_two_gradient, ("blk", "head"), scatter_dimension=0, tiled=True),
        lax.psum_scatter(gate_matrix_gradient, ("blk", "head"), scatter_dimension=0, tiled=True),
        lax.psum_scatter(up_matrix_gradient, ("blk", "head"), scatter_dimension=0, tiled=True),
        lax.psum_scatter(down_gradient, ("blk", "head"), scatter_dimension=0, tiled=True),
    )
    gain_again, query_matrix, key_matrix, value_matrix, query_again, key_again, output_matrix = (
        lax.all_gather(attention_norm, ("blk", "head"), axis=0, tiled=True),
        lax.all_gather(query_weight, ("blk", "head"), axis=0, tiled=True),
        lax.all_gather(key_projection, ("blk", "head"), axis=0, tiled=True),
        lax.all_gather(value_projection, ("blk", "head"), axis=0, tiled=True),
        lax.all_gather(query_norm, ("blk", "head"), axis=0, tiled=True),
        lax.all_gather(key_norm, ("blk", "head"), axis=0, tiled=True),
        lax.all_gather(output_weight, ("blk", "head"), axis=0, tiled=True),
    )
    branch_gradient = resid_gradient.astype(jnp.bfloat16)
    output_matrix_gradient = jnp.einsum(
        "bte,btd->ed", attended_tokens, branch_gradient, preferred_element_type=jnp.float32
    )
    attended_gradient = (
        jnp.einsum(
            "btd,ed->bte", branch_gradient, output_matrix, preferred_element_type=jnp.float32
        )
        .astype(jnp.bfloat16)
        .reshape(sequence_total, local_rows, QUERY_HEADS, HEAD_SIZE)
    )
    attended_grad_group = lax.all_to_all(
        attended_gradient, "head", split_axis=2, concat_axis=1, tiled=True
    ).reshape(sequence_total, group_rows, heads_shared, heads_per_group, HEAD_SIZE)
    delta = jnp.sum(
        jnp.transpose(attended_grad_group.astype(jnp.float32), (0, 2, 3, 1, 4)) * attended_five,
        axis=-1,
    )

    def block_grads(sums_in, key_current, value_current, key_pos):
        key_sum, value_sum, query_sum = sums_in
        scores = (
            jnp.einsum(
                "bqkgd,bckd->bkgqc", query_five, key_current, preferred_element_type=jnp.float32
            )
            * score_scale
        )
        allowed = key_pos[:, None, None, None, :] <= group_pos[:, None, None, :, None]
        weights = jnp.where(allowed, jnp.exp(scores - log_total[..., None]), 0.0)
        probs = weights.astype(jnp.bfloat16)
        value_sum = value_sum + jnp.einsum(
            "bkgqc,bqkgd->bckd", probs, attended_grad_group, preferred_element_type=jnp.float32
        )
        probs_gradient = jnp.einsum(
            "bqkgd,bckd->bkgqc",
            attended_grad_group,
            value_current,
            preferred_element_type=jnp.float32,
        )
        scores_gradient = (weights * (probs_gradient - delta[..., None])).astype(jnp.bfloat16)
        query_sum = (
            query_sum
            + jnp.einsum(
                "bkgqc,bckd->bqkgd",
                scores_gradient,
                key_current,
                preferred_element_type=jnp.float32,
            )
            * score_scale
        )
        key_sum = (
            key_sum
            + jnp.einsum(
                "bkgqc,bqkgd->bckd", scores_gradient, query_five, preferred_element_type=jnp.float32
            )
            * score_scale
        )
        return (key_sum, value_sum, query_sum)

    def pass_step(step_index, carry):
        key_current, value_current, key_sum, value_sum, query_sum = carry
        anchor = (span_index - step_index) % span_count
        key_pos = token_positions(stretch_order, anchor * group_rows, group_rows, stretch_rows)
        key_sum, value_sum, query_sum = block_grads(
            (key_sum, value_sum, query_sum), key_current, value_current, key_pos
        )
        key_current, value_current = passed_along((key_current, value_current), "blk", 1)
        key_sum, value_sum = (
            passed_along(key_sum.astype(jnp.bfloat16), "blk", 1).astype(key_sum.dtype),
            passed_along(value_sum.astype(jnp.bfloat16), "blk", 1).astype(value_sum.dtype),
        )
        return (key_current, value_current, key_sum, value_sum, query_sum)

    kv_zeros = jnp.zeros((sequence_total, group_rows, heads_shared, HEAD_SIZE), jnp.float32)
    query_zeros = jnp.zeros(
        (sequence_total, group_rows, heads_shared, heads_per_group, HEAD_SIZE), jnp.float32
    )
    final_state = lax.fori_loop(
        0, span_count, pass_step, (key_group, value_group, kv_zeros, kv_zeros, query_zeros)
    )
    key_grad_group = final_state[2].astype(jnp.bfloat16)
    value_grad_group = final_state[3].astype(jnp.bfloat16)
    query_grad_group = (
        final_state[4]
        .astype(jnp.bfloat16)
        .reshape(sequence_total, group_rows, heads_shared * heads_per_group, HEAD_SIZE)
    )
    query_grad_tokens, key_grad_tokens, value_gradient_tokens = (
        lax.all_to_all(query_grad_group, "head", split_axis=1, concat_axis=2, tiled=True),
        lax.all_to_all(key_grad_group, "head", split_axis=1, concat_axis=2, tiled=True),
        lax.all_to_all(value_grad_group, "head", split_axis=1, concat_axis=2, tiled=True),
    )
    query_raw_gradient, key_unnormed_gradient, query_gain_gradient, key_gain_gradient = heads_back(
        (query_grad_tokens.astype(jnp.float32), key_grad_tokens.astype(jnp.float32))
    )
    query_raw_gradient = query_raw_gradient.astype(jnp.bfloat16).reshape(
        sequence_total, local_rows, QUERY_HEADS * HEAD_SIZE
    )
    key_unnormed_gradient = key_unnormed_gradient.astype(jnp.bfloat16).reshape(
        sequence_total, local_rows, KEY_VALUE_HEADS * HEAD_SIZE
    )
    value_unnormed_gradient = value_gradient_tokens.reshape(
        sequence_total, local_rows, KEY_VALUE_HEADS * HEAD_SIZE
    )
    query_matrix_gradient = jnp.einsum(
        "btd,bte->de", first_normed, query_raw_gradient, preferred_element_type=jnp.float32
    )
    key_matrix_gradient = jnp.einsum(
        "btd,bte->de", first_normed, key_unnormed_gradient, preferred_element_type=jnp.float32
    )
    value_matrix_gradient = jnp.einsum(
        "btd,bte->de", first_normed, value_unnormed_gradient, preferred_element_type=jnp.float32
    )
    normed_one_gradient = jnp.einsum(
        "bte,de->btd", query_raw_gradient, query_matrix, preferred_element_type=jnp.float32
    )
    normed_one_gradient = normed_one_gradient + jnp.einsum(
        "bte,de->btd", key_unnormed_gradient, key_matrix, preferred_element_type=jnp.float32
    )
    normed_one_gradient = normed_one_gradient + jnp.einsum(
        "bte,de->btd", value_unnormed_gradient, value_matrix, preferred_element_type=jnp.float32
    )
    token_part, gain_one_gradient = norm_one_back(normed_one_gradient)
    tokens_gradient = (resid_gradient + token_part).astype(jnp.bfloat16)
    attention_sums = (
        lax.psum_scatter(gain_one_gradient, ("blk", "head"), scatter_dimension=0, tiled=True),
        lax.psum_scatter(query_matrix_gradient, ("blk", "head"), scatter_dimension=0, tiled=True),
        lax.psum_scatter(key_matrix_gradient, ("blk", "head"), scatter_dimension=0, tiled=True),
        lax.psum_scatter(value_matrix_gradient, ("blk", "head"), scatter_dimension=0, tiled=True),
        lax.psum_scatter(query_gain_gradient, ("blk", "head"), scatter_dimension=0, tiled=True),
        lax.psum_scatter(key_gain_gradient, ("blk", "head"), scatter_dimension=0, tiled=True),
        lax.psum_scatter(output_matrix_gradient, ("blk", "head"), scatter_dimension=0, tiled=True),
    )
    return (
        layer_out,
        tokens_gradient,
        attention_sums[0],
        attention_sums[1],
        attention_sums[2],
        attention_sums[3],
        attention_sums[4],
        attention_sums[5],
        attention_sums[6],
        feedforward_sums[0],
        feedforward_sums[1],
        feedforward_sums[2],
        feedforward_sums[3],
    )


LOG2E = math.log2(math.e)
STRIP = 128
CHUNK = 512
ALONG = (((1,), (1,)), ((), ()))
DOWN = (((0,), (0,)), ((), ()))


def two_heads(block):
    return jnp.concatenate([block[:, :HEAD_SIZE], block[:, HEAD_SIZE:]], axis=0)


def side_by_side(rows):
    half = rows.shape[0] // 2
    return jnp.concatenate([rows[:half], rows[half:]], axis=1)


def attend_kernel(place_ref, order_ref, q_ref, kv_ref, out_ref, lse_ref, keys, values):
    step = pl.program_id(0)

    @pl.when(step == 0)
    def _():
        values[:, HEAD_SIZE:] = jnp.ones((values.shape[0], HEAD_SIZE), jnp.bfloat16)

        def sort(index, carry):
            source = pl.multiple_of(order_ref[index] * STRIP, STRIP)
            target = pl.multiple_of(index * STRIP, STRIP)
            keys[pl.ds(target, STRIP), :] = kv_ref[pl.ds(source, STRIP), :HEAD_SIZE]
            values[pl.ds(target, STRIP), :HEAD_SIZE] = kv_ref[pl.ds(source, STRIP), HEAD_SIZE:]
            return carry

        lax.fori_loop(0, kv_ref.shape[0] // STRIP, sort, 0)

    place = place_ref[step]
    queries = two_heads(q_ref[...])
    last = place // (CHUNK // STRIP)

    def part(index, total, masked):
        first = pl.multiple_of(index * CHUNK, CHUNK)
        scores = lax.dot_general(
            queries, keys[pl.ds(first, CHUNK), :], ALONG, preferred_element_type=jnp.float32
        )
        weights = jnp.exp2(scores)
        if masked:
            row = lax.broadcasted_iota(jnp.int32, scores.shape, 0) % STRIP
            column = lax.broadcasted_iota(jnp.int32, scores.shape, 1)
            weights = jnp.where(column - row <= place * STRIP - first, weights, 0.0)
        return total + jnp.dot(
            weights.astype(jnp.bfloat16),
            values[pl.ds(first, CHUNK), :],
            preferred_element_type=jnp.float32,
        )

    total = jnp.zeros((2 * STRIP, 2 * HEAD_SIZE), jnp.float32)
    total = lax.fori_loop(0, last, lambda index, t: part(index, t, False), total)
    total = part(last, total, True)
    norm = total[:, HEAD_SIZE:]
    out_ref[...] = side_by_side(total[:, :HEAD_SIZE] / norm).astype(jnp.bfloat16)
    lse_ref[0] = jnp.transpose(jnp.log2(norm))[:8]


def attend(place, order, queries, kv):
    rows, width = queries.shape
    steps = rows // STRIP
    whole = pl.BlockSpec(kv.shape, lambda i, *_: (0, 0))
    strip = pl.BlockSpec((STRIP, width), lambda i, *_: (i, 0))
    flops = 4 * rows * 2 * kv.shape[0] * HEAD_SIZE // 2
    return pl.pallas_call(
        attend_kernel,
        grid_spec=pltpu.PrefetchScalarGridSpec(
            num_scalar_prefetch=2,
            grid=(steps,),
            in_specs=[strip, whole],
            out_specs=[strip, pl.BlockSpec((1, 8, 2 * STRIP), lambda i, *_: (i, 0, 0))],
            scratch_shapes=[
                pltpu.VMEM((kv.shape[0], HEAD_SIZE), jnp.bfloat16),
                pltpu.VMEM((kv.shape[0], 2 * HEAD_SIZE), jnp.bfloat16),
            ],
        ),
        out_shape=[
            jax.ShapeDtypeStruct((rows, width), jnp.bfloat16),
            jax.ShapeDtypeStruct((steps, 8, 2 * STRIP), jnp.float32),
        ],
        cost_estimate=pl.CostEstimate(
            flops=flops, bytes_accessed=kv.size * 2 + queries.size * 4, transcendentals=rows * kv.shape[0]
        ),
        name="attend",
    )(place, order, queries, kv)


def attend_back_kernel(
    place_ref, order_ref, q_ref, grad_ref, out_ref, lse_ref, kv_ref, dq_ref, dkv_ref,
    keys, values, key_sums, value_sums,
):
    step = pl.program_id(0)
    strips = kv_ref.shape[0] // STRIP

    @pl.when(step == 0)
    def _():
        key_sums[...] = jnp.zeros_like(key_sums)
        value_sums[...] = jnp.zeros_like(value_sums)

        def sort(index, carry):
            source = pl.multiple_of(order_ref[index] * STRIP, STRIP)
            target = pl.multiple_of(index * STRIP, STRIP)
            keys[pl.ds(target, STRIP), :] = kv_ref[pl.ds(source, STRIP), :HEAD_SIZE]
            values[pl.ds(target, STRIP), :] = kv_ref[pl.ds(source, STRIP), HEAD_SIZE:]
            return carry

        lax.fori_loop(0, strips, sort, 0)

    place = place_ref[step]
    queries = two_heads(q_ref[...])
    grads = two_heads(grad_ref[...])
    product = grads.astype(jnp.float32) * two_heads(out_ref[...]).astype(jnp.float32)
    delta = jnp.sum(jnp.transpose(product), axis=0, keepdims=True)
    lse = lse_ref[0, :1]
    last = place // (CHUNK // STRIP)

    def part(index, total, masked):
        first = pl.multiple_of(index * CHUNK, CHUNK)
        here = pl.ds(first, CHUNK)
        key_rows = keys[here, :]
        scores = lax.dot_general(key_rows, queries, ALONG, preferred_element_type=jnp.float32)
        weights = jnp.exp2(scores - lse)
        if masked:
            row = lax.broadcasted_iota(jnp.int32, scores.shape, 0)
            column = lax.broadcasted_iota(jnp.int32, scores.shape, 1) % STRIP
            weights = jnp.where(row - column <= place * STRIP - first, weights, 0.0)
        slopes = lax.dot_general(
            values[here, :], grads, ALONG, preferred_element_type=jnp.float32
        )
        score_grads = (weights * (slopes - delta)).astype(jnp.bfloat16)
        value_sums[here, :] += jnp.dot(
            weights.astype(jnp.bfloat16), grads, preferred_element_type=jnp.float32
        )
        key_sums[here, :] += jnp.dot(score_grads, queries, preferred_element_type=jnp.float32)
        return total + lax.dot_general(
            score_grads, key_rows, DOWN, preferred_element_type=jnp.float32
        )

    total = jnp.zeros((2 * STRIP, HEAD_SIZE), jnp.float32)
    total = lax.fori_loop(0, last, lambda index, t: part(index, t, False), total)
    total = part(last, total, True)
    dq_ref[...] = side_by_side(total * (1.0 / math.sqrt(HEAD_SIZE))).astype(jnp.bfloat16)

    @pl.when(step == pl.num_programs(0) - 1)
    def _():
        def spread(index, carry):
            target = pl.multiple_of(order_ref[index] * STRIP, STRIP)
            source = pl.multiple_of(index * STRIP, STRIP)
            dkv_ref[pl.ds(target, STRIP), :HEAD_SIZE] = (
                key_sums[pl.ds(source, STRIP), :] * (1.0 / LOG2E)
            ).astype(jnp.bfloat16)
            dkv_ref[pl.ds(target, STRIP), HEAD_SIZE:] = value_sums[
                pl.ds(source, STRIP), :
            ].astype(jnp.bfloat16)
            return carry

        lax.fori_loop(0, strips, spread, 0)


def attend_back(place, order, queries, grads, attended, lse, kv):
    rows, width = queries.shape
    steps = rows // STRIP
    total = kv.shape[0]
    whole = pl.BlockSpec(kv.shape, lambda i, *_: (0, 0))
    strip = pl.BlockSpec((STRIP, width), lambda i, *_: (i, 0))
    return pl.pallas_call(
        attend_back_kernel,
        grid_spec=pltpu.PrefetchScalarGridSpec(
            num_scalar_prefetch=2,
            grid=(steps,),
            in_specs=[
                strip, strip, strip, pl.BlockSpec((1, 8, 2 * STRIP), lambda i, *_: (i, 0, 0)), whole,
            ],
            out_specs=[strip, whole],
            scratch_shapes=[
                pltpu.VMEM((total, HEAD_SIZE), jnp.bfloat16),
                pltpu.VMEM((total, HEAD_SIZE), jnp.bfloat16),
                pltpu.VMEM((total, HEAD_SIZE), jnp.float32),
                pltpu.VMEM((total, HEAD_SIZE), jnp.float32),
            ],
        ),
        out_shape=[
            jax.ShapeDtypeStruct((rows, width), jnp.bfloat16),
            jax.ShapeDtypeStruct(kv.shape, jnp.bfloat16),
        ],
        cost_estimate=pl.CostEstimate(
            flops=10 * rows * 2 * total * HEAD_SIZE // 2,
            bytes_accessed=kv.size * 4 + queries.size * 8,
            transcendentals=rows * total,
        ),
        name="attend_back",
    )(place, order, queries, grads, attended, lse, kv)


def matmul(left, right, dims=(((1,), (0,)), ((), ()))):
    return lax.dot_general(left, right, dims, preferred_element_type=jnp.float32)


RING = (0, 2, 4, 6, 7, 5, 3, 1)
STRIPS = (0, 1, 7, 2, 6, 3, 5, 4)
GROUPS = ((0, 3), (3, 5), (5, 7), (7, 8))


def hop(value, by):
    count = len(RING)
    return lax.ppermute(value, "blk", [(RING[i], RING[(i + by) % count]) for i in range(count)])


def cross(value, by):
    return lax.ppermute(value, "head", [(i, i ^ by) for i in range(4)])


def add(left, right):
    return (left.astype(jnp.float32) + right.astype(jnp.float32)).astype(left.dtype)


class Gather:
    def __init__(self, own):
        self.got, self.step = {0: own}, 0
        self.state = (own, own)

    def go(self):
        self.step += 1
        left, right = self.state
        if self.step < 4:
            self.state = hop(left, -1), hop(right, 1)
            self.got[self.step], self.got[8 - self.step] = self.state
        else:
            half = left.shape[0] // 2
            self.got[4] = jnp.concatenate([hop(left[:half], -1), hop(right[half:], 1)], axis=0)
            self.state = (self.got[4],)

    def strips(self):
        return [self.got[s] for s in STRIPS]

    def group(self, index):
        first, last = GROUPS[index]
        return jnp.concatenate([self.got[s] for s in STRIPS[first:last]], axis=0)


class Scatter:
    def __init__(self, part):
        self.part, self.step = part, 0
        self.half = part[4].shape[0] // 2
        self.state = (part[4][: self.half], part[4][self.half :])

    def go(self):
        self.step += 1
        half, part = self.half, self.part
        up, down = hop(self.state[0], 1), hop(self.state[1], -1)
        if self.step == 1:
            up = jnp.concatenate([add(part[3][:half], up), part[3][half:]], axis=0)
            down = jnp.concatenate([part[5][:half], add(part[5][half:], down)], axis=0)
        elif self.step < 4:
            up, down = add(part[4 - self.step], up), add(part[4 + self.step], down)
        self.state = up, down

    def total(self):
        up, down = self.state
        wide = jnp.float32
        return self.part[0].astype(wide) + up.astype(wide) + down.astype(wide)


class Swap:
    def __init__(self, pieces, rows):
        cut = 4 * rows + rows // 2
        self.rows, self.step = rows, 0
        self.own, self.from_left, self.from_right = pieces[:rows], [], []
        self.state = (pieces[rows:cut], pieces[cut:])

    def go(self):
        self.step += 1
        rows = self.rows
        right, left = hop(self.state[0], 1), hop(self.state[1], -1)
        if self.step < 4:
            self.from_left.append(right[:rows])
            self.from_right.append(left[-rows:])
            right, left = right[rows:], left[:-rows]
        self.state = right, left

    def result(self):
        right, left = self.state
        return jnp.concatenate(
            [self.own, *self.from_right, right, left, *reversed(self.from_left)], axis=0
        )


def hold(rings, *extra):
    states, extra = lax.optimization_barrier(([ring.state for ring in rings], extra))
    for ring, state in zip(rings, states):
        ring.state = state
    return extra[0] if len(extra) == 1 else extra


def scatter_cross(own, far, sent):
    moved = cross(sent, 1)
    half = own.shape[0]
    return add(own, moved[:half]), add(far, moved[half:])


def slice_kernel(at_ref, *refs):
    first = 0
    for ref in refs[:-1]:
        refs[-1][:, first : first + ref.shape[1]] = ref[...]
        first += ref.shape[1]


def slice_pieces(at, *weights):
    count = at.shape[0]
    rows = weights[0].shape[0]
    widths = [w.shape[1] // count for w in weights]
    return pl.pallas_call(
        slice_kernel,
        grid_spec=pltpu.PrefetchScalarGridSpec(
            num_scalar_prefetch=1,
            grid=(count,),
            in_specs=[pl.BlockSpec((rows, w), lambda i, at: (0, at[i])) for w in widths],
            out_specs=pl.BlockSpec((rows, sum(widths)), lambda i, at: (i, 0)),
        ),
        out_shape=jax.ShapeDtypeStruct((count * rows, sum(widths)), jnp.bfloat16),
        name="slice_pieces",
    )(at, *weights)


def assemble_kernel(at_ref, *refs):
    own = at_ref[8]
    for j, piece in enumerate(refs[:4]):
        refs[4][0, own ^ j] = piece[...]


def assemble(at, pieces, rows):
    count = at.shape[0] - 1
    total, cols = pieces[0].shape
    return pl.pallas_call(
        assemble_kernel,
        grid_spec=pltpu.PrefetchScalarGridSpec(
            num_scalar_prefetch=1,
            grid=(count,),
            in_specs=[pl.BlockSpec((rows, cols), lambda i, at: (i, 0))] * 4,
            out_specs=pl.BlockSpec((1, 4, rows, cols), lambda i, at: (at[i], 0, 0, 0)),
        ),
        out_shape=jax.ShapeDtypeStruct((count, 4, rows, cols), jnp.bfloat16),
        name="assemble",
    )(at, *pieces).reshape(4 * total, cols)


def spun(rows, cosine, sine):
    return rows * cosine + pltpu.roll(rows, HEAD_SIZE // 2, 1) * sine


def project_kernel(at_ref, *refs, strips):
    token_refs, refs = refs[:strips], refs[strips:]
    pieces, refs = refs[:4], refs[4:]
    gain_ref, head_gain_ref, cos_ref, sin_ref = refs[:4]
    normed_ref, raw_ref, q_ref, kv_ref, matrix_ref = refs[4:]
    rows = pieces[0].shape[0] // 8
    own = at_ref[8]
    for s in range(8):
        for j in range(4):
            first = pl.multiple_of((at_ref[s] * 4 + (own ^ j)) * rows, rows)
            matrix_ref[pl.ds(first, rows), :] = pieces[j][s * rows : (s + 1) * rows, :]
    first = 0
    for ref in token_refs:
        block = ref[...].astype(jnp.float32)
        here = slice(first, first + ref.shape[0])
        normed_ref[here, :] = (block * inverse_rms(block) * gain_ref[...]).astype(jnp.bfloat16)
        first += ref.shape[0]
    query_cols = q_ref.shape[1]
    step = 256
    for first in range(0, q_ref.shape[0], step):
        here = slice(first, first + step)
        raw = jnp.dot(normed_ref[here, :], matrix_ref[...], preferred_element_type=jnp.float32)
        raw_ref[here, :] = raw
        cosine, sine = cos_ref[here, :], sin_ref[here, :]
        for col in range(0, query_cols + HEAD_SIZE, HEAD_SIZE):
            part = raw[:, col : col + HEAD_SIZE]
            if col < query_cols:
                part = spun(part * inverse_rms(part) * head_gain_ref[:1], cosine, sine)
                part = part * (LOG2E / math.sqrt(HEAD_SIZE))
                q_ref[here, col : col + HEAD_SIZE] = part.astype(jnp.bfloat16)
            else:
                part = spun(part * inverse_rms(part) * head_gain_ref[1:2], cosine, sine)
                kv_ref[here, :HEAD_SIZE] = part.astype(jnp.bfloat16)
        kv_ref[here, HEAD_SIZE:] = raw[:, query_cols + HEAD_SIZE :].astype(jnp.bfloat16)


def project(at, strips, pieces, gain, head_gains, cosine, sine, query_cols):
    rows = sum(strip.shape[0] for strip in strips)
    width = strips[0].shape[1]
    cols = pieces[0].shape[1]
    vmem = pl.BlockSpec(memory_space=pltpu.VMEM)
    operands = (*strips, *pieces, gain, head_gains, cosine, sine)
    narrow = jnp.bfloat16
    return pl.pallas_call(
        lambda *refs: project_kernel(*refs, strips=len(strips)),
        in_specs=[pl.BlockSpec(memory_space=pltpu.SMEM)] + [vmem] * len(operands),
        out_specs=[vmem] * 5,
        out_shape=[
            jax.ShapeDtypeStruct((rows, width), narrow),
            jax.ShapeDtypeStruct((rows, cols), jnp.float32),
            jax.ShapeDtypeStruct((rows, query_cols), narrow),
            jax.ShapeDtypeStruct((rows, 2 * HEAD_SIZE), narrow),
            jax.ShapeDtypeStruct((width, cols), narrow),
        ],
        cost_estimate=pl.CostEstimate(
            flops=2 * rows * width * cols, bytes_accessed=16 << 20, transcendentals=0
        ),
        name="project",
    )(at, *operands)


def project_back_kernel(
    dq_ref, dkv_ref, raw_ref, head_gain_ref, cos_ref, sin_ref, matrix_ref,
    grad_ref, part_ref, gain_ref,
):
    query_cols = dq_ref.shape[1]
    step = 256
    gain_ref[...] = jnp.zeros_like(gain_ref)
    for first in range(0, dq_ref.shape[0], step):
        here = slice(first, first + step)
        cosine, sine = cos_ref[here, :], sin_ref[here, :]
        for col in range(0, query_cols + HEAD_SIZE, HEAD_SIZE):
            cols = slice(col, col + HEAD_SIZE)
            which = 0 if col < query_cols else 1
            grads = dkv_ref[here, :HEAD_SIZE] if which else dq_ref[here, cols]
            raw = raw_ref[here, cols]
            rho = inverse_rms(raw)
            unit = raw * rho
            turned = spun(grads.astype(jnp.float32), cosine, -sine)
            gain_ref[which : which + 1, :] += jnp.sum(turned * unit, axis=0, keepdims=True)
            scaled = turned * head_gain_ref[which : which + 1]
            back = rho * (scaled - unit * jnp.mean(unit * scaled, axis=-1, keepdims=True))
            grad_ref[here, cols] = back.astype(jnp.bfloat16)
        grad_ref[here, query_cols + HEAD_SIZE :] = dkv_ref[here, HEAD_SIZE:]
        part_ref[here, :] = lax.dot_general(
            grad_ref[here, :], matrix_ref[...], ALONG, preferred_element_type=jnp.float32
        ).astype(jnp.bfloat16)


def project_back(query_grads, kv_grads, raw, head_gains, cosine, sine, matrix):
    rows, cols = raw.shape
    vmem = pl.BlockSpec(memory_space=pltpu.VMEM)
    return pl.pallas_call(
        project_back_kernel,
        in_specs=[vmem] * 7,
        out_specs=[vmem] * 3,
        out_shape=[
            jax.ShapeDtypeStruct((rows, cols), jnp.bfloat16),
            jax.ShapeDtypeStruct((rows, matrix.shape[0]), jnp.bfloat16),
            jax.ShapeDtypeStruct((8, HEAD_SIZE), jnp.float32),
        ],
        cost_estimate=pl.CostEstimate(
            flops=2 * rows * matrix.size, bytes_accessed=12 << 20, transcendentals=0
        ),
        name="project_back",
    )(query_grads, kv_grads, raw, head_gains, cosine, sine, matrix)


def dots(lefts, rights, dims):
    return sum(
        lax.dot_general(left[...], right[...], dims, preferred_element_type=jnp.float32)
        for left, right in zip(lefts, rights)
    )


def weight_grads_kernel(at_ref, *refs, groups):
    own_ref, far_ref, sent_ref, held = refs[-4:]
    own = at_ref[8]
    sums = dots(refs[:groups], refs[groups : 2 * groups], DOWN)
    held[...] = sums.astype(jnp.bfloat16).reshape(held.shape)
    own_ref[...] = held[own]
    far_ref[...] = held[own ^ 2]
    sent_ref[0] = held[own ^ 1]
    sent_ref[1] = held[own ^ 3]


def weight_grads(at, lefts, rights, rows):
    count = at.shape[0] - 1
    cols = rights[0].shape[1]
    total = sum(left.shape[0] for left in lefts)
    part = pl.BlockSpec((rows, cols), lambda i, at: (i, 0))
    shape = jax.ShapeDtypeStruct((count * rows, cols), jnp.bfloat16)
    own, far, sent = pl.pallas_call(
        lambda *refs: weight_grads_kernel(*refs, groups=len(lefts)),
        grid_spec=pltpu.PrefetchScalarGridSpec(
            num_scalar_prefetch=1,
            grid=(count,),
            in_specs=[
                pl.BlockSpec((left.shape[0], 4 * rows), lambda i, at: (0, at[i]))
                for left in lefts
            ]
            + [pl.BlockSpec(right.shape, lambda i, at: (0, 0)) for right in rights],
            out_specs=[part, part, pl.BlockSpec((2, rows, cols), lambda i, at: (0, i, 0))],
            scratch_shapes=[pltpu.VMEM((4, rows, cols), jnp.bfloat16)],
        ),
        out_shape=[
            shape, shape, jax.ShapeDtypeStruct((2, count * rows, cols), jnp.bfloat16),
        ],
        cost_estimate=pl.CostEstimate(
            flops=2 * total * lefts[0].shape[1] * cols,
            bytes_accessed=2 * total * (lefts[0].shape[1] + cols),
            transcendentals=0,
        ),
        name="weight_grads",
    )(at, *lefts, *rights)
    return own, far, sent.reshape(2 * count * rows, cols)


def row_grads_kernel(*refs, groups):
    refs[-1][...] = dots(refs[:groups], refs[groups : 2 * groups], DOWN).astype(jnp.bfloat16)


def row_grads(lefts, rights, block=256):
    out_rows, cols = lefts[0].shape[1], rights[0].shape[1]
    total = sum(left.shape[0] for left in lefts)
    return pl.pallas_call(
        lambda *refs: row_grads_kernel(*refs, groups=len(lefts)),
        grid=(out_rows // block,),
        in_specs=[pl.BlockSpec((left.shape[0], block), lambda i: (0, i)) for left in lefts]
        + [pl.BlockSpec(right.shape, lambda i: (0, 0)) for right in rights],
        out_specs=pl.BlockSpec((block, cols), lambda i: (i, 0)),
        out_shape=jax.ShapeDtypeStruct((out_rows, cols), jnp.bfloat16),
        cost_estimate=pl.CostEstimate(
            flops=2 * total * out_rows * cols,
            bytes_accessed=2 * total * (out_rows + cols),
            transcendentals=0,
        ),
        name="row_grads",
    )(*lefts, *rights)


def stack_project_kernel(*refs):
    matrix_ref, out_ref = refs[-2:]
    first = 0
    for ref in refs[:-2]:
        out_ref[first : first + ref.shape[0], :] = lax.dot_general(
            ref[...], matrix_ref[...], ALONG, preferred_element_type=jnp.float32
        ).astype(jnp.bfloat16)
        first += ref.shape[0]


def stack_project(groups, matrix):
    rows = sum(group.shape[0] for group in groups)
    vmem = pl.BlockSpec(memory_space=pltpu.VMEM)
    return pl.pallas_call(
        stack_project_kernel,
        in_specs=[vmem] * (len(groups) + 1),
        out_specs=vmem,
        out_shape=jax.ShapeDtypeStruct((rows, matrix.shape[0]), jnp.bfloat16),
        cost_estimate=pl.CostEstimate(
            flops=2 * rows * matrix.size, bytes_accessed=2 * rows * matrix.shape[1], transcendentals=0
        ),
        name="stack_project",
    )(*groups, matrix)


def lane_sums(block):
    return sum(block[:, i : i + 128] for i in range(0, block.shape[1], 128))


def widen_kernel(at_ref, piece_ref, *refs, count):
    weights, grads, sums_ref = refs[:count], refs[count : 2 * count], refs[2 * count]
    rows = weights[0].shape[0]

    @pl.when(pl.program_id(0) == 0)
    def _():
        sums_ref[...] = jnp.zeros_like(sums_ref)

    first = 0
    for weight, grad in zip(weights, grads):
        cols = weight.shape[1]
        block = piece_ref[:rows, first : first + cols].astype(jnp.float32)
        grad[...] = block
        sums_ref[...] += lane_sums(block * weight[...].astype(jnp.float32))
        first += cols


def widen(at, pieces, *weights):
    count = at.shape[0]
    rows = weights[0].shape[0]
    each, cols = pieces.shape[0] // count, pieces.shape[1]
    specs = [
        pl.BlockSpec((rows, w.shape[1] // count), lambda i, at: (0, at[i])) for w in weights
    ]
    shapes = [w.shape for w in weights] + [(rows, 128)]
    out_specs = specs + [pl.BlockSpec((rows, 128), lambda i, at: (0, 0))]
    return pl.pallas_call(
        lambda *refs: widen_kernel(*refs, count=len(weights)),
        grid_spec=pltpu.PrefetchScalarGridSpec(
            num_scalar_prefetch=1,
            grid=(count,),
            in_specs=[pl.BlockSpec((each, cols), lambda i, at: (i, 0))] + specs,
            out_specs=out_specs,
        ),
        out_shape=[jax.ShapeDtypeStruct(shape, jnp.float32) for shape in shapes],
        name="widen",
    )(at, pieces, *weights)


def grouped(strips):
    return [
        jnp.concatenate(strips[a:b], axis=0) if b - a > 1 else strips[a] for a, b in GROUPS
    ]


def split_groups(groups, rows):
    return [
        group[i * rows : (i + 1) * rows]
        for group in groups
        for i in range(group.shape[0] // rows)
    ]


def gather_head(rows):
    return lax.all_gather(rows, "head", axis=0, tiled=True)


def scatter_head(rows):
    return lax.psum_scatter(rows, "head", scatter_dimension=0, tiled=True)


def inverse_rms(rows):
    return lax.rsqrt(jnp.mean(rows * rows, axis=-1, keepdims=True) + EPS)


def per_device(
    tokens,
    attention_norm,
    query_weight,
    key_projection,
    value_projection,
    query_norm,
    key_norm,
    output_weight,
    feedforward_norm,
    gate_weight,
    up_weight,
    down_weight,
    stretch_order,
    out_cotangent,
):
    blk_count = lax.axis_size("blk")
    head_count = lax.axis_size("head")
    head_index = lax.axis_index("head")
    blk_index = lax.axis_index("blk")
    narrow, wide = jnp.bfloat16, jnp.float32
    tokens, out_cotangent = tokens[0], out_cotangent[0]
    local_rows, model_width = tokens.shape
    group_rows = local_rows * blk_count
    weight_rows = query_weight.shape[0]
    ff_local = gate_weight.shape[1] // blk_count
    query_cols = QUERY_HEADS // blk_count * HEAD_SIZE
    strip_count = blk_count * head_count
    halves = strip_count // stretch_order.shape[1]
    ring_place = jnp.where(blk_index % 2 == 0, blk_index // 2, 7 - blk_index // 2)

    spot = (ring_place + jnp.arange(blk_count, dtype=jnp.int32)) % blk_count
    at = jnp.where(spot < 4, 2 * spot, 15 - 2 * spot).astype(jnp.int32)
    at_own = jnp.concatenate([at, head_index[None].astype(jnp.int32)])
    numbers = jnp.arange(strip_count, dtype=jnp.int32)
    ring_spot = (ring_place + jnp.asarray(STRIPS, jnp.int32)) % blk_count
    strip_blk = jnp.where(ring_spot < 4, 2 * ring_spot, 15 - 2 * ring_spot)
    strip_head = head_index ^ jnp.asarray((0, 2, 1, 3), jnp.int32)
    strip = (strip_blk[None, :] * head_count + strip_head[:, None]).reshape(strip_count)
    slots = jnp.arange(stretch_order.shape[1], dtype=jnp.int32)
    held = jnp.sum(
        jnp.where((strip // halves)[:, None] == slots[None, :], stretch_order, 0), axis=1
    )
    strip_place = held * halves + strip % halves
    order = jnp.sum(
        jnp.where(strip_place[None, :] == numbers[:, None], numbers[None, :], 0), axis=1
    ).astype(jnp.int32)
    place = strip_place[:blk_count].astype(jnp.int32)
    positions = (
        place[:, None] * local_rows + jnp.arange(local_rows, dtype=jnp.int32)[None, :]
    ).reshape(group_rows)
    phases = angles(positions, HEAD_SIZE)[:, 0, :]
    cosine, sine = jnp.cos(phases), jnp.sin(phases)
    cosine = jnp.concatenate([cosine, cosine], axis=1)
    sine = jnp.concatenate([-sine, sine], axis=1)

    small = query_norm.shape[0]
    gains = jnp.concatenate([attention_norm, feedforward_norm, query_norm, key_norm])
    gains = lax.all_gather(gains, ("blk", "head"), axis=0).astype(wide)
    gain_one = gains[:, :weight_rows].reshape(1, model_width)
    gain_two = gains[:, weight_rows : 2 * weight_rows].reshape(1, model_width)
    first = 2 * weight_rows
    head_gains = jnp.concatenate(
        [
            gains[:, first : first + small].reshape(1, HEAD_SIZE),
            gains[:, first + small :].reshape(1, HEAD_SIZE),
            jnp.zeros((6, HEAD_SIZE), wide),
        ],
        axis=0,
    )
    down_matrix = gather_head(down_weight)
    output_rows = gather_head(output_weight)

    attn_swap = Swap(
        slice_pieces(at, query_weight, key_projection, value_projection), weight_rows
    )
    token_ring = Gather(tokens)
    ff_slices = slice_pieces(at, gate_weight, up_weight)
    for step in range(4):
        attn_swap.go()
        token_ring.go()
        if step == 0:
            ff_slices, cosine, sine = hold((attn_swap, token_ring), ff_slices, cosine, sine)
        elif step < 3:
            hold((attn_swap, token_ring))
    ff_swap, cotangent_ring = Swap(ff_slices, weight_rows), Gather(out_cotangent)
    own = hold((token_ring, ff_swap), attn_swap.result())
    near, far = cross(own, 1), cross(own, 2)
    ff_swap.go()
    own, near, far = hold((ff_swap, cotangent_ring), own, near, far)
    both = cross(far, 1)
    ff_swap.go()
    own, near, far, both = hold((ff_swap, cotangent_ring), own, near, far, both)

    first_normed, attn_raw, query_rows, own, attn_matrix = project(
        at_own, token_ring.strips(), (own, near, far, both),
        gain_one, head_gains, cosine, sine, query_cols,
    )
    ff_swap.go()
    cotangent_ring.go()
    own = hold((ff_swap, cotangent_ring), own)
    near, far = cross(own, 1), cross(own, 2)
    ff_swap.go()
    cotangent_ring.go()
    own, near, far, ff_own = hold((cotangent_ring,), own, near, far, ff_swap.result())
    both = cross(far, 1)
    ff_near, ff_far = cross(ff_own, 1), cross(ff_own, 2)
    kv = jnp.concatenate([own, far, near, both], axis=0)
    kv = hold((cotangent_ring,), kv)
    attended, lse = attend(place, order, query_rows, kv)
    cotangent_ring.go()

    def by_groups(rows):
        return [rows[a * local_rows : b * local_rows] for a, b in GROUPS]

    def by_strips(groups):
        return dict(zip(STRIPS, split_groups(groups, local_rows)))

    attended = hold((cotangent_ring,), attended)
    branch_ring = Scatter(
        by_strips([matmul(rows, output_rows).astype(narrow) for rows in by_groups(attended)])
    )
    branch_ring.go()
    cotangent_ring.go()
    hold((branch_ring, cotangent_ring))
    branch_ring.go()
    ff_near, ff_far = hold((branch_ring,), ff_near, ff_far)
    ff_both = cross(ff_far, 1)
    branch_ring.go()
    cotangent_groups = grouped(cotangent_ring.strips())
    hidden_grads = [matmul(rows, down_matrix, ALONG) for rows in cotangent_groups]
    hidden_grads, ff_own, ff_near, ff_far, ff_both = hold(
        (branch_ring,), hidden_grads, ff_own, ff_near, ff_far, ff_both
    )
    branch_ring.go()
    ff_matrix = assemble(at_own, (ff_own, ff_near, ff_far, ff_both), weight_rows)
    ff_matrix = hold((branch_ring,), ff_matrix)
    tokens_wide = tokens.astype(wide)
    resid = tokens_wide + branch_ring.total()
    rho_two = inverse_rms(resid)
    unit_two = resid * rho_two

    second_ring = Gather((unit_two * gain_two).astype(narrow))
    second_groups, hidden_groups, ff_gradient_groups = [], [], []

    def feed_forward(index):
        rows = second_ring.group(index)
        ff_raw = matmul(rows, ff_matrix)
        gate, up_proj = ff_raw[:, :ff_local], ff_raw[:, ff_local:]
        sigma = jax.nn.sigmoid(gate)
        swish = gate * sigma
        hidden_gradient = hidden_grads[index]
        gate_gradient = hidden_gradient * up_proj * (sigma * (1.0 + gate * (1.0 - sigma)))
        hidden = (swish * up_proj).astype(narrow)
        gradient = jnp.concatenate([gate_gradient, hidden_gradient * swish], 1).astype(narrow)
        if index < 3:
            rows, hidden, gradient = hold((second_ring,), rows, hidden, gradient)
        second_groups.append(rows)
        hidden_groups.append(hidden)
        ff_gradient_groups.append(gradient)

    second_ring.go()
    hold((second_ring,))
    for index in range(3):
        second_ring.go()
        feed_forward(index)
    feed_forward(3)

    def back(index):
        return matmul(ff_gradient_groups[index], ff_matrix, ALONG).astype(narrow)

    def split(group):
        return [group[i : i + local_rows] for i in range(0, group.shape[0], local_rows)]

    parts = {4: back(3)}
    resid_ring = Scatter(parts)
    parts[3], parts[5] = split(hold((), back(2)))
    resid_ring.go()
    parts[2], parts[6] = split(hold((resid_ring,), back(1)))
    resid_ring.go()
    parts[0], parts[1], parts[7] = split(hold((resid_ring,), back(0)))
    resid_ring.go()
    ff_own, ff_far, ff_sent = hold(
        (resid_ring,), *weight_grads(at_own, second_groups, ff_gradient_groups, weight_rows)
    )
    resid_ring.go()
    ff_own, ff_far = scatter_cross(ff_own, ff_far, ff_sent)
    down_gradient = row_grads(hidden_groups, cotangent_groups)
    down_gradient, ff_own, ff_far = hold((resid_ring,), down_gradient, ff_own, ff_far)
    down_gradient = scatter_head(down_gradient)
    ff_far = cross(ff_far, 2)
    scaled = gain_two * resid_ring.total()
    resid_gradient = out_cotangent.astype(wide) + rho_two * (
        scaled - unit_two * jnp.mean(unit_two * scaled, axis=-1, keepdims=True)
    )

    grad_ring = Gather(resid_gradient.astype(narrow))
    grad_ring.go()
    out_parts = [matmul(rows, down_matrix).astype(narrow) for rows in hidden_groups]
    out_parts = hold((grad_ring,), *out_parts)
    out_ring = Scatter(by_strips(out_parts))
    grad_ring.go()
    hold((grad_ring,))
    grad_ring.go()
    ff_far = hold((grad_ring,), ff_far)
    ff_swap = Swap(add(ff_own, ff_far), weight_rows)
    grad_ring.go()
    hold((grad_ring, ff_swap, out_ring))
    grad_strips = grad_ring.strips()
    attended_gradient = stack_project(grad_strips, output_rows)
    out_ring.go()
    hold((out_ring,), attended_gradient)
    query_grads, kv_grads = attend_back(
        place, order, query_rows, attended_gradient, attended, lse, kv
    )
    ff_swap.go()
    out_ring.go()
    query_grads, kv_grads = hold((out_ring, ff_swap), query_grads, kv_grads)
    kv_own, kv_far = scatter_cross(
        kv_grads[:group_rows], kv_grads[group_rows : 2 * group_rows], kv_grads[2 * group_rows :]
    )
    kv_far = cross(kv_far, 2)
    out_ring.go()
    ff_swap.go()
    output_weight_gradient = row_grads([attended], [jnp.concatenate(grad_strips, axis=0)])
    output_weight_gradient, kv_grads = hold(
        (out_ring, ff_swap), output_weight_gradient, add(kv_own, kv_far)
    )
    output_weight_gradient = scatter_head(output_weight_gradient).astype(wide)
    attn_gradient, first_parts, gain_sums = project_back(
        query_grads, kv_grads, attn_raw, head_gains, cosine, sine, attn_matrix
    )
    ff_swap.go()
    out_ring.go()
    attn_gradient, first_parts = hold((out_ring, ff_swap), attn_gradient, first_parts)
    layer_out = (resid + out_ring.total()).astype(narrow)
    gain_sums = lax.psum(gain_sums[:2], ("blk", "head"))
    token_ring = Scatter(by_strips(by_groups(first_parts)))
    token_ring.go()
    ff_swap.go()
    attn_own, attn_far, attn_sent = hold(
        (token_ring, ff_swap),
        *weight_grads(at_own, [first_normed], [attn_gradient], weight_rows),
    )
    attn_own, attn_far = scatter_cross(attn_own, attn_far, attn_sent)
    attn_far = cross(attn_far, 2)
    token_ring.go()
    gate_weight_gradient, up_weight_gradient, norm_sums = widen(
        at, ff_swap.result(), gate_weight, up_weight
    )
    feedforward_norm_gradient = jnp.sum(norm_sums, axis=1) / feedforward_norm.astype(wide)
    attn_swap = Swap(add(attn_own, attn_far), weight_rows)
    hold((token_ring, attn_swap), gate_weight_gradient)
    attn_swap.go()
    token_ring.go()
    hold((token_ring, attn_swap))
    attn_swap.go()
    token_ring.go()
    attn_swap.go()
    attn_swap.go()
    query_weight_gradient, key_weight_gradient, value_weight_gradient, norm_sums = widen(
        at, attn_swap.result(), query_weight, key_projection, value_projection
    )
    attention_norm_gradient = jnp.sum(norm_sums, axis=1) / attention_norm.astype(wide)
    own_first = (blk_index * head_count + head_index) * small
    gain_sums = lax.dynamic_slice_in_dim(gain_sums, own_first, small, 1)
    rho_one = inverse_rms(tokens_wide)
    unit_one = tokens_wide * rho_one
    scaled = gain_one * token_ring.total()
    tokens_gradient = resid_gradient + rho_one * (
        scaled - unit_one * jnp.mean(unit_one * scaled, axis=-1, keepdims=True)
    )
    return (
        layer_out[None],
        tokens_gradient.astype(narrow)[None],
        attention_norm_gradient,
        query_weight_gradient,
        key_weight_gradient,
        value_weight_gradient,
        gain_sums[0],
        gain_sums[1],
        output_weight_gradient,
        feedforward_norm_gradient,
        gate_weight_gradient,
        up_weight_gradient,
        down_gradient.astype(wide),
    )


def solution(mesh):
    placed = (
        P(None, ("blk", "head"), None),
        P(("blk", "head")),
        P(("blk", "head"), None),
        P(("blk", "head"), None),
        P(("blk", "head"), None),
        P(("blk", "head")),
        P(("blk", "head")),
        P(("blk", "head"), None),
        P(("blk", "head")),
        P(("blk", "head"), None),
        P(("blk", "head"), None),
        P(("blk", "head"), None),
        P(),
        P(None, ("blk", "head"), None),
    )
    fits = mesh.shape["blk"] == KEY_VALUE_HEADS and mesh.shape["head"] == 4
    return jax.shard_map(
        per_device if fits else per_device_by_tokens,
        mesh=mesh,
        in_specs=placed,
        out_specs=(
            P(None, ("blk", "head"), None),
            P(None, ("blk", "head"), None),
            P(("blk", "head")),
            P(("blk", "head"), None),
            P(("blk", "head"), None),
            P(("blk", "head"), None),
            P(("blk", "head")),
            P(("blk", "head")),
            P(("blk", "head"), None),
            P(("blk", "head")),
            P(("blk", "head"), None),
            P(("blk", "head"), None),
            P(("blk", "head"), None),
        ),
        check_vma=False,
    )
```

```python
import math

import jax
import jax.numpy as jnp
from jax import lax
from jax.experimental import pallas as pl
from jax.experimental.pallas import tpu as pltpu
from jax.sharding import PartitionSpec as P

QUERY_HEADS = 16
KEY_VALUE_HEADS = 8
HEAD_SIZE = 128


EPS = 1e-06
NEG = -1e30
ROPE_BASE = 1000000.0


def passed_along(value, axis, by):
    count = lax.axis_size(axis)
    return lax.ppermute(value, axis, [(i, (i + by) % count) for i in range(count)])


def norm_rows(inputs, norm_gain):
    return inputs * lax.rsqrt(jnp.mean(inputs * inputs, axis=-1, keepdims=True) + EPS) * norm_gain


def rotary(inputs, phases):
    half_width = inputs.shape[-1] // 2
    cosine = jnp.cos(phases)
    sine_term = jnp.sin(phases)
    first_half = inputs[..., :half_width]
    second_half = inputs[..., half_width:]
    return jnp.concatenate(
        [
            first_half * cosine - second_half * sine_term,
            second_half * cosine + first_half * sine_term,
        ],
        axis=-1,
    )


def angles(positions, head_width):
    half_width = head_width // 2
    frequency = jnp.exp(
        jnp.arange(half_width, dtype=jnp.float32) * (-2.0 * math.log(ROPE_BASE) / head_width)
    )
    return positions.astype(jnp.float32)[..., None, None] * frequency


def token_positions(stretch_order, first_row, row_count, stretch_rows):
    row_index = first_row + jnp.arange(row_count, dtype=jnp.int32)
    slot_index = row_index // stretch_rows
    matches = slot_index[:, None] == jnp.arange(stretch_order.shape[1], dtype=jnp.int32)[None, :]
    picked = jnp.sum(jnp.where(matches[None], stretch_order[:, None, :], 0), axis=-1)
    return picked * stretch_rows + row_index % stretch_rows


def per_device_by_tokens(
    tokens,
    attention_norm,
    query_weight,
    key_projection,
    value_projection,
    query_norm,
    key_norm,
    output_weight,
    feedforward_norm,
    gate_weight,
    up_weight,
    down_weight,
    stretch_order,
    out_cotangent,
):
    count_of_heads = lax.axis_size("head")
    span_count = lax.axis_size("blk")
    span_index = lax.axis_index("blk")
    head_index = lax.axis_index("head")
    sequence_total = tokens.shape[0]
    local_rows = tokens.shape[1]
    group_rows = local_rows * count_of_heads
    stretch_rows = group_rows // 2
    heads_shared = KEY_VALUE_HEADS // count_of_heads
    heads_per_group = QUERY_HEADS // KEY_VALUE_HEADS
    score_scale = 1.0 / math.sqrt(HEAD_SIZE)
    gain_one, query_matrix, key_matrix, value_matrix, query_gain, key_gain, output_matrix = (
        lax.all_gather(attention_norm, ("blk", "head"), axis=0, tiled=True),
        lax.all_gather(query_weight, ("blk", "head"), axis=0, tiled=True),
        lax.all_gather(key_projection, ("blk", "head"), axis=0, tiled=True),
        lax.all_gather(value_projection, ("blk", "head"), axis=0, tiled=True),
        lax.all_gather(query_norm, ("blk", "head"), axis=0, tiled=True),
        lax.all_gather(key_norm, ("blk", "head"), axis=0, tiled=True),
        lax.all_gather(output_weight, ("blk", "head"), axis=0, tiled=True),
    )
    gain_two, gate_matrix, up_matrix, down_matrix = (
        lax.all_gather(feedforward_norm, ("blk", "head"), axis=0, tiled=True),
        lax.all_gather(gate_weight, ("blk", "head"), axis=0, tiled=True),
        lax.all_gather(up_weight, ("blk", "head"), axis=0, tiled=True),
        lax.all_gather(down_weight, ("blk", "head"), axis=0, tiled=True),
    )
    gain_one = gain_one.astype(jnp.float32)
    gain_two = gain_two.astype(jnp.float32)
    query_gain = query_gain.astype(jnp.float32)
    key_gain = key_gain.astype(jnp.float32)
    own_first = (span_index * count_of_heads + head_index) * local_rows
    own_pos = token_positions(stretch_order, own_first, local_rows, stretch_rows)
    group_pos = token_positions(stretch_order, span_index * group_rows, group_rows, stretch_rows)
    phases = angles(own_pos, HEAD_SIZE)
    tokens_wide = tokens.astype(jnp.float32)
    first_normed, norm_one_back = jax.vjp(norm_rows, tokens_wide, gain_one)
    first_normed = first_normed.astype(jnp.bfloat16)
    query_raw = jnp.einsum(
        "btd,de->bte", first_normed, query_matrix, preferred_element_type=jnp.float32
    ).reshape(sequence_total, local_rows, QUERY_HEADS, HEAD_SIZE)
    key_unnormed = jnp.einsum(
        "btd,de->bte", first_normed, key_matrix, preferred_element_type=jnp.float32
    ).reshape(sequence_total, local_rows, KEY_VALUE_HEADS, HEAD_SIZE)
    value_tokens = (
        jnp.einsum("btd,de->bte", first_normed, value_matrix, preferred_element_type=jnp.float32)
        .astype(jnp.bfloat16)
        .reshape(sequence_total, local_rows, KEY_VALUE_HEADS, HEAD_SIZE)
    )

    def heads_local(query_in, key_in, query_scale, key_scale):
        return (
            rotary(norm_rows(query_in, query_scale), phases),
            rotary(norm_rows(key_in, key_scale), phases),
        )

    (query_tokens, key_tokens), heads_back = jax.vjp(
        heads_local, query_raw, key_unnormed, query_gain, key_gain
    )
    query_tokens = query_tokens.astype(jnp.bfloat16)
    key_tokens = key_tokens.astype(jnp.bfloat16)
    query_group, key_group, value_group = (
        lax.all_to_all(query_tokens, "head", split_axis=2, concat_axis=1, tiled=True),
        lax.all_to_all(key_tokens, "head", split_axis=2, concat_axis=1, tiled=True),
        lax.all_to_all(value_tokens, "head", split_axis=2, concat_axis=1, tiled=True),
    )
    query_five = query_group.reshape(
        sequence_total, group_rows, heads_shared, heads_per_group, HEAD_SIZE
    )

    def block_update(carry, key_block, value_block, key_pos):
        run_max, run_sum, run_total = carry
        scores = (
            jnp.einsum(
                "bqkgd,bckd->bkgqc", query_five, key_block, preferred_element_type=jnp.float32
            )
            * score_scale
        )
        allowed = key_pos[:, None, None, None, :] <= group_pos[:, None, None, :, None]
        scores = jnp.where(allowed, scores, NEG)
        new_max = jnp.maximum(run_max, jnp.max(scores, axis=-1))
        exponent = jnp.where(allowed, jnp.exp(scores - new_max[..., None]), 0.0)
        factor = jnp.exp(run_max - new_max)
        new_sum = run_sum * factor + jnp.sum(exponent, axis=-1)
        new_total = run_total * factor[..., None] + jnp.einsum(
            "bkgqc,bckd->bkgqd",
            exponent.astype(jnp.bfloat16),
            value_block,
            preferred_element_type=jnp.float32,
        )
        return (new_max, new_sum, new_total)

    def fold_update(carry, key_block, value_block, key_pos):
        result = block_update(carry, key_block, value_block, key_pos)
        return result

    stat_shape = (sequence_total, heads_shared, heads_per_group, group_rows)
    start_state = (
        jnp.full(stat_shape, NEG, jnp.float32),
        jnp.zeros(stat_shape, jnp.float32),
        jnp.zeros(stat_shape + (HEAD_SIZE,), jnp.float32),
    )
    key_piece = lax.all_gather(key_group, "blk", axis=1, tiled=True)
    value_piece = lax.all_gather(value_group, "blk", axis=1, tiled=True)
    piece_rows = key_piece.shape[1]
    block_len = math.gcd(group_rows, piece_rows)

    def inner(block_number, carry_in):
        offset = block_number * block_len
        key_block = lax.dynamic_slice_in_dim(key_piece, offset, block_len, 1)
        value_block = lax.dynamic_slice_in_dim(value_piece, offset, block_len, 1)
        key_pos = token_positions(stretch_order, offset, block_len, stretch_rows)
        return fold_update(carry_in, key_block, value_block, key_pos)

    run_max, run_sum, run_total = lax.fori_loop(0, piece_rows // block_len, inner, start_state)
    log_total = run_max + jnp.log(run_sum)
    attended_five = run_total / run_sum[..., None]
    attended_group = (
        jnp.transpose(attended_five, (0, 3, 1, 2, 4))
        .reshape(sequence_total, group_rows, heads_shared * heads_per_group, HEAD_SIZE)
        .astype(jnp.bfloat16)
    )
    attended_tokens = lax.all_to_all(
        attended_group, "head", split_axis=1, concat_axis=2, tiled=True
    ).reshape(sequence_total, local_rows, QUERY_HEADS * HEAD_SIZE)
    branch = jnp.einsum(
        "bte,ed->btd", attended_tokens, output_matrix, preferred_element_type=jnp.float32
    )
    resid = tokens_wide + branch
    normed_two, norm_two_back = jax.vjp(norm_rows, resid, gain_two)
    normed_two = normed_two.astype(jnp.bfloat16)
    gate = jnp.einsum("btd,df->btf", normed_two, gate_matrix, preferred_element_type=jnp.float32)
    up_proj = jnp.einsum("btd,df->btf", normed_two, up_matrix, preferred_element_type=jnp.float32)

    def swish_product(gate_in, up_in):
        return jax.nn.silu(gate_in) * up_in

    hidden, swish_back = jax.vjp(swish_product, gate, up_proj)
    hidden = hidden.astype(jnp.bfloat16)
    layer_out = (
        resid + jnp.einsum("btf,fd->btd", hidden, down_matrix, preferred_element_type=jnp.float32)
    ).astype(jnp.bfloat16)
    gain_again, gate_matrix, up_matrix, down_matrix = (
        lax.all_gather(feedforward_norm, ("blk", "head"), axis=0, tiled=True),
        lax.all_gather(gate_weight, ("blk", "head"), axis=0, tiled=True),
        lax.all_gather(up_weight, ("blk", "head"), axis=0, tiled=True),
        lax.all_gather(down_weight, ("blk", "head"), axis=0, tiled=True),
    )
    down_gradient = jnp.einsum(
        "btf,btd->fd", hidden, out_cotangent, preferred_element_type=jnp.float32
    )
    hidden_gradient = jnp.einsum(
        "btd,fd->btf", out_cotangent, down_matrix, preferred_element_type=jnp.float32
    )
    gate_gradient, up_gradient = swish_back(hidden_gradient)
    gate_gradient = gate_gradient.astype(jnp.bfloat16)
    up_gradient = up_gradient.astype(jnp.bfloat16)
    gate_matrix_gradient = jnp.einsum(
        "btd,btf->df", normed_two, gate_gradient, preferred_element_type=jnp.float32
    )
    up_matrix_gradient = jnp.einsum(
        "btd,btf->df", normed_two, up_gradient, preferred_element_type=jnp.float32
    )
    normed_two_gradient = jnp.einsum(
        "btf,df->btd", gate_gradient, gate_matrix, preferred_element_type=jnp.float32
    ) + jnp.einsum("btf,df->btd", up_gradient, up_matrix, preferred_element_type=jnp.float32)
    resid_part, gain_two_gradient = norm_two_back(normed_two_gradient)
    resid_gradient = out_cotangent.astype(jnp.float32) + resid_part
    feedforward_sums = (
        lax.psum_scatter(gain_two_gradient, ("blk", "head"), scatter_dimension=0, tiled=True),
        lax.psum_scatter(gate_matrix_gradient, ("blk", "head"), scatter_dimension=0, tiled=True),
        lax.psum_scatter(up_matrix_gradient, ("blk", "head"), scatter_dimension=0, tiled=True),
        lax.psum_scatter(down_gradient, ("blk", "head"), scatter_dimension=0, tiled=True),
    )
    gain_again, query_matrix, key_matrix, value_matrix, query_again, key_again, output_matrix = (
        lax.all_gather(attention_norm, ("blk", "head"), axis=0, tiled=True),
        lax.all_gather(query_weight, ("blk", "head"), axis=0, tiled=True),
        lax.all_gather(key_projection, ("blk", "head"), axis=0, tiled=True),
        lax.all_gather(value_projection, ("blk", "head"), axis=0, tiled=True),
        lax.all_gather(query_norm, ("blk", "head"), axis=0, tiled=True),
        lax.all_gather(key_norm, ("blk", "head"), axis=0, tiled=True),
        lax.all_gather(output_weight, ("blk", "head"), axis=0, tiled=True),
    )
    branch_gradient = resid_gradient.astype(jnp.bfloat16)
    output_matrix_gradient = jnp.einsum(
        "bte,btd->ed", attended_tokens, branch_gradient, preferred_element_type=jnp.float32
    )
    attended_gradient = (
        jnp.einsum(
            "btd,ed->bte", branch_gradient, output_matrix, preferred_element_type=jnp.float32
        )
        .astype(jnp.bfloat16)
        .reshape(sequence_total, local_rows, QUERY_HEADS, HEAD_SIZE)
    )
    attended_grad_group = lax.all_to_all(
        attended_gradient, "head", split_axis=2, concat_axis=1, tiled=True
    ).reshape(sequence_total, group_rows, heads_shared, heads_per_group, HEAD_SIZE)
    delta = jnp.sum(
        jnp.transpose(attended_grad_group.astype(jnp.float32), (0, 2, 3, 1, 4)) * attended_five,
        axis=-1,
    )

    def block_grads(sums_in, key_current, value_current, key_pos):
        key_sum, value_sum, query_sum = sums_in
        scores = (
            jnp.einsum(
                "bqkgd,bckd->bkgqc", query_five, key_current, preferred_element_type=jnp.float32
            )
            * score_scale
        )
        allowed = key_pos[:, None, None, None, :] <= group_pos[:, None, None, :, None]
        weights = jnp.where(allowed, jnp.exp(scores - log_total[..., None]), 0.0)
        probs = weights.astype(jnp.bfloat16)
        value_sum = value_sum + jnp.einsum(
            "bkgqc,bqkgd->bckd", probs, attended_grad_group, preferred_element_type=jnp.float32
        )
        probs_gradient = jnp.einsum(
            "bqkgd,bckd->bkgqc",
            attended_grad_group,
            value_current,
            preferred_element_type=jnp.float32,
        )
        scores_gradient = (weights * (probs_gradient - delta[..., None])).astype(jnp.bfloat16)
        query_sum = (
            query_sum
            + jnp.einsum(
                "bkgqc,bckd->bqkgd",
                scores_gradient,
                key_current,
                preferred_element_type=jnp.float32,
            )
            * score_scale
        )
        key_sum = (
            key_sum
            + jnp.einsum(
                "bkgqc,bqkgd->bckd", scores_gradient, query_five, preferred_element_type=jnp.float32
            )
            * score_scale
        )
        return (key_sum, value_sum, query_sum)

    def pass_step(step_index, carry):
        key_current, value_current, key_sum, value_sum, query_sum = carry
        anchor = (span_index - step_index) % span_count
        key_pos = token_positions(stretch_order, anchor * group_rows, group_rows, stretch_rows)
        key_sum, value_sum, query_sum = block_grads(
            (key_sum, value_sum, query_sum), key_current, value_current, key_pos
        )
        key_current, value_current = passed_along((key_current, value_current), "blk", 1)
        key_sum, value_sum = (
            passed_along(key_sum.astype(jnp.bfloat16), "blk", 1).astype(key_sum.dtype),
            passed_along(value_sum.astype(jnp.bfloat16), "blk", 1).astype(value_sum.dtype),
        )
        return (key_current, value_current, key_sum, value_sum, query_sum)

    kv_zeros = jnp.zeros((sequence_total, group_rows, heads_shared, HEAD_SIZE), jnp.float32)
    query_zeros = jnp.zeros(
        (sequence_total, group_rows, heads_shared, heads_per_group, HEAD_SIZE), jnp.float32
    )
    final_state = lax.fori_loop(
        0, span_count, pass_step, (key_group, value_group, kv_zeros, kv_zeros, query_zeros)
    )
    key_grad_group = final_state[2].astype(jnp.bfloat16)
    value_grad_group = final_state[3].astype(jnp.bfloat16)
    query_grad_group = (
        final_state[4]
        .astype(jnp.bfloat16)
        .reshape(sequence_total, group_rows, heads_shared * heads_per_group, HEAD_SIZE)
    )
    query_grad_tokens, key_grad_tokens, value_gradient_tokens = (
        lax.all_to_all(query_grad_group, "head", split_axis=1, concat_axis=2, tiled=True),
        lax.all_to_all(key_grad_group, "head", split_axis=1, concat_axis=2, tiled=True),
        lax.all_to_all(value_grad_group, "head", split_axis=1, concat_axis=2, tiled=True),
    )
    query_raw_gradient, key_unnormed_gradient, query_gain_gradient, key_gain_gradient = heads_back(
        (query_grad_tokens.astype(jnp.float32), key_grad_tokens.astype(jnp.float32))
    )
    query_raw_gradient = query_raw_gradient.astype(jnp.bfloat16).reshape(
        sequence_total, local_rows, QUERY_HEADS * HEAD_SIZE
    )
    key_unnormed_gradient = key_unnormed_gradient.astype(jnp.bfloat16).reshape(
        sequence_total, local_rows, KEY_VALUE_HEADS * HEAD_SIZE
    )
    value_unnormed_gradient = value_gradient_tokens.reshape(
        sequence_total, local_rows, KEY_VALUE_HEADS * HEAD_SIZE
    )
    query_matrix_gradient = jnp.einsum(
        "btd,bte->de", first_normed, query_raw_gradient, preferred_element_type=jnp.float32
    )
    key_matrix_gradient = jnp.einsum(
        "btd,bte->de", first_normed, key_unnormed_gradient, preferred_element_type=jnp.float32
    )
    value_matrix_gradient = jnp.einsum(
        "btd,bte->de", first_normed, value_unnormed_gradient, preferred_element_type=jnp.float32
    )
    normed_one_gradient = jnp.einsum(
        "bte,de->btd", query_raw_gradient, query_matrix, preferred_element_type=jnp.float32
    )
    normed_one_gradient = normed_one_gradient + jnp.einsum(
        "bte,de->btd", key_unnormed_gradient, key_matrix, preferred_element_type=jnp.float32
    )
    normed_one_gradient = normed_one_gradient + jnp.einsum(
        "bte,de->btd", value_unnormed_gradient, value_matrix, preferred_element_type=jnp.float32
    )
    token_part, gain_one_gradient = norm_one_back(normed_one_gradient)
    tokens_gradient = (resid_gradient + token_part).astype(jnp.bfloat16)
    attention_sums = (
        lax.psum_scatter(gain_one_gradient, ("blk", "head"), scatter_dimension=0, tiled=True),
        lax.psum_scatter(query_matrix_gradient, ("blk", "head"), scatter_dimension=0, tiled=True),
        lax.psum_scatter(key_matrix_gradient, ("blk", "head"), scatter_dimension=0, tiled=True),
        lax.psum_scatter(value_matrix_gradient, ("blk", "head"), scatter_dimension=0, tiled=True),
        lax.psum_scatter(query_gain_gradient, ("blk", "head"), scatter_dimension=0, tiled=True),
        lax.psum_scatter(key_gain_gradient, ("blk", "head"), scatter_dimension=0, tiled=True),
        lax.psum_scatter(output_matrix_gradient, ("blk", "head"), scatter_dimension=0, tiled=True),
    )
    return (
        layer_out,
        tokens_gradient,
        attention_sums[0],
        attention_sums[1],
        attention_sums[2],
        attention_sums[3],
        attention_sums[4],
        attention_sums[5],
        attention_sums[6],
        feedforward_sums[0],
        feedforward_sums[1],
        feedforward_sums[2],
        feedforward_sums[3],
    )


LOG2E = math.log2(math.e)
STRIP = 128
CHUNK = 512
ALONG = (((1,), (1,)), ((), ()))
DOWN = (((0,), (0,)), ((), ()))


def two_heads(block):
    return jnp.concatenate([block[:, :HEAD_SIZE], block[:, HEAD_SIZE:]], axis=0)


def side_by_side(rows):
    half = rows.shape[0] // 2
    return jnp.concatenate([rows[:half], rows[half:]], axis=1)


CHEAP = pl.CostEstimate(flops=1, bytes_accessed=1, transcendentals=0)


def sort_strips(order_ref, kv_refs, keys, values):
    per = kv_refs[0].shape[0] // STRIP
    for j, ref in enumerate(kv_refs):
        for i in range(per):
            target = pl.multiple_of(order_ref[j * per + i] * STRIP, STRIP)
            here = slice(i * STRIP, (i + 1) * STRIP)
            keys[pl.ds(target, STRIP), :] = ref[here, :HEAD_SIZE]
            values[pl.ds(target, STRIP), :HEAD_SIZE] = ref[here, HEAD_SIZE:]


def attend_kernel(place_ref, order_ref, q_ref, *refs):
    kv_refs, (out_ref, lse_ref, keys, values) = refs[:4], refs[4:]
    step = pl.program_id(0)

    @pl.when(step == 0)
    def _():
        values[:, HEAD_SIZE:] = jnp.ones((values.shape[0], HEAD_SIZE), jnp.bfloat16)
        sort_strips(order_ref, kv_refs, keys, values)

    place = place_ref[step]
    queries = two_heads(q_ref[...])
    last = place // (CHUNK // STRIP)

    def part(index, total, masked):
        first = pl.multiple_of(index * CHUNK, CHUNK)
        scores = lax.dot_general(
            queries, keys[pl.ds(first, CHUNK), :], ALONG, preferred_element_type=jnp.float32
        )
        weights = jnp.exp2(scores)
        if masked:
            row = lax.broadcasted_iota(jnp.int32, scores.shape, 0) % STRIP
            column = lax.broadcasted_iota(jnp.int32, scores.shape, 1)
            weights = jnp.where(column - row <= place * STRIP - first, weights, 0.0)
        return total + jnp.dot(
            weights.astype(jnp.bfloat16),
            values[pl.ds(first, CHUNK), :],
            preferred_element_type=jnp.float32,
        )

    total = jnp.zeros((2 * STRIP, 2 * HEAD_SIZE), jnp.float32)
    total = lax.fori_loop(0, last, lambda index, t: part(index, t, False), total)
    total = part(last, total, True)
    norm = total[:, HEAD_SIZE:]
    out_ref[...] = side_by_side(total[:, :HEAD_SIZE] / norm).astype(jnp.bfloat16)
    lse_ref[0] = jnp.transpose(jnp.log2(norm))[:8]


def attend(place, order, queries, kv):
    rows, width = queries.shape
    steps = rows // STRIP
    total = sum(part.shape[0] for part in kv)
    strip = pl.BlockSpec((STRIP, width), lambda i, *_: (i, 0))
    return pl.pallas_call(
        attend_kernel,
        grid_spec=pltpu.PrefetchScalarGridSpec(
            num_scalar_prefetch=2,
            grid=(steps,),
            in_specs=[strip] + [pl.BlockSpec(part.shape, lambda i, *_: (0, 0)) for part in kv],
            out_specs=[strip, pl.BlockSpec((1, 8, 2 * STRIP), lambda i, *_: (i, 0, 0))],
            scratch_shapes=[
                pltpu.VMEM((total, HEAD_SIZE), jnp.bfloat16),
                pltpu.VMEM((total, 2 * HEAD_SIZE), jnp.bfloat16),
            ],
        ),
        out_shape=[
            jax.ShapeDtypeStruct((rows, width), jnp.bfloat16),
            jax.ShapeDtypeStruct((steps, 8, 2 * STRIP), jnp.float32),
        ],
        cost_estimate=CHEAP,
        name="attend",
    )(place, order, queries, *kv)


def attend_back_kernel(place_ref, order_ref, q_ref, out_ref, lse_ref, *refs, groups):
    grad_refs, kv_refs = refs[:groups], refs[groups : groups + 4]
    dq_ref, own_ref, far_ref, sent_ref = refs[groups + 4 : groups + 8]
    keys, values, key_sums, value_sums, grads_all = refs[groups + 8 :]
    step = pl.program_id(0)

    @pl.when(step == 0)
    def _():
        key_sums[...] = jnp.zeros_like(key_sums)
        value_sums[...] = jnp.zeros_like(value_sums)
        sort_strips(order_ref, kv_refs, keys, values)
        first = 0
        for ref in grad_refs:
            grads_all[first : first + ref.shape[0], :] = ref[...]
            first += ref.shape[0]

    place = place_ref[step]
    queries = two_heads(q_ref[...])
    grads = two_heads(grads_all[pl.ds(pl.multiple_of(step * STRIP, STRIP), STRIP), :])
    product = grads.astype(jnp.float32) * two_heads(out_ref[...]).astype(jnp.float32)
    delta = jnp.sum(jnp.transpose(product), axis=0, keepdims=True)
    lse = lse_ref[0, :1]
    last = place // (CHUNK // STRIP)

    def part(index, total, masked):
        first = pl.multiple_of(index * CHUNK, CHUNK)
        here = pl.ds(first, CHUNK)
        key_rows = keys[here, :]
        scores = lax.dot_general(key_rows, queries, ALONG, preferred_element_type=jnp.float32)
        weights = jnp.exp2(scores - lse)
        if masked:
            row = lax.broadcasted_iota(jnp.int32, scores.shape, 0)
            column = lax.broadcasted_iota(jnp.int32, scores.shape, 1) % STRIP
            weights = jnp.where(row - column <= place * STRIP - first, weights, 0.0)
        slopes = lax.dot_general(
            values[here, :], grads, ALONG, preferred_element_type=jnp.float32
        )
        score_grads = (weights * (slopes - delta)).astype(jnp.bfloat16)
        value_sums[here, :] += jnp.dot(
            weights.astype(jnp.bfloat16), grads, preferred_element_type=jnp.float32
        )
        key_sums[here, :] += jnp.dot(score_grads, queries, preferred_element_type=jnp.float32)
        return total + lax.dot_general(
            score_grads, key_rows, DOWN, preferred_element_type=jnp.float32
        )

    total = jnp.zeros((2 * STRIP, HEAD_SIZE), jnp.float32)
    total = lax.fori_loop(0, last, lambda index, t: part(index, t, False), total)
    total = part(last, total, True)
    dq_ref[...] = side_by_side(total * (1.0 / math.sqrt(HEAD_SIZE))).astype(jnp.bfloat16)

    @pl.when(step == pl.num_programs(0) - 1)
    def _():
        per = own_ref.shape[0] // STRIP
        for j in range(4):
            target = (own_ref, far_ref, sent_ref, sent_ref)[j]
            base = per if j == 3 else 0
            for i in range(per):
                source = pl.multiple_of(order_ref[j * per + i] * STRIP, STRIP)
                here = slice((base + i) * STRIP, (base + i + 1) * STRIP)
                target[here, :HEAD_SIZE] = (
                    key_sums[pl.ds(source, STRIP), :] * (1.0 / LOG2E)
                ).astype(jnp.bfloat16)
                target[here, HEAD_SIZE:] = value_sums[pl.ds(source, STRIP), :].astype(
                    jnp.bfloat16
                )


def attend_back(place, order, queries, grads, attended, lse, kv):
    rows, width = queries.shape
    steps = rows // STRIP
    total = sum(part.shape[0] for part in kv)
    strip = pl.BlockSpec((STRIP, width), lambda i, *_: (i, 0))

    def whole(shape):
        return pl.BlockSpec(shape, lambda i, *_: (0, 0))

    outs = [kv[0].shape, kv[0].shape, (2 * kv[0].shape[0], kv[0].shape[1])]
    return pl.pallas_call(
        lambda *refs: attend_back_kernel(*refs, groups=len(grads)),
        grid_spec=pltpu.PrefetchScalarGridSpec(
            num_scalar_prefetch=2,
            grid=(steps,),
            in_specs=[strip, strip, pl.BlockSpec((1, 8, 2 * STRIP), lambda i, *_: (i, 0, 0))]
            + [whole(part.shape) for part in (*grads, *kv)],
            out_specs=[strip] + [whole(shape) for shape in outs],
            scratch_shapes=[
                pltpu.VMEM((total, HEAD_SIZE), jnp.bfloat16),
                pltpu.VMEM((total, HEAD_SIZE), jnp.bfloat16),
                pltpu.VMEM((total, HEAD_SIZE), jnp.float32),
                pltpu.VMEM((total, HEAD_SIZE), jnp.float32),
                pltpu.VMEM((rows, width), jnp.bfloat16),
            ],
        ),
        out_shape=[jax.ShapeDtypeStruct((rows, width), jnp.bfloat16)]
        + [jax.ShapeDtypeStruct(shape, jnp.bfloat16) for shape in outs],
        cost_estimate=CHEAP,
        name="attend_back",
    )(place, order, queries, attended, lse, *grads, *kv)


def matmul(left, right, dims=(((1,), (0,)), ((), ()))):
    return lax.dot_general(left, right, dims, preferred_element_type=jnp.float32)


RING = (0, 2, 4, 6, 7, 5, 3, 1)
STRIPS = (0, 1, 7, 2, 6, 3, 5, 4)
GROUPS = ((0, 3), (3, 5), (5, 7), (7, 8))


def hop(value, by):
    count = len(RING)
    return lax.ppermute(value, "blk", [(RING[i], RING[(i + by) % count]) for i in range(count)])


def cross(value, by):
    return lax.ppermute(value, "head", [(i, i ^ by) for i in range(4)])


def mirror(value, by):
    return lax.ppermute(value, "blk", [(i, i ^ by) for i in range(len(RING))])


def add(left, right):
    return (left.astype(jnp.float32) + right.astype(jnp.float32)).astype(left.dtype)


class Gather:
    def __init__(self, own):
        self.got, self.step = {0: own}, 0
        self.state = (own, own)

    def go(self):
        self.step += 1
        left, right = self.state
        if self.step < 4:
            self.state = hop(left, -1), hop(right, 1)
            self.got[self.step], self.got[8 - self.step] = self.state
        else:
            half = left.shape[0] // 2
            self.got[4] = jnp.concatenate([hop(left[:half], -1), hop(right[half:], 1)], axis=0)
            self.state = (self.got[4],)

    def strips(self):
        return [self.got[s] for s in STRIPS]

    def group(self, index):
        first, last = GROUPS[index]
        return jnp.concatenate([self.got[s] for s in STRIPS[first:last]], axis=0)


class Scatter:
    def __init__(self, part):
        self.part, self.step = part, 0
        self.half = part[4].shape[0] // 2
        self.state = (part[4][: self.half], part[4][self.half :])

    def go(self):
        self.step += 1
        half, part = self.half, self.part
        up, down = hop(self.state[0], 1), hop(self.state[1], -1)
        if self.step == 1:
            up = jnp.concatenate([add(part[3][:half], up), part[3][half:]], axis=0)
            down = jnp.concatenate([part[5][:half], add(part[5][half:], down)], axis=0)
        elif self.step < 4:
            up, down = add(part[4 - self.step], up), add(part[4 + self.step], down)
        self.state = up, down

    def total(self):
        up, down = self.state
        wide = jnp.float32
        return self.part[0].astype(wide) + up.astype(wide) + down.astype(wide)


class Swap:
    def __init__(self, pieces, rows):
        cut = 4 * rows + rows // 2
        self.rows, self.step = rows, 0
        self.own, self.from_left, self.from_right = pieces[:rows], [], []
        self.state = (pieces[rows:cut], pieces[cut:])

    def go(self):
        self.step += 1
        rows = self.rows
        right, left = hop(self.state[0], 1), hop(self.state[1], -1)
        if self.step < 4:
            self.from_left.append(right[:rows])
            self.from_right.append(left[-rows:])
            right, left = right[rows:], left[:-rows]
        self.state = right, left

    def pieces(self):
        right, left = self.state
        return [self.own, *self.from_right, right, left, *reversed(self.from_left)]

    def result(self):
        return jnp.concatenate(self.pieces(), axis=0)


def hold(rings, *extra):
    states, extra = lax.optimization_barrier(([ring.state for ring in rings], extra))
    for ring, state in zip(rings, states):
        ring.state = state
    return extra[0] if len(extra) == 1 else extra


def scatter_cross(own, far, sent):
    moved = cross(sent, 1)
    half = own.shape[0]
    return add(own, moved[:half]), add(far, moved[half:])


def columns(at, width):
    return pl.ds(pl.multiple_of(at * width, width), width)


def slice_kernel(at_ref, *refs, pad):
    weights, out_ref = refs[:-1], refs[-1]
    if pad:
        weights, pad_ref = weights[:-1], weights[-1]
    rows = weights[0].shape[0]
    each = rows + pad
    for s in range(8):
        first = 0
        for ref in weights:
            width = ref.shape[1] // 8
            out_ref[s * each : s * each + rows, first : first + width] = ref[
                :, columns(at_ref[s], width)
            ]
            first += width
        if pad:
            out_ref[s * each + rows : (s + 1) * each, :] = pad_ref[...]


def slice_pieces(at, *weights, pad=None):
    rows = weights[0].shape[0]
    cols = sum(w.shape[1] for w in weights) // 8
    extra = 0 if pad is None else pad.shape[0]
    operands = weights if pad is None else (*weights, pad)
    vmem = pl.BlockSpec(memory_space=pltpu.VMEM)
    return pl.pallas_call(
        lambda *refs: slice_kernel(*refs, pad=extra),
        in_specs=[pl.BlockSpec(memory_space=pltpu.SMEM)] + [vmem] * len(operands),
        out_specs=vmem,
        out_shape=jax.ShapeDtypeStruct((8 * (rows + extra), cols), jnp.bfloat16),
        cost_estimate=CHEAP,
        name="slice_pieces",
    )(at, *operands)


def assemble_kernel(at_ref, *refs):
    own = at_ref[8]
    for j, piece in enumerate(refs[:4]):
        refs[4][0, own ^ j] = piece[...]


def assemble(at, pieces, rows):
    count = at.shape[0] - 1
    total, cols = pieces[0].shape
    return pl.pallas_call(
        assemble_kernel,
        grid_spec=pltpu.PrefetchScalarGridSpec(
            num_scalar_prefetch=1,
            grid=(count,),
            in_specs=[pl.BlockSpec((rows, cols), lambda i, at: (i, 0))] * 4,
            out_specs=pl.BlockSpec((1, 4, rows, cols), lambda i, at: (at[i], 0, 0, 0)),
        ),
        out_shape=jax.ShapeDtypeStruct((count, 4, rows, cols), jnp.bfloat16),
        cost_estimate=CHEAP,
        name="assemble",
    )(at, *pieces).reshape(4 * total, cols)


def spun(rows, cosine, sine):
    return rows * cosine + pltpu.roll(rows, HEAD_SIZE // 2, 1) * sine


def project_kernel(at_ref, *refs, strips):
    token_refs, refs = refs[:strips], refs[strips:]
    pieces, refs = refs[:4], refs[4:]
    cos_ref, sin_ref, normed_ref, raw_ref, q_ref, kv_ref, matrix_ref, gains_ref = refs
    each = pieces[0].shape[0] // 8
    rows = matrix_ref.shape[0] // 32
    own = at_ref[8]
    gains = jnp.zeros(gains_ref.shape, jnp.float32)
    for s in range(8):
        for j in range(4):
            first = pl.multiple_of((at_ref[s] * 4 + (own ^ j)) * rows, rows)
            matrix_ref[pl.ds(first, rows), :] = pieces[j][s * each : s * each + rows, :]
            gains += pieces[j][s * each + rows : (s + 1) * each, :].astype(jnp.float32)
    gains_ref[...] = gains
    width = gains.shape[1]
    first = 0
    for ref in token_refs:
        block = ref[...].astype(jnp.float32)
        block = block * inverse_rms(block)
        here = slice(first, first + ref.shape[0])
        for i in range(block.shape[1] // width):
            cols = slice(i * width, (i + 1) * width)
            normed_ref[here, cols] = (block[:, cols] * gains[i : i + 1]).astype(jnp.bfloat16)
        first += ref.shape[0]
    query_gain, key_gain = gains[8:9, :HEAD_SIZE], gains[8:9, HEAD_SIZE : 2 * HEAD_SIZE]
    query_cols = q_ref.shape[1]
    step = 256
    for first in range(0, q_ref.shape[0], step):
        here = slice(first, first + step)
        raw = jnp.dot(normed_ref[here, :], matrix_ref[...], preferred_element_type=jnp.float32)
        raw_ref[here, :] = raw
        cosine, sine = cos_ref[here, :], sin_ref[here, :]
        for col in range(0, query_cols + HEAD_SIZE, HEAD_SIZE):
            part = raw[:, col : col + HEAD_SIZE]
            if col < query_cols:
                part = spun(part * inverse_rms(part) * query_gain, cosine, sine)
                part = part * (LOG2E / math.sqrt(HEAD_SIZE))
                q_ref[here, col : col + HEAD_SIZE] = part.astype(jnp.bfloat16)
            else:
                part = spun(part * inverse_rms(part) * key_gain, cosine, sine)
                kv_ref[here, :HEAD_SIZE] = part.astype(jnp.bfloat16)
        kv_ref[here, HEAD_SIZE:] = raw[:, query_cols + HEAD_SIZE :].astype(jnp.bfloat16)


def project(at, strips, pieces, cosine, sine, query_cols, pad):
    rows = sum(strip.shape[0] for strip in strips)
    width = strips[0].shape[1]
    cols = pieces[0].shape[1]
    vmem = pl.BlockSpec(memory_space=pltpu.VMEM)
    operands = (*strips, *pieces, cosine, sine)
    narrow, wide = jnp.bfloat16, jnp.float32
    return pl.pallas_call(
        lambda *refs: project_kernel(*refs, strips=len(strips)),
        in_specs=[pl.BlockSpec(memory_space=pltpu.SMEM)] + [vmem] * len(operands),
        out_specs=[vmem] * 6,
        out_shape=[
            jax.ShapeDtypeStruct((rows, width), narrow),
            jax.ShapeDtypeStruct((rows, cols), wide),
            jax.ShapeDtypeStruct((rows, query_cols), narrow),
            jax.ShapeDtypeStruct((rows, 2 * HEAD_SIZE), narrow),
            jax.ShapeDtypeStruct((width, cols), narrow),
            jax.ShapeDtypeStruct((pad, cols), wide),
        ],
        cost_estimate=CHEAP,
        name="project",
    )(at, *operands)


def project_back_kernel(
    dq_ref, dkv_ref, raw_ref, head_gain_ref, cos_ref, sin_ref, matrix_ref,
    grad_ref, part_ref, gain_ref,
):
    query_cols = dq_ref.shape[1]
    step = 256
    gain_ref[...] = jnp.zeros_like(gain_ref)
    for first in range(0, dq_ref.shape[0], step):
        here = slice(first, first + step)
        cosine, sine = cos_ref[here, :], sin_ref[here, :]
        for col in range(0, query_cols + HEAD_SIZE, HEAD_SIZE):
            cols = slice(col, col + HEAD_SIZE)
            which = 0 if col < query_cols else 1
            grads = dkv_ref[here, :HEAD_SIZE] if which else dq_ref[here, cols]
            raw = raw_ref[here, cols]
            rho = inverse_rms(raw)
            unit = raw * rho
            turned = spun(grads.astype(jnp.float32), cosine, -sine)
            gain_ref[which : which + 1, :] += jnp.sum(turned * unit, axis=0, keepdims=True)
            scaled = turned * head_gain_ref[which : which + 1]
            back = rho * (scaled - unit * jnp.mean(unit * scaled, axis=-1, keepdims=True))
            grad_ref[here, cols] = back.astype(jnp.bfloat16)
        grad_ref[here, query_cols + HEAD_SIZE :] = dkv_ref[here, HEAD_SIZE:]
        part_ref[here, :] = lax.dot_general(
            grad_ref[here, :], matrix_ref[...], ALONG, preferred_element_type=jnp.float32
        ).astype(jnp.bfloat16)


def project_back(query_grads, kv_grads, raw, head_gains, cosine, sine, matrix):
    rows, cols = raw.shape
    vmem = pl.BlockSpec(memory_space=pltpu.VMEM)
    return pl.pallas_call(
        project_back_kernel,
        in_specs=[vmem] * 7,
        out_specs=[vmem] * 3,
        out_shape=[
            jax.ShapeDtypeStruct((rows, cols), jnp.bfloat16),
            jax.ShapeDtypeStruct((rows, matrix.shape[0]), jnp.bfloat16),
            jax.ShapeDtypeStruct((8, HEAD_SIZE), jnp.float32),
        ],
        cost_estimate=CHEAP,
        name="project_back",
    )(query_grads, kv_grads, raw, head_gains, cosine, sine, matrix)


def dots(lefts, rights, dims):
    return sum(
        lax.dot_general(left[...], right[...], dims, preferred_element_type=jnp.float32)
        for left, right in zip(lefts, rights)
    )


def weight_grads_kernel(at_ref, *refs, groups):
    own_ref, far_ref, sent_ref, held = refs[-4:]
    own = at_ref[8]
    sums = dots(refs[:groups], refs[groups : 2 * groups], DOWN)
    held[...] = sums.astype(jnp.bfloat16).reshape(held.shape)
    own_ref[...] = held[own]
    far_ref[...] = held[own ^ 2]
    sent_ref[0] = held[own ^ 1]
    sent_ref[1] = held[own ^ 3]


def weight_grads(at, lefts, rights, rows):
    count = at.shape[0] - 1
    cols = rights[0].shape[1]
    total = sum(left.shape[0] for left in lefts)
    part = pl.BlockSpec((rows, cols), lambda i, at: (i, 0))
    shape = jax.ShapeDtypeStruct((count * rows, cols), jnp.bfloat16)
    own, far, sent = pl.pallas_call(
        lambda *refs: weight_grads_kernel(*refs, groups=len(lefts)),
        grid_spec=pltpu.PrefetchScalarGridSpec(
            num_scalar_prefetch=1,
            grid=(count,),
            in_specs=[
                pl.BlockSpec((left.shape[0], 4 * rows), lambda i, at: (0, at[i]))
                for left in lefts
            ]
            + [pl.BlockSpec(right.shape, lambda i, at: (0, 0)) for right in rights],
            out_specs=[part, part, pl.BlockSpec((2, rows, cols), lambda i, at: (0, i, 0))],
            scratch_shapes=[pltpu.VMEM((4, rows, cols), jnp.bfloat16)],
        ),
        out_shape=[
            shape, shape, jax.ShapeDtypeStruct((2, count * rows, cols), jnp.bfloat16),
        ],
        cost_estimate=CHEAP,
        name="weight_grads",
    )(at, *lefts, *rights)
    return own, far, sent.reshape(2 * count * rows, cols)


def row_grads_kernel(*refs, groups):
    refs[-1][...] = dots(refs[:groups], refs[groups : 2 * groups], DOWN).astype(jnp.bfloat16)


def row_grads(lefts, rights, block=256):
    out_rows, cols = lefts[0].shape[1], rights[0].shape[1]
    total = sum(left.shape[0] for left in lefts)
    return pl.pallas_call(
        lambda *refs: row_grads_kernel(*refs, groups=len(lefts)),
        grid=(out_rows // block,),
        in_specs=[pl.BlockSpec((left.shape[0], block), lambda i: (0, i)) for left in lefts]
        + [pl.BlockSpec(right.shape, lambda i: (0, 0)) for right in rights],
        out_specs=pl.BlockSpec((block, cols), lambda i: (i, 0)),
        out_shape=jax.ShapeDtypeStruct((out_rows, cols), jnp.bfloat16),
        cost_estimate=CHEAP,
        name="row_grads",
    )(*lefts, *rights)


def lane_sums(block):
    return sum(block[:, i : i + 128] for i in range(0, block.shape[1], 128))


def widen_kernel(at_ref, *refs, pieces, count):
    piece_refs, refs = refs[:pieces], refs[pieces:]
    weights, grads, sums_ref = refs[:count], refs[count : 2 * count], refs[2 * count]
    rows = weights[0].shape[0]
    sums_ref[...] = jnp.zeros_like(sums_ref)
    spots = [0, 1, 2, 3, 4, 4, 5, 6, 7]
    tops = [0] * 5 + [rows // 2] + [0] * 3
    for ref, s, top in zip(piece_refs, spots, tops):
        here = slice(top, top + ref.shape[0])
        first = 0
        for weight, grad in zip(weights, grads):
            width = weight.shape[1] // 8
            there = columns(at_ref[s], width)
            block = ref[:, first : first + width].astype(jnp.float32)
            grad[here, there] = block
            sums_ref[here, :] += lane_sums(block * weight[here, there].astype(jnp.float32))
            first += width


def widen(at, pieces, *weights):
    vmem = pl.BlockSpec(memory_space=pltpu.VMEM)
    shapes = [w.shape for w in weights] + [(weights[0].shape[0], 128)]
    return pl.pallas_call(
        lambda *refs: widen_kernel(*refs, pieces=len(pieces), count=len(weights)),
        in_specs=[pl.BlockSpec(memory_space=pltpu.SMEM)] + [vmem] * (len(pieces) + len(weights)),
        out_specs=[vmem] * len(shapes),
        out_shape=[jax.ShapeDtypeStruct(shape, jnp.float32) for shape in shapes],
        cost_estimate=CHEAP,
        name="widen",
    )(at, *pieces, *weights)


def grouped(strips):
    return [
        jnp.concatenate(strips[a:b], axis=0) if b - a > 1 else strips[a] for a, b in GROUPS
    ]


def split_groups(groups, rows):
    return [
        group[i * rows : (i + 1) * rows]
        for group in groups
        for i in range(group.shape[0] // rows)
    ]


def gather_head(rows):
    return lax.all_gather(rows, "head", axis=0, tiled=True)


def scatter_head(rows):
    return lax.psum_scatter(rows, "head", scatter_dimension=0, tiled=True)


def inverse_rms(rows):
    return lax.rsqrt(jnp.mean(rows * rows, axis=-1, keepdims=True) + EPS)


def per_device(
    tokens,
    attention_norm,
    query_weight,
    key_projection,
    value_projection,
    query_norm,
    key_norm,
    output_weight,
    feedforward_norm,
    gate_weight,
    up_weight,
    down_weight,
    stretch_order,
    out_cotangent,
):
    blk_count = lax.axis_size("blk")
    head_count = lax.axis_size("head")
    head_index = lax.axis_index("head")
    blk_index = lax.axis_index("blk")
    narrow, wide = jnp.bfloat16, jnp.float32
    tokens, out_cotangent = tokens[0], out_cotangent[0]
    local_rows, model_width = tokens.shape
    group_rows = local_rows * blk_count
    weight_rows = query_weight.shape[0]
    ff_local = gate_weight.shape[1] // blk_count
    query_cols = QUERY_HEADS // blk_count * HEAD_SIZE
    attn_cols = query_cols + 2 * HEAD_SIZE
    device_count = blk_count * head_count
    strip_count = blk_count * head_count
    halves = strip_count // stretch_order.shape[1]
    ring_place = jnp.where(blk_index % 2 == 0, blk_index // 2, 7 - blk_index // 2)

    spot = (ring_place + jnp.arange(blk_count, dtype=jnp.int32)) % blk_count
    at = jnp.where(spot < 4, 2 * spot, 15 - 2 * spot).astype(jnp.int32)
    at_own = jnp.concatenate([at, head_index[None].astype(jnp.int32)])
    ring_spot = (ring_place + jnp.asarray(STRIPS, jnp.int32)) % blk_count
    strip_blk = jnp.where(ring_spot < 4, 2 * ring_spot, 15 - 2 * ring_spot)
    strip_head = head_index ^ jnp.asarray((0, 2, 1, 3), jnp.int32)
    strip = (strip_blk[None, :] * head_count + strip_head[:, None]).reshape(strip_count)
    slots = jnp.arange(stretch_order.shape[1], dtype=jnp.int32)
    held = jnp.sum(
        jnp.where((strip // halves)[:, None] == slots[None, :], stretch_order, 0), axis=1
    )
    strip_place = held * halves + strip % halves
    order = strip_place.astype(jnp.int32)
    place = strip_place[:blk_count].astype(jnp.int32)
    positions = (
        place[:, None] * local_rows + jnp.arange(local_rows, dtype=jnp.int32)[None, :]
    ).reshape(group_rows)
    phases = angles(positions, HEAD_SIZE)[:, 0, :]
    cosine, sine = jnp.cos(phases), jnp.sin(phases)
    cosine = jnp.concatenate([cosine, cosine], axis=1)
    sine = jnp.concatenate([-sine, sine], axis=1)

    small = query_norm.shape[0]
    number = blk_index * head_count + head_index
    pad = 16

    def placed(share):
        return jnp.where(
            jnp.arange(device_count, dtype=jnp.int32)[:, None] == number, share[None, :], 0
        ).reshape(-1)

    gains = jnp.concatenate(
        [placed(attention_norm), placed(feedforward_norm), placed(query_norm), placed(key_norm)]
    ).astype(narrow)
    gains = jnp.pad(gains, (0, pad * attn_cols - gains.shape[0])).reshape(pad, attn_cols)
    down_matrix = gather_head(down_weight)
    output_rows = gather_head(output_weight)

    attn_swap = Swap(
        slice_pieces(at, query_weight, key_projection, value_projection, pad=gains),
        weight_rows + pad,
    )
    token_ring = Gather(tokens)
    ff_slices = slice_pieces(at, gate_weight, up_weight)
    for step in range(4):
        attn_swap.go()
        token_ring.go()
        if step == 0:
            ff_slices, cosine, sine = hold((attn_swap, token_ring), ff_slices, cosine, sine)
        elif step < 3:
            hold((attn_swap, token_ring))
    ff_swap, cotangent_ring = Swap(ff_slices, weight_rows), Gather(out_cotangent)
    own = hold((token_ring, ff_swap), attn_swap.result())
    near, far = cross(own, 1), cross(own, 2)
    ff_swap.go()
    own, near, far = hold((ff_swap, cotangent_ring), own, near, far)
    both = cross(far, 1)
    ff_swap.go()
    own, near, far, both = hold((ff_swap, cotangent_ring), own, near, far, both)

    first_normed, attn_raw, query_rows, own, attn_matrix, gains = project(
        at_own, token_ring.strips(), (own, near, far, both), cosine, sine, query_cols, pad
    )
    gain_one = gains[:4].reshape(1, model_width)
    gain_two = gains[4:8].reshape(1, model_width)
    head_gains = jnp.pad(gains[8, : 2 * HEAD_SIZE].reshape(2, HEAD_SIZE), ((0, 6), (0, 0)))
    ff_swap.go()
    cotangent_ring.go()
    own = hold((ff_swap, cotangent_ring), own)
    near, far = cross(own, 1), cross(own, 2)
    ff_swap.go()
    cotangent_ring.go()
    own, near, far = hold((), own, near, far)
    both = cross(far, 1)
    kv = own, far, near, both
    *kv, ff_own = hold((cotangent_ring,), *kv, ff_swap.result())
    ff_near, ff_far = cross(ff_own, 1), cross(ff_own, 2)
    cotangent_ring.go()
    attended, lse = attend(place, order, query_rows, kv)

    def by_groups(rows):
        return [rows[a * local_rows : b * local_rows] for a, b in GROUPS]

    def by_strips(groups):
        return dict(zip(STRIPS, split_groups(groups, local_rows)))

    attended = hold((cotangent_ring,), attended)
    branch_ring = Scatter(
        by_strips([matmul(rows, output_rows).astype(narrow) for rows in by_groups(attended)])
    )
    branch_ring.go()
    cotangent_ring.go()
    hold((branch_ring, cotangent_ring))
    branch_ring.go()
    ff_near, ff_far = hold((branch_ring,), ff_near, ff_far)
    ff_both = cross(ff_far, 1)
    branch_ring.go()
    cotangent_groups = grouped(cotangent_ring.strips())
    hidden_grads = [matmul(rows, down_matrix, ALONG) for rows in cotangent_groups]
    hidden_grads, ff_own, ff_near, ff_far, ff_both = hold(
        (branch_ring,), hidden_grads, ff_own, ff_near, ff_far, ff_both
    )
    branch_ring.go()
    ff_matrix = assemble(at_own, (ff_own, ff_near, ff_far, ff_both), weight_rows)
    ff_matrix = hold((branch_ring,), ff_matrix)
    tokens_wide = tokens.astype(wide)
    resid = tokens_wide + branch_ring.total()
    rho_two = inverse_rms(resid)
    unit_two = resid * rho_two

    second_ring = Gather((unit_two * gain_two).astype(narrow))
    second_groups, hidden_groups, ff_gradient_groups = [], [], []

    def feed_forward(index):
        rows = second_ring.group(index)
        ff_raw = matmul(rows, ff_matrix)
        gate, up_proj = ff_raw[:, :ff_local], ff_raw[:, ff_local:]
        sigma = jax.nn.sigmoid(gate)
        swish = gate * sigma
        hidden_gradient = hidden_grads[index]
        gate_gradient = hidden_gradient * up_proj * (sigma * (1.0 + gate * (1.0 - sigma)))
        hidden = (swish * up_proj).astype(narrow)
        gradient = jnp.concatenate([gate_gradient, hidden_gradient * swish], 1).astype(narrow)
        if index < 3:
            rows, hidden, gradient = hold((second_ring,), rows, hidden, gradient)
        second_groups.append(rows)
        hidden_groups.append(hidden)
        ff_gradient_groups.append(gradient)

    second_ring.go()
    hold((second_ring,))
    for index in range(3):
        second_ring.go()
        feed_forward(index)
    feed_forward(3)

    def back(index):
        return matmul(ff_gradient_groups[index], ff_matrix, ALONG).astype(narrow)

    def split(group):
        return [group[i : i + local_rows] for i in range(0, group.shape[0], local_rows)]

    parts = {4: back(3)}
    resid_ring = Scatter(parts)
    parts[3], parts[5] = split(hold((), back(2)))
    parts[2], parts[6] = split(hold((), back(1)))
    resid_ring.go()
    hold((resid_ring,), parts[2], parts[6])
    resid_ring.go()
    ff_own, ff_far, ff_sent = hold(
        (resid_ring,), *weight_grads(at_own, second_groups, ff_gradient_groups, weight_rows)
    )
    parts[0], parts[1], parts[7] = split(hold((), back(0)))
    resid_ring.go()
    ff_own, ff_far = scatter_cross(ff_own, ff_far, ff_sent)
    down_gradient = row_grads(hidden_groups, cotangent_groups)
    ff_own, ff_far, down_gradient = hold((resid_ring,), ff_own, ff_far, down_gradient)
    down_gradient = scatter_head(down_gradient)
    ff_far = cross(ff_far, 2)
    resid_ring.go()
    out_parts = [matmul(rows, down_matrix).astype(narrow) for rows in hidden_groups]
    out_parts = hold((resid_ring,), *out_parts)
    out_ring = Scatter(by_strips(out_parts))
    scaled = gain_two * resid_ring.total()
    resid_gradient = out_cotangent.astype(wide) + rho_two * (
        scaled - unit_two * jnp.mean(unit_two * scaled, axis=-1, keepdims=True)
    )

    grad_ring = Gather(resid_gradient.astype(narrow))
    grad_groups, attended_grads = [], []

    def attention_back(index):
        rows = grad_ring.group(index)
        grads = matmul(rows, output_rows, ALONG).astype(narrow)
        if index < 3:
            rows, grads = hold((grad_ring,), rows, grads)
        grad_groups.append(rows)
        attended_grads.append(grads)

    grad_ring.go()
    hold((grad_ring,))
    for index in range(3):
        grad_ring.go()
        attention_back(index)
    ff_swap = Swap(add(ff_own, ff_far), weight_rows)
    hold((grad_ring, ff_swap, out_ring))
    out_ring.go()
    ff_swap.go()
    attention_back(3)
    query_grads, kv_own, kv_far, kv_sent = attend_back(
        place, order, query_rows, attended_grads, attended, lse, kv
    )
    query_grads, kv_own, kv_far, kv_sent = hold(
        (out_ring, ff_swap), query_grads, kv_own, kv_far, kv_sent
    )
    out_ring.go()
    ff_swap.go()
    kv_own, kv_far = scatter_cross(kv_own, kv_far, kv_sent)
    kv_own, kv_far = hold((), kv_own, kv_far)
    kv_grads = add(kv_own, cross(kv_far, 2))
    output_weight_gradient = row_grads([attended], [jnp.concatenate(grad_groups, axis=0)])
    kv_grads, output_weight_gradient = hold(
        (out_ring, ff_swap), kv_grads, output_weight_gradient
    )
    output_weight_gradient = scatter_head(output_weight_gradient).astype(wide)
    out_ring.go()
    ff_swap.go()
    attn_gradient, first_parts, gain_sums = project_back(
        query_grads, kv_grads, attn_raw, head_gains, cosine, sine, attn_matrix
    )
    attn_gradient, first_parts, gain_sums = hold(
        (out_ring, ff_swap), attn_gradient, first_parts, gain_sums
    )
    token_ring = Scatter(by_strips(by_groups(first_parts)))
    token_ring.go()
    attn_own, attn_far, attn_sent = weight_grads(
        at_own, [first_normed], [attn_gradient], weight_rows
    )
    gain_sums = gain_sums + cross(gain_sums, 1)
    attn_own, attn_far, attn_sent, gain_sums = hold(
        (token_ring,), attn_own, attn_far, attn_sent, gain_sums
    )
    token_ring.go()
    ff_swap.go()
    attn_own, attn_far = scatter_cross(attn_own, attn_far, attn_sent)
    gain_sums = gain_sums + cross(gain_sums, 2)
    attn_own, attn_far, gain_sums = hold(
        (token_ring, ff_swap), attn_own, attn_far, gain_sums
    )
    attn_far = cross(attn_far, 2)
    token_ring.go()
    out_ring.go()
    gain_sums = gain_sums + mirror(gain_sums, 1)
    gate_weight_gradient, up_weight_gradient, norm_sums = widen(
        at, ff_swap.pieces(), gate_weight, up_weight
    )
    attn_swap = Swap(add(attn_own, attn_far), weight_rows)
    gate_weight_gradient, up_weight_gradient, norm_sums, gain_sums = hold(
        (token_ring, attn_swap, out_ring),
        gate_weight_gradient, up_weight_gradient, norm_sums, gain_sums,
    )
    feedforward_norm_gradient = jnp.sum(norm_sums, axis=1) / feedforward_norm.astype(wide)
    attn_swap.go()
    token_ring.go()
    gain_sums = gain_sums + mirror(gain_sums, 2)
    gain_sums = hold((token_ring, attn_swap), gain_sums)
    attn_swap.go()
    gain_sums = gain_sums + mirror(gain_sums, 4)
    layer_out = (resid + out_ring.total()).astype(narrow)
    layer_out, gain_sums = hold((attn_swap,), layer_out, gain_sums)
    attn_swap.go()
    hold((attn_swap,))
    attn_swap.go()
    query_weight_gradient, key_weight_gradient, value_weight_gradient, norm_sums = widen(
        at, attn_swap.pieces(), query_weight, key_projection, value_projection
    )
    attention_norm_gradient = jnp.sum(norm_sums, axis=1) / attention_norm.astype(wide)
    gain_sums = lax.dynamic_slice_in_dim(gain_sums, number * small, small, 1)
    rho_one = inverse_rms(tokens_wide)
    unit_one = tokens_wide * rho_one
    scaled = gain_one * token_ring.total()
    tokens_gradient = resid_gradient + rho_one * (
        scaled - unit_one * jnp.mean(unit_one * scaled, axis=-1, keepdims=True)
    )
    return (
        layer_out[None],
        tokens_gradient.astype(narrow)[None],
        attention_norm_gradient,
        query_weight_gradient,
        key_weight_gradient,
        value_weight_gradient,
        gain_sums[0],
        gain_sums[1],
        output_weight_gradient,
        feedforward_norm_gradient,
        gate_weight_gradient,
        up_weight_gradient,
        down_gradient.astype(wide),
    )


def solution(mesh):
    placed = (
        P(None, ("blk", "head"), None),
        P(("blk", "head")),
        P(("blk", "head"), None),
        P(("blk", "head"), None),
        P(("blk", "head"), None),
        P(("blk", "head")),
        P(("blk", "head")),
        P(("blk", "head"), None),
        P(("blk", "head")),
        P(("blk", "head"), None),
        P(("blk", "head"), None),
        P(("blk", "head"), None),
        P(),
        P(None, ("blk", "head"), None),
    )
    fits = mesh.shape["blk"] == KEY_VALUE_HEADS and mesh.shape["head"] == 4
    return jax.shard_map(
        per_device if fits else per_device_by_tokens,
        mesh=mesh,
        in_specs=placed,
        out_specs=(
            P(None, ("blk", "head"), None),
            P(None, ("blk", "head"), None),
            P(("blk", "head")),
            P(("blk", "head"), None),
            P(("blk", "head"), None),
            P(("blk", "head"), None),
            P(("blk", "head")),
            P(("blk", "head")),
            P(("blk", "head"), None),
            P(("blk", "head")),
            P(("blk", "head"), None),
            P(("blk", "head"), None),
            P(("blk", "head"), None),
        ),
        check_vma=False,
    )
```

```python
import math

import jax
import jax.numpy as jnp
from jax import lax
from jax.experimental import pallas as pl
from jax.experimental.pallas import tpu as pltpu
from jax.sharding import PartitionSpec as P

QUERY_HEADS = 16
KEY_VALUE_HEADS = 8
HEAD_SIZE = 128


EPS = 1e-06
NEG = -1e30
ROPE_BASE = 1000000.0


def passed_along(value, axis, by):
    count = lax.axis_size(axis)
    return lax.ppermute(value, axis, [(i, (i + by) % count) for i in range(count)])


def norm_rows(inputs, norm_gain):
    return inputs * lax.rsqrt(jnp.mean(inputs * inputs, axis=-1, keepdims=True) + EPS) * norm_gain


def rotary(inputs, phases):
    half_width = inputs.shape[-1] // 2
    cosine = jnp.cos(phases)
    sine_term = jnp.sin(phases)
    first_half = inputs[..., :half_width]
    second_half = inputs[..., half_width:]
    return jnp.concatenate(
        [
            first_half * cosine - second_half * sine_term,
            second_half * cosine + first_half * sine_term,
        ],
        axis=-1,
    )


def angles(positions, head_width):
    half_width = head_width // 2
    frequency = jnp.exp(
        jnp.arange(half_width, dtype=jnp.float32) * (-2.0 * math.log(ROPE_BASE) / head_width)
    )
    return positions.astype(jnp.float32)[..., None, None] * frequency


def token_positions(stretch_order, first_row, row_count, stretch_rows):
    row_index = first_row + jnp.arange(row_count, dtype=jnp.int32)
    slot_index = row_index // stretch_rows
    matches = slot_index[:, None] == jnp.arange(stretch_order.shape[1], dtype=jnp.int32)[None, :]
    picked = jnp.sum(jnp.where(matches[None], stretch_order[:, None, :], 0), axis=-1)
    return picked * stretch_rows + row_index % stretch_rows


def per_device_by_tokens(
    tokens,
    attention_norm,
    query_weight,
    key_projection,
    value_projection,
    query_norm,
    key_norm,
    output_weight,
    feedforward_norm,
    gate_weight,
    up_weight,
    down_weight,
    stretch_order,
    out_cotangent,
):
    count_of_heads = lax.axis_size("head")
    span_count = lax.axis_size("blk")
    span_index = lax.axis_index("blk")
    head_index = lax.axis_index("head")
    sequence_total = tokens.shape[0]
    local_rows = tokens.shape[1]
    group_rows = local_rows * count_of_heads
    stretch_rows = group_rows // 2
    heads_shared = KEY_VALUE_HEADS // count_of_heads
    heads_per_group = QUERY_HEADS // KEY_VALUE_HEADS
    score_scale = 1.0 / math.sqrt(HEAD_SIZE)
    gain_one, query_matrix, key_matrix, value_matrix, query_gain, key_gain, output_matrix = (
        lax.all_gather(attention_norm, ("blk", "head"), axis=0, tiled=True),
        lax.all_gather(query_weight, ("blk", "head"), axis=0, tiled=True),
        lax.all_gather(key_projection, ("blk", "head"), axis=0, tiled=True),
        lax.all_gather(value_projection, ("blk", "head"), axis=0, tiled=True),
        lax.all_gather(query_norm, ("blk", "head"), axis=0, tiled=True),
        lax.all_gather(key_norm, ("blk", "head"), axis=0, tiled=True),
        lax.all_gather(output_weight, ("blk", "head"), axis=0, tiled=True),
    )
    gain_two, gate_matrix, up_matrix, down_matrix = (
        lax.all_gather(feedforward_norm, ("blk", "head"), axis=0, tiled=True),
        lax.all_gather(gate_weight, ("blk", "head"), axis=0, tiled=True),
        lax.all_gather(up_weight, ("blk", "head"), axis=0, tiled=True),
        lax.all_gather(down_weight, ("blk", "head"), axis=0, tiled=True),
    )
    gain_one = gain_one.astype(jnp.float32)
    gain_two = gain_two.astype(jnp.float32)
    query_gain = query_gain.astype(jnp.float32)
    key_gain = key_gain.astype(jnp.float32)
    own_first = (span_index * count_of_heads + head_index) * local_rows
    own_pos = token_positions(stretch_order, own_first, local_rows, stretch_rows)
    group_pos = token_positions(stretch_order, span_index * group_rows, group_rows, stretch_rows)
    phases = angles(own_pos, HEAD_SIZE)
    tokens_wide = tokens.astype(jnp.float32)
    first_normed, norm_one_back = jax.vjp(norm_rows, tokens_wide, gain_one)
    first_normed = first_normed.astype(jnp.bfloat16)
    query_raw = jnp.einsum(
        "btd,de->bte", first_normed, query_matrix, preferred_element_type=jnp.float32
    ).reshape(sequence_total, local_rows, QUERY_HEADS, HEAD_SIZE)
    key_unnormed = jnp.einsum(
        "btd,de->bte", first_normed, key_matrix, preferred_element_type=jnp.float32
    ).reshape(sequence_total, local_rows, KEY_VALUE_HEADS, HEAD_SIZE)
    value_tokens = (
        jnp.einsum("btd,de->bte", first_normed, value_matrix, preferred_element_type=jnp.float32)
        .astype(jnp.bfloat16)
        .reshape(sequence_total, local_rows, KEY_VALUE_HEADS, HEAD_SIZE)
    )

    def heads_local(query_in, key_in, query_scale, key_scale):
        return (
            rotary(norm_rows(query_in, query_scale), phases),
            rotary(norm_rows(key_in, key_scale), phases),
        )

    (query_tokens, key_tokens), heads_back = jax.vjp(
        heads_local, query_raw, key_unnormed, query_gain, key_gain
    )
    query_tokens = query_tokens.astype(jnp.bfloat16)
    key_tokens = key_tokens.astype(jnp.bfloat16)
    query_group, key_group, value_group = (
        lax.all_to_all(query_tokens, "head", split_axis=2, concat_axis=1, tiled=True),
        lax.all_to_all(key_tokens, "head", split_axis=2, concat_axis=1, tiled=True),
        lax.all_to_all(value_tokens, "head", split_axis=2, concat_axis=1, tiled=True),
    )
    query_five = query_group.reshape(
        sequence_total, group_rows, heads_shared, heads_per_group, HEAD_SIZE
    )

    def block_update(carry, key_block, value_block, key_pos):
        run_max, run_sum, run_total = carry
        scores = (
            jnp.einsum(
                "bqkgd,bckd->bkgqc", query_five, key_block, preferred_element_type=jnp.float32
            )
            * score_scale
        )
        allowed = key_pos[:, None, None, None, :] <= group_pos[:, None, None, :, None]
        scores = jnp.where(allowed, scores, NEG)
        new_max = jnp.maximum(run_max, jnp.max(scores, axis=-1))
        exponent = jnp.where(allowed, jnp.exp(scores - new_max[..., None]), 0.0)
        factor = jnp.exp(run_max - new_max)
        new_sum = run_sum * factor + jnp.sum(exponent, axis=-1)
        new_total = run_total * factor[..., None] + jnp.einsum(
            "bkgqc,bckd->bkgqd",
            exponent.astype(jnp.bfloat16),
            value_block,
            preferred_element_type=jnp.float32,
        )
        return (new_max, new_sum, new_total)

    def fold_update(carry, key_block, value_block, key_pos):
        result = block_update(carry, key_block, value_block, key_pos)
        return result

    stat_shape = (sequence_total, heads_shared, heads_per_group, group_rows)
    start_state = (
        jnp.full(stat_shape, NEG, jnp.float32),
        jnp.zeros(stat_shape, jnp.float32),
        jnp.zeros(stat_shape + (HEAD_SIZE,), jnp.float32),
    )
    key_piece = lax.all_gather(key_group, "blk", axis=1, tiled=True)
    value_piece = lax.all_gather(value_group, "blk", axis=1, tiled=True)
    piece_rows = key_piece.shape[1]
    block_len = math.gcd(group_rows, piece_rows)

    def inner(block_number, carry_in):
        offset = block_number * block_len
        key_block = lax.dynamic_slice_in_dim(key_piece, offset, block_len, 1)
        value_block = lax.dynamic_slice_in_dim(value_piece, offset, block_len, 1)
        key_pos = token_positions(stretch_order, offset, block_len, stretch_rows)
        return fold_update(carry_in, key_block, value_block, key_pos)

    run_max, run_sum, run_total = lax.fori_loop(0, piece_rows // block_len, inner, start_state)
    log_total = run_max + jnp.log(run_sum)
    attended_five = run_total / run_sum[..., None]
    attended_group = (
        jnp.transpose(attended_five, (0, 3, 1, 2, 4))
        .reshape(sequence_total, group_rows, heads_shared * heads_per_group, HEAD_SIZE)
        .astype(jnp.bfloat16)
    )
    attended_tokens = lax.all_to_all(
        attended_group, "head", split_axis=1, concat_axis=2, tiled=True
    ).reshape(sequence_total, local_rows, QUERY_HEADS * HEAD_SIZE)
    branch = jnp.einsum(
        "bte,ed->btd", attended_tokens, output_matrix, preferred_element_type=jnp.float32
    )
    resid = tokens_wide + branch
    normed_two, norm_two_back = jax.vjp(norm_rows, resid, gain_two)
    normed_two = normed_two.astype(jnp.bfloat16)
    gate = jnp.einsum("btd,df->btf", normed_two, gate_matrix, preferred_element_type=jnp.float32)
    up_proj = jnp.einsum("btd,df->btf", normed_two, up_matrix, preferred_element_type=jnp.float32)

    def swish_product(gate_in, up_in):
        return jax.nn.silu(gate_in) * up_in

    hidden, swish_back = jax.vjp(swish_product, gate, up_proj)
    hidden = hidden.astype(jnp.bfloat16)
    layer_out = (
        resid + jnp.einsum("btf,fd->btd", hidden, down_matrix, preferred_element_type=jnp.float32)
    ).astype(jnp.bfloat16)
    gain_again, gate_matrix, up_matrix, down_matrix = (
        lax.all_gather(feedforward_norm, ("blk", "head"), axis=0, tiled=True),
        lax.all_gather(gate_weight, ("blk", "head"), axis=0, tiled=True),
        lax.all_gather(up_weight, ("blk", "head"), axis=0, tiled=True),
        lax.all_gather(down_weight, ("blk", "head"), axis=0, tiled=True),
    )
    down_gradient = jnp.einsum(
        "btf,btd->fd", hidden, out_cotangent, preferred_element_type=jnp.float32
    )
    hidden_gradient = jnp.einsum(
        "btd,fd->btf", out_cotangent, down_matrix, preferred_element_type=jnp.float32
    )
    gate_gradient, up_gradient = swish_back(hidden_gradient)
    gate_gradient = gate_gradient.astype(jnp.bfloat16)
    up_gradient = up_gradient.astype(jnp.bfloat16)
    gate_matrix_gradient = jnp.einsum(
        "btd,btf->df", normed_two, gate_gradient, preferred_element_type=jnp.float32
    )
    up_matrix_gradient = jnp.einsum(
        "btd,btf->df", normed_two, up_gradient, preferred_element_type=jnp.float32
    )
    normed_two_gradient = jnp.einsum(
        "btf,df->btd", gate_gradient, gate_matrix, preferred_element_type=jnp.float32
    ) + jnp.einsum("btf,df->btd", up_gradient, up_matrix, preferred_element_type=jnp.float32)
    resid_part, gain_two_gradient = norm_two_back(normed_two_gradient)
    resid_gradient = out_cotangent.astype(jnp.float32) + resid_part
    feedforward_sums = (
        lax.psum_scatter(gain_two_gradient, ("blk", "head"), scatter_dimension=0, tiled=True),
        lax.psum_scatter(gate_matrix_gradient, ("blk", "head"), scatter_dimension=0, tiled=True),
        lax.psum_scatter(up_matrix_gradient, ("blk", "head"), scatter_dimension=0, tiled=True),
        lax.psum_scatter(down_gradient, ("blk", "head"), scatter_dimension=0, tiled=True),
    )
    gain_again, query_matrix, key_matrix, value_matrix, query_again, key_again, output_matrix = (
        lax.all_gather(attention_norm, ("blk", "head"), axis=0, tiled=True),
        lax.all_gather(query_weight, ("blk", "head"), axis=0, tiled=True),
        lax.all_gather(key_projection, ("blk", "head"), axis=0, tiled=True),
        lax.all_gather(value_projection, ("blk", "head"), axis=0, tiled=True),
        lax.all_gather(query_norm, ("blk", "head"), axis=0, tiled=True),
        lax.all_gather(key_norm, ("blk", "head"), axis=0, tiled=True),
        lax.all_gather(output_weight, ("blk", "head"), axis=0, tiled=True),
    )
    branch_gradient = resid_gradient.astype(jnp.bfloat16)
    output_matrix_gradient = jnp.einsum(
        "bte,btd->ed", attended_tokens, branch_gradient, preferred_element_type=jnp.float32
    )
    attended_gradient = (
        jnp.einsum(
            "btd,ed->bte", branch_gradient, output_matrix, preferred_element_type=jnp.float32
        )
        .astype(jnp.bfloat16)
        .reshape(sequence_total, local_rows, QUERY_HEADS, HEAD_SIZE)
    )
    attended_grad_group = lax.all_to_all(
        attended_gradient, "head", split_axis=2, concat_axis=1, tiled=True
    ).reshape(sequence_total, group_rows, heads_shared, heads_per_group, HEAD_SIZE)
    delta = jnp.sum(
        jnp.transpose(attended_grad_group.astype(jnp.float32), (0, 2, 3, 1, 4)) * attended_five,
        axis=-1,
    )

    def block_grads(sums_in, key_current, value_current, key_pos):
        key_sum, value_sum, query_sum = sums_in
        scores = (
            jnp.einsum(
                "bqkgd,bckd->bkgqc", query_five, key_current, preferred_element_type=jnp.float32
            )
            * score_scale
        )
        allowed = key_pos[:, None, None, None, :] <= group_pos[:, None, None, :, None]
        weights = jnp.where(allowed, jnp.exp(scores - log_total[..., None]), 0.0)
        probs = weights.astype(jnp.bfloat16)
        value_sum = value_sum + jnp.einsum(
            "bkgqc,bqkgd->bckd", probs, attended_grad_group, preferred_element_type=jnp.float32
        )
        probs_gradient = jnp.einsum(
            "bqkgd,bckd->bkgqc",
            attended_grad_group,
            value_current,
            preferred_element_type=jnp.float32,
        )
        scores_gradient = (weights * (probs_gradient - delta[..., None])).astype(jnp.bfloat16)
        query_sum = (
            query_sum
            + jnp.einsum(
                "bkgqc,bckd->bqkgd",
                scores_gradient,
                key_current,
                preferred_element_type=jnp.float32,
            )
            * score_scale
        )
        key_sum = (
            key_sum
            + jnp.einsum(
                "bkgqc,bqkgd->bckd", scores_gradient, query_five, preferred_element_type=jnp.float32
            )
            * score_scale
        )
        return (key_sum, value_sum, query_sum)

    def pass_step(step_index, carry):
        key_current, value_current, key_sum, value_sum, query_sum = carry
        anchor = (span_index - step_index) % span_count
        key_pos = token_positions(stretch_order, anchor * group_rows, group_rows, stretch_rows)
        key_sum, value_sum, query_sum = block_grads(
            (key_sum, value_sum, query_sum), key_current, value_current, key_pos
        )
        key_current, value_current = passed_along((key_current, value_current), "blk", 1)
        key_sum, value_sum = (
            passed_along(key_sum.astype(jnp.bfloat16), "blk", 1).astype(key_sum.dtype),
            passed_along(value_sum.astype(jnp.bfloat16), "blk", 1).astype(value_sum.dtype),
        )
        return (key_current, value_current, key_sum, value_sum, query_sum)

    kv_zeros = jnp.zeros((sequence_total, group_rows, heads_shared, HEAD_SIZE), jnp.float32)
    query_zeros = jnp.zeros(
        (sequence_total, group_rows, heads_shared, heads_per_group, HEAD_SIZE), jnp.float32
    )
    final_state = lax.fori_loop(
        0, span_count, pass_step, (key_group, value_group, kv_zeros, kv_zeros, query_zeros)
    )
    key_grad_group = final_state[2].astype(jnp.bfloat16)
    value_grad_group = final_state[3].astype(jnp.bfloat16)
    query_grad_group = (
        final_state[4]
        .astype(jnp.bfloat16)
        .reshape(sequence_total, group_rows, heads_shared * heads_per_group, HEAD_SIZE)
    )
    query_grad_tokens, key_grad_tokens, value_gradient_tokens = (
        lax.all_to_all(query_grad_group, "head", split_axis=1, concat_axis=2, tiled=True),
        lax.all_to_all(key_grad_group, "head", split_axis=1, concat_axis=2, tiled=True),
        lax.all_to_all(value_grad_group, "head", split_axis=1, concat_axis=2, tiled=True),
    )
    query_raw_gradient, key_unnormed_gradient, query_gain_gradient, key_gain_gradient = heads_back(
        (query_grad_tokens.astype(jnp.float32), key_grad_tokens.astype(jnp.float32))
    )
    query_raw_gradient = query_raw_gradient.astype(jnp.bfloat16).reshape(
        sequence_total, local_rows, QUERY_HEADS * HEAD_SIZE
    )
    key_unnormed_gradient = key_unnormed_gradient.astype(jnp.bfloat16).reshape(
        sequence_total, local_rows, KEY_VALUE_HEADS * HEAD_SIZE
    )
    value_unnormed_gradient = value_gradient_tokens.reshape(
        sequence_total, local_rows, KEY_VALUE_HEADS * HEAD_SIZE
    )
    query_matrix_gradient = jnp.einsum(
        "btd,bte->de", first_normed, query_raw_gradient, preferred_element_type=jnp.float32
    )
    key_matrix_gradient = jnp.einsum(
        "btd,bte->de", first_normed, key_unnormed_gradient, preferred_element_type=jnp.float32
    )
    value_matrix_gradient = jnp.einsum(
        "btd,bte->de", first_normed, value_unnormed_gradient, preferred_element_type=jnp.float32
    )
    normed_one_gradient = jnp.einsum(
        "bte,de->btd", query_raw_gradient, query_matrix, preferred_element_type=jnp.float32
    )
    normed_one_gradient = normed_one_gradient + jnp.einsum(
        "bte,de->btd", key_unnormed_gradient, key_matrix, preferred_element_type=jnp.float32
    )
    normed_one_gradient = normed_one_gradient + jnp.einsum(
        "bte,de->btd", value_unnormed_gradient, value_matrix, preferred_element_type=jnp.float32
    )
    token_part, gain_one_gradient = norm_one_back(normed_one_gradient)
    tokens_gradient = (resid_gradient + token_part).astype(jnp.bfloat16)
    attention_sums = (
        lax.psum_scatter(gain_one_gradient, ("blk", "head"), scatter_dimension=0, tiled=True),
        lax.psum_scatter(query_matrix_gradient, ("blk", "head"), scatter_dimension=0, tiled=True),
        lax.psum_scatter(key_matrix_gradient, ("blk", "head"), scatter_dimension=0, tiled=True),
        lax.psum_scatter(value_matrix_gradient, ("blk", "head"), scatter_dimension=0, tiled=True),
        lax.psum_scatter(query_gain_gradient, ("blk", "head"), scatter_dimension=0, tiled=True),
        lax.psum_scatter(key_gain_gradient, ("blk", "head"), scatter_dimension=0, tiled=True),
        lax.psum_scatter(output_matrix_gradient, ("blk", "head"), scatter_dimension=0, tiled=True),
    )
    return (
        layer_out,
        tokens_gradient,
        attention_sums[0],
        attention_sums[1],
        attention_sums[2],
        attention_sums[3],
        attention_sums[4],
        attention_sums[5],
        attention_sums[6],
        feedforward_sums[0],
        feedforward_sums[1],
        feedforward_sums[2],
        feedforward_sums[3],
    )


LOG2E = math.log2(math.e)
STRIP = 128
CHUNK = 512
ALONG = (((1,), (1,)), ((), ()))
DOWN = (((0,), (0,)), ((), ()))


def two_heads(block):
    return jnp.concatenate([block[:, :HEAD_SIZE], block[:, HEAD_SIZE:]], axis=0)


def side_by_side(rows):
    half = rows.shape[0] // 2
    return jnp.concatenate([rows[:half], rows[half:]], axis=1)


CHEAP = pl.CostEstimate(flops=1, bytes_accessed=1, transcendentals=0)
LONG = pl.CostEstimate(flops=3 * 10**10, bytes_accessed=1 << 25, transcendentals=0)


def sort_strips(order_ref, kv_refs, keys, values):
    per = kv_refs[0].shape[0] // STRIP
    for j, ref in enumerate(kv_refs):
        for i in range(per):
            target = pl.multiple_of(order_ref[j * per + i] * STRIP, STRIP)
            here = slice(i * STRIP, (i + 1) * STRIP)
            keys[pl.ds(target, STRIP), :] = ref[here, :HEAD_SIZE]
            values[pl.ds(target, STRIP), :HEAD_SIZE] = ref[here, HEAD_SIZE:]


def attend_kernel(place_ref, order_ref, q_ref, *refs):
    kv_refs, (out_ref, lse_ref, keys, values) = refs[:4], refs[4:]
    step = pl.program_id(0)

    @pl.when(step == 0)
    def _():
        values[:, HEAD_SIZE:] = jnp.ones((values.shape[0], HEAD_SIZE), jnp.bfloat16)
        sort_strips(order_ref, kv_refs, keys, values)

    place = place_ref[step]
    queries = two_heads(q_ref[...])
    last = place // (CHUNK // STRIP)

    def part(index, total, masked):
        first = pl.multiple_of(index * CHUNK, CHUNK)
        scores = lax.dot_general(
            queries, keys[pl.ds(first, CHUNK), :], ALONG, preferred_element_type=jnp.float32
        )
        weights = jnp.exp2(scores)
        if masked:
            row = lax.broadcasted_iota(jnp.int32, scores.shape, 0) % STRIP
            column = lax.broadcasted_iota(jnp.int32, scores.shape, 1)
            weights = jnp.where(column - row <= place * STRIP - first, weights, 0.0)
        return total + jnp.dot(
            weights.astype(jnp.bfloat16),
            values[pl.ds(first, CHUNK), :],
            preferred_element_type=jnp.float32,
        )

    total = jnp.zeros((2 * STRIP, 2 * HEAD_SIZE), jnp.float32)
    total = lax.fori_loop(0, last, lambda index, t: part(index, t, False), total)
    total = part(last, total, True)
    norm = total[:, HEAD_SIZE:]
    out_ref[...] = side_by_side(total[:, :HEAD_SIZE] / norm).astype(jnp.bfloat16)
    lse_ref[0] = jnp.transpose(jnp.log2(norm))[:8]


def attend(place, order, queries, kv):
    rows, width = queries.shape
    steps = rows // STRIP
    total = sum(part.shape[0] for part in kv)
    strip = pl.BlockSpec((STRIP, width), lambda i, *_: (i, 0))
    return pl.pallas_call(
        attend_kernel,
        grid_spec=pltpu.PrefetchScalarGridSpec(
            num_scalar_prefetch=2,
            grid=(steps,),
            in_specs=[strip] + [pl.BlockSpec(part.shape, lambda i, *_: (0, 0)) for part in kv],
            out_specs=[strip, pl.BlockSpec((1, 8, 2 * STRIP), lambda i, *_: (i, 0, 0))],
            scratch_shapes=[
                pltpu.VMEM((total, HEAD_SIZE), jnp.bfloat16),
                pltpu.VMEM((total, 2 * HEAD_SIZE), jnp.bfloat16),
            ],
        ),
        out_shape=[
            jax.ShapeDtypeStruct((rows, width), jnp.bfloat16),
            jax.ShapeDtypeStruct((steps, 8, 2 * STRIP), jnp.float32),
        ],
        cost_estimate=LONG,
        name="attend",
    )(place, order, queries, *kv)


def attend_back_kernel(place_ref, order_ref, q_ref, out_ref, lse_ref, *refs, groups):
    grad_refs, kv_refs = refs[:groups], refs[groups : groups + 4]
    dq_ref, own_ref, far_ref, sent_ref = refs[groups + 4 : groups + 8]
    keys, values, key_sums, value_sums, grads_all = refs[groups + 8 :]
    step = pl.program_id(0)

    @pl.when(step == 0)
    def _():
        key_sums[...] = jnp.zeros_like(key_sums)
        value_sums[...] = jnp.zeros_like(value_sums)
        sort_strips(order_ref, kv_refs, keys, values)
        first = 0
        for ref in grad_refs:
            grads_all[first : first + ref.shape[0], :] = ref[...]
            first += ref.shape[0]

    place = place_ref[step]
    queries = two_heads(q_ref[...])
    grads = two_heads(grads_all[pl.ds(pl.multiple_of(step * STRIP, STRIP), STRIP), :])
    product = grads.astype(jnp.float32) * two_heads(out_ref[...]).astype(jnp.float32)
    delta = jnp.sum(jnp.transpose(product), axis=0, keepdims=True)
    lse = lse_ref[0, :1]
    last = place // (CHUNK // STRIP)

    def part(index, total, masked):
        first = pl.multiple_of(index * CHUNK, CHUNK)
        here = pl.ds(first, CHUNK)
        key_rows = keys[here, :]
        scores = lax.dot_general(key_rows, queries, ALONG, preferred_element_type=jnp.float32)
        weights = jnp.exp2(scores - lse)
        if masked:
            row = lax.broadcasted_iota(jnp.int32, scores.shape, 0)
            column = lax.broadcasted_iota(jnp.int32, scores.shape, 1) % STRIP
            weights = jnp.where(row - column <= place * STRIP - first, weights, 0.0)
        slopes = lax.dot_general(
            values[here, :], grads, ALONG, preferred_element_type=jnp.float32
        )
        score_grads = (weights * (slopes - delta)).astype(jnp.bfloat16)
        value_sums[here, :] += jnp.dot(
            weights.astype(jnp.bfloat16), grads, preferred_element_type=jnp.float32
        )
        key_sums[here, :] += jnp.dot(score_grads, queries, preferred_element_type=jnp.float32)
        return total + lax.dot_general(
            score_grads, key_rows, DOWN, preferred_element_type=jnp.float32
        )

    total = jnp.zeros((2 * STRIP, HEAD_SIZE), jnp.float32)
    total = lax.fori_loop(0, last, lambda index, t: part(index, t, False), total)
    total = part(last, total, True)
    dq_ref[...] = side_by_side(total * (1.0 / math.sqrt(HEAD_SIZE))).astype(jnp.bfloat16)

    @pl.when(step == pl.num_programs(0) - 1)
    def _():
        per = own_ref.shape[0] // STRIP
        for j in range(4):
            target = (own_ref, far_ref, sent_ref, sent_ref)[j]
            base = per if j == 3 else 0
            for i in range(per):
                source = pl.multiple_of(order_ref[j * per + i] * STRIP, STRIP)
                here = slice((base + i) * STRIP, (base + i + 1) * STRIP)
                target[here, :HEAD_SIZE] = (
                    key_sums[pl.ds(source, STRIP), :] * (1.0 / LOG2E)
                ).astype(jnp.bfloat16)
                target[here, HEAD_SIZE:] = value_sums[pl.ds(source, STRIP), :].astype(
                    jnp.bfloat16
                )


def attend_back(place, order, queries, grads, attended, lse, kv):
    rows, width = queries.shape
    steps = rows // STRIP
    total = sum(part.shape[0] for part in kv)
    strip = pl.BlockSpec((STRIP, width), lambda i, *_: (i, 0))

    def whole(shape):
        return pl.BlockSpec(shape, lambda i, *_: (0, 0))

    outs = [kv[0].shape, kv[0].shape, (2 * kv[0].shape[0], kv[0].shape[1])]
    return pl.pallas_call(
        lambda *refs: attend_back_kernel(*refs, groups=len(grads)),
        grid_spec=pltpu.PrefetchScalarGridSpec(
            num_scalar_prefetch=2,
            grid=(steps,),
            in_specs=[strip, strip, pl.BlockSpec((1, 8, 2 * STRIP), lambda i, *_: (i, 0, 0))]
            + [whole(part.shape) for part in (*grads, *kv)],
            out_specs=[strip] + [whole(shape) for shape in outs],
            scratch_shapes=[
                pltpu.VMEM((total, HEAD_SIZE), jnp.bfloat16),
                pltpu.VMEM((total, HEAD_SIZE), jnp.bfloat16),
                pltpu.VMEM((total, HEAD_SIZE), jnp.float32),
                pltpu.VMEM((total, HEAD_SIZE), jnp.float32),
                pltpu.VMEM((rows, width), jnp.bfloat16),
            ],
        ),
        out_shape=[jax.ShapeDtypeStruct((rows, width), jnp.bfloat16)]
        + [jax.ShapeDtypeStruct(shape, jnp.bfloat16) for shape in outs],
        cost_estimate=LONG,
        name="attend_back",
    )(place, order, queries, attended, lse, *grads, *kv)


def matmul(left, right, dims=(((1,), (0,)), ((), ()))):
    return lax.dot_general(left, right, dims, preferred_element_type=jnp.float32)


RING = (0, 2, 4, 6, 7, 5, 3, 1)
STRIPS = (0, 1, 7, 2, 6, 3, 5, 4)
GROUPS = ((0, 3), (3, 5), (5, 7), (7, 8))


def hop(value, by):
    count = len(RING)
    return lax.ppermute(value, "blk", [(RING[i], RING[(i + by) % count]) for i in range(count)])


def cross(value, by):
    return lax.ppermute(value, "head", [(i, i ^ by) for i in range(4)])


def mirror(value, by):
    return lax.ppermute(value, "blk", [(i, i ^ by) for i in range(len(RING))])


def add(left, right):
    return (left.astype(jnp.float32) + right.astype(jnp.float32)).astype(left.dtype)


class Gather:
    def __init__(self, own):
        self.got, self.step = {0: own}, 0
        self.state = (own, own)

    def go(self):
        self.step += 1
        left, right = self.state
        if self.step < 4:
            self.state = hop(left, -1), hop(right, 1)
            self.got[self.step], self.got[8 - self.step] = self.state
        else:
            half = left.shape[0] // 2
            self.got[4] = jnp.concatenate([hop(left[:half], -1), hop(right[half:], 1)], axis=0)
            self.state = (self.got[4],)

    def strips(self):
        return [self.got[s] for s in STRIPS]

    def group(self, index):
        first, last = GROUPS[index]
        return jnp.concatenate([self.got[s] for s in STRIPS[first:last]], axis=0)


class Scatter:
    def __init__(self, part):
        self.part, self.step = part, 0
        self.half = part[4].shape[0] // 2
        self.state = (part[4][: self.half], part[4][self.half :])

    def go(self):
        self.step += 1
        half, part = self.half, self.part
        up, down = hop(self.state[0], 1), hop(self.state[1], -1)
        if self.step == 1:
            up = jnp.concatenate([add(part[3][:half], up), part[3][half:]], axis=0)
            down = jnp.concatenate([part[5][:half], add(part[5][half:], down)], axis=0)
        elif self.step < 4:
            up, down = add(part[4 - self.step], up), add(part[4 + self.step], down)
        self.state = up, down

    def total(self):
        up, down = self.state
        wide = jnp.float32
        return self.part[0].astype(wide) + up.astype(wide) + down.astype(wide)


class Swap:
    def __init__(self, pieces, rows):
        cut = 4 * rows + rows // 2
        self.rows, self.step = rows, 0
        self.taken = [(pieces, 0, rows, 0, 0)]
        self.state = (pieces[rows:cut], pieces[cut:])

    def go(self):
        self.step += 1
        rows, step = self.rows, self.step
        right, left = hop(self.state[0], 1), hop(self.state[1], -1)
        if step < 4:
            self.taken.append((right, 0, rows, 8 - step, 0))
            self.taken.append((left, left.shape[0] - rows, rows, step, 0))
            self.state = right[rows:], left[:-rows]
        else:
            self.taken.append((right, 0, rows // 2, 4, 0))
            self.taken.append((left, 0, rows // 2, 4, rows // 2))
            self.state = right, left

    def operands(self):
        return [item[0] for item in self.taken]

    def specs(self):
        vmem = pl.BlockSpec(memory_space=pltpu.VMEM)
        own = pl.BlockSpec((self.rows, self.taken[0][0].shape[1]), lambda i: (0, 0))
        return [own] + [vmem] * (len(self.taken) - 1)

    def result(self):
        rows, taken = self.rows, [item[1:] for item in self.taken]

        def stack_kernel(*refs):
            for ref, (first, count, spot, top) in zip(refs[:-1], taken):
                at = spot * rows + top
                refs[-1][at : at + count, :] = ref[first : first + count, :]

        return pl.pallas_call(
            stack_kernel,
            grid=(1,),
            in_specs=self.specs(),
            out_specs=pl.BlockSpec(memory_space=pltpu.VMEM),
            out_shape=jax.ShapeDtypeStruct((8 * rows, self.taken[0][0].shape[1]), jnp.bfloat16),
            cost_estimate=CHEAP,
            name="stack",
        )(*self.operands())


def hold(rings, *extra):
    states, extra = lax.optimization_barrier(([ring.state for ring in rings], extra))
    for ring, state in zip(rings, states):
        ring.state = state
    return extra[0] if len(extra) == 1 else extra


def scatter_cross(own, far, sent):
    moved = cross(sent, 1)
    half = own.shape[0]
    return add(own, moved[:half]), add(far, moved[half:])


def columns(at, width):
    return pl.ds(pl.multiple_of(at * width, width), width)


def slice_kernel(at_ref, *refs, pad):
    weights, out_ref = refs[:-1], refs[-1]
    if pad:
        weights, pad_ref = weights[:-1], weights[-1]
    rows = weights[0].shape[0]
    each = rows + pad
    for s in range(8):
        first = 0
        for ref in weights:
            width = ref.shape[1] // 8
            out_ref[s * each : s * each + rows, first : first + width] = ref[
                :, columns(at_ref[s], width)
            ]
            first += width
        if pad:
            out_ref[s * each + rows : (s + 1) * each, :] = pad_ref[...]


def slice_pieces(at, *weights, pad=None):
    rows = weights[0].shape[0]
    cols = sum(w.shape[1] for w in weights) // 8
    extra = 0 if pad is None else pad.shape[0]
    operands = weights if pad is None else (*weights, pad)
    vmem = pl.BlockSpec(memory_space=pltpu.VMEM)
    return pl.pallas_call(
        lambda *refs: slice_kernel(*refs, pad=extra),
        in_specs=[pl.BlockSpec(memory_space=pltpu.SMEM)] + [vmem] * len(operands),
        out_specs=vmem,
        out_shape=jax.ShapeDtypeStruct((8 * (rows + extra), cols), jnp.bfloat16),
        cost_estimate=CHEAP,
        name="slice_pieces",
    )(at, *operands)


def assemble_kernel(at_ref, *refs):
    own = at_ref[8]
    for j, piece in enumerate(refs[:4]):
        refs[4][0, own ^ j] = piece[...]


def assemble(at, pieces, rows):
    count = at.shape[0] - 1
    total, cols = pieces[0].shape
    return pl.pallas_call(
        assemble_kernel,
        grid_spec=pltpu.PrefetchScalarGridSpec(
            num_scalar_prefetch=1,
            grid=(count,),
            in_specs=[pl.BlockSpec((rows, cols), lambda i, at: (i, 0))] * 4,
            out_specs=pl.BlockSpec((1, 4, rows, cols), lambda i, at: (at[i], 0, 0, 0)),
        ),
        out_shape=jax.ShapeDtypeStruct((count, 4, rows, cols), jnp.bfloat16),
        cost_estimate=CHEAP,
        name="assemble",
    )(at, *pieces).reshape(4 * total, cols)


def spun(rows, cosine, sine):
    return rows * cosine + pltpu.roll(rows, HEAD_SIZE // 2, 1) * sine


def project_kernel(at_ref, *refs, strips):
    token_refs, refs = refs[:strips], refs[strips:]
    pieces, refs = refs[:4], refs[4:]
    cos_ref, sin_ref, normed_ref, raw_ref, q_ref, kv_ref, matrix_ref, gains_ref = refs
    each = pieces[0].shape[0] // 8
    rows = matrix_ref.shape[0] // 32
    own = at_ref[8]
    gains = jnp.zeros(gains_ref.shape, jnp.float32)
    for s in range(8):
        for j in range(4):
            first = pl.multiple_of((at_ref[s] * 4 + (own ^ j)) * rows, rows)
            matrix_ref[pl.ds(first, rows), :] = pieces[j][s * each : s * each + rows, :]
            gains += pieces[j][s * each + rows : (s + 1) * each, :].astype(jnp.float32)
    gains_ref[...] = gains
    width = gains.shape[1]
    first = 0
    for ref in token_refs:
        block = ref[...].astype(jnp.float32)
        block = block * inverse_rms(block)
        here = slice(first, first + ref.shape[0])
        for i in range(block.shape[1] // width):
            cols = slice(i * width, (i + 1) * width)
            normed_ref[here, cols] = (block[:, cols] * gains[i : i + 1]).astype(jnp.bfloat16)
        first += ref.shape[0]
    query_gain, key_gain = gains[8:9, :HEAD_SIZE], gains[8:9, HEAD_SIZE : 2 * HEAD_SIZE]
    query_cols = q_ref.shape[1]
    step = 256
    for first in range(0, q_ref.shape[0], step):
        here = slice(first, first + step)
        raw = jnp.dot(normed_ref[here, :], matrix_ref[...], preferred_element_type=jnp.float32)
        raw_ref[here, :] = raw
        cosine, sine = cos_ref[here, :], sin_ref[here, :]
        for col in range(0, query_cols + HEAD_SIZE, HEAD_SIZE):
            part = raw[:, col : col + HEAD_SIZE]
            if col < query_cols:
                part = spun(part * inverse_rms(part) * query_gain, cosine, sine)
                part = part * (LOG2E / math.sqrt(HEAD_SIZE))
                q_ref[here, col : col + HEAD_SIZE] = part.astype(jnp.bfloat16)
            else:
                part = spun(part * inverse_rms(part) * key_gain, cosine, sine)
                kv_ref[here, :HEAD_SIZE] = part.astype(jnp.bfloat16)
        kv_ref[here, HEAD_SIZE:] = raw[:, query_cols + HEAD_SIZE :].astype(jnp.bfloat16)


def project(at, strips, pieces, cosine, sine, query_cols, pad):
    rows = sum(strip.shape[0] for strip in strips)
    width = strips[0].shape[1]
    cols = pieces[0].shape[1]
    vmem = pl.BlockSpec(memory_space=pltpu.VMEM)
    operands = (*strips, *pieces, cosine, sine)
    narrow, wide = jnp.bfloat16, jnp.float32
    return pl.pallas_call(
        lambda *refs: project_kernel(*refs, strips=len(strips)),
        in_specs=[pl.BlockSpec(memory_space=pltpu.SMEM)] + [vmem] * len(operands),
        out_specs=[vmem] * 6,
        out_shape=[
            jax.ShapeDtypeStruct((rows, width), narrow),
            jax.ShapeDtypeStruct((rows, cols), wide),
            jax.ShapeDtypeStruct((rows, query_cols), narrow),
            jax.ShapeDtypeStruct((rows, 2 * HEAD_SIZE), narrow),
            jax.ShapeDtypeStruct((width, cols), narrow),
            jax.ShapeDtypeStruct((pad, cols), wide),
        ],
        cost_estimate=LONG,
        name="project",
    )(at, *operands)


def project_back_kernel(
    dq_ref, dkv_ref, raw_ref, head_gain_ref, cos_ref, sin_ref, matrix_ref,
    grad_ref, part_ref, gain_ref,
):
    query_cols = dq_ref.shape[1]
    step = 256
    gain_ref[...] = jnp.zeros_like(gain_ref)
    for first in range(0, dq_ref.shape[0], step):
        here = slice(first, first + step)
        cosine, sine = cos_ref[here, :], sin_ref[here, :]
        for col in range(0, query_cols + HEAD_SIZE, HEAD_SIZE):
            cols = slice(col, col + HEAD_SIZE)
            which = 0 if col < query_cols else 1
            grads = dkv_ref[here, :HEAD_SIZE] if which else dq_ref[here, cols]
            raw = raw_ref[here, cols]
            rho = inverse_rms(raw)
            unit = raw * rho
            turned = spun(grads.astype(jnp.float32), cosine, -sine)
            gain_ref[which : which + 1, :] += jnp.sum(turned * unit, axis=0, keepdims=True)
            scaled = turned * head_gain_ref[which : which + 1]
            back = rho * (scaled - unit * jnp.mean(unit * scaled, axis=-1, keepdims=True))
            grad_ref[here, cols] = back.astype(jnp.bfloat16)
        grad_ref[here, query_cols + HEAD_SIZE :] = dkv_ref[here, HEAD_SIZE:]
        part_ref[here, :] = lax.dot_general(
            grad_ref[here, :], matrix_ref[...], ALONG, preferred_element_type=jnp.float32
        ).astype(jnp.bfloat16)


def project_back(query_grads, kv_grads, raw, head_gains, cosine, sine, matrix):
    rows, cols = raw.shape
    vmem = pl.BlockSpec(memory_space=pltpu.VMEM)
    return pl.pallas_call(
        project_back_kernel,
        in_specs=[vmem] * 7,
        out_specs=[vmem] * 3,
        out_shape=[
            jax.ShapeDtypeStruct((rows, cols), jnp.bfloat16),
            jax.ShapeDtypeStruct((rows, matrix.shape[0]), jnp.bfloat16),
            jax.ShapeDtypeStruct((8, HEAD_SIZE), jnp.float32),
        ],
        cost_estimate=CHEAP,
        name="project_back",
    )(query_grads, kv_grads, raw, head_gains, cosine, sine, matrix)


def dots(lefts, rights, dims):
    if len(lefts) == 1:
        parts, first = [], 0
        for right in rights:
            parts.append(lefts[0][first : first + right.shape[0], :])
            first += right.shape[0]
    else:
        parts = [left[...] for left in lefts]
    return sum(
        lax.dot_general(part, right[...], dims, preferred_element_type=jnp.float32)
        for part, right in zip(parts, rights)
    )


def weight_grads_kernel(at_ref, *refs, groups):
    own_ref, far_ref, sent_ref, held = refs[-4:]
    own = at_ref[8]
    sums = dots(refs[:groups], refs[groups : 2 * groups], DOWN)
    held[...] = sums.astype(jnp.bfloat16).reshape(held.shape)
    own_ref[...] = held[own]
    far_ref[...] = held[own ^ 2]
    sent_ref[0] = held[own ^ 1]
    sent_ref[1] = held[own ^ 3]


def weight_grads(at, lefts, rights, rows):
    count = at.shape[0] - 1
    cols = rights[0].shape[1]
    total = sum(left.shape[0] for left in lefts)
    part = pl.BlockSpec((rows, cols), lambda i, at: (i, 0))
    shape = jax.ShapeDtypeStruct((count * rows, cols), jnp.bfloat16)
    own, far, sent = pl.pallas_call(
        lambda *refs: weight_grads_kernel(*refs, groups=len(lefts)),
        grid_spec=pltpu.PrefetchScalarGridSpec(
            num_scalar_prefetch=1,
            grid=(count,),
            in_specs=[
                pl.BlockSpec((left.shape[0], 4 * rows), lambda i, at: (0, at[i]))
                for left in lefts
            ]
            + [pl.BlockSpec(right.shape, lambda i, at: (0, 0)) for right in rights],
            out_specs=[part, part, pl.BlockSpec((2, rows, cols), lambda i, at: (0, i, 0))],
            scratch_shapes=[pltpu.VMEM((4, rows, cols), jnp.bfloat16)],
        ),
        out_shape=[
            shape, shape, jax.ShapeDtypeStruct((2, count * rows, cols), jnp.bfloat16),
        ],
        cost_estimate=CHEAP,
        name="weight_grads",
    )(at, *lefts, *rights)
    return own, far, sent.reshape(2 * count * rows, cols)


def row_grads_kernel(*refs, groups):
    refs[-1][...] = dots(refs[:groups], refs[groups:-1], DOWN).astype(jnp.bfloat16)


def row_grads(lefts, rights, block=256):
    out_rows, cols = lefts[0].shape[1], rights[0].shape[1]
    total = sum(left.shape[0] for left in lefts)
    return pl.pallas_call(
        lambda *refs: row_grads_kernel(*refs, groups=len(lefts)),
        grid=(out_rows // block,),
        in_specs=[pl.BlockSpec((left.shape[0], block), lambda i: (0, i)) for left in lefts]
        + [pl.BlockSpec(right.shape, lambda i: (0, 0)) for right in rights],
        out_specs=pl.BlockSpec((block, cols), lambda i: (i, 0)),
        out_shape=jax.ShapeDtypeStruct((out_rows, cols), jnp.bfloat16),
        cost_estimate=CHEAP,
        name="row_grads",
    )(*lefts, *rights)


def lane_sums(block):
    return sum(block[:, i : i + 128] for i in range(0, block.shape[1], 128))


def widen(at, swap, *weights):
    rows, taken, count = weights[0].shape[0], [item[1:] for item in swap.taken], len(weights)

    def widen_kernel(at_ref, *refs):
        piece_refs, refs = refs[: len(taken)], refs[len(taken) :]
        grads, sums_ref = refs[count : 2 * count], refs[2 * count]
        sums_ref[...] = jnp.zeros_like(sums_ref)
        for ref, (start, size, spot, top) in zip(piece_refs, taken):
            here = slice(top, top + size)
            first = 0
            for weight, grad in zip(refs[:count], grads):
                width = weight.shape[1] // 8
                there = columns(at_ref[spot], width)
                block = ref[start : start + size, first : first + width].astype(jnp.float32)
                grad[here, there] = block
                sums_ref[here, :] += lane_sums(block * weight[here, there].astype(jnp.float32))
                first += width

    vmem = pl.BlockSpec(memory_space=pltpu.VMEM)
    shapes = [w.shape for w in weights] + [(rows, 128)]
    return pl.pallas_call(
        widen_kernel,
        grid=(1,),
        in_specs=[pl.BlockSpec(memory_space=pltpu.SMEM), *swap.specs()] + [vmem] * count,
        out_specs=[vmem] * len(shapes),
        out_shape=[jax.ShapeDtypeStruct(shape, jnp.float32) for shape in shapes],
        cost_estimate=CHEAP,
        name="widen",
    )(at, *swap.operands(), *weights)


def grouped(strips):
    return [
        jnp.concatenate(strips[a:b], axis=0) if b - a > 1 else strips[a] for a, b in GROUPS
    ]


def split_groups(groups, rows):
    return [
        group[i * rows : (i + 1) * rows]
        for group in groups
        for i in range(group.shape[0] // rows)
    ]


def gather_head(rows):
    return lax.all_gather(rows, "head", axis=0, tiled=True)


def scatter_head(rows):
    return lax.psum_scatter(rows, "head", scatter_dimension=0, tiled=True)


def inverse_rms(rows):
    return lax.rsqrt(jnp.mean(rows * rows, axis=-1, keepdims=True) + EPS)


def per_device(
    tokens,
    attention_norm,
    query_weight,
    key_projection,
    value_projection,
    query_norm,
    key_norm,
    output_weight,
    feedforward_norm,
    gate_weight,
    up_weight,
    down_weight,
    stretch_order,
    out_cotangent,
):
    blk_count = lax.axis_size("blk")
    head_count = lax.axis_size("head")
    head_index = lax.axis_index("head")
    blk_index = lax.axis_index("blk")
    narrow, wide = jnp.bfloat16, jnp.float32
    tokens, out_cotangent = tokens[0], out_cotangent[0]
    local_rows, model_width = tokens.shape
    group_rows = local_rows * blk_count
    weight_rows = query_weight.shape[0]
    ff_local = gate_weight.shape[1] // blk_count
    query_cols = QUERY_HEADS // blk_count * HEAD_SIZE
    attn_cols = query_cols + 2 * HEAD_SIZE
    device_count = blk_count * head_count
    strip_count = blk_count * head_count
    halves = strip_count // stretch_order.shape[1]
    ring_place = jnp.where(blk_index % 2 == 0, blk_index // 2, 7 - blk_index // 2)

    spot = (ring_place + jnp.arange(blk_count, dtype=jnp.int32)) % blk_count
    at = jnp.where(spot < 4, 2 * spot, 15 - 2 * spot).astype(jnp.int32)
    at_own = jnp.concatenate([at, head_index[None].astype(jnp.int32)])
    ring_spot = (ring_place + jnp.asarray(STRIPS, jnp.int32)) % blk_count
    strip_blk = jnp.where(ring_spot < 4, 2 * ring_spot, 15 - 2 * ring_spot)
    strip_head = head_index ^ jnp.asarray((0, 2, 1, 3), jnp.int32)
    strip = (strip_blk[None, :] * head_count + strip_head[:, None]).reshape(strip_count)
    slots = jnp.arange(stretch_order.shape[1], dtype=jnp.int32)
    held = jnp.sum(
        jnp.where((strip // halves)[:, None] == slots[None, :], stretch_order, 0), axis=1
    )
    strip_place = held * halves + strip % halves
    order = strip_place.astype(jnp.int32)
    place = strip_place[:blk_count].astype(jnp.int32)
    positions = (
        place[:, None] * local_rows + jnp.arange(local_rows, dtype=jnp.int32)[None, :]
    ).reshape(group_rows)
    phases = angles(positions, HEAD_SIZE)[:, 0, :]
    cosine, sine = jnp.cos(phases), jnp.sin(phases)
    cosine = jnp.concatenate([cosine, cosine], axis=1)
    sine = jnp.concatenate([-sine, sine], axis=1)

    small = query_norm.shape[0]
    number = blk_index * head_count + head_index
    pad = 16

    def placed(share):
        return jnp.where(
            jnp.arange(device_count, dtype=jnp.int32)[:, None] == number, share[None, :], 0
        ).reshape(-1)

    gains = jnp.concatenate(
        [placed(attention_norm), placed(feedforward_norm), placed(query_norm), placed(key_norm)]
    ).astype(narrow)
    gains = jnp.pad(gains, (0, pad * attn_cols - gains.shape[0])).reshape(pad, attn_cols)
    down_matrix = gather_head(down_weight)
    output_rows = gather_head(output_weight)

    attn_swap = Swap(
        slice_pieces(at, query_weight, key_projection, value_projection, pad=gains),
        weight_rows + pad,
    )
    token_ring = Gather(tokens)
    ff_slices = slice_pieces(at, gate_weight, up_weight)
    token_ring.go()
    attn_swap.go()
    hold((attn_swap,))
    attn_swap.go()
    ff_slices, cosine, sine = hold((attn_swap, token_ring), ff_slices, cosine, sine)
    token_ring.go()
    attn_swap.go()
    hold((attn_swap,))
    attn_swap.go()
    own = hold((token_ring,), attn_swap.result())
    token_ring.go()
    near, far = cross(own, 1), cross(own, 2)
    ff_swap, cotangent_ring = Swap(ff_slices, weight_rows), Gather(out_cotangent)
    own, near, far = hold((token_ring, ff_swap), own, near, far)
    token_ring.go()
    both = cross(far, 1)
    ff_swap.go()
    own, near, far, both = hold((token_ring,), own, near, far, both)

    first_normed, attn_raw, query_rows, own, attn_matrix, gains = project(
        at_own, token_ring.strips(), (own, near, far, both), cosine, sine, query_cols, pad
    )
    gain_one = gains[:4].reshape(1, model_width)
    gain_two = gains[4:8].reshape(1, model_width)
    head_gains = jnp.pad(gains[8, : 2 * HEAD_SIZE].reshape(2, HEAD_SIZE), ((0, 6), (0, 0)))
    own = hold((ff_swap,), own)
    near, far = cross(own, 1), cross(own, 2)
    ff_swap.go()
    own, near, far = hold((ff_swap, cotangent_ring), own, near, far)
    both = cross(far, 1)
    ff_swap.go()
    kv = hold((ff_swap, cotangent_ring), own, far, near, both)
    ff_swap.go()
    cotangent_ring.go()
    attended, lse = attend(place, order, query_rows, kv)

    def by_groups(rows):
        return [rows[a * local_rows : b * local_rows] for a, b in GROUPS]

    def by_strips(groups):
        return dict(zip(STRIPS, split_groups(groups, local_rows)))

    attended, ff_own = hold((cotangent_ring,), attended, ff_swap.result())
    branch_parts = [matmul(rows, output_rows).astype(narrow) for rows in by_groups(attended)]
    branch_ring = Scatter(by_strips(branch_parts))
    branch_ring.go()
    cotangent_ring.go()
    ff_near, ff_far = cross(ff_own, 1), cross(ff_own, 2)
    hold((branch_ring, cotangent_ring))
    branch_ring.go()
    cotangent_ring.go()
    hold((branch_ring, cotangent_ring))
    branch_ring.go()
    cotangent_ring.go()
    ff_near, ff_far = hold((branch_ring, cotangent_ring), ff_near, ff_far)
    branch_ring.go()
    ff_both = cross(ff_far, 1)
    cotangent_groups = grouped(cotangent_ring.strips())
    hidden_grads = [matmul(rows, down_matrix, ALONG) for rows in cotangent_groups]
    hidden_grads, ff_both = hold((branch_ring,), hidden_grads, ff_both)
    tokens_wide = tokens.astype(wide)
    resid = tokens_wide + branch_ring.total()
    rho_two = inverse_rms(resid)
    unit_two = resid * rho_two

    second_ring = Gather((unit_two * gain_two).astype(narrow))
    second_groups, hidden_groups, ff_gradient_groups = [], [], []

    def feed_forward(index):
        rows = second_ring.group(index)
        ff_raw = matmul(rows, ff_matrix)
        gate, up_proj = ff_raw[:, :ff_local], ff_raw[:, ff_local:]
        sigma = jax.nn.sigmoid(gate)
        swish = gate * sigma
        hidden_gradient = hidden_grads[index]
        gate_gradient = hidden_gradient * up_proj * (sigma * (1.0 + gate * (1.0 - sigma)))
        hidden = (swish * up_proj).astype(narrow)
        gradient = jnp.concatenate([gate_gradient, hidden_gradient * swish], 1).astype(narrow)
        if index < 3:
            rows, hidden, gradient = hold((second_ring,), rows, hidden, gradient)
        second_groups.append(rows)
        hidden_groups.append(hidden)
        ff_gradient_groups.append(gradient)

    second_ring.go()
    ff_matrix = assemble(at_own, (ff_own, ff_near, ff_far, ff_both), weight_rows)
    ff_matrix = hold((second_ring,), ff_matrix)
    for index in range(3):
        second_ring.go()
        feed_forward(index)
    feed_forward(3)

    def back(index):
        return matmul(ff_gradient_groups[index], ff_matrix, ALONG).astype(narrow)

    def split(group):
        return [group[i : i + local_rows] for i in range(0, group.shape[0], local_rows)]

    parts = {4: back(3)}
    resid_ring = Scatter(parts)
    parts[3], parts[5] = split(hold((), back(2)))
    parts[2], parts[6] = split(hold((), back(1)))
    resid_ring.go()
    hold((resid_ring,), parts[2], parts[6])
    resid_ring.go()
    back_zero = hold((resid_ring,), back(0))
    parts[0], parts[1], parts[7] = split(back_zero)
    resid_ring.go()
    ff_own, ff_far, ff_sent = hold(
        (resid_ring,), *weight_grads(at_own, second_groups, ff_gradient_groups, weight_rows)
    )
    resid_ring.go()
    ff_own, ff_far = hold((resid_ring,), *scatter_cross(ff_own, ff_far, ff_sent))
    ff_far = cross(ff_far, 2)
    scaled = gain_two * resid_ring.total()
    resid_gradient = out_cotangent.astype(wide) + rho_two * (
        scaled - unit_two * jnp.mean(unit_two * scaled, axis=-1, keepdims=True)
    )

    grad_ring = Gather(resid_gradient.astype(narrow))
    grad_groups, attended_grads = [], []

    def attention_back(index):
        rows = grad_ring.group(index)
        grads = matmul(rows, output_rows, ALONG).astype(narrow)
        if index < 3:
            rows, grads = hold((grad_ring,), rows, grads)
        grad_groups.append(rows)
        attended_grads.append(grads)

    grad_ring.go()
    out_parts = [matmul(rows, down_matrix).astype(narrow) for rows in hidden_groups]
    out_parts = hold((grad_ring,), *out_parts)
    out_ring = Scatter(by_strips(out_parts))
    grad_ring.go()
    down_gradient = row_grads(hidden_groups, cotangent_groups)
    down_gradient = hold((grad_ring,), down_gradient)
    down_gradient = scatter_head(down_gradient)
    grad_ring.go()
    attention_back(0)
    hold((out_ring, grad_ring))
    out_ring.go()
    grad_ring.go()
    attention_back(1)
    attention_back(2)
    ff_swap = Swap(add(ff_own, ff_far), weight_rows)
    hold((grad_ring, ff_swap, out_ring))
    out_ring.go()
    ff_swap.go()
    attention_back(3)
    query_grads, kv_own, kv_far, kv_sent = attend_back(
        place, order, query_rows, attended_grads, attended, lse, kv
    )
    query_grads, kv_own, kv_far, kv_sent = hold(
        (out_ring, ff_swap), query_grads, kv_own, kv_far, kv_sent
    )
    kv_own, kv_far = hold((), *scatter_cross(kv_own, kv_far, kv_sent))
    ff_swap.go()
    out_ring.go()
    kv_grads = add(kv_own, cross(kv_far, 2))
    output_weight_gradient = row_grads([attended], grad_groups)
    kv_grads, output_weight_gradient = hold((ff_swap,), kv_grads, output_weight_gradient)
    output_weight_gradient = scatter_head(output_weight_gradient).astype(wide)
    ff_swap.go()
    attn_gradient, first_parts, gain_sums = project_back(
        query_grads, kv_grads, attn_raw, head_gains, cosine, sine, attn_matrix
    )
    attn_gradient, first_parts, gain_sums = hold(
        (out_ring, ff_swap), attn_gradient, first_parts, gain_sums
    )
    token_ring = Scatter(by_strips(by_groups(first_parts)))
    token_ring.go()
    ff_swap.go()
    gain_sums = gain_sums + cross(gain_sums, 1)
    attn_own, attn_far, attn_sent = weight_grads(
        at_own, [first_normed], [attn_gradient], weight_rows
    )
    attn_own, attn_far, attn_sent, gain_sums = hold(
        (token_ring,), attn_own, attn_far, attn_sent, gain_sums
    )
    token_ring.go()
    attn_own, attn_far = hold((), *scatter_cross(attn_own, attn_far, attn_sent))
    attn_far = cross(attn_far, 2)
    gain_sums = gain_sums + cross(gain_sums, 2)
    gain_sums = hold((token_ring, ff_swap), gain_sums)
    token_ring.go()
    gain_sums = gain_sums + mirror(gain_sums, 1)
    gate_weight_gradient, up_weight_gradient, ff_sums = widen(at, ff_swap, gate_weight, up_weight)
    attn_swap = Swap(add(attn_own, attn_far), weight_rows)
    gate_weight_gradient, up_weight_gradient, ff_sums, gain_sums = hold(
        (token_ring, attn_swap), gate_weight_gradient, up_weight_gradient, ff_sums, gain_sums
    )
    feedforward_norm_gradient = jnp.sum(ff_sums, axis=1) / feedforward_norm.astype(wide)
    attn_swap.go()
    token_ring.go()
    gain_sums = gain_sums + mirror(gain_sums, 2)
    gain_sums = hold((token_ring, attn_swap, out_ring), gain_sums)
    attn_swap.go()
    out_ring.go()
    gain_sums = gain_sums + mirror(gain_sums, 4)
    gain_sums = hold((attn_swap,), gain_sums)
    attn_swap.go()
    hold((attn_swap,))
    attn_swap.go()
    layer_out = (resid + out_ring.total()).astype(narrow)
    query_weight_gradient, key_weight_gradient, value_weight_gradient, norm_sums = widen(
        at, attn_swap, query_weight, key_projection, value_projection
    )
    attention_norm_gradient = jnp.sum(norm_sums, axis=1) / attention_norm.astype(wide)
    gain_sums = lax.dynamic_slice_in_dim(gain_sums, number * small, small, 1)
    rho_one = inverse_rms(tokens_wide)
    unit_one = tokens_wide * rho_one
    scaled = gain_one * token_ring.total()
    tokens_gradient = resid_gradient + rho_one * (
        scaled - unit_one * jnp.mean(unit_one * scaled, axis=-1, keepdims=True)
    )
    return (
        layer_out[None],
        tokens_gradient.astype(narrow)[None],
        attention_norm_gradient,
        query_weight_gradient,
        key_weight_gradient,
        value_weight_gradient,
        gain_sums[0],
        gain_sums[1],
        output_weight_gradient,
        feedforward_norm_gradient,
        gate_weight_gradient,
        up_weight_gradient,
        down_gradient.astype(wide),
    )


def solution(mesh):
    placed = (
        P(None, ("blk", "head"), None),
        P(("blk", "head")),
        P(("blk", "head"), None),
        P(("blk", "head"), None),
        P(("blk", "head"), None),
        P(("blk", "head")),
        P(("blk", "head")),
        P(("blk", "head"), None),
        P(("blk", "head")),
        P(("blk", "head"), None),
        P(("blk", "head"), None),
        P(("blk", "head"), None),
        P(),
        P(None, ("blk", "head"), None),
    )
    fits = mesh.shape["blk"] == KEY_VALUE_HEADS and mesh.shape["head"] == 4
    return jax.shard_map(
        per_device if fits else per_device_by_tokens,
        mesh=mesh,
        in_specs=placed,
        out_specs=(
            P(None, ("blk", "head"), None),
            P(None, ("blk", "head"), None),
            P(("blk", "head")),
            P(("blk", "head"), None),
            P(("blk", "head"), None),
            P(("blk", "head"), None),
            P(("blk", "head")),
            P(("blk", "head")),
            P(("blk", "head"), None),
            P(("blk", "head")),
            P(("blk", "head"), None),
            P(("blk", "head"), None),
            P(("blk", "head"), None),
        ),
        check_vma=False,
    )
```

```python
import math

import jax
import jax.numpy as jnp
from jax import lax
from jax.experimental import pallas as pl
from jax.experimental.pallas import tpu as pltpu
from jax.sharding import PartitionSpec as P

QUERY_HEADS = 16
KEY_VALUE_HEADS = 8
HEAD_SIZE = 128


EPS = 1e-06
NEG = -1e30
ROPE_BASE = 1000000.0


def passed_along(value, axis, by):
    count = lax.axis_size(axis)
    return lax.ppermute(value, axis, [(i, (i + by) % count) for i in range(count)])


def norm_rows(inputs, norm_gain):
    return inputs * lax.rsqrt(jnp.mean(inputs * inputs, axis=-1, keepdims=True) + EPS) * norm_gain


def rotary(inputs, phases):
    half_width = inputs.shape[-1] // 2
    cosine = jnp.cos(phases)
    sine_term = jnp.sin(phases)
    first_half = inputs[..., :half_width]
    second_half = inputs[..., half_width:]
    return jnp.concatenate(
        [
            first_half * cosine - second_half * sine_term,
            second_half * cosine + first_half * sine_term,
        ],
        axis=-1,
    )


def angles(positions, head_width):
    half_width = head_width // 2
    frequency = jnp.exp(
        jnp.arange(half_width, dtype=jnp.float32) * (-2.0 * math.log(ROPE_BASE) / head_width)
    )
    return positions.astype(jnp.float32)[..., None, None] * frequency


def token_positions(stretch_order, first_row, row_count, stretch_rows):
    row_index = first_row + jnp.arange(row_count, dtype=jnp.int32)
    slot_index = row_index // stretch_rows
    matches = slot_index[:, None] == jnp.arange(stretch_order.shape[1], dtype=jnp.int32)[None, :]
    picked = jnp.sum(jnp.where(matches[None], stretch_order[:, None, :], 0), axis=-1)
    return picked * stretch_rows + row_index % stretch_rows


def per_device_by_tokens(
    tokens,
    attention_norm,
    query_weight,
    key_projection,
    value_projection,
    query_norm,
    key_norm,
    output_weight,
    feedforward_norm,
    gate_weight,
    up_weight,
    down_weight,
    stretch_order,
    out_cotangent,
):
    count_of_heads = lax.axis_size("head")
    span_count = lax.axis_size("blk")
    span_index = lax.axis_index("blk")
    head_index = lax.axis_index("head")
    sequence_total = tokens.shape[0]
    local_rows = tokens.shape[1]
    group_rows = local_rows * count_of_heads
    stretch_rows = group_rows // 2
    heads_shared = KEY_VALUE_HEADS // count_of_heads
    heads_per_group = QUERY_HEADS // KEY_VALUE_HEADS
    score_scale = 1.0 / math.sqrt(HEAD_SIZE)
    gain_one, query_matrix, key_matrix, value_matrix, query_gain, key_gain, output_matrix = (
        lax.all_gather(attention_norm, ("blk", "head"), axis=0, tiled=True),
        lax.all_gather(query_weight, ("blk", "head"), axis=0, tiled=True),
        lax.all_gather(key_projection, ("blk", "head"), axis=0, tiled=True),
        lax.all_gather(value_projection, ("blk", "head"), axis=0, tiled=True),
        lax.all_gather(query_norm, ("blk", "head"), axis=0, tiled=True),
        lax.all_gather(key_norm, ("blk", "head"), axis=0, tiled=True),
        lax.all_gather(output_weight, ("blk", "head"), axis=0, tiled=True),
    )
    gain_two, gate_matrix, up_matrix, down_matrix = (
        lax.all_gather(feedforward_norm, ("blk", "head"), axis=0, tiled=True),
        lax.all_gather(gate_weight, ("blk", "head"), axis=0, tiled=True),
        lax.all_gather(up_weight, ("blk", "head"), axis=0, tiled=True),
        lax.all_gather(down_weight, ("blk", "head"), axis=0, tiled=True),
    )
    gain_one = gain_one.astype(jnp.float32)
    gain_two = gain_two.astype(jnp.float32)
    query_gain = query_gain.astype(jnp.float32)
    key_gain = key_gain.astype(jnp.float32)
    own_first = (span_index * count_of_heads + head_index) * local_rows
    own_pos = token_positions(stretch_order, own_first, local_rows, stretch_rows)
    group_pos = token_positions(stretch_order, span_index * group_rows, group_rows, stretch_rows)
    phases = angles(own_pos, HEAD_SIZE)
    tokens_wide = tokens.astype(jnp.float32)
    first_normed, norm_one_back = jax.vjp(norm_rows, tokens_wide, gain_one)
    first_normed = first_normed.astype(jnp.bfloat16)
    query_raw = jnp.einsum(
        "btd,de->bte", first_normed, query_matrix, preferred_element_type=jnp.float32
    ).reshape(sequence_total, local_rows, QUERY_HEADS, HEAD_SIZE)
    key_unnormed = jnp.einsum(
        "btd,de->bte", first_normed, key_matrix, preferred_element_type=jnp.float32
    ).reshape(sequence_total, local_rows, KEY_VALUE_HEADS, HEAD_SIZE)
    value_tokens = (
        jnp.einsum("btd,de->bte", first_normed, value_matrix, preferred_element_type=jnp.float32)
        .astype(jnp.bfloat16)
        .reshape(sequence_total, local_rows, KEY_VALUE_HEADS, HEAD_SIZE)
    )

    def heads_local(query_in, key_in, query_scale, key_scale):
        return (
            rotary(norm_rows(query_in, query_scale), phases),
            rotary(norm_rows(key_in, key_scale), phases),
        )

    (query_tokens, key_tokens), heads_back = jax.vjp(
        heads_local, query_raw, key_unnormed, query_gain, key_gain
    )
    query_tokens = query_tokens.astype(jnp.bfloat16)
    key_tokens = key_tokens.astype(jnp.bfloat16)
    query_group, key_group, value_group = (
        lax.all_to_all(query_tokens, "head", split_axis=2, concat_axis=1, tiled=True),
        lax.all_to_all(key_tokens, "head", split_axis=2, concat_axis=1, tiled=True),
        lax.all_to_all(value_tokens, "head", split_axis=2, concat_axis=1, tiled=True),
    )
    query_five = query_group.reshape(
        sequence_total, group_rows, heads_shared, heads_per_group, HEAD_SIZE
    )

    def block_update(carry, key_block, value_block, key_pos):
        run_max, run_sum, run_total = carry
        scores = (
            jnp.einsum(
                "bqkgd,bckd->bkgqc", query_five, key_block, preferred_element_type=jnp.float32
            )
            * score_scale
        )
        allowed = key_pos[:, None, None, None, :] <= group_pos[:, None, None, :, None]
        scores = jnp.where(allowed, scores, NEG)
        new_max = jnp.maximum(run_max, jnp.max(scores, axis=-1))
        exponent = jnp.where(allowed, jnp.exp(scores - new_max[..., None]), 0.0)
        factor = jnp.exp(run_max - new_max)
        new_sum = run_sum * factor + jnp.sum(exponent, axis=-1)
        new_total = run_total * factor[..., None] + jnp.einsum(
            "bkgqc,bckd->bkgqd",
            exponent.astype(jnp.bfloat16),
            value_block,
            preferred_element_type=jnp.float32,
        )
        return (new_max, new_sum, new_total)

    def fold_update(carry, key_block, value_block, key_pos):
        result = block_update(carry, key_block, value_block, key_pos)
        return result

    stat_shape = (sequence_total, heads_shared, heads_per_group, group_rows)
    start_state = (
        jnp.full(stat_shape, NEG, jnp.float32),
        jnp.zeros(stat_shape, jnp.float32),
        jnp.zeros(stat_shape + (HEAD_SIZE,), jnp.float32),
    )
    key_piece = lax.all_gather(key_group, "blk", axis=1, tiled=True)
    value_piece = lax.all_gather(value_group, "blk", axis=1, tiled=True)
    piece_rows = key_piece.shape[1]
    block_len = math.gcd(group_rows, piece_rows)

    def inner(block_number, carry_in):
        offset = block_number * block_len
        key_block = lax.dynamic_slice_in_dim(key_piece, offset, block_len, 1)
        value_block = lax.dynamic_slice_in_dim(value_piece, offset, block_len, 1)
        key_pos = token_positions(stretch_order, offset, block_len, stretch_rows)
        return fold_update(carry_in, key_block, value_block, key_pos)

    run_max, run_sum, run_total = lax.fori_loop(0, piece_rows // block_len, inner, start_state)
    log_total = run_max + jnp.log(run_sum)
    attended_five = run_total / run_sum[..., None]
    attended_group = (
        jnp.transpose(attended_five, (0, 3, 1, 2, 4))
        .reshape(sequence_total, group_rows, heads_shared * heads_per_group, HEAD_SIZE)
        .astype(jnp.bfloat16)
    )
    attended_tokens = lax.all_to_all(
        attended_group, "head", split_axis=1, concat_axis=2, tiled=True
    ).reshape(sequence_total, local_rows, QUERY_HEADS * HEAD_SIZE)
    branch = jnp.einsum(
        "bte,ed->btd", attended_tokens, output_matrix, preferred_element_type=jnp.float32
    )
    resid = tokens_wide + branch
    normed_two, norm_two_back = jax.vjp(norm_rows, resid, gain_two)
    normed_two = normed_two.astype(jnp.bfloat16)
    gate = jnp.einsum("btd,df->btf", normed_two, gate_matrix, preferred_element_type=jnp.float32)
    up_proj = jnp.einsum("btd,df->btf", normed_two, up_matrix, preferred_element_type=jnp.float32)

    def swish_product(gate_in, up_in):
        return jax.nn.silu(gate_in) * up_in

    hidden, swish_back = jax.vjp(swish_product, gate, up_proj)
    hidden = hidden.astype(jnp.bfloat16)
    layer_out = (
        resid + jnp.einsum("btf,fd->btd", hidden, down_matrix, preferred_element_type=jnp.float32)
    ).astype(jnp.bfloat16)
    gain_again, gate_matrix, up_matrix, down_matrix = (
        lax.all_gather(feedforward_norm, ("blk", "head"), axis=0, tiled=True),
        lax.all_gather(gate_weight, ("blk", "head"), axis=0, tiled=True),
        lax.all_gather(up_weight, ("blk", "head"), axis=0, tiled=True),
        lax.all_gather(down_weight, ("blk", "head"), axis=0, tiled=True),
    )
    down_gradient = jnp.einsum(
        "btf,btd->fd", hidden, out_cotangent, preferred_element_type=jnp.float32
    )
    hidden_gradient = jnp.einsum(
        "btd,fd->btf", out_cotangent, down_matrix, preferred_element_type=jnp.float32
    )
    gate_gradient, up_gradient = swish_back(hidden_gradient)
    gate_gradient = gate_gradient.astype(jnp.bfloat16)
    up_gradient = up_gradient.astype(jnp.bfloat16)
    gate_matrix_gradient = jnp.einsum(
        "btd,btf->df", normed_two, gate_gradient, preferred_element_type=jnp.float32
    )
    up_matrix_gradient = jnp.einsum(
        "btd,btf->df", normed_two, up_gradient, preferred_element_type=jnp.float32
    )
    normed_two_gradient = jnp.einsum(
        "btf,df->btd", gate_gradient, gate_matrix, preferred_element_type=jnp.float32
    ) + jnp.einsum("btf,df->btd", up_gradient, up_matrix, preferred_element_type=jnp.float32)
    resid_part, gain_two_gradient = norm_two_back(normed_two_gradient)
    resid_gradient = out_cotangent.astype(jnp.float32) + resid_part
    feedforward_sums = (
        lax.psum_scatter(gain_two_gradient, ("blk", "head"), scatter_dimension=0, tiled=True),
        lax.psum_scatter(gate_matrix_gradient, ("blk", "head"), scatter_dimension=0, tiled=True),
        lax.psum_scatter(up_matrix_gradient, ("blk", "head"), scatter_dimension=0, tiled=True),
        lax.psum_scatter(down_gradient, ("blk", "head"), scatter_dimension=0, tiled=True),
    )
    gain_again, query_matrix, key_matrix, value_matrix, query_again, key_again, output_matrix = (
        lax.all_gather(attention_norm, ("blk", "head"), axis=0, tiled=True),
        lax.all_gather(query_weight, ("blk", "head"), axis=0, tiled=True),
        lax.all_gather(key_projection, ("blk", "head"), axis=0, tiled=True),
        lax.all_gather(value_projection, ("blk", "head"), axis=0, tiled=True),
        lax.all_gather(query_norm, ("blk", "head"), axis=0, tiled=True),
        lax.all_gather(key_norm, ("blk", "head"), axis=0, tiled=True),
        lax.all_gather(output_weight, ("blk", "head"), axis=0, tiled=True),
    )
    branch_gradient = resid_gradient.astype(jnp.bfloat16)
    output_matrix_gradient = jnp.einsum(
        "bte,btd->ed", attended_tokens, branch_gradient, preferred_element_type=jnp.float32
    )
    attended_gradient = (
        jnp.einsum(
            "btd,ed->bte", branch_gradient, output_matrix, preferred_element_type=jnp.float32
        )
        .astype(jnp.bfloat16)
        .reshape(sequence_total, local_rows, QUERY_HEADS, HEAD_SIZE)
    )
    attended_grad_group = lax.all_to_all(
        attended_gradient, "head", split_axis=2, concat_axis=1, tiled=True
    ).reshape(sequence_total, group_rows, heads_shared, heads_per_group, HEAD_SIZE)
    delta = jnp.sum(
        jnp.transpose(attended_grad_group.astype(jnp.float32), (0, 2, 3, 1, 4)) * attended_five,
        axis=-1,
    )

    def block_grads(sums_in, key_current, value_current, key_pos):
        key_sum, value_sum, query_sum = sums_in
        scores = (
            jnp.einsum(
                "bqkgd,bckd->bkgqc", query_five, key_current, preferred_element_type=jnp.float32
            )
            * score_scale
        )
        allowed = key_pos[:, None, None, None, :] <= group_pos[:, None, None, :, None]
        weights = jnp.where(allowed, jnp.exp(scores - log_total[..., None]), 0.0)
        probs = weights.astype(jnp.bfloat16)
        value_sum = value_sum + jnp.einsum(
            "bkgqc,bqkgd->bckd", probs, attended_grad_group, preferred_element_type=jnp.float32
        )
        probs_gradient = jnp.einsum(
            "bqkgd,bckd->bkgqc",
            attended_grad_group,
            value_current,
            preferred_element_type=jnp.float32,
        )
        scores_gradient = (weights * (probs_gradient - delta[..., None])).astype(jnp.bfloat16)
        query_sum = (
            query_sum
            + jnp.einsum(
                "bkgqc,bckd->bqkgd",
                scores_gradient,
                key_current,
                preferred_element_type=jnp.float32,
            )
            * score_scale
        )
        key_sum = (
            key_sum
            + jnp.einsum(
                "bkgqc,bqkgd->bckd", scores_gradient, query_five, preferred_element_type=jnp.float32
            )
            * score_scale
        )
        return (key_sum, value_sum, query_sum)

    def pass_step(step_index, carry):
        key_current, value_current, key_sum, value_sum, query_sum = carry
        anchor = (span_index - step_index) % span_count
        key_pos = token_positions(stretch_order, anchor * group_rows, group_rows, stretch_rows)
        key_sum, value_sum, query_sum = block_grads(
            (key_sum, value_sum, query_sum), key_current, value_current, key_pos
        )
        key_current, value_current = passed_along((key_current, value_current), "blk", 1)
        key_sum, value_sum = (
            passed_along(key_sum.astype(jnp.bfloat16), "blk", 1).astype(key_sum.dtype),
            passed_along(value_sum.astype(jnp.bfloat16), "blk", 1).astype(value_sum.dtype),
        )
        return (key_current, value_current, key_sum, value_sum, query_sum)

    kv_zeros = jnp.zeros((sequence_total, group_rows, heads_shared, HEAD_SIZE), jnp.float32)
    query_zeros = jnp.zeros(
        (sequence_total, group_rows, heads_shared, heads_per_group, HEAD_SIZE), jnp.float32
    )
    final_state = lax.fori_loop(
        0, span_count, pass_step, (key_group, value_group, kv_zeros, kv_zeros, query_zeros)
    )
    key_grad_group = final_state[2].astype(jnp.bfloat16)
    value_grad_group = final_state[3].astype(jnp.bfloat16)
    query_grad_group = (
        final_state[4]
        .astype(jnp.bfloat16)
        .reshape(sequence_total, group_rows, heads_shared * heads_per_group, HEAD_SIZE)
    )
    query_grad_tokens, key_grad_tokens, value_gradient_tokens = (
        lax.all_to_all(query_grad_group, "head", split_axis=1, concat_axis=2, tiled=True),
        lax.all_to_all(key_grad_group, "head", split_axis=1, concat_axis=2, tiled=True),
        lax.all_to_all(value_grad_group, "head", split_axis=1, concat_axis=2, tiled=True),
    )
    query_raw_gradient, key_unnormed_gradient, query_gain_gradient, key_gain_gradient = heads_back(
        (query_grad_tokens.astype(jnp.float32), key_grad_tokens.astype(jnp.float32))
    )
    query_raw_gradient = query_raw_gradient.astype(jnp.bfloat16).reshape(
        sequence_total, local_rows, QUERY_HEADS * HEAD_SIZE
    )
    key_unnormed_gradient = key_unnormed_gradient.astype(jnp.bfloat16).reshape(
        sequence_total, local_rows, KEY_VALUE_HEADS * HEAD_SIZE
    )
    value_unnormed_gradient = value_gradient_tokens.reshape(
        sequence_total, local_rows, KEY_VALUE_HEADS * HEAD_SIZE
    )
    query_matrix_gradient = jnp.einsum(
        "btd,bte->de", first_normed, query_raw_gradient, preferred_element_type=jnp.float32
    )
    key_matrix_gradient = jnp.einsum(
        "btd,bte->de", first_normed, key_unnormed_gradient, preferred_element_type=jnp.float32
    )
    value_matrix_gradient = jnp.einsum(
        "btd,bte->de", first_normed, value_unnormed_gradient, preferred_element_type=jnp.float32
    )
    normed_one_gradient = jnp.einsum(
        "bte,de->btd", query_raw_gradient, query_matrix, preferred_element_type=jnp.float32
    )
    normed_one_gradient = normed_one_gradient + jnp.einsum(
        "bte,de->btd", key_unnormed_gradient, key_matrix, preferred_element_type=jnp.float32
    )
    normed_one_gradient = normed_one_gradient + jnp.einsum(
        "bte,de->btd", value_unnormed_gradient, value_matrix, preferred_element_type=jnp.float32
    )
    token_part, gain_one_gradient = norm_one_back(normed_one_gradient)
    tokens_gradient = (resid_gradient + token_part).astype(jnp.bfloat16)
    attention_sums = (
        lax.psum_scatter(gain_one_gradient, ("blk", "head"), scatter_dimension=0, tiled=True),
        lax.psum_scatter(query_matrix_gradient, ("blk", "head"), scatter_dimension=0, tiled=True),
        lax.psum_scatter(key_matrix_gradient, ("blk", "head"), scatter_dimension=0, tiled=True),
        lax.psum_scatter(value_matrix_gradient, ("blk", "head"), scatter_dimension=0, tiled=True),
        lax.psum_scatter(query_gain_gradient, ("blk", "head"), scatter_dimension=0, tiled=True),
        lax.psum_scatter(key_gain_gradient, ("blk", "head"), scatter_dimension=0, tiled=True),
        lax.psum_scatter(output_matrix_gradient, ("blk", "head"), scatter_dimension=0, tiled=True),
    )
    return (
        layer_out,
        tokens_gradient,
        attention_sums[0],
        attention_sums[1],
        attention_sums[2],
        attention_sums[3],
        attention_sums[4],
        attention_sums[5],
        attention_sums[6],
        feedforward_sums[0],
        feedforward_sums[1],
        feedforward_sums[2],
        feedforward_sums[3],
    )


LOG2E = math.log2(math.e)
STRIP = 128
CHUNK = 512
ALONG = (((1,), (1,)), ((), ()))
DOWN = (((0,), (0,)), ((), ()))


def two_heads(block):
    return jnp.concatenate([block[:, :HEAD_SIZE], block[:, HEAD_SIZE:]], axis=0)


def side_by_side(rows):
    half = rows.shape[0] // 2
    return jnp.concatenate([rows[:half], rows[half:]], axis=1)


CHEAP = pl.CostEstimate(flops=1, bytes_accessed=1, transcendentals=0)
LONG = pl.CostEstimate(flops=3 * 10**10, bytes_accessed=1 << 25, transcendentals=0)


def sort_strips(order_ref, kv_refs, keys, values):
    per = kv_refs[0].shape[0] // STRIP
    for j, ref in enumerate(kv_refs):

        def sort(i, carry, j=j, ref=ref):
            target = pl.multiple_of(order_ref[j * per + i] * STRIP, STRIP)
            here = pl.ds(pl.multiple_of(i * STRIP, STRIP), STRIP)
            keys[pl.ds(target, STRIP), :] = ref[here, :HEAD_SIZE]
            values[pl.ds(target, STRIP), :HEAD_SIZE] = ref[here, HEAD_SIZE:]
            return carry

        lax.fori_loop(0, per, sort, 0)


def attend_kernel(place_ref, order_ref, q_ref, *refs):
    kv_refs, (out_ref, lse_ref, keys, values) = refs[:4], refs[4:]
    step = pl.program_id(0)

    @pl.when(step == 0)
    def _():
        values[:, HEAD_SIZE:] = jnp.ones((values.shape[0], HEAD_SIZE), jnp.bfloat16)
        sort_strips(order_ref, kv_refs, keys, values)

    place = place_ref[step]
    queries = two_heads(q_ref[...])
    last = place // (CHUNK // STRIP)

    def part(index, total, masked):
        first = pl.multiple_of(index * CHUNK, CHUNK)
        scores = lax.dot_general(
            queries, keys[pl.ds(first, CHUNK), :], ALONG, preferred_element_type=jnp.float32
        )
        weights = jnp.exp2(scores)
        if masked:
            row = lax.broadcasted_iota(jnp.int32, scores.shape, 0) % STRIP
            column = lax.broadcasted_iota(jnp.int32, scores.shape, 1)
            weights = jnp.where(column - row <= place * STRIP - first, weights, 0.0)
        return total + jnp.dot(
            weights.astype(jnp.bfloat16),
            values[pl.ds(first, CHUNK), :],
            preferred_element_type=jnp.float32,
        )

    total = jnp.zeros((2 * STRIP, 2 * HEAD_SIZE), jnp.float32)
    total = lax.fori_loop(0, last, lambda index, t: part(index, t, False), total)
    total = part(last, total, True)
    norm = total[:, HEAD_SIZE:]
    out_ref[...] = side_by_side(total[:, :HEAD_SIZE] / norm).astype(jnp.bfloat16)
    lse_ref[0] = jnp.transpose(jnp.log2(norm))[:8]


def attend(place, order, queries, kv):
    rows, width = queries.shape
    steps = rows // STRIP
    total = sum(part.shape[0] for part in kv)
    strip = pl.BlockSpec((STRIP, width), lambda i, *_: (i, 0))
    return pl.pallas_call(
        attend_kernel,
        grid_spec=pltpu.PrefetchScalarGridSpec(
            num_scalar_prefetch=2,
            grid=(steps,),
            in_specs=[strip] + [pl.BlockSpec(part.shape, lambda i, *_: (0, 0)) for part in kv],
            out_specs=[strip, pl.BlockSpec((1, 8, 2 * STRIP), lambda i, *_: (i, 0, 0))],
            scratch_shapes=[
                pltpu.VMEM((total, HEAD_SIZE), jnp.bfloat16),
                pltpu.VMEM((total, 2 * HEAD_SIZE), jnp.bfloat16),
            ],
        ),
        out_shape=[
            jax.ShapeDtypeStruct((rows, width), jnp.bfloat16),
            jax.ShapeDtypeStruct((steps, 8, 2 * STRIP), jnp.float32),
        ],
        cost_estimate=LONG,
        name="attend",
    )(place, order, queries, *kv)


def attend_back_kernel(place_ref, order_ref, q_ref, out_ref, lse_ref, *refs, groups):
    grad_refs, kv_refs = refs[:groups], refs[groups : groups + 4]
    dq_ref, own_ref, far_ref, sent_ref = refs[groups + 4 : groups + 8]
    keys, values, key_sums, value_sums, grads_all = refs[groups + 8 :]
    step = pl.program_id(0)

    @pl.when(step == 0)
    def _():
        key_sums[...] = jnp.zeros_like(key_sums)
        value_sums[...] = jnp.zeros_like(value_sums)
        sort_strips(order_ref, kv_refs, keys, values)
        first = 0
        for ref in grad_refs:
            grads_all[first : first + ref.shape[0], :] = ref[...]
            first += ref.shape[0]

    place = place_ref[step]
    queries = two_heads(q_ref[...])
    grads = two_heads(grads_all[pl.ds(pl.multiple_of(step * STRIP, STRIP), STRIP), :])
    product = grads.astype(jnp.float32) * two_heads(out_ref[...]).astype(jnp.float32)
    delta = jnp.sum(jnp.transpose(product), axis=0, keepdims=True)
    lse = lse_ref[0, :1]
    last = place // (CHUNK // STRIP)

    def part(index, total, masked):
        first = pl.multiple_of(index * CHUNK, CHUNK)
        here = pl.ds(first, CHUNK)
        key_rows = keys[here, :]
        scores = lax.dot_general(key_rows, queries, ALONG, preferred_element_type=jnp.float32)
        weights = jnp.exp2(scores - lse)
        if masked:
            row = lax.broadcasted_iota(jnp.int32, scores.shape, 0)
            column = lax.broadcasted_iota(jnp.int32, scores.shape, 1) % STRIP
            weights = jnp.where(row - column <= place * STRIP - first, weights, 0.0)
        slopes = lax.dot_general(
            values[here, :], grads, ALONG, preferred_element_type=jnp.float32
        )
        score_grads = (weights * (slopes - delta)).astype(jnp.bfloat16)
        value_sums[here, :] += jnp.dot(
            weights.astype(jnp.bfloat16), grads, preferred_element_type=jnp.float32
        )
        key_sums[here, :] += jnp.dot(score_grads, queries, preferred_element_type=jnp.float32)
        return total + lax.dot_general(
            score_grads, key_rows, DOWN, preferred_element_type=jnp.float32
        )

    total = jnp.zeros((2 * STRIP, HEAD_SIZE), jnp.float32)
    total = lax.fori_loop(0, last, lambda index, t: part(index, t, False), total)
    total = part(last, total, True)
    dq_ref[...] = side_by_side(total * (1.0 / math.sqrt(HEAD_SIZE))).astype(jnp.bfloat16)

    @pl.when(step == pl.num_programs(0) - 1)
    def _():
        per = own_ref.shape[0] // STRIP
        for j in range(4):
            target = (own_ref, far_ref, sent_ref, sent_ref)[j]
            base = per if j == 3 else 0

            def spread(i, carry, j=j, target=target, base=base):
                source = pl.multiple_of(order_ref[j * per + i] * STRIP, STRIP)
                here = pl.ds(pl.multiple_of((base + i) * STRIP, STRIP), STRIP)
                target[here, :HEAD_SIZE] = (
                    key_sums[pl.ds(source, STRIP), :] * (1.0 / LOG2E)
                ).astype(jnp.bfloat16)
                target[here, HEAD_SIZE:] = value_sums[pl.ds(source, STRIP), :].astype(
                    jnp.bfloat16
                )
                return carry

            lax.fori_loop(0, per, spread, 0)


def attend_back(place, order, queries, grads, attended, lse, kv):
    rows, width = queries.shape
    steps = rows // STRIP
    total = sum(part.shape[0] for part in kv)
    strip = pl.BlockSpec((STRIP, width), lambda i, *_: (i, 0))

    def whole(shape):
        return pl.BlockSpec(shape, lambda i, *_: (0, 0))

    outs = [kv[0].shape, kv[0].shape, (2 * kv[0].shape[0], kv[0].shape[1])]
    return pl.pallas_call(
        lambda *refs: attend_back_kernel(*refs, groups=len(grads)),
        grid_spec=pltpu.PrefetchScalarGridSpec(
            num_scalar_prefetch=2,
            grid=(steps,),
            in_specs=[strip, strip, pl.BlockSpec((1, 8, 2 * STRIP), lambda i, *_: (i, 0, 0))]
            + [whole(part.shape) for part in (*grads, *kv)],
            out_specs=[strip] + [whole(shape) for shape in outs],
            scratch_shapes=[
                pltpu.VMEM((total, HEAD_SIZE), jnp.bfloat16),
                pltpu.VMEM((total, HEAD_SIZE), jnp.bfloat16),
                pltpu.VMEM((total, HEAD_SIZE), jnp.float32),
                pltpu.VMEM((total, HEAD_SIZE), jnp.float32),
                pltpu.VMEM((rows, width), jnp.bfloat16),
            ],
        ),
        out_shape=[jax.ShapeDtypeStruct((rows, width), jnp.bfloat16)]
        + [jax.ShapeDtypeStruct(shape, jnp.bfloat16) for shape in outs],
        cost_estimate=LONG,
        name="attend_back",
    )(place, order, queries, attended, lse, *grads, *kv)


def matmul(left, right, dims=(((1,), (0,)), ((), ()))):
    return lax.dot_general(left, right, dims, preferred_element_type=jnp.float32)


RING = (0, 2, 4, 6, 7, 5, 3, 1)
STRIPS = (0, 1, 7, 2, 6, 3, 5, 4)
GROUPS = ((0, 3), (3, 5), (5, 7), (7, 8))


def hop(value, by):
    count = len(RING)
    return lax.ppermute(value, "blk", [(RING[i], RING[(i + by) % count]) for i in range(count)])


def cross(value, by):
    return lax.ppermute(value, "head", [(i, i ^ by) for i in range(4)])


def mirror(value, by):
    return lax.ppermute(value, "blk", [(i, i ^ by) for i in range(len(RING))])


def add(left, right):
    return (left.astype(jnp.float32) + right.astype(jnp.float32)).astype(left.dtype)


class Gather:
    def __init__(self, own):
        self.got, self.step = {0: own}, 0
        self.state = (own, own)

    def go(self):
        self.step += 1
        left, right = self.state
        if self.step < 4:
            self.state = hop(left, -1), hop(right, 1)
            self.got[self.step], self.got[8 - self.step] = self.state
        else:
            half = left.shape[0] // 2
            self.got[4] = jnp.concatenate([hop(left[:half], -1), hop(right[half:], 1)], axis=0)
            self.state = (self.got[4],)

    def strips(self):
        return [self.got[s] for s in STRIPS]

    def group(self, index):
        first, last = GROUPS[index]
        return jnp.concatenate([self.got[s] for s in STRIPS[first:last]], axis=0)


class Scatter:
    def __init__(self, part):
        self.part, self.step = part, 0
        self.half = part[4].shape[0] // 2
        self.state = (part[4][: self.half], part[4][self.half :])

    def go(self):
        self.step += 1
        half, part = self.half, self.part
        up, down = hop(self.state[0], 1), hop(self.state[1], -1)
        if self.step == 1:
            up = jnp.concatenate([add(part[3][:half], up), part[3][half:]], axis=0)
            down = jnp.concatenate([part[5][:half], add(part[5][half:], down)], axis=0)
        elif self.step < 4:
            up, down = add(part[4 - self.step], up), add(part[4 + self.step], down)
        self.state = up, down

    def total(self):
        up, down = self.state
        wide = jnp.float32
        return self.part[0].astype(wide) + up.astype(wide) + down.astype(wide)


class Swap:
    def __init__(self, pieces, rows):
        cut = 4 * rows + rows // 2
        self.rows, self.step = rows, 0
        self.taken = [(pieces, 0, rows, 0, 0)]
        self.state = (pieces[rows:cut], pieces[cut:])

    def go(self):
        self.step += 1
        rows, step = self.rows, self.step
        right, left = hop(self.state[0], 1), hop(self.state[1], -1)
        if step < 4:
            self.taken.append((right, 0, rows, 8 - step, 0))
            self.taken.append((left, left.shape[0] - rows, rows, step, 0))
            self.state = right[rows:], left[:-rows]
        else:
            self.taken.append((right, 0, rows // 2, 4, 0))
            self.taken.append((left, 0, rows // 2, 4, rows // 2))
            self.state = right, left

    def operands(self):
        return [item[0] for item in self.taken]

    def specs(self):
        vmem = pl.BlockSpec(memory_space=pltpu.VMEM)
        own = pl.BlockSpec((self.rows, self.taken[0][0].shape[1]), lambda i: (0, 0))
        return [own] + [vmem] * (len(self.taken) - 1)

    def result(self):
        rows, taken = self.rows, [item[1:] for item in self.taken]

        def stack_kernel(*refs):
            for ref, (first, count, spot, top) in zip(refs[:-1], taken):
                at = spot * rows + top
                refs[-1][at : at + count, :] = ref[first : first + count, :]

        return pl.pallas_call(
            stack_kernel,
            grid=(1,),
            in_specs=self.specs(),
            out_specs=pl.BlockSpec(memory_space=pltpu.VMEM),
            out_shape=jax.ShapeDtypeStruct((8 * rows, self.taken[0][0].shape[1]), jnp.bfloat16),
            cost_estimate=CHEAP,
            name="stack",
        )(*self.operands())


def hold(rings, *extra):
    states, extra = lax.optimization_barrier(([ring.state for ring in rings], extra))
    for ring, state in zip(rings, states):
        ring.state = state
    return extra[0] if len(extra) == 1 else extra


def scatter_cross(own, far, sent):
    moved = cross(sent, 1)
    half = own.shape[0]
    return add(own, moved[:half]), add(far, moved[half:])


def columns(at, width):
    return pl.ds(pl.multiple_of(at * width, width), width)


def slice_kernel(at_ref, *refs, pad):
    weights, out_ref = refs[:-1], refs[-1]
    if pad:
        weights, pad_ref = weights[:-1], weights[-1]
    rows = weights[0].shape[0]
    each = rows + pad
    for s in range(8):
        first = 0
        for ref in weights:
            width = ref.shape[1] // 8
            out_ref[s * each : s * each + rows, first : first + width] = ref[
                :, columns(at_ref[s], width)
            ]
            first += width
        if pad:
            out_ref[s * each + rows : (s + 1) * each, :] = pad_ref[...]


def slice_pieces(at, *weights, pad=None):
    rows = weights[0].shape[0]
    cols = sum(w.shape[1] for w in weights) // 8
    extra = 0 if pad is None else pad.shape[0]
    operands = weights if pad is None else (*weights, pad)
    vmem = pl.BlockSpec(memory_space=pltpu.VMEM)
    return pl.pallas_call(
        lambda *refs: slice_kernel(*refs, pad=extra),
        in_specs=[pl.BlockSpec(memory_space=pltpu.SMEM)] + [vmem] * len(operands),
        out_specs=vmem,
        out_shape=jax.ShapeDtypeStruct((8 * (rows + extra), cols), jnp.bfloat16),
        cost_estimate=CHEAP,
        name="slice_pieces",
    )(at, *operands)


def assemble_kernel(at_ref, *refs):
    own = at_ref[8]
    for j, piece in enumerate(refs[:4]):
        refs[4][0, own ^ j] = piece[...]


def assemble(at, pieces, rows):
    count = at.shape[0] - 1
    total, cols = pieces[0].shape
    return pl.pallas_call(
        assemble_kernel,
        grid_spec=pltpu.PrefetchScalarGridSpec(
            num_scalar_prefetch=1,
            grid=(count,),
            in_specs=[pl.BlockSpec((rows, cols), lambda i, at: (i, 0))] * 4,
            out_specs=pl.BlockSpec((1, 4, rows, cols), lambda i, at: (at[i], 0, 0, 0)),
        ),
        out_shape=jax.ShapeDtypeStruct((count, 4, rows, cols), jnp.bfloat16),
        cost_estimate=CHEAP,
        name="assemble",
    )(at, *pieces).reshape(4 * total, cols)


def spun(rows, cosine, sine):
    return rows * cosine + pltpu.roll(rows, HEAD_SIZE // 2, 1) * sine


def project_kernel(at_ref, *refs, strips):
    token_refs, refs = refs[:strips], refs[strips:]
    pieces, refs = refs[:4], refs[4:]
    cos_ref, sin_ref, normed_ref, raw_ref, q_ref, kv_ref, matrix_ref, gains_ref = refs
    each = pieces[0].shape[0] // 8
    rows = matrix_ref.shape[0] // 32
    own = at_ref[8]
    gains_ref[...] = jnp.zeros_like(gains_ref)

    def place(s, carry):
        piece_at = pl.multiple_of(s * each, 16)
        for j in range(4):
            first = pl.multiple_of((at_ref[s] * 4 + (own ^ j)) * rows, rows)
            matrix_ref[pl.ds(first, rows), :] = pieces[j][pl.ds(piece_at, rows), :]
            gains_ref[...] += pieces[j][
                pl.ds(pl.multiple_of(piece_at + rows, 16), each - rows), :
            ].astype(jnp.float32)
        return carry

    lax.fori_loop(0, 8, place, 0)
    width = gains_ref.shape[1]
    first = 0
    for ref in token_refs:
        normed_ref[first : first + ref.shape[0], :] = ref[...]
        first += ref.shape[0]

    def norm(index, carry):
        here = pl.ds(pl.multiple_of(index * 32, 32), 32)
        block = normed_ref[here, :].astype(jnp.float32)
        block = block * inverse_rms(block)
        for i in range(block.shape[1] // width):
            cols = slice(i * width, (i + 1) * width)
            normed_ref[here, cols] = (block[:, cols] * gains_ref[i : i + 1, :]).astype(
                jnp.bfloat16
            )
        return carry

    lax.fori_loop(0, normed_ref.shape[0] // 32, norm, 0)
    query_gain = gains_ref[8:9, :HEAD_SIZE]
    key_gain = gains_ref[8:9, HEAD_SIZE : 2 * HEAD_SIZE]
    query_cols = q_ref.shape[1]
    step = 256

    def heads(index, carry):
        here = pl.ds(pl.multiple_of(index * step, step), step)
        raw = jnp.dot(normed_ref[here, :], matrix_ref[...], preferred_element_type=jnp.float32)
        raw_ref[here, :] = raw
        cosine, sine = cos_ref[here, :], sin_ref[here, :]
        for col in range(0, query_cols + HEAD_SIZE, HEAD_SIZE):
            part = raw[:, col : col + HEAD_SIZE]
            if col < query_cols:
                part = spun(part * inverse_rms(part) * query_gain, cosine, sine)
                part = part * (LOG2E / math.sqrt(HEAD_SIZE))
                q_ref[here, col : col + HEAD_SIZE] = part.astype(jnp.bfloat16)
            else:
                part = spun(part * inverse_rms(part) * key_gain, cosine, sine)
                kv_ref[here, :HEAD_SIZE] = part.astype(jnp.bfloat16)
        kv_ref[here, HEAD_SIZE:] = raw[:, query_cols + HEAD_SIZE :].astype(jnp.bfloat16)
        return carry

    lax.fori_loop(0, q_ref.shape[0] // step, heads, 0)


def project(at, strips, pieces, cosine, sine, query_cols, pad):
    rows = sum(strip.shape[0] for strip in strips)
    width = strips[0].shape[1]
    cols = pieces[0].shape[1]
    vmem = pl.BlockSpec(memory_space=pltpu.VMEM)
    operands = (*strips, *pieces, cosine, sine)
    narrow, wide = jnp.bfloat16, jnp.float32
    return pl.pallas_call(
        lambda *refs: project_kernel(*refs, strips=len(strips)),
        in_specs=[pl.BlockSpec(memory_space=pltpu.SMEM)] + [vmem] * len(operands),
        out_specs=[vmem] * 6,
        out_shape=[
            jax.ShapeDtypeStruct((rows, width), narrow),
            jax.ShapeDtypeStruct((rows, cols), wide),
            jax.ShapeDtypeStruct((rows, query_cols), narrow),
            jax.ShapeDtypeStruct((rows, 2 * HEAD_SIZE), narrow),
            jax.ShapeDtypeStruct((width, cols), narrow),
            jax.ShapeDtypeStruct((pad, cols), wide),
        ],
        cost_estimate=LONG,
        name="project",
    )(at, *operands)


def project_back_kernel(
    dq_ref, dkv_ref, raw_ref, head_gain_ref, cos_ref, sin_ref, matrix_ref,
    grad_ref, part_ref, gain_ref,
):
    query_cols = dq_ref.shape[1]
    step = 256
    gain_ref[...] = jnp.zeros_like(gain_ref)

    def block(index, carry):
        here = pl.ds(pl.multiple_of(index * step, step), step)
        cosine, sine = cos_ref[here, :], sin_ref[here, :]
        for col in range(0, query_cols + HEAD_SIZE, HEAD_SIZE):
            cols = slice(col, col + HEAD_SIZE)
            which = 0 if col < query_cols else 1
            grads = dkv_ref[here, :HEAD_SIZE] if which else dq_ref[here, cols]
            raw = raw_ref[here, cols]
            rho = inverse_rms(raw)
            unit = raw * rho
            turned = spun(grads.astype(jnp.float32), cosine, -sine)
            gain_ref[which : which + 1, :] += jnp.sum(turned * unit, axis=0, keepdims=True)
            scaled = turned * head_gain_ref[which : which + 1]
            back = rho * (scaled - unit * jnp.mean(unit * scaled, axis=-1, keepdims=True))
            grad_ref[here, cols] = back.astype(jnp.bfloat16)
        grad_ref[here, query_cols + HEAD_SIZE :] = dkv_ref[here, HEAD_SIZE:]
        part_ref[here, :] = lax.dot_general(
            grad_ref[here, :], matrix_ref[...], ALONG, preferred_element_type=jnp.float32
        ).astype(jnp.bfloat16)
        return carry

    lax.fori_loop(0, dq_ref.shape[0] // step, block, 0)


def project_back(query_grads, kv_grads, raw, head_gains, cosine, sine, matrix):
    rows, cols = raw.shape
    vmem = pl.BlockSpec(memory_space=pltpu.VMEM)
    return pl.pallas_call(
        project_back_kernel,
        in_specs=[vmem] * 7,
        out_specs=[vmem] * 3,
        out_shape=[
            jax.ShapeDtypeStruct((rows, cols), jnp.bfloat16),
            jax.ShapeDtypeStruct((rows, matrix.shape[0]), jnp.bfloat16),
            jax.ShapeDtypeStruct((8, HEAD_SIZE), jnp.float32),
        ],
        cost_estimate=LONG,
        name="project_back",
    )(query_grads, kv_grads, raw, head_gains, cosine, sine, matrix)


def dots(lefts, rights, dims):
    if len(lefts) == 1:
        parts, first = [], 0
        for right in rights:
            parts.append(lefts[0][first : first + right.shape[0], :])
            first += right.shape[0]
    else:
        parts = [left[...] for left in lefts]
    return sum(
        lax.dot_general(part, right[...], dims, preferred_element_type=jnp.float32)
        for part, right in zip(parts, rights)
    )


def weight_grads_kernel(at_ref, *refs, groups):
    own_ref, far_ref, sent_ref, held = refs[-4:]
    own = at_ref[8]
    sums = dots(refs[:groups], refs[groups : 2 * groups], DOWN)
    held[...] = sums.astype(jnp.bfloat16).reshape(held.shape)
    own_ref[...] = held[own]
    far_ref[...] = held[own ^ 2]
    sent_ref[0] = held[own ^ 1]
    sent_ref[1] = held[own ^ 3]


def weight_grads(at, lefts, rights, rows):
    count = at.shape[0] - 1
    cols = rights[0].shape[1]
    total = sum(left.shape[0] for left in lefts)
    part = pl.BlockSpec((rows, cols), lambda i, at: (i, 0))
    shape = jax.ShapeDtypeStruct((count * rows, cols), jnp.bfloat16)
    own, far, sent = pl.pallas_call(
        lambda *refs: weight_grads_kernel(*refs, groups=len(lefts)),
        grid_spec=pltpu.PrefetchScalarGridSpec(
            num_scalar_prefetch=1,
            grid=(count,),
            in_specs=[
                pl.BlockSpec((left.shape[0], 4 * rows), lambda i, at: (0, at[i]))
                for left in lefts
            ]
            + [pl.BlockSpec(right.shape, lambda i, at: (0, 0)) for right in rights],
            out_specs=[part, part, pl.BlockSpec((2, rows, cols), lambda i, at: (0, i, 0))],
            scratch_shapes=[pltpu.VMEM((4, rows, cols), jnp.bfloat16)],
        ),
        out_shape=[
            shape, shape, jax.ShapeDtypeStruct((2, count * rows, cols), jnp.bfloat16),
        ],
        cost_estimate=CHEAP,
        name="weight_grads",
    )(at, *lefts, *rights)
    return own, far, sent.reshape(2 * count * rows, cols)


def row_grads_kernel(*refs, lefts):
    left_refs, right_refs, (out_ref, held) = refs[:lefts], refs[lefts:-2], refs[-2:]

    @pl.when(pl.program_id(0) == 0)
    def _():
        first = 0
        for ref in right_refs:
            held[first : first + ref.shape[0], :] = ref[...]
            first += ref.shape[0]

    sums, first = 0.0, 0
    for ref in left_refs:
        sums += lax.dot_general(
            ref[...],
            held[first : first + ref.shape[0], :],
            DOWN,
            preferred_element_type=jnp.float32,
        )
        first += ref.shape[0]
    out_ref[...] = sums.astype(jnp.bfloat16)


def row_grads(lefts, rights, block=256):
    out_rows, cols = lefts[0].shape[1], rights[0].shape[1]
    total = sum(left.shape[0] for left in lefts)
    return pl.pallas_call(
        lambda *refs: row_grads_kernel(*refs, lefts=len(lefts)),
        grid=(out_rows // block,),
        in_specs=[pl.BlockSpec((left.shape[0], block), lambda i: (0, i)) for left in lefts]
        + [pl.BlockSpec(right.shape, lambda i: (0, 0)) for right in rights],
        out_specs=pl.BlockSpec((block, cols), lambda i: (i, 0)),
        out_shape=jax.ShapeDtypeStruct((out_rows, cols), jnp.bfloat16),
        scratch_shapes=[pltpu.VMEM((total, cols), jnp.bfloat16)],
        cost_estimate=CHEAP,
        name="row_grads",
    )(*lefts, *rights)


def hidden_grads_kernel(*refs, strips):
    matrix_ref, outs, held = refs[strips], refs[strips + 1 : -1], refs[-1]

    @pl.when(pl.program_id(0) == 0)
    def _():
        first = 0
        for ref in refs[:strips]:
            held[first : first + ref.shape[0], :] = ref[...]
            first += ref.shape[0]

    first = 0
    for out in outs:
        out[...] = lax.dot_general(
            held[first : first + out.shape[0], :],
            matrix_ref[...],
            ALONG,
            preferred_element_type=jnp.float32,
        )
        first += out.shape[0]


def hidden_grads_of(strips, matrix, block=256):
    rows = [(last - first) * strips[0].shape[0] for first, last in GROUPS]
    cols = matrix.shape[0]
    return pl.pallas_call(
        lambda *refs: hidden_grads_kernel(*refs, strips=len(strips)),
        grid=(cols // block,),
        in_specs=[pl.BlockSpec(strip.shape, lambda i: (0, 0)) for strip in strips]
        + [pl.BlockSpec((block, matrix.shape[1]), lambda i: (i, 0))],
        out_specs=[pl.BlockSpec((n, block), lambda i: (0, i)) for n in rows],
        out_shape=[jax.ShapeDtypeStruct((n, cols), jnp.float32) for n in rows],
        scratch_shapes=[pltpu.VMEM((sum(rows), matrix.shape[1]), jnp.bfloat16)],
        cost_estimate=CHEAP,
        name="hidden_grads",
    )(*strips, matrix)


def lane_sums(block):
    return sum(block[:, i : i + 128] for i in range(0, block.shape[1], 128))


def widen(at, swap, *weights):
    rows, taken, count = weights[0].shape[0], [item[1:] for item in swap.taken], len(weights)

    def widen_kernel(at_ref, *refs):
        piece_refs, refs = refs[: len(taken)], refs[len(taken) :]
        grads, sums_ref = refs[count : 2 * count], refs[2 * count]
        sums_ref[...] = jnp.zeros_like(sums_ref)
        for ref, (start, size, spot, top) in zip(piece_refs, taken):
            here = slice(top, top + size)
            first = 0
            for weight, grad in zip(refs[:count], grads):
                width = weight.shape[1] // 8
                there = columns(at_ref[spot], width)
                block = ref[start : start + size, first : first + width].astype(jnp.float32)
                grad[here, there] = block
                sums_ref[here, :] += lane_sums(block * weight[here, there].astype(jnp.float32))
                first += width

    vmem = pl.BlockSpec(memory_space=pltpu.VMEM)
    shapes = [w.shape for w in weights] + [(rows, 128)]
    return pl.pallas_call(
        widen_kernel,
        grid=(1,),
        in_specs=[pl.BlockSpec(memory_space=pltpu.SMEM), *swap.specs()] + [vmem] * count,
        out_specs=[vmem] * len(shapes),
        out_shape=[jax.ShapeDtypeStruct(shape, jnp.float32) for shape in shapes],
        cost_estimate=CHEAP,
        name="widen",
    )(at, *swap.operands(), *weights)


def grouped(strips):
    return [
        jnp.concatenate(strips[a:b], axis=0) if b - a > 1 else strips[a] for a, b in GROUPS
    ]


def split_groups(groups, rows):
    return [
        group[i * rows : (i + 1) * rows]
        for group in groups
        for i in range(group.shape[0] // rows)
    ]


def gather_head(rows):
    return lax.all_gather(rows, "head", axis=0, tiled=True)


def scatter_head(rows):
    return lax.psum_scatter(rows, "head", scatter_dimension=0, tiled=True)


def inverse_rms(rows):
    return lax.rsqrt(jnp.mean(rows * rows, axis=-1, keepdims=True) + EPS)


def per_device(
    tokens,
    attention_norm,
    query_weight,
    key_projection,
    value_projection,
    query_norm,
    key_norm,
    output_weight,
    feedforward_norm,
    gate_weight,
    up_weight,
    down_weight,
    stretch_order,
    out_cotangent,
):
    blk_count = lax.axis_size("blk")
    head_count = lax.axis_size("head")
    head_index = lax.axis_index("head")
    blk_index = lax.axis_index("blk")
    narrow, wide = jnp.bfloat16, jnp.float32
    tokens, out_cotangent = tokens[0], out_cotangent[0]
    local_rows, model_width = tokens.shape
    group_rows = local_rows * blk_count
    weight_rows = query_weight.shape[0]
    ff_local = gate_weight.shape[1] // blk_count
    query_cols = QUERY_HEADS // blk_count * HEAD_SIZE
    attn_cols = query_cols + 2 * HEAD_SIZE
    device_count = blk_count * head_count
    strip_count = blk_count * head_count
    halves = strip_count // stretch_order.shape[1]
    ring_place = jnp.where(blk_index % 2 == 0, blk_index // 2, 7 - blk_index // 2)

    spot = (ring_place + jnp.arange(blk_count, dtype=jnp.int32)) % blk_count
    at = jnp.where(spot < 4, 2 * spot, 15 - 2 * spot).astype(jnp.int32)
    at_own = jnp.concatenate([at, head_index[None].astype(jnp.int32)])
    ring_spot = (ring_place + jnp.asarray(STRIPS, jnp.int32)) % blk_count
    strip_blk = jnp.where(ring_spot < 4, 2 * ring_spot, 15 - 2 * ring_spot)
    strip_head = head_index ^ jnp.asarray((0, 2, 1, 3), jnp.int32)
    strip = (strip_blk[None, :] * head_count + strip_head[:, None]).reshape(strip_count)
    slots = jnp.arange(stretch_order.shape[1], dtype=jnp.int32)
    held = jnp.sum(
        jnp.where((strip // halves)[:, None] == slots[None, :], stretch_order, 0), axis=1
    )
    strip_place = held * halves + strip % halves
    order = strip_place.astype(jnp.int32)
    place = strip_place[:blk_count].astype(jnp.int32)
    positions = (
        place[:, None] * local_rows + jnp.arange(local_rows, dtype=jnp.int32)[None, :]
    ).reshape(group_rows)
    phases = angles(positions, HEAD_SIZE)[:, 0, :]
    cosine, sine = jnp.cos(phases), jnp.sin(phases)
    cosine = jnp.concatenate([cosine, cosine], axis=1)
    sine = jnp.concatenate([-sine, sine], axis=1)

    small = query_norm.shape[0]
    number = blk_index * head_count + head_index
    pad = 16

    def placed(share):
        return jnp.where(
            jnp.arange(device_count, dtype=jnp.int32)[:, None] == number, share[None, :], 0
        ).reshape(-1)

    gains = jnp.concatenate(
        [placed(attention_norm), placed(feedforward_norm), placed(query_norm), placed(key_norm)]
    ).astype(narrow)
    gains = jnp.pad(gains, (0, pad * attn_cols - gains.shape[0])).reshape(pad, attn_cols)
    down_matrix = gather_head(down_weight)
    output_rows = gather_head(output_weight)

    attn_swap = Swap(
        slice_pieces(at, query_weight, key_projection, value_projection, pad=gains),
        weight_rows + pad,
    )
    token_ring = Gather(tokens)
    ff_slices = slice_pieces(at, gate_weight, up_weight)
    token_ring.go()
    attn_swap.go()
    hold((attn_swap, token_ring))
    token_ring.go()
    attn_swap.go()
    ff_slices, cosine, sine = hold((attn_swap, token_ring), ff_slices, cosine, sine)
    token_ring.go()
    attn_swap.go()
    hold((attn_swap,))
    attn_swap.go()
    own = hold((), attn_swap.result())
    near, far = cross(own, 1), cross(own, 2)
    ff_swap, cotangent_ring = Swap(ff_slices, weight_rows), Gather(out_cotangent)
    hold((token_ring, ff_swap, cotangent_ring))
    token_ring.go()
    own, near, far = hold((token_ring, ff_swap), own, near, far)
    ff_swap.go()
    both = hold((), cross(far, 1))

    first_normed, attn_raw, query_rows, own, attn_matrix, gains = project(
        at_own, token_ring.strips(), (own, near, far, both), cosine, sine, query_cols, pad
    )
    gain_one = gains[:4].reshape(1, model_width)
    gain_two = gains[4:8].reshape(1, model_width)
    head_gains = jnp.pad(gains[8, : 2 * HEAD_SIZE].reshape(2, HEAD_SIZE), ((0, 6), (0, 0)))
    near, far = cross(own, 1), cross(own, 2)
    hold((ff_swap,))
    ff_swap.go()
    own, near, far = hold((), own, near, far)
    both = cross(far, 1)
    kv = hold((ff_swap, cotangent_ring), own, far, near, both)
    ff_swap.go()
    cotangent_ring.go()
    attended, lse = attend(place, order, query_rows, kv)

    def by_groups(rows):
        return [rows[a * local_rows : b * local_rows] for a, b in GROUPS]

    def by_strips(groups):
        return dict(zip(STRIPS, split_groups(groups, local_rows)))

    attended = hold((cotangent_ring, ff_swap), attended)
    branch_parts = [matmul(rows, output_rows).astype(narrow) for rows in by_groups(attended)]
    branch_ring = Scatter(by_strips(branch_parts))
    branch_ring.go()
    cotangent_ring.go()
    ff_swap.go()
    ff_own = hold((), ff_swap.result())
    ff_near, ff_far = cross(ff_own, 1), cross(ff_own, 2)
    hold((branch_ring, cotangent_ring))
    branch_ring.go()
    cotangent_ring.go()
    hold((branch_ring, cotangent_ring))
    branch_ring.go()
    cotangent_ring.go()
    ff_near, ff_far, cotangent_strips, down_matrix = hold(
        (branch_ring, cotangent_ring), ff_near, ff_far, cotangent_ring.strips(), down_matrix
    )
    branch_ring.go()
    ff_both = cross(ff_far, 1)
    hidden_grads = hidden_grads_of(cotangent_strips, down_matrix)
    ff_own, ff_near, ff_far, hidden_grads, ff_both = hold(
        (branch_ring,), ff_own, ff_near, ff_far, hidden_grads, ff_both
    )
    tokens_wide = tokens.astype(wide)
    resid = tokens_wide + branch_ring.total()
    rho_two = inverse_rms(resid)
    unit_two = resid * rho_two

    second_ring = Gather((unit_two * gain_two).astype(narrow))
    second_groups, hidden_groups, ff_gradient_groups = [], [], []

    def feed_forward(index):
        rows = second_ring.group(index)
        ff_raw = matmul(rows, ff_matrix)
        gate, up_proj = ff_raw[:, :ff_local], ff_raw[:, ff_local:]
        sigma = jax.nn.sigmoid(gate)
        swish = gate * sigma
        hidden_gradient = hidden_grads[index]
        gate_gradient = hidden_gradient * up_proj * (sigma * (1.0 + gate * (1.0 - sigma)))
        hidden = (swish * up_proj).astype(narrow)
        gradient = jnp.concatenate([gate_gradient, hidden_gradient * swish], 1).astype(narrow)
        if index < 3:
            rows, hidden, gradient = hold((second_ring,), rows, hidden, gradient)
        second_groups.append(rows)
        hidden_groups.append(hidden)
        ff_gradient_groups.append(gradient)

    second_ring.go()
    ff_matrix = assemble(at_own, (ff_own, ff_near, ff_far, ff_both), weight_rows)
    ff_matrix = hold((second_ring,), ff_matrix)
    for index in range(3):
        second_ring.go()
        feed_forward(index)
    feed_forward(3)

    def back(index):
        return matmul(ff_gradient_groups[index], ff_matrix, ALONG).astype(narrow)

    def split(group):
        return [group[i : i + local_rows] for i in range(0, group.shape[0], local_rows)]

    parts = {4: back(3)}
    resid_ring = Scatter(parts)
    parts[3], parts[5] = split(hold((), back(2)))
    parts[2], parts[6] = split(hold((), back(1)))
    resid_ring.go()
    hold((resid_ring,), parts[2], parts[6])
    resid_ring.go()
    back_zero, second_groups, ff_gradient_groups = hold(
        (resid_ring,), back(0), second_groups, ff_gradient_groups
    )
    parts[0], parts[1], parts[7] = split(back_zero)
    resid_ring.go()
    ff_own, ff_far, ff_sent = hold(
        (resid_ring,), *weight_grads(at_own, second_groups, ff_gradient_groups, weight_rows)
    )
    resid_ring.go()
    ff_own, ff_far = scatter_cross(ff_own, ff_far, ff_sent)
    ff_own, ff_far, hidden_groups, cotangent_strips = hold(
        (resid_ring,), ff_own, ff_far, hidden_groups, cotangent_strips
    )
    ff_far = cross(ff_far, 2)
    scaled = gain_two * resid_ring.total()
    resid_gradient = out_cotangent.astype(wide) + rho_two * (
        scaled - unit_two * jnp.mean(unit_two * scaled, axis=-1, keepdims=True)
    )

    grad_ring = Gather(resid_gradient.astype(narrow))
    grad_groups, attended_grads = [], []

    def attention_back(index):
        rows = grad_ring.group(index)
        grads = matmul(rows, output_rows, ALONG).astype(narrow)
        if index < 3:
            rows, grads = hold((grad_ring,), rows, grads)
        grad_groups.append(rows)
        attended_grads.append(grads)

    grad_ring.go()
    out_parts = [matmul(rows, down_matrix).astype(narrow) for rows in hidden_groups]
    out_parts, hidden_groups = hold((grad_ring,), out_parts, hidden_groups)
    out_ring = Scatter(by_strips(out_parts))
    grad_ring.go()
    down_gradient = row_grads(hidden_groups, cotangent_strips)
    down_gradient = hold((grad_ring,), down_gradient)
    down_gradient = scatter_head(down_gradient)
    grad_ring.go()
    attention_back(0)
    hold((out_ring, grad_ring))
    out_ring.go()
    grad_ring.go()
    attention_back(1)
    attention_back(2)
    ff_swap = Swap(add(ff_own, ff_far), weight_rows)
    hold((grad_ring, ff_swap, out_ring))
    out_ring.go()
    ff_swap.go()
    attention_back(3)
    query_grads, kv_own, kv_far, kv_sent = attend_back(
        place, order, query_rows, attended_grads, attended, lse, kv
    )
    query_grads, kv_own, kv_far, kv_sent, grad_groups, attended = hold(
        (out_ring, ff_swap), query_grads, kv_own, kv_far, kv_sent, grad_groups, attended
    )
    out_ring.go()
    kv_own, kv_far = scatter_cross(kv_own, kv_far, kv_sent)
    output_weight_gradient = row_grads([attended], grad_groups)
    kv_own, kv_far, output_weight_gradient = hold(
        (out_ring, ff_swap), kv_own, kv_far, output_weight_gradient
    )
    output_weight_gradient = scatter_head(output_weight_gradient)
    ff_swap.go()
    kv_grads = hold((ff_swap,), add(kv_own, cross(kv_far, 2)))
    ff_swap.go()
    attn_gradient, first_parts, gain_sums = project_back(
        query_grads, kv_grads, attn_raw, head_gains, cosine, sine, attn_matrix
    )
    attn_gradient, first_parts, gain_sums = hold(
        (ff_swap,), attn_gradient, first_parts, gain_sums
    )
    token_ring = Scatter(by_strips(by_groups(first_parts)))
    token_ring.go()
    ff_swap.go()
    gain_sums = gain_sums + cross(gain_sums, 1)
    gain_sums = gain_sums + cross(gain_sums, 2)
    attn_own, attn_far, attn_sent = weight_grads(
        at_own, [first_normed], [attn_gradient], weight_rows
    )
    attn_own, attn_far, attn_sent, gain_sums = hold(
        (token_ring, ff_swap), attn_own, attn_far, attn_sent, gain_sums
    )
    token_ring.go()
    attn_own, attn_far = hold((), *scatter_cross(attn_own, attn_far, attn_sent))
    attn_far = cross(attn_far, 2)
    gain_sums = gain_sums + mirror(gain_sums, 1)
    gate_weight_gradient, up_weight_gradient, ff_sums = widen(at, ff_swap, gate_weight, up_weight)
    gate_weight_gradient, up_weight_gradient, ff_sums, gain_sums = hold(
        (token_ring,), gate_weight_gradient, up_weight_gradient, ff_sums, gain_sums
    )
    token_ring.go()
    gain_sums = gain_sums + mirror(gain_sums, 2)
    feedforward_norm_gradient = jnp.sum(ff_sums, axis=1) / feedforward_norm.astype(wide)
    attn_swap = Swap(add(attn_own, attn_far), weight_rows)
    feedforward_norm_gradient, gain_sums, down_gradient = hold(
        (token_ring, attn_swap),
        feedforward_norm_gradient, gain_sums, down_gradient.astype(wide),
    )
    attn_swap.go()
    token_ring.go()
    gain_sums = gain_sums + mirror(gain_sums, 4)
    output_weight_gradient, gain_sums = hold(
        (token_ring, attn_swap, out_ring), output_weight_gradient.astype(wide), gain_sums
    )
    attn_swap.go()
    out_ring.go()
    hold((attn_swap,))
    attn_swap.go()
    hold((attn_swap,))
    attn_swap.go()
    layer_out = (resid + out_ring.total()).astype(narrow)
    query_weight_gradient, key_weight_gradient, value_weight_gradient, norm_sums = widen(
        at, attn_swap, query_weight, key_projection, value_projection
    )
    attention_norm_gradient = jnp.sum(norm_sums, axis=1) / attention_norm.astype(wide)
    gain_sums = lax.dynamic_slice_in_dim(gain_sums, number * small, small, 1)
    rho_one = inverse_rms(tokens_wide)
    unit_one = tokens_wide * rho_one
    scaled = gain_one * token_ring.total()
    tokens_gradient = resid_gradient + rho_one * (
        scaled - unit_one * jnp.mean(unit_one * scaled, axis=-1, keepdims=True)
    )
    return (
        layer_out[None],
        tokens_gradient.astype(narrow)[None],
        attention_norm_gradient,
        query_weight_gradient,
        key_weight_gradient,
        value_weight_gradient,
        gain_sums[0],
        gain_sums[1],
        output_weight_gradient,
        feedforward_norm_gradient,
        gate_weight_gradient,
        up_weight_gradient,
        down_gradient,
    )


def solution(mesh):
    placed = (
        P(None, ("blk", "head"), None),
        P(("blk", "head")),
        P(("blk", "head"), None),
        P(("blk", "head"), None),
        P(("blk", "head"), None),
        P(("blk", "head")),
        P(("blk", "head")),
        P(("blk", "head"), None),
        P(("blk", "head")),
        P(("blk", "head"), None),
        P(("blk", "head"), None),
        P(("blk", "head"), None),
        P(),
        P(None, ("blk", "head"), None),
    )
    fits = mesh.shape["blk"] == KEY_VALUE_HEADS and mesh.shape["head"] == 4
    return jax.shard_map(
        per_device if fits else per_device_by_tokens,
        mesh=mesh,
        in_specs=placed,
        out_specs=(
            P(None, ("blk", "head"), None),
            P(None, ("blk", "head"), None),
            P(("blk", "head")),
            P(("blk", "head"), None),
            P(("blk", "head"), None),
            P(("blk", "head"), None),
            P(("blk", "head")),
            P(("blk", "head")),
            P(("blk", "head"), None),
            P(("blk", "head")),
            P(("blk", "head"), None),
            P(("blk", "head"), None),
            P(("blk", "head"), None),
        ),
        check_vma=False,
    )
```

```python
import math

import jax
import jax.numpy as jnp
from jax import lax
from jax.experimental import pallas as pl
from jax.experimental.pallas import tpu as pltpu
from jax.sharding import PartitionSpec as P

QUERY_HEADS = 16
KEY_VALUE_HEADS = 8
HEAD_SIZE = 128


EPS = 1e-06
NEG = -1e30
ROPE_BASE = 1000000.0


def passed_along(value, axis, by):
    count = lax.axis_size(axis)
    return lax.ppermute(value, axis, [(i, (i + by) % count) for i in range(count)])


def norm_rows(inputs, norm_gain):
    return inputs * lax.rsqrt(jnp.mean(inputs * inputs, axis=-1, keepdims=True) + EPS) * norm_gain


def rotary(inputs, phases):
    half_width = inputs.shape[-1] // 2
    cosine = jnp.cos(phases)
    sine_term = jnp.sin(phases)
    first_half = inputs[..., :half_width]
    second_half = inputs[..., half_width:]
    return jnp.concatenate(
        [
            first_half * cosine - second_half * sine_term,
            second_half * cosine + first_half * sine_term,
        ],
        axis=-1,
    )


def angles(positions, head_width):
    half_width = head_width // 2
    frequency = jnp.exp(
        jnp.arange(half_width, dtype=jnp.float32) * (-2.0 * math.log(ROPE_BASE) / head_width)
    )
    return positions.astype(jnp.float32)[..., None, None] * frequency


def token_positions(stretch_order, first_row, row_count, stretch_rows):
    row_index = first_row + jnp.arange(row_count, dtype=jnp.int32)
    slot_index = row_index // stretch_rows
    matches = slot_index[:, None] == jnp.arange(stretch_order.shape[1], dtype=jnp.int32)[None, :]
    picked = jnp.sum(jnp.where(matches[None], stretch_order[:, None, :], 0), axis=-1)
    return picked * stretch_rows + row_index % stretch_rows


def per_device_by_tokens(
    tokens,
    attention_norm,
    query_weight,
    key_projection,
    value_projection,
    query_norm,
    key_norm,
    output_weight,
    feedforward_norm,
    gate_weight,
    up_weight,
    down_weight,
    stretch_order,
    out_cotangent,
):
    count_of_heads = lax.axis_size("head")
    span_count = lax.axis_size("blk")
    span_index = lax.axis_index("blk")
    head_index = lax.axis_index("head")
    sequence_total = tokens.shape[0]
    local_rows = tokens.shape[1]
    group_rows = local_rows * count_of_heads
    stretch_rows = group_rows // 2
    heads_shared = KEY_VALUE_HEADS // count_of_heads
    heads_per_group = QUERY_HEADS // KEY_VALUE_HEADS
    score_scale = 1.0 / math.sqrt(HEAD_SIZE)
    gain_one, query_matrix, key_matrix, value_matrix, query_gain, key_gain, output_matrix = (
        lax.all_gather(attention_norm, ("blk", "head"), axis=0, tiled=True),
        lax.all_gather(query_weight, ("blk", "head"), axis=0, tiled=True),
        lax.all_gather(key_projection, ("blk", "head"), axis=0, tiled=True),
        lax.all_gather(value_projection, ("blk", "head"), axis=0, tiled=True),
        lax.all_gather(query_norm, ("blk", "head"), axis=0, tiled=True),
        lax.all_gather(key_norm, ("blk", "head"), axis=0, tiled=True),
        lax.all_gather(output_weight, ("blk", "head"), axis=0, tiled=True),
    )
    gain_two, gate_matrix, up_matrix, down_matrix = (
        lax.all_gather(feedforward_norm, ("blk", "head"), axis=0, tiled=True),
        lax.all_gather(gate_weight, ("blk", "head"), axis=0, tiled=True),
        lax.all_gather(up_weight, ("blk", "head"), axis=0, tiled=True),
        lax.all_gather(down_weight, ("blk", "head"), axis=0, tiled=True),
    )
    gain_one = gain_one.astype(jnp.float32)
    gain_two = gain_two.astype(jnp.float32)
    query_gain = query_gain.astype(jnp.float32)
    key_gain = key_gain.astype(jnp.float32)
    own_first = (span_index * count_of_heads + head_index) * local_rows
    own_pos = token_positions(stretch_order, own_first, local_rows, stretch_rows)
    group_pos = token_positions(stretch_order, span_index * group_rows, group_rows, stretch_rows)
    phases = angles(own_pos, HEAD_SIZE)
    tokens_wide = tokens.astype(jnp.float32)
    first_normed, norm_one_back = jax.vjp(norm_rows, tokens_wide, gain_one)
    first_normed = first_normed.astype(jnp.bfloat16)
    query_raw = jnp.einsum(
        "btd,de->bte", first_normed, query_matrix, preferred_element_type=jnp.float32
    ).reshape(sequence_total, local_rows, QUERY_HEADS, HEAD_SIZE)
    key_unnormed = jnp.einsum(
        "btd,de->bte", first_normed, key_matrix, preferred_element_type=jnp.float32
    ).reshape(sequence_total, local_rows, KEY_VALUE_HEADS, HEAD_SIZE)
    value_tokens = (
        jnp.einsum("btd,de->bte", first_normed, value_matrix, preferred_element_type=jnp.float32)
        .astype(jnp.bfloat16)
        .reshape(sequence_total, local_rows, KEY_VALUE_HEADS, HEAD_SIZE)
    )

    def heads_local(query_in, key_in, query_scale, key_scale):
        return (
            rotary(norm_rows(query_in, query_scale), phases),
            rotary(norm_rows(key_in, key_scale), phases),
        )

    (query_tokens, key_tokens), heads_back = jax.vjp(
        heads_local, query_raw, key_unnormed, query_gain, key_gain
    )
    query_tokens = query_tokens.astype(jnp.bfloat16)
    key_tokens = key_tokens.astype(jnp.bfloat16)
    query_group, key_group, value_group = (
        lax.all_to_all(query_tokens, "head", split_axis=2, concat_axis=1, tiled=True),
        lax.all_to_all(key_tokens, "head", split_axis=2, concat_axis=1, tiled=True),
        lax.all_to_all(value_tokens, "head", split_axis=2, concat_axis=1, tiled=True),
    )
    query_five = query_group.reshape(
        sequence_total, group_rows, heads_shared, heads_per_group, HEAD_SIZE
    )

    def block_update(carry, key_block, value_block, key_pos):
        run_max, run_sum, run_total = carry
        scores = (
            jnp.einsum(
                "bqkgd,bckd->bkgqc", query_five, key_block, preferred_element_type=jnp.float32
            )
            * score_scale
        )
        allowed = key_pos[:, None, None, None, :] <= group_pos[:, None, None, :, None]
        scores = jnp.where(allowed, scores, NEG)
        new_max = jnp.maximum(run_max, jnp.max(scores, axis=-1))
        exponent = jnp.where(allowed, jnp.exp(scores - new_max[..., None]), 0.0)
        factor = jnp.exp(run_max - new_max)
        new_sum = run_sum * factor + jnp.sum(exponent, axis=-1)
        new_total = run_total * factor[..., None] + jnp.einsum(
            "bkgqc,bckd->bkgqd",
            exponent.astype(jnp.bfloat16),
            value_block,
            preferred_element_type=jnp.float32,
        )
        return (new_max, new_sum, new_total)

    def fold_update(carry, key_block, value_block, key_pos):
        result = block_update(carry, key_block, value_block, key_pos)
        return result

    stat_shape = (sequence_total, heads_shared, heads_per_group, group_rows)
    start_state = (
        jnp.full(stat_shape, NEG, jnp.float32),
        jnp.zeros(stat_shape, jnp.float32),
        jnp.zeros(stat_shape + (HEAD_SIZE,), jnp.float32),
    )
    key_piece = lax.all_gather(key_group, "blk", axis=1, tiled=True)
    value_piece = lax.all_gather(value_group, "blk", axis=1, tiled=True)
    piece_rows = key_piece.shape[1]
    block_len = math.gcd(group_rows, piece_rows)

    def inner(block_number, carry_in):
        offset = block_number * block_len
        key_block = lax.dynamic_slice_in_dim(key_piece, offset, block_len, 1)
        value_block = lax.dynamic_slice_in_dim(value_piece, offset, block_len, 1)
        key_pos = token_positions(stretch_order, offset, block_len, stretch_rows)
        return fold_update(carry_in, key_block, value_block, key_pos)

    run_max, run_sum, run_total = lax.fori_loop(0, piece_rows // block_len, inner, start_state)
    log_total = run_max + jnp.log(run_sum)
    attended_five = run_total / run_sum[..., None]
    attended_group = (
        jnp.transpose(attended_five, (0, 3, 1, 2, 4))
        .reshape(sequence_total, group_rows, heads_shared * heads_per_group, HEAD_SIZE)
        .astype(jnp.bfloat16)
    )
    attended_tokens = lax.all_to_all(
        attended_group, "head", split_axis=1, concat_axis=2, tiled=True
    ).reshape(sequence_total, local_rows, QUERY_HEADS * HEAD_SIZE)
    branch = jnp.einsum(
        "bte,ed->btd", attended_tokens, output_matrix, preferred_element_type=jnp.float32
    )
    resid = tokens_wide + branch
    normed_two, norm_two_back = jax.vjp(norm_rows, resid, gain_two)
    normed_two = normed_two.astype(jnp.bfloat16)
    gate = jnp.einsum("btd,df->btf", normed_two, gate_matrix, preferred_element_type=jnp.float32)
    up_proj = jnp.einsum("btd,df->btf", normed_two, up_matrix, preferred_element_type=jnp.float32)

    def swish_product(gate_in, up_in):
        return jax.nn.silu(gate_in) * up_in

    hidden, swish_back = jax.vjp(swish_product, gate, up_proj)
    hidden = hidden.astype(jnp.bfloat16)
    layer_out = (
        resid + jnp.einsum("btf,fd->btd", hidden, down_matrix, preferred_element_type=jnp.float32)
    ).astype(jnp.bfloat16)
    gain_again, gate_matrix, up_matrix, down_matrix = (
        lax.all_gather(feedforward_norm, ("blk", "head"), axis=0, tiled=True),
        lax.all_gather(gate_weight, ("blk", "head"), axis=0, tiled=True),
        lax.all_gather(up_weight, ("blk", "head"), axis=0, tiled=True),
        lax.all_gather(down_weight, ("blk", "head"), axis=0, tiled=True),
    )
    down_gradient = jnp.einsum(
        "btf,btd->fd", hidden, out_cotangent, preferred_element_type=jnp.float32
    )
    hidden_gradient = jnp.einsum(
        "btd,fd->btf", out_cotangent, down_matrix, preferred_element_type=jnp.float32
    )
    gate_gradient, up_gradient = swish_back(hidden_gradient)
    gate_gradient = gate_gradient.astype(jnp.bfloat16)
    up_gradient = up_gradient.astype(jnp.bfloat16)
    gate_matrix_gradient = jnp.einsum(
        "btd,btf->df", normed_two, gate_gradient, preferred_element_type=jnp.float32
    )
    up_matrix_gradient = jnp.einsum(
        "btd,btf->df", normed_two, up_gradient, preferred_element_type=jnp.float32
    )
    normed_two_gradient = jnp.einsum(
        "btf,df->btd", gate_gradient, gate_matrix, preferred_element_type=jnp.float32
    ) + jnp.einsum("btf,df->btd", up_gradient, up_matrix, preferred_element_type=jnp.float32)
    resid_part, gain_two_gradient = norm_two_back(normed_two_gradient)
    resid_gradient = out_cotangent.astype(jnp.float32) + resid_part
    feedforward_sums = (
        lax.psum_scatter(gain_two_gradient, ("blk", "head"), scatter_dimension=0, tiled=True),
        lax.psum_scatter(gate_matrix_gradient, ("blk", "head"), scatter_dimension=0, tiled=True),
        lax.psum_scatter(up_matrix_gradient, ("blk", "head"), scatter_dimension=0, tiled=True),
        lax.psum_scatter(down_gradient, ("blk", "head"), scatter_dimension=0, tiled=True),
    )
    gain_again, query_matrix, key_matrix, value_matrix, query_again, key_again, output_matrix = (
        lax.all_gather(attention_norm, ("blk", "head"), axis=0, tiled=True),
        lax.all_gather(query_weight, ("blk", "head"), axis=0, tiled=True),
        lax.all_gather(key_projection, ("blk", "head"), axis=0, tiled=True),
        lax.all_gather(value_projection, ("blk", "head"), axis=0, tiled=True),
        lax.all_gather(query_norm, ("blk", "head"), axis=0, tiled=True),
        lax.all_gather(key_norm, ("blk", "head"), axis=0, tiled=True),
        lax.all_gather(output_weight, ("blk", "head"), axis=0, tiled=True),
    )
    branch_gradient = resid_gradient.astype(jnp.bfloat16)
    output_matrix_gradient = jnp.einsum(
        "bte,btd->ed", attended_tokens, branch_gradient, preferred_element_type=jnp.float32
    )
    attended_gradient = (
        jnp.einsum(
            "btd,ed->bte", branch_gradient, output_matrix, preferred_element_type=jnp.float32
        )
        .astype(jnp.bfloat16)
        .reshape(sequence_total, local_rows, QUERY_HEADS, HEAD_SIZE)
    )
    attended_grad_group = lax.all_to_all(
        attended_gradient, "head", split_axis=2, concat_axis=1, tiled=True
    ).reshape(sequence_total, group_rows, heads_shared, heads_per_group, HEAD_SIZE)
    delta = jnp.sum(
        jnp.transpose(attended_grad_group.astype(jnp.float32), (0, 2, 3, 1, 4)) * attended_five,
        axis=-1,
    )

    def block_grads(sums_in, key_current, value_current, key_pos):
        key_sum, value_sum, query_sum = sums_in
        scores = (
            jnp.einsum(
                "bqkgd,bckd->bkgqc", query_five, key_current, preferred_element_type=jnp.float32
            )
            * score_scale
        )
        allowed = key_pos[:, None, None, None, :] <= group_pos[:, None, None, :, None]
        weights = jnp.where(allowed, jnp.exp(scores - log_total[..., None]), 0.0)
        probs = weights.astype(jnp.bfloat16)
        value_sum = value_sum + jnp.einsum(
            "bkgqc,bqkgd->bckd", probs, attended_grad_group, preferred_element_type=jnp.float32
        )
        probs_gradient = jnp.einsum(
            "bqkgd,bckd->bkgqc",
            attended_grad_group,
            value_current,
            preferred_element_type=jnp.float32,
        )
        scores_gradient = (weights * (probs_gradient - delta[..., None])).astype(jnp.bfloat16)
        query_sum = (
            query_sum
            + jnp.einsum(
                "bkgqc,bckd->bqkgd",
                scores_gradient,
                key_current,
                preferred_element_type=jnp.float32,
            )
            * score_scale
        )
        key_sum = (
            key_sum
            + jnp.einsum(
                "bkgqc,bqkgd->bckd", scores_gradient, query_five, preferred_element_type=jnp.float32
            )
            * score_scale
        )
        return (key_sum, value_sum, query_sum)

    def pass_step(step_index, carry):
        key_current, value_current, key_sum, value_sum, query_sum = carry
        anchor = (span_index - step_index) % span_count
        key_pos = token_positions(stretch_order, anchor * group_rows, group_rows, stretch_rows)
        key_sum, value_sum, query_sum = block_grads(
            (key_sum, value_sum, query_sum), key_current, value_current, key_pos
        )
        key_current, value_current = passed_along((key_current, value_current), "blk", 1)
        key_sum, value_sum = (
            passed_along(key_sum.astype(jnp.bfloat16), "blk", 1).astype(key_sum.dtype),
            passed_along(value_sum.astype(jnp.bfloat16), "blk", 1).astype(value_sum.dtype),
        )
        return (key_current, value_current, key_sum, value_sum, query_sum)

    kv_zeros = jnp.zeros((sequence_total, group_rows, heads_shared, HEAD_SIZE), jnp.float32)
    query_zeros = jnp.zeros(
        (sequence_total, group_rows, heads_shared, heads_per_group, HEAD_SIZE), jnp.float32
    )
    final_state = lax.fori_loop(
        0, span_count, pass_step, (key_group, value_group, kv_zeros, kv_zeros, query_zeros)
    )
    key_grad_group = final_state[2].astype(jnp.bfloat16)
    value_grad_group = final_state[3].astype(jnp.bfloat16)
    query_grad_group = (
        final_state[4]
        .astype(jnp.bfloat16)
        .reshape(sequence_total, group_rows, heads_shared * heads_per_group, HEAD_SIZE)
    )
    query_grad_tokens, key_grad_tokens, value_gradient_tokens = (
        lax.all_to_all(query_grad_group, "head", split_axis=1, concat_axis=2, tiled=True),
        lax.all_to_all(key_grad_group, "head", split_axis=1, concat_axis=2, tiled=True),
        lax.all_to_all(value_grad_group, "head", split_axis=1, concat_axis=2, tiled=True),
    )
    query_raw_gradient, key_unnormed_gradient, query_gain_gradient, key_gain_gradient = heads_back(
        (query_grad_tokens.astype(jnp.float32), key_grad_tokens.astype(jnp.float32))
    )
    query_raw_gradient = query_raw_gradient.astype(jnp.bfloat16).reshape(
        sequence_total, local_rows, QUERY_HEADS * HEAD_SIZE
    )
    key_unnormed_gradient = key_unnormed_gradient.astype(jnp.bfloat16).reshape(
        sequence_total, local_rows, KEY_VALUE_HEADS * HEAD_SIZE
    )
    value_unnormed_gradient = value_gradient_tokens.reshape(
        sequence_total, local_rows, KEY_VALUE_HEADS * HEAD_SIZE
    )
    query_matrix_gradient = jnp.einsum(
        "btd,bte->de", first_normed, query_raw_gradient, preferred_element_type=jnp.float32
    )
    key_matrix_gradient = jnp.einsum(
        "btd,bte->de", first_normed, key_unnormed_gradient, preferred_element_type=jnp.float32
    )
    value_matrix_gradient = jnp.einsum(
        "btd,bte->de", first_normed, value_unnormed_gradient, preferred_element_type=jnp.float32
    )
    normed_one_gradient = jnp.einsum(
        "bte,de->btd", query_raw_gradient, query_matrix, preferred_element_type=jnp.float32
    )
    normed_one_gradient = normed_one_gradient + jnp.einsum(
        "bte,de->btd", key_unnormed_gradient, key_matrix, preferred_element_type=jnp.float32
    )
    normed_one_gradient = normed_one_gradient + jnp.einsum(
        "bte,de->btd", value_unnormed_gradient, value_matrix, preferred_element_type=jnp.float32
    )
    token_part, gain_one_gradient = norm_one_back(normed_one_gradient)
    tokens_gradient = (resid_gradient + token_part).astype(jnp.bfloat16)
    attention_sums = (
        lax.psum_scatter(gain_one_gradient, ("blk", "head"), scatter_dimension=0, tiled=True),
        lax.psum_scatter(query_matrix_gradient, ("blk", "head"), scatter_dimension=0, tiled=True),
        lax.psum_scatter(key_matrix_gradient, ("blk", "head"), scatter_dimension=0, tiled=True),
        lax.psum_scatter(value_matrix_gradient, ("blk", "head"), scatter_dimension=0, tiled=True),
        lax.psum_scatter(query_gain_gradient, ("blk", "head"), scatter_dimension=0, tiled=True),
        lax.psum_scatter(key_gain_gradient, ("blk", "head"), scatter_dimension=0, tiled=True),
        lax.psum_scatter(output_matrix_gradient, ("blk", "head"), scatter_dimension=0, tiled=True),
    )
    return (
        layer_out,
        tokens_gradient,
        attention_sums[0],
        attention_sums[1],
        attention_sums[2],
        attention_sums[3],
        attention_sums[4],
        attention_sums[5],
        attention_sums[6],
        feedforward_sums[0],
        feedforward_sums[1],
        feedforward_sums[2],
        feedforward_sums[3],
    )


LOG2E = math.log2(math.e)
STRIP = 128
CHUNK = 512
ALONG = (((1,), (1,)), ((), ()))
DOWN = (((0,), (0,)), ((), ()))


def two_heads(block):
    return jnp.concatenate([block[:, :HEAD_SIZE], block[:, HEAD_SIZE:]], axis=0)


def side_by_side(rows):
    half = rows.shape[0] // 2
    return jnp.concatenate([rows[:half], rows[half:]], axis=1)


CHEAP = pl.CostEstimate(flops=1, bytes_accessed=1, transcendentals=0)
LONG = pl.CostEstimate(flops=3 * 10**10, bytes_accessed=1 << 25, transcendentals=0)


def sort_strips(order_ref, kv_refs, keys, values):
    per = kv_refs[0].shape[0] // STRIP
    for j, ref in enumerate(kv_refs):
        for i in range(per):
            target = pl.multiple_of(order_ref[j * per + i] * STRIP, STRIP)
            here = slice(i * STRIP, (i + 1) * STRIP)
            keys[pl.ds(target, STRIP), :] = ref[here, :HEAD_SIZE]
            values[pl.ds(target, STRIP), :HEAD_SIZE] = ref[here, HEAD_SIZE:]


def attend_kernel(place_ref, order_ref, q_ref, *refs):
    kv_refs, (out_ref, lse_ref, keys, values) = refs[:4], refs[4:]
    step = pl.program_id(0)

    @pl.when(step == 0)
    def _():
        values[:, HEAD_SIZE:] = jnp.ones((values.shape[0], HEAD_SIZE), jnp.bfloat16)
        sort_strips(order_ref, kv_refs, keys, values)

    place = place_ref[step]
    queries = two_heads(q_ref[...])
    last = place // (CHUNK // STRIP)

    def part(index, total, masked):
        first = pl.multiple_of(index * CHUNK, CHUNK)
        scores = lax.dot_general(
            queries, keys[pl.ds(first, CHUNK), :], ALONG, preferred_element_type=jnp.float32
        )
        weights = jnp.exp2(scores)
        if masked:
            row = lax.broadcasted_iota(jnp.int32, scores.shape, 0) % STRIP
            column = lax.broadcasted_iota(jnp.int32, scores.shape, 1)
            weights = jnp.where(column - row <= place * STRIP - first, weights, 0.0)
        return total + jnp.dot(
            weights.astype(jnp.bfloat16),
            values[pl.ds(first, CHUNK), :],
            preferred_element_type=jnp.float32,
        )

    total = jnp.zeros((2 * STRIP, 2 * HEAD_SIZE), jnp.float32)
    total = lax.fori_loop(0, last, lambda index, t: part(index, t, False), total)
    total = part(last, total, True)
    norm = total[:, HEAD_SIZE:]
    out_ref[...] = side_by_side(total[:, :HEAD_SIZE] / norm).astype(jnp.bfloat16)
    lse_ref[0] = jnp.transpose(jnp.log2(norm))[:8]


def attend(place, order, queries, kv):
    rows, width = queries.shape
    steps = rows // STRIP
    total = sum(part.shape[0] for part in kv)
    strip = pl.BlockSpec((STRIP, width), lambda i, *_: (i, 0))
    return pl.pallas_call(
        attend_kernel,
        grid_spec=pltpu.PrefetchScalarGridSpec(
            num_scalar_prefetch=2,
            grid=(steps,),
            in_specs=[strip] + [pl.BlockSpec(part.shape, lambda i, *_: (0, 0)) for part in kv],
            out_specs=[strip, pl.BlockSpec((1, 8, 2 * STRIP), lambda i, *_: (i, 0, 0))],
            scratch_shapes=[
                pltpu.VMEM((total, HEAD_SIZE), jnp.bfloat16),
                pltpu.VMEM((total, 2 * HEAD_SIZE), jnp.bfloat16),
            ],
        ),
        out_shape=[
            jax.ShapeDtypeStruct((rows, width), jnp.bfloat16),
            jax.ShapeDtypeStruct((steps, 8, 2 * STRIP), jnp.float32),
        ],
        cost_estimate=LONG,
        name="attend",
    )(place, order, queries, *kv)


def attend_back_kernel(place_ref, order_ref, q_ref, out_ref, lse_ref, *refs, groups):
    grad_refs, kv_refs = refs[:groups], refs[groups : groups + 4]
    dq_ref, own_ref, far_ref, sent_ref = refs[groups + 4 : groups + 8]
    keys, values, key_sums, value_sums, grads_all = refs[groups + 8 :]
    step = pl.program_id(0)

    @pl.when(step == 0)
    def _():
        key_sums[...] = jnp.zeros_like(key_sums)
        value_sums[...] = jnp.zeros_like(value_sums)
        sort_strips(order_ref, kv_refs, keys, values)
        first = 0
        for ref in grad_refs:
            grads_all[first : first + ref.shape[0], :] = ref[...]
            first += ref.shape[0]

    place = place_ref[step]
    queries = two_heads(q_ref[...])
    grads = two_heads(grads_all[pl.ds(pl.multiple_of(step * STRIP, STRIP), STRIP), :])
    product = grads.astype(jnp.float32) * two_heads(out_ref[...]).astype(jnp.float32)
    delta = jnp.sum(jnp.transpose(product), axis=0, keepdims=True)
    lse = lse_ref[0, :1]
    last = place // (CHUNK // STRIP)

    def part(index, total, masked):
        first = pl.multiple_of(index * CHUNK, CHUNK)
        here = pl.ds(first, CHUNK)
        key_rows = keys[here, :]
        scores = lax.dot_general(key_rows, queries, ALONG, preferred_element_type=jnp.float32)
        weights = jnp.exp2(scores - lse)
        if masked:
            row = lax.broadcasted_iota(jnp.int32, scores.shape, 0)
            column = lax.broadcasted_iota(jnp.int32, scores.shape, 1) % STRIP
            weights = jnp.where(row - column <= place * STRIP - first, weights, 0.0)
        slopes = lax.dot_general(
            values[here, :], grads, ALONG, preferred_element_type=jnp.float32
        )
        score_grads = (weights * (slopes - delta)).astype(jnp.bfloat16)
        value_sums[here, :] += jnp.dot(
            weights.astype(jnp.bfloat16), grads, preferred_element_type=jnp.float32
        )
        key_sums[here, :] += jnp.dot(score_grads, queries, preferred_element_type=jnp.float32)
        return total + lax.dot_general(
            score_grads, key_rows, DOWN, preferred_element_type=jnp.float32
        )

    total = jnp.zeros((2 * STRIP, HEAD_SIZE), jnp.float32)
    total = lax.fori_loop(0, last, lambda index, t: part(index, t, False), total)
    total = part(last, total, True)
    dq_ref[...] = side_by_side(total * (1.0 / math.sqrt(HEAD_SIZE))).astype(jnp.bfloat16)

    @pl.when(step == pl.num_programs(0) - 1)
    def _():
        per = own_ref.shape[0] // STRIP
        for j in range(4):
            target = (own_ref, far_ref, sent_ref, sent_ref)[j]
            base = per if j == 3 else 0
            for i in range(per):
                source = pl.multiple_of(order_ref[j * per + i] * STRIP, STRIP)
                here = slice((base + i) * STRIP, (base + i + 1) * STRIP)
                target[here, :HEAD_SIZE] = (
                    key_sums[pl.ds(source, STRIP), :] * (1.0 / LOG2E)
                ).astype(jnp.bfloat16)
                target[here, HEAD_SIZE:] = value_sums[pl.ds(source, STRIP), :].astype(
                    jnp.bfloat16
                )


def attend_back(place, order, queries, grads, attended, lse, kv):
    rows, width = queries.shape
    steps = rows // STRIP
    total = sum(part.shape[0] for part in kv)
    strip = pl.BlockSpec((STRIP, width), lambda i, *_: (i, 0))

    def whole(shape):
        return pl.BlockSpec(shape, lambda i, *_: (0, 0))

    outs = [kv[0].shape, kv[0].shape, (2 * kv[0].shape[0], kv[0].shape[1])]
    return pl.pallas_call(
        lambda *refs: attend_back_kernel(*refs, groups=len(grads)),
        grid_spec=pltpu.PrefetchScalarGridSpec(
            num_scalar_prefetch=2,
            grid=(steps,),
            in_specs=[strip, strip, pl.BlockSpec((1, 8, 2 * STRIP), lambda i, *_: (i, 0, 0))]
            + [whole(part.shape) for part in (*grads, *kv)],
            out_specs=[strip] + [whole(shape) for shape in outs],
            scratch_shapes=[
                pltpu.VMEM((total, HEAD_SIZE), jnp.bfloat16),
                pltpu.VMEM((total, HEAD_SIZE), jnp.bfloat16),
                pltpu.VMEM((total, HEAD_SIZE), jnp.float32),
                pltpu.VMEM((total, HEAD_SIZE), jnp.float32),
                pltpu.VMEM((rows, width), jnp.bfloat16),
            ],
        ),
        out_shape=[jax.ShapeDtypeStruct((rows, width), jnp.bfloat16)]
        + [jax.ShapeDtypeStruct(shape, jnp.bfloat16) for shape in outs],
        cost_estimate=LONG,
        name="attend_back",
    )(place, order, queries, attended, lse, *grads, *kv)


def matmul(left, right, dims=(((1,), (0,)), ((), ()))):
    return lax.dot_general(left, right, dims, preferred_element_type=jnp.float32)


RING = (0, 2, 4, 6, 7, 5, 3, 1)
STRIPS = (0, 1, 7, 2, 6, 3, 5, 4)
GROUPS = ((0, 3), (3, 5), (5, 7), (7, 8))


def hop(value, by):
    count = len(RING)
    return lax.ppermute(value, "blk", [(RING[i], RING[(i + by) % count]) for i in range(count)])


def cross(value, by):
    return lax.ppermute(value, "head", [(i, i ^ by) for i in range(4)])


def add(left, right):
    return (left.astype(jnp.float32) + right.astype(jnp.float32)).astype(left.dtype)


class Gather:
    def __init__(self, own):
        self.got, self.step = {0: own}, 0
        self.state = (own, own)

    def go(self):
        self.step += 1
        left, right = self.state
        if self.step < 4:
            self.state = hop(left, -1), hop(right, 1)
            self.got[self.step], self.got[8 - self.step] = self.state
        else:
            half = left.shape[0] // 2
            self.got[4] = jnp.concatenate([hop(left[:half], -1), hop(right[half:], 1)], axis=0)
            self.state = (self.got[4],)

    def strips(self):
        return [self.got[s] for s in STRIPS]

    def group(self, index):
        first, last = GROUPS[index]
        return jnp.concatenate([self.got[s] for s in STRIPS[first:last]], axis=0)


class Scatter:
    def __init__(self, part):
        self.part, self.step = part, 0
        self.half = part[4].shape[0] // 2
        self.state = (part[4][: self.half], part[4][self.half :])

    def go(self):
        self.step += 1
        half, part = self.half, self.part
        up, down = hop(self.state[0], 1), hop(self.state[1], -1)
        if self.step == 1:
            up = jnp.concatenate([add(part[3][:half], up), part[3][half:]], axis=0)
            down = jnp.concatenate([part[5][:half], add(part[5][half:], down)], axis=0)
        elif self.step < 4:
            up, down = add(part[4 - self.step], up), add(part[4 + self.step], down)
        self.state = up, down

    def total(self):
        up, down = self.state
        wide = jnp.float32
        return self.part[0].astype(wide) + up.astype(wide) + down.astype(wide)


class Swap:
    def __init__(self, pieces, rows):
        cut = 4 * rows + rows // 2
        self.rows, self.step = rows, 0
        self.taken = [(pieces, 0, rows, 0, 0)]
        self.state = (pieces[rows:cut], pieces[cut:])

    def go(self):
        self.step += 1
        rows, step = self.rows, self.step
        right, left = hop(self.state[0], 1), hop(self.state[1], -1)
        if step < 4:
            self.taken.append((right, 0, rows, 8 - step, 0))
            self.taken.append((left, left.shape[0] - rows, rows, step, 0))
            self.state = right[rows:], left[:-rows]
        else:
            self.taken.append((right, 0, rows // 2, 4, 0))
            self.taken.append((left, 0, rows // 2, 4, rows // 2))
            self.state = right, left

    def operands(self):
        return [item[0] for item in self.taken]

    def specs(self):
        vmem = pl.BlockSpec(memory_space=pltpu.VMEM)
        own = pl.BlockSpec((self.rows, self.taken[0][0].shape[1]), lambda i: (0, 0))
        return [own] + [vmem] * (len(self.taken) - 1)

    def result(self):
        rows, taken = self.rows, [item[1:] for item in self.taken]

        def stack_kernel(*refs):
            for ref, (first, count, spot, top) in zip(refs[:-1], taken):
                at = spot * rows + top
                refs[-1][at : at + count, :] = ref[first : first + count, :]

        return pl.pallas_call(
            stack_kernel,
            grid=(1,),
            in_specs=self.specs(),
            out_specs=pl.BlockSpec(memory_space=pltpu.VMEM),
            out_shape=jax.ShapeDtypeStruct((8 * rows, self.taken[0][0].shape[1]), jnp.bfloat16),
            cost_estimate=CHEAP,
            name="stack",
        )(*self.operands())


def hold(rings, *extra):
    states, extra = lax.optimization_barrier(([ring.state for ring in rings], extra))
    for ring, state in zip(rings, states):
        ring.state = state
    return extra[0] if len(extra) == 1 else extra


def scatter_cross(own, far, sent):
    moved = cross(sent, 1)
    half = own.shape[0]
    return add(own, moved[:half]), add(far, moved[half:])


def columns(at, width):
    return pl.ds(pl.multiple_of(at * width, width), width)


def slice_kernel(at_ref, *refs, pad):
    weights, out_ref = refs[:-1], refs[-1]
    if pad:
        weights, pad_ref = weights[:-1], weights[-1]
    rows = weights[0].shape[0]
    each = rows + pad
    for s in range(8):
        first = 0
        for ref in weights:
            width = ref.shape[1] // 8
            out_ref[s * each : s * each + rows, first : first + width] = ref[
                :, columns(at_ref[s], width)
            ]
            first += width
        if pad:
            out_ref[s * each + rows : (s + 1) * each, :] = pad_ref[...]


def slice_pieces(at, *weights, pad=None):
    rows = weights[0].shape[0]
    cols = sum(w.shape[1] for w in weights) // 8
    extra = 0 if pad is None else pad.shape[0]
    operands = weights if pad is None else (*weights, pad)
    vmem = pl.BlockSpec(memory_space=pltpu.VMEM)
    return pl.pallas_call(
        lambda *refs: slice_kernel(*refs, pad=extra),
        in_specs=[pl.BlockSpec(memory_space=pltpu.SMEM)] + [vmem] * len(operands),
        out_specs=vmem,
        out_shape=jax.ShapeDtypeStruct((8 * (rows + extra), cols), jnp.bfloat16),
        cost_estimate=CHEAP,
        name="slice_pieces",
    )(at, *operands)


def assemble_kernel(at_ref, *refs):
    own = at_ref[8]
    for j, piece in enumerate(refs[:4]):
        refs[4][0, own ^ j] = piece[...]


def assemble(at, pieces, rows):
    count = at.shape[0] - 1
    total, cols = pieces[0].shape
    return pl.pallas_call(
        assemble_kernel,
        grid_spec=pltpu.PrefetchScalarGridSpec(
            num_scalar_prefetch=1,
            grid=(count,),
            in_specs=[pl.BlockSpec((rows, cols), lambda i, at: (i, 0))] * 4,
            out_specs=pl.BlockSpec((1, 4, rows, cols), lambda i, at: (at[i], 0, 0, 0)),
        ),
        out_shape=jax.ShapeDtypeStruct((count, 4, rows, cols), jnp.bfloat16),
        cost_estimate=CHEAP,
        name="assemble",
    )(at, *pieces).reshape(4 * total, cols)


def spun(rows, cosine, sine):
    return rows * cosine + pltpu.roll(rows, HEAD_SIZE // 2, 1) * sine


def project_kernel(at_ref, *refs, strips):
    token_refs, refs = refs[:strips], refs[strips:]
    pieces, refs = refs[:4], refs[4:]
    cos_ref, sin_ref, normed_ref, raw_ref, q_ref, kv_ref, matrix_ref, gains_ref = refs
    each = pieces[0].shape[0] // 8
    rows = matrix_ref.shape[0] // 32
    own = at_ref[8]
    gains = jnp.zeros(gains_ref.shape, jnp.float32)
    for s in range(8):
        for j in range(4):
            first = pl.multiple_of((at_ref[s] * 4 + (own ^ j)) * rows, rows)
            matrix_ref[pl.ds(first, rows), :] = pieces[j][s * each : s * each + rows, :]
            gains += pieces[j][s * each + rows : (s + 1) * each, :].astype(jnp.float32)
    gains_ref[...] = gains
    width = gains.shape[1]
    first = 0
    for ref in token_refs:
        block = ref[...].astype(jnp.float32)
        block = block * inverse_rms(block)
        here = slice(first, first + ref.shape[0])
        for i in range(block.shape[1] // width):
            cols = slice(i * width, (i + 1) * width)
            normed_ref[here, cols] = (block[:, cols] * gains[i : i + 1]).astype(jnp.bfloat16)
        first += ref.shape[0]
    query_gain, key_gain = gains[8:9, :HEAD_SIZE], gains[8:9, HEAD_SIZE : 2 * HEAD_SIZE]
    query_cols = q_ref.shape[1]
    step = 256
    for first in range(0, q_ref.shape[0], step):
        here = slice(first, first + step)
        raw = jnp.dot(normed_ref[here, :], matrix_ref[...], preferred_element_type=jnp.float32)
        raw_ref[here, :] = raw
        cosine, sine = cos_ref[here, :], sin_ref[here, :]
        for col in range(0, query_cols + HEAD_SIZE, HEAD_SIZE):
            part = raw[:, col : col + HEAD_SIZE]
            if col < query_cols:
                part = spun(part * inverse_rms(part) * query_gain, cosine, sine)
                part = part * (LOG2E / math.sqrt(HEAD_SIZE))
                q_ref[here, col : col + HEAD_SIZE] = part.astype(jnp.bfloat16)
            else:
                part = spun(part * inverse_rms(part) * key_gain, cosine, sine)
                kv_ref[here, :HEAD_SIZE] = part.astype(jnp.bfloat16)
        kv_ref[here, HEAD_SIZE:] = raw[:, query_cols + HEAD_SIZE :].astype(jnp.bfloat16)


def project(at, strips, pieces, cosine, sine, query_cols, pad):
    rows = sum(strip.shape[0] for strip in strips)
    width = strips[0].shape[1]
    cols = pieces[0].shape[1]
    vmem = pl.BlockSpec(memory_space=pltpu.VMEM)
    operands = (*strips, *pieces, cosine, sine)
    narrow, wide = jnp.bfloat16, jnp.float32
    return pl.pallas_call(
        lambda *refs: project_kernel(*refs, strips=len(strips)),
        in_specs=[pl.BlockSpec(memory_space=pltpu.SMEM)] + [vmem] * len(operands),
        out_specs=[vmem] * 6,
        out_shape=[
            jax.ShapeDtypeStruct((rows, width), narrow),
            jax.ShapeDtypeStruct((rows, cols), wide),
            jax.ShapeDtypeStruct((rows, query_cols), narrow),
            jax.ShapeDtypeStruct((rows, 2 * HEAD_SIZE), narrow),
            jax.ShapeDtypeStruct((width, cols), narrow),
            jax.ShapeDtypeStruct((pad, cols), wide),
        ],
        cost_estimate=LONG,
        name="project",
    )(at, *operands)


def project_back_kernel(
    dq_ref, dkv_ref, raw_ref, head_gain_ref, cos_ref, sin_ref, matrix_ref,
    grad_ref, part_ref, gain_ref,
):
    query_cols = dq_ref.shape[1]
    step = 256
    gain_ref[...] = jnp.zeros_like(gain_ref)
    for first in range(0, dq_ref.shape[0], step):
        here = slice(first, first + step)
        cosine, sine = cos_ref[here, :], sin_ref[here, :]
        for col in range(0, query_cols + HEAD_SIZE, HEAD_SIZE):
            cols = slice(col, col + HEAD_SIZE)
            which = 0 if col < query_cols else 1
            grads = dkv_ref[here, :HEAD_SIZE] if which else dq_ref[here, cols]
            raw = raw_ref[here, cols]
            rho = inverse_rms(raw)
            unit = raw * rho
            turned = spun(grads.astype(jnp.float32), cosine, -sine)
            gain_ref[which : which + 1, :] += jnp.sum(turned * unit, axis=0, keepdims=True)
            scaled = turned * head_gain_ref[which : which + 1]
            back = rho * (scaled - unit * jnp.mean(unit * scaled, axis=-1, keepdims=True))
            grad_ref[here, cols] = back.astype(jnp.bfloat16)
        grad_ref[here, query_cols + HEAD_SIZE :] = dkv_ref[here, HEAD_SIZE:]
        part_ref[here, :] = lax.dot_general(
            grad_ref[here, :], matrix_ref[...], ALONG, preferred_element_type=jnp.float32
        ).astype(jnp.bfloat16)


def project_back(query_grads, kv_grads, raw, head_gains, cosine, sine, matrix):
    rows, cols = raw.shape
    vmem = pl.BlockSpec(memory_space=pltpu.VMEM)
    return pl.pallas_call(
        project_back_kernel,
        in_specs=[vmem] * 7,
        out_specs=[vmem] * 3,
        out_shape=[
            jax.ShapeDtypeStruct((rows, cols), jnp.bfloat16),
            jax.ShapeDtypeStruct((rows, matrix.shape[0]), jnp.bfloat16),
            jax.ShapeDtypeStruct((8, HEAD_SIZE), jnp.float32),
        ],
        cost_estimate=LONG,
        name="project_back",
    )(query_grads, kv_grads, raw, head_gains, cosine, sine, matrix)


def dots(lefts, rights, dims):
    return sum(
        lax.dot_general(left[...], right[...], dims, preferred_element_type=jnp.float32)
        for left, right in zip(lefts, rights)
    )


def weight_grads_kernel(at_ref, *refs, groups, rows):
    own_ref, far_ref, sent_ref, held = refs[-4:]
    own = at_ref[8]
    sums = dots(refs[:groups], refs[groups : 2 * groups], DOWN)
    held[...] = sums.astype(jnp.bfloat16).reshape(held.shape)
    own_ref[:rows, :] = held[own]
    far_ref[:rows, :] = held[own ^ 2]
    sent_ref[0, :rows] = held[own ^ 1]
    sent_ref[1, :rows] = held[own ^ 3]
    if own_ref.shape[0] > rows:
        pad = refs[2 * groups][...]
        own_ref[rows:, :] = pad
        far_ref[rows:, :] = pad
        sent_ref[0, rows:] = pad
        sent_ref[1, rows:] = pad


def weight_grads(at, lefts, rights, rows, pad=None):
    count = at.shape[0] - 1
    cols = rights[0].shape[1]
    pads = [] if pad is None else [pad]
    each = rows + sum(p.shape[0] for p in pads)
    part = pl.BlockSpec((each, cols), lambda i, at: (i, 0))
    shape = jax.ShapeDtypeStruct((count * each, cols), jnp.bfloat16)
    own, far, sent = pl.pallas_call(
        lambda *refs: weight_grads_kernel(*refs, groups=len(lefts), rows=rows),
        grid_spec=pltpu.PrefetchScalarGridSpec(
            num_scalar_prefetch=1,
            grid=(count,),
            in_specs=[
                pl.BlockSpec((left.shape[0], 4 * rows), lambda i, at: (0, at[i]))
                for left in lefts
            ]
            + [pl.BlockSpec(right.shape, lambda i, at: (0, 0)) for right in (*rights, *pads)],
            out_specs=[part, part, pl.BlockSpec((2, each, cols), lambda i, at: (0, i, 0))],
            scratch_shapes=[pltpu.VMEM((4, rows, cols), jnp.bfloat16)],
        ),
        out_shape=[
            shape, shape, jax.ShapeDtypeStruct((2, count * each, cols), jnp.bfloat16),
        ],
        cost_estimate=CHEAP,
        name="weight_grads",
    )(at, *lefts, *rights, *pads)
    return own, far, sent.reshape(2 * count * each, cols)


def row_grads_kernel(*refs, lefts):
    left_refs, right_refs, (out_ref, held) = refs[:lefts], refs[lefts:-2], refs[-2:]

    @pl.when(pl.program_id(0) == 0)
    def _():
        first = 0
        for ref in right_refs:
            held[first : first + ref.shape[0], :] = ref[...]
            first += ref.shape[0]

    sums, first = 0.0, 0
    for ref in left_refs:
        sums += lax.dot_general(
            ref[...],
            held[first : first + ref.shape[0], :],
            DOWN,
            preferred_element_type=jnp.float32,
        )
        first += ref.shape[0]
    out_ref[...] = sums.astype(jnp.bfloat16)


def row_grads(lefts, rights, block=256):
    out_rows, cols = lefts[0].shape[1], rights[0].shape[1]
    total = sum(left.shape[0] for left in lefts)
    return pl.pallas_call(
        lambda *refs: row_grads_kernel(*refs, lefts=len(lefts)),
        grid=(out_rows // block,),
        in_specs=[pl.BlockSpec((left.shape[0], block), lambda i: (0, i)) for left in lefts]
        + [pl.BlockSpec(right.shape, lambda i: (0, 0)) for right in rights],
        out_specs=pl.BlockSpec((block, cols), lambda i: (i, 0)),
        out_shape=jax.ShapeDtypeStruct((out_rows, cols), jnp.bfloat16),
        scratch_shapes=[pltpu.VMEM((total, cols), jnp.bfloat16)],
        cost_estimate=CHEAP,
        name="row_grads",
    )(*lefts, *rights)


def hidden_grads_kernel(*refs, strips):
    matrix_ref, outs, held = refs[strips], refs[strips + 1 : -1], refs[-1]

    @pl.when(pl.program_id(0) == 0)
    def _():
        first = 0
        for ref in refs[:strips]:
            held[first : first + ref.shape[0], :] = ref[...]
            first += ref.shape[0]

    first = 0
    for out in outs:
        out[...] = lax.dot_general(
            held[first : first + out.shape[0], :],
            matrix_ref[...],
            ALONG,
            preferred_element_type=jnp.float32,
        )
        first += out.shape[0]


def hidden_grads_of(strips, matrix, block=256):
    rows = [(last - first) * strips[0].shape[0] for first, last in GROUPS]
    cols = matrix.shape[0]
    return pl.pallas_call(
        lambda *refs: hidden_grads_kernel(*refs, strips=len(strips)),
        grid=(cols // block,),
        in_specs=[pl.BlockSpec(strip.shape, lambda i: (0, 0)) for strip in strips]
        + [pl.BlockSpec((block, matrix.shape[1]), lambda i: (i, 0))],
        out_specs=[pl.BlockSpec((n, block), lambda i: (0, i)) for n in rows],
        out_shape=[jax.ShapeDtypeStruct((n, cols), jnp.float32) for n in rows],
        scratch_shapes=[pltpu.VMEM((sum(rows), matrix.shape[1]), jnp.bfloat16)],
        cost_estimate=CHEAP,
        name="hidden_grads",
    )(*strips, matrix)


def lane_sums(block):
    return sum(block[:, i : i + 128] for i in range(0, block.shape[1], 128))


def widen(at, swap, *weights):
    rows, taken, count = weights[0].shape[0], [item[1:] for item in swap.taken], len(weights)
    pad = swap.rows - rows

    def widen_kernel(at_ref, *refs):
        piece_refs, refs = refs[: len(taken)], refs[len(taken) :]
        grads, sums_ref = refs[count : 2 * count], refs[2 * count]
        for ref in refs[2 * count :]:
            ref[...] = jnp.zeros_like(ref)
        for ref, (start, size, spot, top) in zip(piece_refs, taken):
            used = min(size, rows - top)
            here = slice(top, top + used)
            first = 0
            for weight, grad in zip(refs[:count], grads):
                width = weight.shape[1] // 8
                there = columns(at_ref[spot], width)
                block = ref[start : start + used, first : first + width].astype(jnp.float32)
                grad[here, there] = block
                sums_ref[here, :] += lane_sums(block * weight[here, there].astype(jnp.float32))
                first += width
            if used < size:
                refs[-1][...] += ref[start + used : start + size, :].astype(jnp.float32)

    vmem = pl.BlockSpec(memory_space=pltpu.VMEM)
    shapes = [w.shape for w in weights] + [(rows, 128)]
    if pad:
        shapes.append((pad, swap.taken[0][0].shape[1]))
    return pl.pallas_call(
        widen_kernel,
        grid=(1,),
        in_specs=[pl.BlockSpec(memory_space=pltpu.SMEM), *swap.specs()] + [vmem] * count,
        out_specs=[vmem] * len(shapes),
        out_shape=[jax.ShapeDtypeStruct(shape, jnp.float32) for shape in shapes],
        cost_estimate=CHEAP,
        name="widen",
    )(at, *swap.operands(), *weights)


def grouped(strips):
    return [
        jnp.concatenate(strips[a:b], axis=0) if b - a > 1 else strips[a] for a, b in GROUPS
    ]


def split_groups(groups, rows):
    return [
        group[i * rows : (i + 1) * rows]
        for group in groups
        for i in range(group.shape[0] // rows)
    ]


def gather_head(rows):
    return lax.all_gather(rows, "head", axis=0, tiled=True)


def scatter_head(rows):
    return lax.psum_scatter(rows, "head", scatter_dimension=0, tiled=True)


def inverse_rms(rows):
    return lax.rsqrt(jnp.mean(rows * rows, axis=-1, keepdims=True) + EPS)


def per_device(
    tokens,
    attention_norm,
    query_weight,
    key_projection,
    value_projection,
    query_norm,
    key_norm,
    output_weight,
    feedforward_norm,
    gate_weight,
    up_weight,
    down_weight,
    stretch_order,
    out_cotangent,
):
    blk_count = lax.axis_size("blk")
    head_count = lax.axis_size("head")
    head_index = lax.axis_index("head")
    blk_index = lax.axis_index("blk")
    narrow, wide = jnp.bfloat16, jnp.float32
    tokens, out_cotangent = tokens[0], out_cotangent[0]
    local_rows, model_width = tokens.shape
    group_rows = local_rows * blk_count
    weight_rows = query_weight.shape[0]
    ff_local = gate_weight.shape[1] // blk_count
    query_cols = QUERY_HEADS // blk_count * HEAD_SIZE
    attn_cols = query_cols + 2 * HEAD_SIZE
    device_count = blk_count * head_count
    strip_count = blk_count * head_count
    halves = strip_count // stretch_order.shape[1]
    ring_place = jnp.where(blk_index % 2 == 0, blk_index // 2, 7 - blk_index // 2)

    spot = (ring_place + jnp.arange(blk_count, dtype=jnp.int32)) % blk_count
    at = jnp.where(spot < 4, 2 * spot, 15 - 2 * spot).astype(jnp.int32)
    at_own = jnp.concatenate([at, head_index[None].astype(jnp.int32)])
    ring_spot = (ring_place + jnp.asarray(STRIPS, jnp.int32)) % blk_count
    strip_blk = jnp.where(ring_spot < 4, 2 * ring_spot, 15 - 2 * ring_spot)
    strip_head = head_index ^ jnp.asarray((0, 2, 1, 3), jnp.int32)
    strip = (strip_blk[None, :] * head_count + strip_head[:, None]).reshape(strip_count)
    slots = jnp.arange(stretch_order.shape[1], dtype=jnp.int32)
    held = jnp.sum(
        jnp.where((strip // halves)[:, None] == slots[None, :], stretch_order, 0), axis=1
    )
    strip_place = held * halves + strip % halves
    order = strip_place.astype(jnp.int32)
    place = strip_place[:blk_count].astype(jnp.int32)
    positions = (
        place[:, None] * local_rows + jnp.arange(local_rows, dtype=jnp.int32)[None, :]
    ).reshape(group_rows)
    phases = angles(positions, HEAD_SIZE)[:, 0, :]
    cosine, sine = jnp.cos(phases), jnp.sin(phases)
    cosine = jnp.concatenate([cosine, cosine], axis=1)
    sine = jnp.concatenate([-sine, sine], axis=1)

    small = query_norm.shape[0]
    number = blk_index * head_count + head_index
    pad = 16

    def placed(share):
        return jnp.where(
            jnp.arange(device_count, dtype=jnp.int32)[:, None] == number, share[None, :], 0
        ).reshape(-1)

    gains = jnp.concatenate(
        [placed(attention_norm), placed(feedforward_norm), placed(query_norm), placed(key_norm)]
    ).astype(narrow)
    gains = jnp.pad(gains, (0, pad * attn_cols - gains.shape[0])).reshape(pad, attn_cols)
    down_matrix = gather_head(down_weight)
    output_rows = gather_head(output_weight)

    attn_swap = Swap(
        slice_pieces(at, query_weight, key_projection, value_projection, pad=gains),
        weight_rows + pad,
    )
    token_ring = Gather(tokens)
    ff_slices = slice_pieces(at, gate_weight, up_weight)
    token_ring.go()
    attn_swap.go()
    hold((attn_swap,))
    attn_swap.go()
    hold((attn_swap,))
    attn_swap.go()
    hold((attn_swap,))
    attn_swap.go()
    own = hold((token_ring,), attn_swap.result())
    near, far = cross(own, 1), cross(own, 2)
    token_ring.go()
    ff_slices, cosine, sine = hold((token_ring,), ff_slices, cosine, sine)
    ff_swap, cotangent_ring = Swap(ff_slices, weight_rows), Gather(out_cotangent)
    token_ring.go()
    own, near, far = hold((token_ring,), own, near, far)
    both = cross(far, 1)
    token_ring.go()
    own, near, far, both = hold((token_ring, ff_swap), own, near, far, both)
    ff_swap.go()

    first_normed, attn_raw, query_rows, own, attn_matrix, gains = project(
        at_own, token_ring.strips(), (own, near, far, both), cosine, sine, query_cols, pad
    )
    gain_one = gains[:4].reshape(1, model_width)
    gain_two = gains[4:8].reshape(1, model_width)
    head_gains = jnp.pad(gains[8, : 2 * HEAD_SIZE].reshape(2, HEAD_SIZE), ((0, 6), (0, 0)))
    near, far = cross(own, 1), cross(own, 2)
    own, near, far = hold((ff_swap, cotangent_ring), own, near, far)
    both = cross(far, 1)
    ff_swap.go()
    cotangent_ring.go()
    kv = hold((), own, far, near, both)
    attended, lse = attend(place, order, query_rows, kv)

    def by_groups(rows):
        return [rows[a * local_rows : b * local_rows] for a, b in GROUPS]

    def by_strips(groups):
        return dict(zip(STRIPS, split_groups(groups, local_rows)))

    attended = hold((cotangent_ring, ff_swap), attended)
    branch_parts = [matmul(rows, output_rows).astype(narrow) for rows in by_groups(attended)]
    branch_ring = Scatter(by_strips(branch_parts))
    branch_ring.go()
    ff_swap.go()
    cotangent_ring.go()
    hold((branch_ring, cotangent_ring, ff_swap))
    branch_ring.go()
    ff_swap.go()
    ff_own = hold((), ff_swap.result())
    ff_near, ff_far = cross(ff_own, 1), cross(ff_own, 2)
    cotangent_ring.go()
    hold((branch_ring, cotangent_ring))
    branch_ring.go()
    cotangent_ring.go()
    cotangent_strips, down_matrix = hold(
        (branch_ring, cotangent_ring), cotangent_ring.strips(), down_matrix
    )
    branch_ring.go()
    hidden_grads = hidden_grads_of(cotangent_strips, down_matrix)
    hidden_grads, ff_near, ff_far = hold((branch_ring,), hidden_grads, ff_near, ff_far)
    ff_both = cross(ff_far, 1)
    tokens_wide = tokens.astype(wide)
    resid = tokens_wide + branch_ring.total()
    rho_two = inverse_rms(resid)
    unit_two = resid * rho_two

    second_ring = Gather((unit_two * gain_two).astype(narrow))
    second_groups, hidden_groups, ff_gradient_groups = [], [], []

    def feed_forward(index):
        rows = second_ring.group(index)
        ff_raw = matmul(rows, ff_matrix)
        gate, up_proj = ff_raw[:, :ff_local], ff_raw[:, ff_local:]
        sigma = jax.nn.sigmoid(gate)
        swish = gate * sigma
        hidden_gradient = hidden_grads[index]
        gate_gradient = hidden_gradient * up_proj * (sigma * (1.0 + gate * (1.0 - sigma)))
        hidden = (swish * up_proj).astype(narrow)
        gradient = jnp.concatenate([gate_gradient, hidden_gradient * swish], 1).astype(narrow)
        if index < 3:
            rows, hidden, gradient = hold((second_ring,), rows, hidden, gradient)
        second_groups.append(rows)
        hidden_groups.append(hidden)
        ff_gradient_groups.append(gradient)

    second_ring.go()
    ff_matrix = assemble(at_own, (ff_own, ff_near, ff_far, ff_both), weight_rows)
    ff_matrix = hold((second_ring,), ff_matrix)
    for index in range(3):
        second_ring.go()
        feed_forward(index)
    feed_forward(3)

    def back(index):
        return matmul(ff_gradient_groups[index], ff_matrix, ALONG).astype(narrow)

    def split(group):
        return [group[i : i + local_rows] for i in range(0, group.shape[0], local_rows)]

    parts = {4: back(3)}
    resid_ring = Scatter(parts)
    parts[3], parts[5] = split(hold((), back(2)))
    parts[2], parts[6] = split(hold((), back(1)))
    resid_ring.go()
    _, _, hidden_groups, cotangent_strips = hold(
        (resid_ring,), parts[2], parts[6], hidden_groups, cotangent_strips
    )
    resid_ring.go()
    down_gradient = row_grads(hidden_groups, cotangent_strips)
    back_zero, down_gradient, second_groups, ff_gradient_groups = hold(
        (resid_ring,), back(0), down_gradient, second_groups, ff_gradient_groups
    )
    down_gradient = scatter_head(down_gradient)
    parts[0], parts[1], parts[7] = split(back_zero)
    resid_ring.go()
    ff_own, ff_far, ff_sent = hold(
        (resid_ring,), *weight_grads(at_own, second_groups, ff_gradient_groups, weight_rows)
    )
    resid_ring.go()
    ff_own, ff_far = scatter_cross(ff_own, ff_far, ff_sent)
    ff_own, ff_far, hidden_groups = hold((resid_ring,), ff_own, ff_far, hidden_groups)
    ff_far = cross(ff_far, 2)
    scaled = gain_two * resid_ring.total()
    resid_gradient = out_cotangent.astype(wide) + rho_two * (
        scaled - unit_two * jnp.mean(unit_two * scaled, axis=-1, keepdims=True)
    )

    grad_ring = Gather(resid_gradient.astype(narrow))
    grad_groups, attended_grads = [], []

    def attention_back(index):
        rows = grad_ring.group(index)
        grads = matmul(rows, output_rows, ALONG).astype(narrow)
        if index < 3:
            rows, grads = hold((grad_ring,), rows, grads)
        grad_groups.append(rows)
        attended_grads.append(grads)

    grad_ring.go()
    out_parts = [matmul(rows, down_matrix).astype(narrow) for rows in hidden_groups]
    out_parts = hold((grad_ring,), *out_parts)
    out_ring = Scatter(by_strips(out_parts))
    grad_ring.go()
    hold((grad_ring,))
    grad_ring.go()
    attention_back(0)
    hold((out_ring, grad_ring))
    out_ring.go()
    grad_ring.go()
    attention_back(1)
    attention_back(2)
    ff_swap = Swap(add(ff_own, ff_far), weight_rows)
    hold((grad_ring, ff_swap, out_ring))
    out_ring.go()
    ff_swap.go()
    attention_back(3)
    query_grads, kv_own, kv_far, kv_sent = attend_back(
        place, order, query_rows, attended_grads, attended, lse, kv
    )
    query_grads, kv_own, kv_far, kv_sent, grad_groups, attended = hold(
        (out_ring, ff_swap), query_grads, kv_own, kv_far, kv_sent, grad_groups, attended
    )
    out_ring.go()
    kv_own, kv_far = scatter_cross(kv_own, kv_far, kv_sent)
    output_weight_gradient = row_grads([attended], grad_groups)
    kv_own, kv_far, output_weight_gradient = hold(
        (out_ring, ff_swap), kv_own, kv_far, output_weight_gradient
    )
    ff_swap.go()
    kv_grads = hold((ff_swap,), add(kv_own, cross(kv_far, 2)))
    ff_swap.go()
    attn_gradient, first_parts, gain_sums = project_back(
        query_grads, kv_grads, attn_raw, head_gains, cosine, sine, attn_matrix
    )
    gain_sums = jnp.pad(
        gain_sums[:2].reshape(1, 2 * HEAD_SIZE).astype(narrow),
        ((0, pad - 1), (0, attn_cols - 2 * HEAD_SIZE)),
    )
    attn_gradient, first_parts, gain_sums, output_weight_gradient = hold(
        (ff_swap,), attn_gradient, first_parts, gain_sums, output_weight_gradient
    )
    token_ring = Scatter(by_strips(by_groups(first_parts)))
    token_ring.go()
    ff_swap.go()
    attn_own, attn_far, attn_sent = weight_grads(
        at_own, [first_normed], [attn_gradient], weight_rows, gain_sums
    )
    attn_own, attn_far, attn_sent = hold(
        (token_ring, ff_swap), attn_own, attn_far, attn_sent
    )
    token_ring.go()
    attn_own, attn_far = hold((), *scatter_cross(attn_own, attn_far, attn_sent))
    attn_far = cross(attn_far, 2)
    gate_weight_gradient, up_weight_gradient, ff_sums = widen(at, ff_swap, gate_weight, up_weight)
    gate_weight_gradient, up_weight_gradient, ff_sums = hold(
        (token_ring,), gate_weight_gradient, up_weight_gradient, ff_sums
    )
    token_ring.go()
    feedforward_norm_gradient = jnp.sum(ff_sums, axis=1) / feedforward_norm.astype(wide)
    attn_swap = Swap(add(attn_own, attn_far), weight_rows + pad)
    feedforward_norm_gradient, down_gradient, output_weight_gradient = hold(
        (token_ring, attn_swap),
        feedforward_norm_gradient, down_gradient.astype(wide), output_weight_gradient,
    )
    output_weight_gradient = scatter_head(output_weight_gradient).astype(wide)
    attn_swap.go()
    token_ring.go()
    hold((token_ring, attn_swap, out_ring))
    attn_swap.go()
    out_ring.go()
    hold((attn_swap,))
    attn_swap.go()
    hold((attn_swap,))
    attn_swap.go()
    layer_out = (resid + out_ring.total()).astype(narrow)
    query_weight_gradient, key_weight_gradient, value_weight_gradient, norm_sums, gain_sums = widen(
        at, attn_swap, query_weight, key_projection, value_projection
    )
    attention_norm_gradient = jnp.sum(norm_sums, axis=1) / attention_norm.astype(wide)
    gain_sums = gain_sums[0, : 2 * HEAD_SIZE].reshape(2, HEAD_SIZE)
    gain_sums = lax.dynamic_slice_in_dim(gain_sums, number * small, small, 1)
    rho_one = inverse_rms(tokens_wide)
    unit_one = tokens_wide * rho_one
    scaled = gain_one * token_ring.total()
    tokens_gradient = resid_gradient + rho_one * (
        scaled - unit_one * jnp.mean(unit_one * scaled, axis=-1, keepdims=True)
    )
    return (
        layer_out[None],
        tokens_gradient.astype(narrow)[None],
        attention_norm_gradient,
        query_weight_gradient,
        key_weight_gradient,
        value_weight_gradient,
        gain_sums[0],
        gain_sums[1],
        output_weight_gradient,
        feedforward_norm_gradient,
        gate_weight_gradient,
        up_weight_gradient,
        down_gradient,
    )


def solution(mesh):
    placed = (
        P(None, ("blk", "head"), None),
        P(("blk", "head")),
        P(("blk", "head"), None),
        P(("blk", "head"), None),
        P(("blk", "head"), None),
        P(("blk", "head")),
        P(("blk", "head")),
        P(("blk", "head"), None),
        P(("blk", "head")),
        P(("blk", "head"), None),
        P(("blk", "head"), None),
        P(("blk", "head"), None),
        P(),
        P(None, ("blk", "head"), None),
    )
    fits = mesh.shape["blk"] == KEY_VALUE_HEADS and mesh.shape["head"] == 4
    return jax.shard_map(
        per_device if fits else per_device_by_tokens,
        mesh=mesh,
        in_specs=placed,
        out_specs=(
            P(None, ("blk", "head"), None),
            P(None, ("blk", "head"), None),
            P(("blk", "head")),
            P(("blk", "head"), None),
            P(("blk", "head"), None),
            P(("blk", "head"), None),
            P(("blk", "head")),
            P(("blk", "head")),
            P(("blk", "head"), None),
            P(("blk", "head")),
            P(("blk", "head"), None),
            P(("blk", "head"), None),
            P(("blk", "head"), None),
        ),
        check_vma=False,
    )
```

```python
import math

import jax
import jax.numpy as jnp
from jax import lax
from jax.experimental import pallas as pl
from jax.experimental.pallas import tpu as pltpu
from jax.sharding import PartitionSpec as P

QUERY_HEADS = 16
KEY_VALUE_HEADS = 8
HEAD_SIZE = 128


EPS = 1e-06
NEG = -1e30
ROPE_BASE = 1000000.0


def passed_along(value, axis, by):
    count = lax.axis_size(axis)
    return lax.ppermute(value, axis, [(i, (i + by) % count) for i in range(count)])


def norm_rows(inputs, norm_gain):
    return inputs * lax.rsqrt(jnp.mean(inputs * inputs, axis=-1, keepdims=True) + EPS) * norm_gain


def rotary(inputs, phases):
    half_width = inputs.shape[-1] // 2
    cosine = jnp.cos(phases)
    sine_term = jnp.sin(phases)
    first_half = inputs[..., :half_width]
    second_half = inputs[..., half_width:]
    return jnp.concatenate(
        [
            first_half * cosine - second_half * sine_term,
            second_half * cosine + first_half * sine_term,
        ],
        axis=-1,
    )


def angles(positions, head_width):
    half_width = head_width // 2
    frequency = jnp.exp(
        jnp.arange(half_width, dtype=jnp.float32) * (-2.0 * math.log(ROPE_BASE) / head_width)
    )
    return positions.astype(jnp.float32)[..., None, None] * frequency


def token_positions(stretch_order, first_row, row_count, stretch_rows):
    row_index = first_row + jnp.arange(row_count, dtype=jnp.int32)
    slot_index = row_index // stretch_rows
    matches = slot_index[:, None] == jnp.arange(stretch_order.shape[1], dtype=jnp.int32)[None, :]
    picked = jnp.sum(jnp.where(matches[None], stretch_order[:, None, :], 0), axis=-1)
    return picked * stretch_rows + row_index % stretch_rows


def per_device_by_tokens(
    tokens,
    attention_norm,
    query_weight,
    key_projection,
    value_projection,
    query_norm,
    key_norm,
    output_weight,
    feedforward_norm,
    gate_weight,
    up_weight,
    down_weight,
    stretch_order,
    out_cotangent,
):
    count_of_heads = lax.axis_size("head")
    span_count = lax.axis_size("blk")
    span_index = lax.axis_index("blk")
    head_index = lax.axis_index("head")
    sequence_total = tokens.shape[0]
    local_rows = tokens.shape[1]
    group_rows = local_rows * count_of_heads
    stretch_rows = group_rows // 2
    heads_shared = KEY_VALUE_HEADS // count_of_heads
    heads_per_group = QUERY_HEADS // KEY_VALUE_HEADS
    score_scale = 1.0 / math.sqrt(HEAD_SIZE)
    gain_one, query_matrix, key_matrix, value_matrix, query_gain, key_gain, output_matrix = (
        lax.all_gather(attention_norm, ("blk", "head"), axis=0, tiled=True),
        lax.all_gather(query_weight, ("blk", "head"), axis=0, tiled=True),
        lax.all_gather(key_projection, ("blk", "head"), axis=0, tiled=True),
        lax.all_gather(value_projection, ("blk", "head"), axis=0, tiled=True),
        lax.all_gather(query_norm, ("blk", "head"), axis=0, tiled=True),
        lax.all_gather(key_norm, ("blk", "head"), axis=0, tiled=True),
        lax.all_gather(output_weight, ("blk", "head"), axis=0, tiled=True),
    )
    gain_two, gate_matrix, up_matrix, down_matrix = (
        lax.all_gather(feedforward_norm, ("blk", "head"), axis=0, tiled=True),
        lax.all_gather(gate_weight, ("blk", "head"), axis=0, tiled=True),
        lax.all_gather(up_weight, ("blk", "head"), axis=0, tiled=True),
        lax.all_gather(down_weight, ("blk", "head"), axis=0, tiled=True),
    )
    gain_one = gain_one.astype(jnp.float32)
    gain_two = gain_two.astype(jnp.float32)
    query_gain = query_gain.astype(jnp.float32)
    key_gain = key_gain.astype(jnp.float32)
    own_first = (span_index * count_of_heads + head_index) * local_rows
    own_pos = token_positions(stretch_order, own_first, local_rows, stretch_rows)
    group_pos = token_positions(stretch_order, span_index * group_rows, group_rows, stretch_rows)
    phases = angles(own_pos, HEAD_SIZE)
    tokens_wide = tokens.astype(jnp.float32)
    first_normed, norm_one_back = jax.vjp(norm_rows, tokens_wide, gain_one)
    first_normed = first_normed.astype(jnp.bfloat16)
    query_raw = jnp.einsum(
        "btd,de->bte", first_normed, query_matrix, preferred_element_type=jnp.float32
    ).reshape(sequence_total, local_rows, QUERY_HEADS, HEAD_SIZE)
    key_unnormed = jnp.einsum(
        "btd,de->bte", first_normed, key_matrix, preferred_element_type=jnp.float32
    ).reshape(sequence_total, local_rows, KEY_VALUE_HEADS, HEAD_SIZE)
    value_tokens = (
        jnp.einsum("btd,de->bte", first_normed, value_matrix, preferred_element_type=jnp.float32)
        .astype(jnp.bfloat16)
        .reshape(sequence_total, local_rows, KEY_VALUE_HEADS, HEAD_SIZE)
    )

    def heads_local(query_in, key_in, query_scale, key_scale):
        return (
            rotary(norm_rows(query_in, query_scale), phases),
            rotary(norm_rows(key_in, key_scale), phases),
        )

    (query_tokens, key_tokens), heads_back = jax.vjp(
        heads_local, query_raw, key_unnormed, query_gain, key_gain
    )
    query_tokens = query_tokens.astype(jnp.bfloat16)
    key_tokens = key_tokens.astype(jnp.bfloat16)
    query_group, key_group, value_group = (
        lax.all_to_all(query_tokens, "head", split_axis=2, concat_axis=1, tiled=True),
        lax.all_to_all(key_tokens, "head", split_axis=2, concat_axis=1, tiled=True),
        lax.all_to_all(value_tokens, "head", split_axis=2, concat_axis=1, tiled=True),
    )
    query_five = query_group.reshape(
        sequence_total, group_rows, heads_shared, heads_per_group, HEAD_SIZE
    )

    def block_update(carry, key_block, value_block, key_pos):
        run_max, run_sum, run_total = carry
        scores = (
            jnp.einsum(
                "bqkgd,bckd->bkgqc", query_five, key_block, preferred_element_type=jnp.float32
            )
            * score_scale
        )
        allowed = key_pos[:, None, None, None, :] <= group_pos[:, None, None, :, None]
        scores = jnp.where(allowed, scores, NEG)
        new_max = jnp.maximum(run_max, jnp.max(scores, axis=-1))
        exponent = jnp.where(allowed, jnp.exp(scores - new_max[..., None]), 0.0)
        factor = jnp.exp(run_max - new_max)
        new_sum = run_sum * factor + jnp.sum(exponent, axis=-1)
        new_total = run_total * factor[..., None] + jnp.einsum(
            "bkgqc,bckd->bkgqd",
            exponent.astype(jnp.bfloat16),
            value_block,
            preferred_element_type=jnp.float32,
        )
        return (new_max, new_sum, new_total)

    def fold_update(carry, key_block, value_block, key_pos):
        result = block_update(carry, key_block, value_block, key_pos)
        return result

    stat_shape = (sequence_total, heads_shared, heads_per_group, group_rows)
    start_state = (
        jnp.full(stat_shape, NEG, jnp.float32),
        jnp.zeros(stat_shape, jnp.float32),
        jnp.zeros(stat_shape + (HEAD_SIZE,), jnp.float32),
    )
    key_piece = lax.all_gather(key_group, "blk", axis=1, tiled=True)
    value_piece = lax.all_gather(value_group, "blk", axis=1, tiled=True)
    piece_rows = key_piece.shape[1]
    block_len = math.gcd(group_rows, piece_rows)

    def inner(block_number, carry_in):
        offset = block_number * block_len
        key_block = lax.dynamic_slice_in_dim(key_piece, offset, block_len, 1)
        value_block = lax.dynamic_slice_in_dim(value_piece, offset, block_len, 1)
        key_pos = token_positions(stretch_order, offset, block_len, stretch_rows)
        return fold_update(carry_in, key_block, value_block, key_pos)

    run_max, run_sum, run_total = lax.fori_loop(0, piece_rows // block_len, inner, start_state)
    log_total = run_max + jnp.log(run_sum)
    attended_five = run_total / run_sum[..., None]
    attended_group = (
        jnp.transpose(attended_five, (0, 3, 1, 2, 4))
        .reshape(sequence_total, group_rows, heads_shared * heads_per_group, HEAD_SIZE)
        .astype(jnp.bfloat16)
    )
    attended_tokens = lax.all_to_all(
        attended_group, "head", split_axis=1, concat_axis=2, tiled=True
    ).reshape(sequence_total, local_rows, QUERY_HEADS * HEAD_SIZE)
    branch = jnp.einsum(
        "bte,ed->btd", attended_tokens, output_matrix, preferred_element_type=jnp.float32
    )
    resid = tokens_wide + branch
    normed_two, norm_two_back = jax.vjp(norm_rows, resid, gain_two)
    normed_two = normed_two.astype(jnp.bfloat16)
    gate = jnp.einsum("btd,df->btf", normed_two, gate_matrix, preferred_element_type=jnp.float32)
    up_proj = jnp.einsum("btd,df->btf", normed_two, up_matrix, preferred_element_type=jnp.float32)

    def swish_product(gate_in, up_in):
        return jax.nn.silu(gate_in) * up_in

    hidden, swish_back = jax.vjp(swish_product, gate, up_proj)
    hidden = hidden.astype(jnp.bfloat16)
    layer_out = (
        resid + jnp.einsum("btf,fd->btd", hidden, down_matrix, preferred_element_type=jnp.float32)
    ).astype(jnp.bfloat16)
    gain_again, gate_matrix, up_matrix, down_matrix = (
        lax.all_gather(feedforward_norm, ("blk", "head"), axis=0, tiled=True),
        lax.all_gather(gate_weight, ("blk", "head"), axis=0, tiled=True),
        lax.all_gather(up_weight, ("blk", "head"), axis=0, tiled=True),
        lax.all_gather(down_weight, ("blk", "head"), axis=0, tiled=True),
    )
    down_gradient = jnp.einsum(
        "btf,btd->fd", hidden, out_cotangent, preferred_element_type=jnp.float32
    )
    hidden_gradient = jnp.einsum(
        "btd,fd->btf", out_cotangent, down_matrix, preferred_element_type=jnp.float32
    )
    gate_gradient, up_gradient = swish_back(hidden_gradient)
    gate_gradient = gate_gradient.astype(jnp.bfloat16)
    up_gradient = up_gradient.astype(jnp.bfloat16)
    gate_matrix_gradient = jnp.einsum(
        "btd,btf->df", normed_two, gate_gradient, preferred_element_type=jnp.float32
    )
    up_matrix_gradient = jnp.einsum(
        "btd,btf->df", normed_two, up_gradient, preferred_element_type=jnp.float32
    )
    normed_two_gradient = jnp.einsum(
        "btf,df->btd", gate_gradient, gate_matrix, preferred_element_type=jnp.float32
    ) + jnp.einsum("btf,df->btd", up_gradient, up_matrix, preferred_element_type=jnp.float32)
    resid_part, gain_two_gradient = norm_two_back(normed_two_gradient)
    resid_gradient = out_cotangent.astype(jnp.float32) + resid_part
    feedforward_sums = (
        lax.psum_scatter(gain_two_gradient, ("blk", "head"), scatter_dimension=0, tiled=True),
        lax.psum_scatter(gate_matrix_gradient, ("blk", "head"), scatter_dimension=0, tiled=True),
        lax.psum_scatter(up_matrix_gradient, ("blk", "head"), scatter_dimension=0, tiled=True),
        lax.psum_scatter(down_gradient, ("blk", "head"), scatter_dimension=0, tiled=True),
    )
    gain_again, query_matrix, key_matrix, value_matrix, query_again, key_again, output_matrix = (
        lax.all_gather(attention_norm, ("blk", "head"), axis=0, tiled=True),
        lax.all_gather(query_weight, ("blk", "head"), axis=0, tiled=True),
        lax.all_gather(key_projection, ("blk", "head"), axis=0, tiled=True),
        lax.all_gather(value_projection, ("blk", "head"), axis=0, tiled=True),
        lax.all_gather(query_norm, ("blk", "head"), axis=0, tiled=True),
        lax.all_gather(key_norm, ("blk", "head"), axis=0, tiled=True),
        lax.all_gather(output_weight, ("blk", "head"), axis=0, tiled=True),
    )
    branch_gradient = resid_gradient.astype(jnp.bfloat16)
    output_matrix_gradient = jnp.einsum(
        "bte,btd->ed", attended_tokens, branch_gradient, preferred_element_type=jnp.float32
    )
    attended_gradient = (
        jnp.einsum(
            "btd,ed->bte", branch_gradient, output_matrix, preferred_element_type=jnp.float32
        )
        .astype(jnp.bfloat16)
        .reshape(sequence_total, local_rows, QUERY_HEADS, HEAD_SIZE)
    )
    attended_grad_group = lax.all_to_all(
        attended_gradient, "head", split_axis=2, concat_axis=1, tiled=True
    ).reshape(sequence_total, group_rows, heads_shared, heads_per_group, HEAD_SIZE)
    delta = jnp.sum(
        jnp.transpose(attended_grad_group.astype(jnp.float32), (0, 2, 3, 1, 4)) * attended_five,
        axis=-1,
    )

    def block_grads(sums_in, key_current, value_current, key_pos):
        key_sum, value_sum, query_sum = sums_in
        scores = (
            jnp.einsum(
                "bqkgd,bckd->bkgqc", query_five, key_current, preferred_element_type=jnp.float32
            )
            * score_scale
        )
        allowed = key_pos[:, None, None, None, :] <= group_pos[:, None, None, :, None]
        weights = jnp.where(allowed, jnp.exp(scores - log_total[..., None]), 0.0)
        probs = weights.astype(jnp.bfloat16)
        value_sum = value_sum + jnp.einsum(
            "bkgqc,bqkgd->bckd", probs, attended_grad_group, preferred_element_type=jnp.float32
        )
        probs_gradient = jnp.einsum(
            "bqkgd,bckd->bkgqc",
            attended_grad_group,
            value_current,
            preferred_element_type=jnp.float32,
        )
        scores_gradient = (weights * (probs_gradient - delta[..., None])).astype(jnp.bfloat16)
        query_sum = (
            query_sum
            + jnp.einsum(
                "bkgqc,bckd->bqkgd",
                scores_gradient,
                key_current,
                preferred_element_type=jnp.float32,
            )
            * score_scale
        )
        key_sum = (
            key_sum
            + jnp.einsum(
                "bkgqc,bqkgd->bckd", scores_gradient, query_five, preferred_element_type=jnp.float32
            )
            * score_scale
        )
        return (key_sum, value_sum, query_sum)

    def pass_step(step_index, carry):
        key_current, value_current, key_sum, value_sum, query_sum = carry
        anchor = (span_index - step_index) % span_count
        key_pos = token_positions(stretch_order, anchor * group_rows, group_rows, stretch_rows)
        key_sum, value_sum, query_sum = block_grads(
            (key_sum, value_sum, query_sum), key_current, value_current, key_pos
        )
        key_current, value_current = passed_along((key_current, value_current), "blk", 1)
        key_sum, value_sum = (
            passed_along(key_sum.astype(jnp.bfloat16), "blk", 1).astype(key_sum.dtype),
            passed_along(value_sum.astype(jnp.bfloat16), "blk", 1).astype(value_sum.dtype),
        )
        return (key_current, value_current, key_sum, value_sum, query_sum)

    kv_zeros = jnp.zeros((sequence_total, group_rows, heads_shared, HEAD_SIZE), jnp.float32)
    query_zeros = jnp.zeros(
        (sequence_total, group_rows, heads_shared, heads_per_group, HEAD_SIZE), jnp.float32
    )
    final_state = lax.fori_loop(
        0, span_count, pass_step, (key_group, value_group, kv_zeros, kv_zeros, query_zeros)
    )
    key_grad_group = final_state[2].astype(jnp.bfloat16)
    value_grad_group = final_state[3].astype(jnp.bfloat16)
    query_grad_group = (
        final_state[4]
        .astype(jnp.bfloat16)
        .reshape(sequence_total, group_rows, heads_shared * heads_per_group, HEAD_SIZE)
    )
    query_grad_tokens, key_grad_tokens, value_gradient_tokens = (
        lax.all_to_all(query_grad_group, "head", split_axis=1, concat_axis=2, tiled=True),
        lax.all_to_all(key_grad_group, "head", split_axis=1, concat_axis=2, tiled=True),
        lax.all_to_all(value_grad_group, "head", split_axis=1, concat_axis=2, tiled=True),
    )
    query_raw_gradient, key_unnormed_gradient, query_gain_gradient, key_gain_gradient = heads_back(
        (query_grad_tokens.astype(jnp.float32), key_grad_tokens.astype(jnp.float32))
    )
    query_raw_gradient = query_raw_gradient.astype(jnp.bfloat16).reshape(
        sequence_total, local_rows, QUERY_HEADS * HEAD_SIZE
    )
    key_unnormed_gradient = key_unnormed_gradient.astype(jnp.bfloat16).reshape(
        sequence_total, local_rows, KEY_VALUE_HEADS * HEAD_SIZE
    )
    value_unnormed_gradient = value_gradient_tokens.reshape(
        sequence_total, local_rows, KEY_VALUE_HEADS * HEAD_SIZE
    )
    query_matrix_gradient = jnp.einsum(
        "btd,bte->de", first_normed, query_raw_gradient, preferred_element_type=jnp.float32
    )
    key_matrix_gradient = jnp.einsum(
        "btd,bte->de", first_normed, key_unnormed_gradient, preferred_element_type=jnp.float32
    )
    value_matrix_gradient = jnp.einsum(
        "btd,bte->de", first_normed, value_unnormed_gradient, preferred_element_type=jnp.float32
    )
    normed_one_gradient = jnp.einsum(
        "bte,de->btd", query_raw_gradient, query_matrix, preferred_element_type=jnp.float32
    )
    normed_one_gradient = normed_one_gradient + jnp.einsum(
        "bte,de->btd", key_unnormed_gradient, key_matrix, preferred_element_type=jnp.float32
    )
    normed_one_gradient = normed_one_gradient + jnp.einsum(
        "bte,de->btd", value_unnormed_gradient, value_matrix, preferred_element_type=jnp.float32
    )
    token_part, gain_one_gradient = norm_one_back(normed_one_gradient)
    tokens_gradient = (resid_gradient + token_part).astype(jnp.bfloat16)
    attention_sums = (
        lax.psum_scatter(gain_one_gradient, ("blk", "head"), scatter_dimension=0, tiled=True),
        lax.psum_scatter(query_matrix_gradient, ("blk", "head"), scatter_dimension=0, tiled=True),
        lax.psum_scatter(key_matrix_gradient, ("blk", "head"), scatter_dimension=0, tiled=True),
        lax.psum_scatter(value_matrix_gradient, ("blk", "head"), scatter_dimension=0, tiled=True),
        lax.psum_scatter(query_gain_gradient, ("blk", "head"), scatter_dimension=0, tiled=True),
        lax.psum_scatter(key_gain_gradient, ("blk", "head"), scatter_dimension=0, tiled=True),
        lax.psum_scatter(output_matrix_gradient, ("blk", "head"), scatter_dimension=0, tiled=True),
    )
    return (
        layer_out,
        tokens_gradient,
        attention_sums[0],
        attention_sums[1],
        attention_sums[2],
        attention_sums[3],
        attention_sums[4],
        attention_sums[5],
        attention_sums[6],
        feedforward_sums[0],
        feedforward_sums[1],
        feedforward_sums[2],
        feedforward_sums[3],
    )


LOG2E = math.log2(math.e)
STRIP = 128
CHUNK = 512
ALONG = (((1,), (1,)), ((), ()))
DOWN = (((0,), (0,)), ((), ()))


def two_heads(block):
    return jnp.concatenate([block[:, :HEAD_SIZE], block[:, HEAD_SIZE:]], axis=0)


def side_by_side(rows):
    half = rows.shape[0] // 2
    return jnp.concatenate([rows[:half], rows[half:]], axis=1)


CHEAP = pl.CostEstimate(flops=1, bytes_accessed=1, transcendentals=0)
LONG = pl.CostEstimate(flops=3 * 10**10, bytes_accessed=1 << 25, transcendentals=0)


def sort_strips(order_ref, kv_refs, keys, values):
    per = kv_refs[0].shape[0] // STRIP
    for j, ref in enumerate(kv_refs):
        for i in range(per):
            target = pl.multiple_of(order_ref[j * per + i] * STRIP, STRIP)
            here = slice(i * STRIP, (i + 1) * STRIP)
            keys[pl.ds(target, STRIP), :] = ref[here, :HEAD_SIZE]
            values[pl.ds(target, STRIP), :HEAD_SIZE] = ref[here, HEAD_SIZE:]


def attend_kernel(place_ref, order_ref, q_ref, *refs):
    kv_refs, (out_ref, lse_ref, keys, values) = refs[:4], refs[4:]
    step = pl.program_id(0)

    @pl.when(step == 0)
    def _():
        values[:, HEAD_SIZE:] = jnp.ones((values.shape[0], HEAD_SIZE), jnp.bfloat16)
        sort_strips(order_ref, kv_refs, keys, values)

    place = place_ref[step]
    queries = two_heads(q_ref[...])
    last = place // (CHUNK // STRIP)

    def part(index, total, masked):
        first = pl.multiple_of(index * CHUNK, CHUNK)
        scores = lax.dot_general(
            queries, keys[pl.ds(first, CHUNK), :], ALONG, preferred_element_type=jnp.float32
        )
        weights = jnp.exp2(scores)
        if masked:
            row = lax.broadcasted_iota(jnp.int32, scores.shape, 0) % STRIP
            column = lax.broadcasted_iota(jnp.int32, scores.shape, 1)
            weights = jnp.where(column - row <= place * STRIP - first, weights, 0.0)
        return total + jnp.dot(
            weights.astype(jnp.bfloat16),
            values[pl.ds(first, CHUNK), :],
            preferred_element_type=jnp.float32,
        )

    total = jnp.zeros((2 * STRIP, 2 * HEAD_SIZE), jnp.float32)
    total = lax.fori_loop(0, last, lambda index, t: part(index, t, False), total)
    total = part(last, total, True)
    norm = total[:, HEAD_SIZE:]
    out_ref[...] = side_by_side(total[:, :HEAD_SIZE] / norm).astype(jnp.bfloat16)
    lse_ref[0] = jnp.transpose(jnp.log2(norm))[:8]


def attend(place, order, queries, kv):
    rows, width = queries.shape
    steps = rows // STRIP
    total = sum(part.shape[0] for part in kv)
    strip = pl.BlockSpec((STRIP, width), lambda i, *_: (i, 0))
    return pl.pallas_call(
        attend_kernel,
        grid_spec=pltpu.PrefetchScalarGridSpec(
            num_scalar_prefetch=2,
            grid=(steps,),
            in_specs=[strip] + [pl.BlockSpec(part.shape, lambda i, *_: (0, 0)) for part in kv],
            out_specs=[strip, pl.BlockSpec((1, 8, 2 * STRIP), lambda i, *_: (i, 0, 0))],
            scratch_shapes=[
                pltpu.VMEM((total, HEAD_SIZE), jnp.bfloat16),
                pltpu.VMEM((total, 2 * HEAD_SIZE), jnp.bfloat16),
            ],
        ),
        out_shape=[
            jax.ShapeDtypeStruct((rows, width), jnp.bfloat16),
            jax.ShapeDtypeStruct((steps, 8, 2 * STRIP), jnp.float32),
        ],
        cost_estimate=LONG,
        name="attend",
    )(place, order, queries, *kv)


def attend_back_kernel(place_ref, order_ref, q_ref, out_ref, lse_ref, *refs, groups):
    grad_refs, kv_refs = refs[:groups], refs[groups : groups + 4]
    dq_ref, own_ref, far_ref, sent_ref = refs[groups + 4 : groups + 8]
    keys, values, key_sums, value_sums, grads_all = refs[groups + 8 :]
    step = pl.program_id(0)

    @pl.when(step == 0)
    def _():
        key_sums[...] = jnp.zeros_like(key_sums)
        value_sums[...] = jnp.zeros_like(value_sums)
        sort_strips(order_ref, kv_refs, keys, values)
        first = 0
        for ref in grad_refs:
            grads_all[first : first + ref.shape[0], :] = ref[...]
            first += ref.shape[0]

    place = place_ref[step]
    queries = two_heads(q_ref[...])
    grads = two_heads(grads_all[pl.ds(pl.multiple_of(step * STRIP, STRIP), STRIP), :])
    product = grads.astype(jnp.float32) * two_heads(out_ref[...]).astype(jnp.float32)
    delta = jnp.sum(jnp.transpose(product), axis=0, keepdims=True)
    lse = lse_ref[0, :1]
    last = place // (CHUNK // STRIP)

    def part(index, total, masked):
        first = pl.multiple_of(index * CHUNK, CHUNK)
        here = pl.ds(first, CHUNK)
        key_rows = keys[here, :]
        scores = lax.dot_general(key_rows, queries, ALONG, preferred_element_type=jnp.float32)
        weights = jnp.exp2(scores - lse)
        if masked:
            row = lax.broadcasted_iota(jnp.int32, scores.shape, 0)
            column = lax.broadcasted_iota(jnp.int32, scores.shape, 1) % STRIP
            weights = jnp.where(row - column <= place * STRIP - first, weights, 0.0)
        slopes = lax.dot_general(
            values[here, :], grads, ALONG, preferred_element_type=jnp.float32
        )
        score_grads = (weights * (slopes - delta)).astype(jnp.bfloat16)
        value_sums[here, :] += jnp.dot(
            weights.astype(jnp.bfloat16), grads, preferred_element_type=jnp.float32
        )
        key_sums[here, :] += jnp.dot(score_grads, queries, preferred_element_type=jnp.float32)
        return total + lax.dot_general(
            score_grads, key_rows, DOWN, preferred_element_type=jnp.float32
        )

    total = jnp.zeros((2 * STRIP, HEAD_SIZE), jnp.float32)
    total = lax.fori_loop(0, last, lambda index, t: part(index, t, False), total)
    total = part(last, total, True)
    dq_ref[...] = side_by_side(total * (1.0 / math.sqrt(HEAD_SIZE))).astype(jnp.bfloat16)

    @pl.when(step == pl.num_programs(0) - 1)
    def _():
        per = own_ref.shape[0] // STRIP
        for j in range(4):
            target = (own_ref, far_ref, sent_ref, sent_ref)[j]
            base = per if j == 3 else 0
            for i in range(per):
                source = pl.multiple_of(order_ref[j * per + i] * STRIP, STRIP)
                here = slice((base + i) * STRIP, (base + i + 1) * STRIP)
                target[here, :HEAD_SIZE] = (
                    key_sums[pl.ds(source, STRIP), :] * (1.0 / LOG2E)
                ).astype(jnp.bfloat16)
                target[here, HEAD_SIZE:] = value_sums[pl.ds(source, STRIP), :].astype(
                    jnp.bfloat16
                )


def attend_back(place, order, queries, grads, attended, lse, kv):
    rows, width = queries.shape
    steps = rows // STRIP
    total = sum(part.shape[0] for part in kv)
    strip = pl.BlockSpec((STRIP, width), lambda i, *_: (i, 0))

    def whole(shape):
        return pl.BlockSpec(shape, lambda i, *_: (0, 0))

    outs = [kv[0].shape, kv[0].shape, (2 * kv[0].shape[0], kv[0].shape[1])]
    return pl.pallas_call(
        lambda *refs: attend_back_kernel(*refs, groups=len(grads)),
        grid_spec=pltpu.PrefetchScalarGridSpec(
            num_scalar_prefetch=2,
            grid=(steps,),
            in_specs=[strip, strip, pl.BlockSpec((1, 8, 2 * STRIP), lambda i, *_: (i, 0, 0))]
            + [whole(part.shape) for part in (*grads, *kv)],
            out_specs=[strip] + [whole(shape) for shape in outs],
            scratch_shapes=[
                pltpu.VMEM((total, HEAD_SIZE), jnp.bfloat16),
                pltpu.VMEM((total, HEAD_SIZE), jnp.bfloat16),
                pltpu.VMEM((total, HEAD_SIZE), jnp.float32),
                pltpu.VMEM((total, HEAD_SIZE), jnp.float32),
                pltpu.VMEM((rows, width), jnp.bfloat16),
            ],
        ),
        out_shape=[jax.ShapeDtypeStruct((rows, width), jnp.bfloat16)]
        + [jax.ShapeDtypeStruct(shape, jnp.bfloat16) for shape in outs],
        cost_estimate=LONG,
        name="attend_back",
    )(place, order, queries, attended, lse, *grads, *kv)


def matmul(left, right, dims=(((1,), (0,)), ((), ()))):
    return lax.dot_general(left, right, dims, preferred_element_type=jnp.float32)


RING = (0, 2, 4, 6, 7, 5, 3, 1)
STRIPS = (0, 1, 7, 2, 6, 3, 5, 4)
GROUPS = ((0, 3), (3, 5), (5, 7), (7, 8))


def hop(value, by):
    count = len(RING)
    return lax.ppermute(value, "blk", [(RING[i], RING[(i + by) % count]) for i in range(count)])


def cross(value, by):
    return lax.ppermute(value, "head", [(i, i ^ by) for i in range(4)])


def add(left, right):
    return (left.astype(jnp.float32) + right.astype(jnp.float32)).astype(left.dtype)


class Gather:
    def __init__(self, own):
        self.got, self.step = {0: own}, 0
        self.state = (own, own)

    def go(self):
        self.step += 1
        left, right = self.state
        if self.step < 4:
            self.state = hop(left, -1), hop(right, 1)
            self.got[self.step], self.got[8 - self.step] = self.state
        else:
            half = left.shape[0] // 2
            self.got[4] = jnp.concatenate([hop(left[:half], -1), hop(right[half:], 1)], axis=0)
            self.state = (self.got[4],)

    def strips(self):
        return [self.got[s] for s in STRIPS]

    def group(self, index):
        first, last = GROUPS[index]
        return jnp.concatenate([self.got[s] for s in STRIPS[first:last]], axis=0)


class Scatter:
    def __init__(self, part):
        self.part, self.step = part, 0
        self.half = part[4].shape[0] // 2
        self.state = (part[4][: self.half], part[4][self.half :])

    def go(self):
        self.step += 1
        half, part = self.half, self.part
        up, down = hop(self.state[0], 1), hop(self.state[1], -1)
        if self.step == 1:
            up = jnp.concatenate([add(part[3][:half], up), part[3][half:]], axis=0)
            down = jnp.concatenate([part[5][:half], add(part[5][half:], down)], axis=0)
        elif self.step < 4:
            up, down = add(part[4 - self.step], up), add(part[4 + self.step], down)
        self.state = up, down

    def total(self):
        up, down = self.state
        wide = jnp.float32
        return self.part[0].astype(wide) + up.astype(wide) + down.astype(wide)


class Swap:
    def __init__(self, pieces, rows):
        cut = 4 * rows + rows // 2
        self.rows, self.step = rows, 0
        self.taken = [(pieces, 0, rows, 0, 0)]
        self.state = (pieces[rows:cut], pieces[cut:])

    def go(self):
        self.step += 1
        rows, step = self.rows, self.step
        right, left = hop(self.state[0], 1), hop(self.state[1], -1)
        if step < 4:
            self.taken.append((right, 0, rows, 8 - step, 0))
            self.taken.append((left, left.shape[0] - rows, rows, step, 0))
            self.state = right[rows:], left[:-rows]
        else:
            self.taken.append((right, 0, rows // 2, 4, 0))
            self.taken.append((left, 0, rows // 2, 4, rows // 2))
            self.state = right, left

    def operands(self):
        return [item[0] for item in self.taken]

    def specs(self):
        vmem = pl.BlockSpec(memory_space=pltpu.VMEM)
        own = pl.BlockSpec((self.rows, self.taken[0][0].shape[1]), lambda i: (0, 0))
        return [own] + [vmem] * (len(self.taken) - 1)

    def result(self):
        rows, taken = self.rows, [item[1:] for item in self.taken]

        def stack_kernel(*refs):
            for ref, (first, count, spot, top) in zip(refs[:-1], taken):
                at = spot * rows + top
                refs[-1][at : at + count, :] = ref[first : first + count, :]

        return pl.pallas_call(
            stack_kernel,
            grid=(1,),
            in_specs=self.specs(),
            out_specs=pl.BlockSpec(memory_space=pltpu.VMEM),
            out_shape=jax.ShapeDtypeStruct((8 * rows, self.taken[0][0].shape[1]), jnp.bfloat16),
            cost_estimate=CHEAP,
            name="stack",
        )(*self.operands())


def hold(rings, *extra):
    states, extra = lax.optimization_barrier(([ring.state for ring in rings], extra))
    for ring, state in zip(rings, states):
        ring.state = state
    return extra[0] if len(extra) == 1 else extra


def scatter_cross(own, far, sent):
    moved = cross(sent, 1)
    half = own.shape[0]
    return add(own, moved[:half]), add(far, moved[half:])


def columns(at, width):
    return pl.ds(pl.multiple_of(at * width, width), width)


def slice_kernel(at_ref, *refs, pad):
    weights, out_ref = refs[:-1], refs[-1]
    if pad:
        weights, pad_ref = weights[:-1], weights[-1]
    rows = weights[0].shape[0]
    each = rows + pad
    for s in range(8):
        first = 0
        for ref in weights:
            width = ref.shape[1] // 8
            out_ref[s * each : s * each + rows, first : first + width] = ref[
                :, columns(at_ref[s], width)
            ]
            first += width
        if pad:
            out_ref[s * each + rows : (s + 1) * each, :] = pad_ref[...]


def slice_pieces(at, *weights, pad=None):
    rows = weights[0].shape[0]
    cols = sum(w.shape[1] for w in weights) // 8
    extra = 0 if pad is None else pad.shape[0]
    operands = weights if pad is None else (*weights, pad)
    vmem = pl.BlockSpec(memory_space=pltpu.VMEM)
    return pl.pallas_call(
        lambda *refs: slice_kernel(*refs, pad=extra),
        in_specs=[pl.BlockSpec(memory_space=pltpu.SMEM)] + [vmem] * len(operands),
        out_specs=vmem,
        out_shape=jax.ShapeDtypeStruct((8 * (rows + extra), cols), jnp.bfloat16),
        cost_estimate=CHEAP,
        name="slice_pieces",
    )(at, *operands)


def assemble_kernel(at_ref, *refs):
    own = at_ref[8]
    for j, piece in enumerate(refs[:4]):
        refs[4][0, own ^ j] = piece[...]


def assemble(at, pieces, rows):
    count = at.shape[0] - 1
    total, cols = pieces[0].shape
    return pl.pallas_call(
        assemble_kernel,
        grid_spec=pltpu.PrefetchScalarGridSpec(
            num_scalar_prefetch=1,
            grid=(count,),
            in_specs=[pl.BlockSpec((rows, cols), lambda i, at: (i, 0))] * 4,
            out_specs=pl.BlockSpec((1, 4, rows, cols), lambda i, at: (at[i], 0, 0, 0)),
        ),
        out_shape=jax.ShapeDtypeStruct((count, 4, rows, cols), jnp.bfloat16),
        cost_estimate=CHEAP,
        name="assemble",
    )(at, *pieces).reshape(4 * total, cols)


def spun(rows, cosine, sine):
    return rows * cosine + pltpu.roll(rows, HEAD_SIZE // 2, 1) * sine


def project_kernel(at_ref, *refs, strips):
    token_refs, refs = refs[:strips], refs[strips:]
    pieces, refs = refs[:4], refs[4:]
    cos_ref, sin_ref, normed_ref, raw_ref, q_ref, kv_ref, matrix_ref, gains_ref = refs
    each = pieces[0].shape[0] // 8
    rows = matrix_ref.shape[0] // 32
    own = at_ref[8]
    gains = jnp.zeros(gains_ref.shape, jnp.float32)
    for s in range(8):
        for j in range(4):
            first = pl.multiple_of((at_ref[s] * 4 + (own ^ j)) * rows, rows)
            matrix_ref[pl.ds(first, rows), :] = pieces[j][s * each : s * each + rows, :]
            gains += pieces[j][s * each + rows : (s + 1) * each, :].astype(jnp.float32)
    gains_ref[...] = gains
    width = gains.shape[1]
    first = 0
    for ref in token_refs:
        block = ref[...].astype(jnp.float32)
        block = block * inverse_rms(block)
        here = slice(first, first + ref.shape[0])
        for i in range(block.shape[1] // width):
            cols = slice(i * width, (i + 1) * width)
            normed_ref[here, cols] = (block[:, cols] * gains[i : i + 1]).astype(jnp.bfloat16)
        first += ref.shape[0]
    query_gain, key_gain = gains[8:9, :HEAD_SIZE], gains[8:9, HEAD_SIZE : 2 * HEAD_SIZE]
    query_cols = q_ref.shape[1]
    step = 256
    for first in range(0, q_ref.shape[0], step):
        here = slice(first, first + step)
        raw = jnp.dot(normed_ref[here, :], matrix_ref[...], preferred_element_type=jnp.float32)
        raw_ref[here, :] = raw
        cosine, sine = cos_ref[here, :], sin_ref[here, :]
        for col in range(0, query_cols + HEAD_SIZE, HEAD_SIZE):
            part = raw[:, col : col + HEAD_SIZE]
            if col < query_cols:
                part = spun(part * inverse_rms(part) * query_gain, cosine, sine)
                part = part * (LOG2E / math.sqrt(HEAD_SIZE))
                q_ref[here, col : col + HEAD_SIZE] = part.astype(jnp.bfloat16)
            else:
                part = spun(part * inverse_rms(part) * key_gain, cosine, sine)
                kv_ref[here, :HEAD_SIZE] = part.astype(jnp.bfloat16)
        kv_ref[here, HEAD_SIZE:] = raw[:, query_cols + HEAD_SIZE :].astype(jnp.bfloat16)


def project(at, strips, pieces, cosine, sine, query_cols, pad):
    rows = sum(strip.shape[0] for strip in strips)
    width = strips[0].shape[1]
    cols = pieces[0].shape[1]
    vmem = pl.BlockSpec(memory_space=pltpu.VMEM)
    operands = (*strips, *pieces, cosine, sine)
    narrow, wide = jnp.bfloat16, jnp.float32
    return pl.pallas_call(
        lambda *refs: project_kernel(*refs, strips=len(strips)),
        in_specs=[pl.BlockSpec(memory_space=pltpu.SMEM)] + [vmem] * len(operands),
        out_specs=[vmem] * 6,
        out_shape=[
            jax.ShapeDtypeStruct((rows, width), narrow),
            jax.ShapeDtypeStruct((rows, cols), wide),
            jax.ShapeDtypeStruct((rows, query_cols), narrow),
            jax.ShapeDtypeStruct((rows, 2 * HEAD_SIZE), narrow),
            jax.ShapeDtypeStruct((width, cols), narrow),
            jax.ShapeDtypeStruct((pad, cols), wide),
        ],
        cost_estimate=LONG,
        name="project",
    )(at, *operands)


def project_back_kernel(
    dq_ref, dkv_ref, raw_ref, head_gain_ref, cos_ref, sin_ref, matrix_ref,
    grad_ref, part_ref, gain_ref,
):
    query_cols = dq_ref.shape[1]
    step = 256
    gain_ref[...] = jnp.zeros_like(gain_ref)
    for first in range(0, dq_ref.shape[0], step):
        here = slice(first, first + step)
        cosine, sine = cos_ref[here, :], sin_ref[here, :]
        for col in range(0, query_cols + HEAD_SIZE, HEAD_SIZE):
            cols = slice(col, col + HEAD_SIZE)
            which = 0 if col < query_cols else 1
            grads = dkv_ref[here, :HEAD_SIZE] if which else dq_ref[here, cols]
            raw = raw_ref[here, cols]
            rho = inverse_rms(raw)
            unit = raw * rho
            turned = spun(grads.astype(jnp.float32), cosine, -sine)
            gain_ref[which : which + 1, :] += jnp.sum(turned * unit, axis=0, keepdims=True)
            scaled = turned * head_gain_ref[which : which + 1]
            back = rho * (scaled - unit * jnp.mean(unit * scaled, axis=-1, keepdims=True))
            grad_ref[here, cols] = back.astype(jnp.bfloat16)
        grad_ref[here, query_cols + HEAD_SIZE :] = dkv_ref[here, HEAD_SIZE:]
        part_ref[here, :] = lax.dot_general(
            grad_ref[here, :], matrix_ref[...], ALONG, preferred_element_type=jnp.float32
        ).astype(jnp.bfloat16)


def project_back(query_grads, kv_grads, raw, head_gains, cosine, sine, matrix):
    rows, cols = raw.shape
    vmem = pl.BlockSpec(memory_space=pltpu.VMEM)
    return pl.pallas_call(
        project_back_kernel,
        in_specs=[vmem] * 7,
        out_specs=[vmem] * 3,
        out_shape=[
            jax.ShapeDtypeStruct((rows, cols), jnp.bfloat16),
            jax.ShapeDtypeStruct((rows, matrix.shape[0]), jnp.bfloat16),
            jax.ShapeDtypeStruct((8, HEAD_SIZE), jnp.float32),
        ],
        cost_estimate=LONG,
        name="project_back",
    )(query_grads, kv_grads, raw, head_gains, cosine, sine, matrix)


def dots(lefts, rights, dims):
    return sum(
        lax.dot_general(left[...], right[...], dims, preferred_element_type=jnp.float32)
        for left, right in zip(lefts, rights)
    )


def weight_grads_kernel(at_ref, *refs, groups, rows):
    own_ref, far_ref, sent_ref, held = refs[-4:]
    own = at_ref[8]
    sums = dots(refs[:groups], refs[groups : 2 * groups], DOWN)
    held[...] = sums.astype(jnp.bfloat16).reshape(held.shape)
    own_ref[:rows, :] = held[own]
    far_ref[:rows, :] = held[own ^ 2]
    sent_ref[0, :rows] = held[own ^ 1]
    sent_ref[1, :rows] = held[own ^ 3]
    if own_ref.shape[0] > rows:
        pad = refs[2 * groups][...]
        own_ref[rows:, :] = pad
        far_ref[rows:, :] = pad
        sent_ref[0, rows:] = pad
        sent_ref[1, rows:] = pad


def weight_grads(at, lefts, rights, rows, pad=None):
    count = at.shape[0] - 1
    cols = rights[0].shape[1]
    pads = [] if pad is None else [pad]
    each = rows + sum(p.shape[0] for p in pads)
    part = pl.BlockSpec((each, cols), lambda i, at: (i, 0))
    shape = jax.ShapeDtypeStruct((count * each, cols), jnp.bfloat16)
    own, far, sent = pl.pallas_call(
        lambda *refs: weight_grads_kernel(*refs, groups=len(lefts), rows=rows),
        grid_spec=pltpu.PrefetchScalarGridSpec(
            num_scalar_prefetch=1,
            grid=(count,),
            in_specs=[
                pl.BlockSpec((left.shape[0], 4 * rows), lambda i, at: (0, at[i]))
                for left in lefts
            ]
            + [pl.BlockSpec(right.shape, lambda i, at: (0, 0)) for right in (*rights, *pads)],
            out_specs=[part, part, pl.BlockSpec((2, each, cols), lambda i, at: (0, i, 0))],
            scratch_shapes=[pltpu.VMEM((4, rows, cols), jnp.bfloat16)],
        ),
        out_shape=[
            shape, shape, jax.ShapeDtypeStruct((2, count * each, cols), jnp.bfloat16),
        ],
        cost_estimate=CHEAP,
        name="weight_grads",
    )(at, *lefts, *rights, *pads)
    return own, far, sent.reshape(2 * count * each, cols)


def row_grads_kernel(*refs, lefts):
    left_refs, right_refs, (out_ref, held) = refs[:lefts], refs[lefts:-2], refs[-2:]

    @pl.when(pl.program_id(0) == 0)
    def _():
        first = 0
        for ref in right_refs:
            held[first : first + ref.shape[0], :] = ref[...]
            first += ref.shape[0]

    sums, first = 0.0, 0
    for ref in left_refs:
        sums += lax.dot_general(
            ref[...],
            held[first : first + ref.shape[0], :],
            DOWN,
            preferred_element_type=jnp.float32,
        )
        first += ref.shape[0]
    out_ref[...] = sums.astype(jnp.bfloat16)


def row_grads(lefts, rights, block=256):
    out_rows, cols = lefts[0].shape[1], rights[0].shape[1]
    total = sum(left.shape[0] for left in lefts)
    return pl.pallas_call(
        lambda *refs: row_grads_kernel(*refs, lefts=len(lefts)),
        grid=(out_rows // block,),
        in_specs=[pl.BlockSpec((left.shape[0], block), lambda i: (0, i)) for left in lefts]
        + [pl.BlockSpec(right.shape, lambda i: (0, 0)) for right in rights],
        out_specs=pl.BlockSpec((block, cols), lambda i: (i, 0)),
        out_shape=jax.ShapeDtypeStruct((out_rows, cols), jnp.bfloat16),
        scratch_shapes=[pltpu.VMEM((total, cols), jnp.bfloat16)],
        cost_estimate=CHEAP,
        name="row_grads",
    )(*lefts, *rights)


def hidden_grads_kernel(*refs, strips):
    matrix_ref, outs, held = refs[strips], refs[strips + 1 : -1], refs[-1]

    @pl.when(pl.program_id(0) == 0)
    def _():
        first = 0
        for ref in refs[:strips]:
            held[first : first + ref.shape[0], :] = ref[...]
            first += ref.shape[0]

    first = 0
    for out in outs:
        out[...] = lax.dot_general(
            held[first : first + out.shape[0], :],
            matrix_ref[...],
            ALONG,
            preferred_element_type=jnp.float32,
        )
        first += out.shape[0]


def hidden_grads_of(strips, matrix, block=256):
    rows = [(last - first) * strips[0].shape[0] for first, last in GROUPS]
    cols = matrix.shape[0]
    return pl.pallas_call(
        lambda *refs: hidden_grads_kernel(*refs, strips=len(strips)),
        grid=(cols // block,),
        in_specs=[pl.BlockSpec(strip.shape, lambda i: (0, 0)) for strip in strips]
        + [pl.BlockSpec((block, matrix.shape[1]), lambda i: (i, 0))],
        out_specs=[pl.BlockSpec((n, block), lambda i: (0, i)) for n in rows],
        out_shape=[jax.ShapeDtypeStruct((n, cols), jnp.float32) for n in rows],
        scratch_shapes=[pltpu.VMEM((sum(rows), matrix.shape[1]), jnp.bfloat16)],
        cost_estimate=CHEAP,
        name="hidden_grads",
    )(*strips, matrix)


def lane_sums(block):
    return sum(block[:, i : i + 128] for i in range(0, block.shape[1], 128))


def widen(at, swap, *weights):
    rows, taken, count = weights[0].shape[0], [item[1:] for item in swap.taken], len(weights)
    pad = swap.rows - rows

    def widen_kernel(at_ref, *refs):
        piece_refs, refs = refs[: len(taken)], refs[len(taken) :]
        grads, sums_ref = refs[count : 2 * count], refs[2 * count]
        for ref in refs[2 * count :]:
            ref[...] = jnp.zeros_like(ref)
        for ref, (start, size, spot, top) in zip(piece_refs, taken):
            used = min(size, rows - top)
            here = slice(top, top + used)
            first = 0
            for weight, grad in zip(refs[:count], grads):
                width = weight.shape[1] // 8
                there = columns(at_ref[spot], width)
                block = ref[start : start + used, first : first + width].astype(jnp.float32)
                grad[here, there] = block
                sums_ref[here, :] += lane_sums(block * weight[here, there].astype(jnp.float32))
                first += width
            if used < size:
                refs[-1][...] += ref[start + used : start + size, :].astype(jnp.float32)

    vmem = pl.BlockSpec(memory_space=pltpu.VMEM)
    shapes = [w.shape for w in weights] + [(rows, 128)]
    if pad:
        shapes.append((pad, swap.taken[0][0].shape[1]))
    return pl.pallas_call(
        widen_kernel,
        grid=(1,),
        in_specs=[pl.BlockSpec(memory_space=pltpu.SMEM), *swap.specs()] + [vmem] * count,
        out_specs=[vmem] * len(shapes),
        out_shape=[jax.ShapeDtypeStruct(shape, jnp.float32) for shape in shapes],
        cost_estimate=CHEAP,
        name="widen",
    )(at, *swap.operands(), *weights)


def grouped(strips):
    return [
        jnp.concatenate(strips[a:b], axis=0) if b - a > 1 else strips[a] for a, b in GROUPS
    ]


def split_groups(groups, rows):
    return [
        group[i * rows : (i + 1) * rows]
        for group in groups
        for i in range(group.shape[0] // rows)
    ]


def gather_head(rows):
    return lax.all_gather(rows, "head", axis=0, tiled=True)


def scatter_head(rows):
    return lax.psum_scatter(rows, "head", scatter_dimension=0, tiled=True)


def inverse_rms(rows):
    return lax.rsqrt(jnp.mean(rows * rows, axis=-1, keepdims=True) + EPS)


def per_device(
    tokens,
    attention_norm,
    query_weight,
    key_projection,
    value_projection,
    query_norm,
    key_norm,
    output_weight,
    feedforward_norm,
    gate_weight,
    up_weight,
    down_weight,
    stretch_order,
    out_cotangent,
):
    blk_count = lax.axis_size("blk")
    head_count = lax.axis_size("head")
    head_index = lax.axis_index("head")
    blk_index = lax.axis_index("blk")
    narrow, wide = jnp.bfloat16, jnp.float32
    tokens, out_cotangent = tokens[0], out_cotangent[0]
    local_rows, model_width = tokens.shape
    group_rows = local_rows * blk_count
    weight_rows = query_weight.shape[0]
    ff_local = gate_weight.shape[1] // blk_count
    query_cols = QUERY_HEADS // blk_count * HEAD_SIZE
    attn_cols = query_cols + 2 * HEAD_SIZE
    device_count = blk_count * head_count
    strip_count = blk_count * head_count
    halves = strip_count // stretch_order.shape[1]
    ring_place = jnp.where(blk_index % 2 == 0, blk_index // 2, 7 - blk_index // 2)

    spot = (ring_place + jnp.arange(blk_count, dtype=jnp.int32)) % blk_count
    at = jnp.where(spot < 4, 2 * spot, 15 - 2 * spot).astype(jnp.int32)
    at_own = jnp.concatenate([at, head_index[None].astype(jnp.int32)])
    ring_spot = (ring_place + jnp.asarray(STRIPS, jnp.int32)) % blk_count
    strip_blk = jnp.where(ring_spot < 4, 2 * ring_spot, 15 - 2 * ring_spot)
    strip_head = head_index ^ jnp.asarray((0, 2, 1, 3), jnp.int32)
    strip = (strip_blk[None, :] * head_count + strip_head[:, None]).reshape(strip_count)
    slots = jnp.arange(stretch_order.shape[1], dtype=jnp.int32)
    held = jnp.sum(
        jnp.where((strip // halves)[:, None] == slots[None, :], stretch_order, 0), axis=1
    )
    strip_place = held * halves + strip % halves
    order = strip_place.astype(jnp.int32)
    place = strip_place[:blk_count].astype(jnp.int32)
    positions = (
        place[:, None] * local_rows + jnp.arange(local_rows, dtype=jnp.int32)[None, :]
    ).reshape(group_rows)
    phases = angles(positions, HEAD_SIZE)[:, 0, :]
    cosine, sine = jnp.cos(phases), jnp.sin(phases)
    cosine = jnp.concatenate([cosine, cosine], axis=1)
    sine = jnp.concatenate([-sine, sine], axis=1)

    small = query_norm.shape[0]
    number = blk_index * head_count + head_index
    pad = 16

    def placed(share):
        return jnp.where(
            jnp.arange(device_count, dtype=jnp.int32)[:, None] == number, share[None, :], 0
        ).reshape(-1)

    gains = jnp.concatenate(
        [placed(attention_norm), placed(feedforward_norm), placed(query_norm), placed(key_norm)]
    ).astype(narrow)
    gains = jnp.pad(gains, (0, pad * attn_cols - gains.shape[0])).reshape(pad, attn_cols)
    down_matrix = gather_head(down_weight)
    output_rows = gather_head(output_weight)

    attn_swap = Swap(
        slice_pieces(at, query_weight, key_projection, value_projection, pad=gains),
        weight_rows + pad,
    )
    token_ring = Gather(tokens)
    ff_slices = slice_pieces(at, gate_weight, up_weight)
    token_ring.go()
    attn_swap.go()
    hold((attn_swap,))
    attn_swap.go()
    hold((attn_swap,))
    attn_swap.go()
    hold((attn_swap,))
    attn_swap.go()
    own = hold((token_ring,), attn_swap.result())
    near, far = cross(own, 1), cross(own, 2)
    token_ring.go()
    ff_slices, cosine, sine = hold((token_ring,), ff_slices, cosine, sine)
    ff_swap, cotangent_ring = Swap(ff_slices, weight_rows), Gather(out_cotangent)
    token_ring.go()
    own, near, far = hold((token_ring,), own, near, far)
    both = cross(far, 1)
    token_ring.go()
    own, near, far, both = hold((token_ring, ff_swap), own, near, far, both)
    ff_swap.go()

    first_normed, attn_raw, query_rows, own, attn_matrix, gains = project(
        at_own, token_ring.strips(), (own, near, far, both), cosine, sine, query_cols, pad
    )
    gain_one = gains[:4].reshape(1, model_width)
    gain_two = gains[4:8].reshape(1, model_width)
    head_gains = jnp.pad(gains[8, : 2 * HEAD_SIZE].reshape(2, HEAD_SIZE), ((0, 6), (0, 0)))
    own = hold((ff_swap,), own)
    near, far = cross(own, 1), cross(own, 2)
    ff_swap.go()
    own, near, far = hold((ff_swap, cotangent_ring), own, near, far)
    both = cross(far, 1)
    ff_swap.go()
    kv = hold((ff_swap, cotangent_ring), own, far, near, both)
    ff_swap.go()
    cotangent_ring.go()
    attended, lse = attend(place, order, query_rows, kv)

    def by_groups(rows):
        return [rows[a * local_rows : b * local_rows] for a, b in GROUPS]

    def by_strips(groups):
        return dict(zip(STRIPS, split_groups(groups, local_rows)))

    attended = hold((cotangent_ring, ff_swap), attended)
    branch_parts = [matmul(rows, output_rows).astype(narrow) for rows in by_groups(attended)]
    branch_ring = Scatter(by_strips(branch_parts))
    branch_ring.go()
    cotangent_ring.go()
    ff_own = hold((), ff_swap.result())
    ff_near, ff_far = cross(ff_own, 1), cross(ff_own, 2)
    hold((branch_ring, cotangent_ring))
    branch_ring.go()
    cotangent_ring.go()
    hold((branch_ring, cotangent_ring))
    branch_ring.go()
    cotangent_ring.go()
    ff_near, ff_far, cotangent_strips, down_matrix = hold(
        (branch_ring, cotangent_ring), ff_near, ff_far, cotangent_ring.strips(), down_matrix
    )
    branch_ring.go()
    ff_both = cross(ff_far, 1)
    hidden_grads = hidden_grads_of(cotangent_strips, down_matrix)
    hidden_grads, ff_both = hold((branch_ring,), hidden_grads, ff_both)
    tokens_wide = tokens.astype(wide)
    resid = tokens_wide + branch_ring.total()
    rho_two = inverse_rms(resid)
    unit_two = resid * rho_two

    second_ring = Gather((unit_two * gain_two).astype(narrow))
    second_groups, hidden_groups, ff_gradient_groups = [], [], []

    def feed_forward(index):
        rows = second_ring.group(index)
        ff_raw = matmul(rows, ff_matrix)
        gate, up_proj = ff_raw[:, :ff_local], ff_raw[:, ff_local:]
        sigma = jax.nn.sigmoid(gate)
        swish = gate * sigma
        hidden_gradient = hidden_grads[index]
        gate_gradient = hidden_gradient * up_proj * (sigma * (1.0 + gate * (1.0 - sigma)))
        hidden = (swish * up_proj).astype(narrow)
        gradient = jnp.concatenate([gate_gradient, hidden_gradient * swish], 1).astype(narrow)
        if index < 3:
            rows, hidden, gradient = hold((second_ring,), rows, hidden, gradient)
        second_groups.append(rows)
        hidden_groups.append(hidden)
        ff_gradient_groups.append(gradient)

    second_ring.go()
    ff_matrix = assemble(at_own, (ff_own, ff_near, ff_far, ff_both), weight_rows)
    ff_matrix = hold((second_ring,), ff_matrix)
    for index in range(3):
        second_ring.go()
        feed_forward(index)
    feed_forward(3)

    def back(index):
        return matmul(ff_gradient_groups[index], ff_matrix, ALONG).astype(narrow)

    def split(group):
        return [group[i : i + local_rows] for i in range(0, group.shape[0], local_rows)]

    parts = {4: back(3)}
    resid_ring = Scatter(parts)
    parts[3], parts[5] = split(hold((), back(2)))
    parts[2], parts[6] = split(hold((), back(1)))
    resid_ring.go()
    _, _, hidden_groups, cotangent_strips = hold(
        (resid_ring,), parts[2], parts[6], hidden_groups, cotangent_strips
    )
    resid_ring.go()
    down_gradient = row_grads(hidden_groups, cotangent_strips)
    back_zero, down_gradient, second_groups, ff_gradient_groups = hold(
        (resid_ring,), back(0), down_gradient, second_groups, ff_gradient_groups
    )
    down_gradient = scatter_head(down_gradient)
    parts[0], parts[1], parts[7] = split(back_zero)
    resid_ring.go()
    ff_own, ff_far, ff_sent = hold(
        (resid_ring,), *weight_grads(at_own, second_groups, ff_gradient_groups, weight_rows)
    )
    resid_ring.go()
    ff_own, ff_far = scatter_cross(ff_own, ff_far, ff_sent)
    ff_own, ff_far, hidden_groups = hold((resid_ring,), ff_own, ff_far, hidden_groups)
    ff_far = cross(ff_far, 2)
    scaled = gain_two * resid_ring.total()
    resid_gradient = out_cotangent.astype(wide) + rho_two * (
        scaled - unit_two * jnp.mean(unit_two * scaled, axis=-1, keepdims=True)
    )

    grad_ring = Gather(resid_gradient.astype(narrow))
    grad_groups, attended_grads = [], []

    def attention_back(index):
        rows = grad_ring.group(index)
        grads = matmul(rows, output_rows, ALONG).astype(narrow)
        if index < 3:
            rows, grads = hold((grad_ring,), rows, grads)
        grad_groups.append(rows)
        attended_grads.append(grads)

    grad_ring.go()
    out_parts = [matmul(rows, down_matrix).astype(narrow) for rows in hidden_groups]
    out_parts = hold((grad_ring,), *out_parts)
    out_ring = Scatter(by_strips(out_parts))
    grad_ring.go()
    hold((grad_ring,))
    grad_ring.go()
    attention_back(0)
    hold((out_ring, grad_ring))
    out_ring.go()
    grad_ring.go()
    attention_back(1)
    attention_back(2)
    ff_swap = Swap(add(ff_own, ff_far), weight_rows)
    hold((grad_ring, ff_swap, out_ring))
    out_ring.go()
    ff_swap.go()
    attention_back(3)
    query_grads, kv_own, kv_far, kv_sent = attend_back(
        place, order, query_rows, attended_grads, attended, lse, kv
    )
    query_grads, kv_own, kv_far, kv_sent, grad_groups, attended = hold(
        (out_ring, ff_swap), query_grads, kv_own, kv_far, kv_sent, grad_groups, attended
    )
    out_ring.go()
    kv_own, kv_far = scatter_cross(kv_own, kv_far, kv_sent)
    output_weight_gradient = row_grads([attended], grad_groups)
    kv_own, kv_far, output_weight_gradient = hold(
        (out_ring, ff_swap), kv_own, kv_far, output_weight_gradient
    )
    ff_swap.go()
    kv_grads = hold((ff_swap,), add(kv_own, cross(kv_far, 2)))
    ff_swap.go()
    attn_gradient, first_parts, gain_sums = project_back(
        query_grads, kv_grads, attn_raw, head_gains, cosine, sine, attn_matrix
    )
    gain_sums = jnp.pad(
        gain_sums[:2].reshape(1, 2 * HEAD_SIZE).astype(narrow),
        ((0, pad - 1), (0, attn_cols - 2 * HEAD_SIZE)),
    )
    attn_gradient, first_parts, gain_sums, output_weight_gradient = hold(
        (ff_swap,), attn_gradient, first_parts, gain_sums, output_weight_gradient
    )
    token_ring = Scatter(by_strips(by_groups(first_parts)))
    token_ring.go()
    ff_swap.go()
    attn_own, attn_far, attn_sent = weight_grads(
        at_own, [first_normed], [attn_gradient], weight_rows, gain_sums
    )
    attn_own, attn_far, attn_sent = hold(
        (token_ring, ff_swap), attn_own, attn_far, attn_sent
    )
    token_ring.go()
    attn_own, attn_far = scatter_cross(attn_own, attn_far, attn_sent)
    attn_far = cross(attn_far, 2)
    gate_weight_gradient, up_weight_gradient, ff_sums = widen(at, ff_swap, gate_weight, up_weight)
    attn_swap = Swap(add(attn_own, attn_far), weight_rows + pad)
    gate_weight_gradient, up_weight_gradient, ff_sums, output_weight_gradient = hold(
        (token_ring, attn_swap),
        gate_weight_gradient, up_weight_gradient, ff_sums, output_weight_gradient,
    )
    output_weight_gradient = scatter_head(output_weight_gradient)
    attn_swap.go()
    token_ring.go()
    feedforward_norm_gradient = jnp.sum(ff_sums, axis=1) / feedforward_norm.astype(wide)
    feedforward_norm_gradient, down_gradient = hold(
        (token_ring, attn_swap), feedforward_norm_gradient, down_gradient.astype(wide)
    )
    attn_swap.go()
    token_ring.go()
    output_weight_gradient = hold(
        (token_ring, attn_swap, out_ring), output_weight_gradient.astype(wide)
    )
    attn_swap.go()
    out_ring.go()
    hold((attn_swap,))
    attn_swap.go()
    layer_out = (resid + out_ring.total()).astype(narrow)
    query_weight_gradient, key_weight_gradient, value_weight_gradient, norm_sums, gain_sums = widen(
        at, attn_swap, query_weight, key_projection, value_projection
    )
    attention_norm_gradient = jnp.sum(norm_sums, axis=1) / attention_norm.astype(wide)
    gain_sums = gain_sums[0, : 2 * HEAD_SIZE].reshape(2, HEAD_SIZE)
    gain_sums = lax.dynamic_slice_in_dim(gain_sums, number * small, small, 1)
    rho_one = inverse_rms(tokens_wide)
    unit_one = tokens_wide * rho_one
    scaled = gain_one * token_ring.total()
    tokens_gradient = resid_gradient + rho_one * (
        scaled - unit_one * jnp.mean(unit_one * scaled, axis=-1, keepdims=True)
    )
    return (
        layer_out[None],
        tokens_gradient.astype(narrow)[None],
        attention_norm_gradient,
        query_weight_gradient,
        key_weight_gradient,
        value_weight_gradient,
        gain_sums[0],
        gain_sums[1],
        output_weight_gradient,
        feedforward_norm_gradient,
        gate_weight_gradient,
        up_weight_gradient,
        down_gradient,
    )


def solution(mesh):
    placed = (
        P(None, ("blk", "head"), None),
        P(("blk", "head")),
        P(("blk", "head"), None),
        P(("blk", "head"), None),
        P(("blk", "head"), None),
        P(("blk", "head")),
        P(("blk", "head")),
        P(("blk", "head"), None),
        P(("blk", "head")),
        P(("blk", "head"), None),
        P(("blk", "head"), None),
        P(("blk", "head"), None),
        P(),
        P(None, ("blk", "head"), None),
    )
    fits = mesh.shape["blk"] == KEY_VALUE_HEADS and mesh.shape["head"] == 4
    return jax.shard_map(
        per_device if fits else per_device_by_tokens,
        mesh=mesh,
        in_specs=placed,
        out_specs=(
            P(None, ("blk", "head"), None),
            P(None, ("blk", "head"), None),
            P(("blk", "head")),
            P(("blk", "head"), None),
            P(("blk", "head"), None),
            P(("blk", "head"), None),
            P(("blk", "head")),
            P(("blk", "head")),
            P(("blk", "head"), None),
            P(("blk", "head")),
            P(("blk", "head"), None),
            P(("blk", "head"), None),
            P(("blk", "head"), None),
        ),
        check_vma=False,
    )
```

```python
import math

import jax
import jax.numpy as jnp
from jax import lax
from jax.experimental import pallas as pl
from jax.experimental.pallas import tpu as pltpu
from jax.sharding import PartitionSpec as P

QUERY_HEADS = 16
KEY_VALUE_HEADS = 8
HEAD_SIZE = 128


EPS = 1e-06
NEG = -1e30
ROPE_BASE = 1000000.0


def passed_along(value, axis, by):
    count = lax.axis_size(axis)
    return lax.ppermute(value, axis, [(i, (i + by) % count) for i in range(count)])


def norm_rows(inputs, norm_gain):
    return inputs * lax.rsqrt(jnp.mean(inputs * inputs, axis=-1, keepdims=True) + EPS) * norm_gain


def rotary(inputs, phases):
    half_width = inputs.shape[-1] // 2
    cosine = jnp.cos(phases)
    sine_term = jnp.sin(phases)
    first_half = inputs[..., :half_width]
    second_half = inputs[..., half_width:]
    return jnp.concatenate(
        [
            first_half * cosine - second_half * sine_term,
            second_half * cosine + first_half * sine_term,
        ],
        axis=-1,
    )


def angles(positions, head_width):
    half_width = head_width // 2
    frequency = jnp.exp(
        jnp.arange(half_width, dtype=jnp.float32) * (-2.0 * math.log(ROPE_BASE) / head_width)
    )
    return positions.astype(jnp.float32)[..., None, None] * frequency


def token_positions(stretch_order, first_row, row_count, stretch_rows):
    row_index = first_row + jnp.arange(row_count, dtype=jnp.int32)
    slot_index = row_index // stretch_rows
    matches = slot_index[:, None] == jnp.arange(stretch_order.shape[1], dtype=jnp.int32)[None, :]
    picked = jnp.sum(jnp.where(matches[None], stretch_order[:, None, :], 0), axis=-1)
    return picked * stretch_rows + row_index % stretch_rows


def per_device_by_tokens(
    tokens,
    attention_norm,
    query_weight,
    key_projection,
    value_projection,
    query_norm,
    key_norm,
    output_weight,
    feedforward_norm,
    gate_weight,
    up_weight,
    down_weight,
    stretch_order,
    out_cotangent,
):
    count_of_heads = lax.axis_size("head")
    span_count = lax.axis_size("blk")
    span_index = lax.axis_index("blk")
    head_index = lax.axis_index("head")
    sequence_total = tokens.shape[0]
    local_rows = tokens.shape[1]
    group_rows = local_rows * count_of_heads
    stretch_rows = group_rows // 2
    heads_shared = KEY_VALUE_HEADS // count_of_heads
    heads_per_group = QUERY_HEADS // KEY_VALUE_HEADS
    score_scale = 1.0 / math.sqrt(HEAD_SIZE)
    gain_one, query_matrix, key_matrix, value_matrix, query_gain, key_gain, output_matrix = (
        lax.all_gather(attention_norm, ("blk", "head"), axis=0, tiled=True),
        lax.all_gather(query_weight, ("blk", "head"), axis=0, tiled=True),
        lax.all_gather(key_projection, ("blk", "head"), axis=0, tiled=True),
        lax.all_gather(value_projection, ("blk", "head"), axis=0, tiled=True),
        lax.all_gather(query_norm, ("blk", "head"), axis=0, tiled=True),
        lax.all_gather(key_norm, ("blk", "head"), axis=0, tiled=True),
        lax.all_gather(output_weight, ("blk", "head"), axis=0, tiled=True),
    )
    gain_two, gate_matrix, up_matrix, down_matrix = (
        lax.all_gather(feedforward_norm, ("blk", "head"), axis=0, tiled=True),
        lax.all_gather(gate_weight, ("blk", "head"), axis=0, tiled=True),
        lax.all_gather(up_weight, ("blk", "head"), axis=0, tiled=True),
        lax.all_gather(down_weight, ("blk", "head"), axis=0, tiled=True),
    )
    gain_one = gain_one.astype(jnp.float32)
    gain_two = gain_two.astype(jnp.float32)
    query_gain = query_gain.astype(jnp.float32)
    key_gain = key_gain.astype(jnp.float32)
    own_first = (span_index * count_of_heads + head_index) * local_rows
    own_pos = token_positions(stretch_order, own_first, local_rows, stretch_rows)
    group_pos = token_positions(stretch_order, span_index * group_rows, group_rows, stretch_rows)
    phases = angles(own_pos, HEAD_SIZE)
    tokens_wide = tokens.astype(jnp.float32)
    first_normed, norm_one_back = jax.vjp(norm_rows, tokens_wide, gain_one)
    first_normed = first_normed.astype(jnp.bfloat16)
    query_raw = jnp.einsum(
        "btd,de->bte", first_normed, query_matrix, preferred_element_type=jnp.float32
    ).reshape(sequence_total, local_rows, QUERY_HEADS, HEAD_SIZE)
    key_unnormed = jnp.einsum(
        "btd,de->bte", first_normed, key_matrix, preferred_element_type=jnp.float32
    ).reshape(sequence_total, local_rows, KEY_VALUE_HEADS, HEAD_SIZE)
    value_tokens = (
        jnp.einsum("btd,de->bte", first_normed, value_matrix, preferred_element_type=jnp.float32)
        .astype(jnp.bfloat16)
        .reshape(sequence_total, local_rows, KEY_VALUE_HEADS, HEAD_SIZE)
    )

    def heads_local(query_in, key_in, query_scale, key_scale):
        return (
            rotary(norm_rows(query_in, query_scale), phases),
            rotary(norm_rows(key_in, key_scale), phases),
        )

    (query_tokens, key_tokens), heads_back = jax.vjp(
        heads_local, query_raw, key_unnormed, query_gain, key_gain
    )
    query_tokens = query_tokens.astype(jnp.bfloat16)
    key_tokens = key_tokens.astype(jnp.bfloat16)
    query_group, key_group, value_group = (
        lax.all_to_all(query_tokens, "head", split_axis=2, concat_axis=1, tiled=True),
        lax.all_to_all(key_tokens, "head", split_axis=2, concat_axis=1, tiled=True),
        lax.all_to_all(value_tokens, "head", split_axis=2, concat_axis=1, tiled=True),
    )
    query_five = query_group.reshape(
        sequence_total, group_rows, heads_shared, heads_per_group, HEAD_SIZE
    )

    def block_update(carry, key_block, value_block, key_pos):
        run_max, run_sum, run_total = carry
        scores = (
            jnp.einsum(
                "bqkgd,bckd->bkgqc", query_five, key_block, preferred_element_type=jnp.float32
            )
            * score_scale
        )
        allowed = key_pos[:, None, None, None, :] <= group_pos[:, None, None, :, None]
        scores = jnp.where(allowed, scores, NEG)
        new_max = jnp.maximum(run_max, jnp.max(scores, axis=-1))
        exponent = jnp.where(allowed, jnp.exp(scores - new_max[..., None]), 0.0)
        factor = jnp.exp(run_max - new_max)
        new_sum = run_sum * factor + jnp.sum(exponent, axis=-1)
        new_total = run_total * factor[..., None] + jnp.einsum(
            "bkgqc,bckd->bkgqd",
            exponent.astype(jnp.bfloat16),
            value_block,
            preferred_element_type=jnp.float32,
        )
        return (new_max, new_sum, new_total)

    def fold_update(carry, key_block, value_block, key_pos):
        result = block_update(carry, key_block, value_block, key_pos)
        return result

    stat_shape = (sequence_total, heads_shared, heads_per_group, group_rows)
    start_state = (
        jnp.full(stat_shape, NEG, jnp.float32),
        jnp.zeros(stat_shape, jnp.float32),
        jnp.zeros(stat_shape + (HEAD_SIZE,), jnp.float32),
    )
    key_piece = lax.all_gather(key_group, "blk", axis=1, tiled=True)
    value_piece = lax.all_gather(value_group, "blk", axis=1, tiled=True)
    piece_rows = key_piece.shape[1]
    block_len = math.gcd(group_rows, piece_rows)

    def inner(block_number, carry_in):
        offset = block_number * block_len
        key_block = lax.dynamic_slice_in_dim(key_piece, offset, block_len, 1)
        value_block = lax.dynamic_slice_in_dim(value_piece, offset, block_len, 1)
        key_pos = token_positions(stretch_order, offset, block_len, stretch_rows)
        return fold_update(carry_in, key_block, value_block, key_pos)

    run_max, run_sum, run_total = lax.fori_loop(0, piece_rows // block_len, inner, start_state)
    log_total = run_max + jnp.log(run_sum)
    attended_five = run_total / run_sum[..., None]
    attended_group = (
        jnp.transpose(attended_five, (0, 3, 1, 2, 4))
        .reshape(sequence_total, group_rows, heads_shared * heads_per_group, HEAD_SIZE)
        .astype(jnp.bfloat16)
    )
    attended_tokens = lax.all_to_all(
        attended_group, "head", split_axis=1, concat_axis=2, tiled=True
    ).reshape(sequence_total, local_rows, QUERY_HEADS * HEAD_SIZE)
    branch = jnp.einsum(
        "bte,ed->btd", attended_tokens, output_matrix, preferred_element_type=jnp.float32
    )
    resid = tokens_wide + branch
    normed_two, norm_two_back = jax.vjp(norm_rows, resid, gain_two)
    normed_two = normed_two.astype(jnp.bfloat16)
    gate = jnp.einsum("btd,df->btf", normed_two, gate_matrix, preferred_element_type=jnp.float32)
    up_proj = jnp.einsum("btd,df->btf", normed_two, up_matrix, preferred_element_type=jnp.float32)

    def swish_product(gate_in, up_in):
        return jax.nn.silu(gate_in) * up_in

    hidden, swish_back = jax.vjp(swish_product, gate, up_proj)
    hidden = hidden.astype(jnp.bfloat16)
    layer_out = (
        resid + jnp.einsum("btf,fd->btd", hidden, down_matrix, preferred_element_type=jnp.float32)
    ).astype(jnp.bfloat16)
    gain_again, gate_matrix, up_matrix, down_matrix = (
        lax.all_gather(feedforward_norm, ("blk", "head"), axis=0, tiled=True),
        lax.all_gather(gate_weight, ("blk", "head"), axis=0, tiled=True),
        lax.all_gather(up_weight, ("blk", "head"), axis=0, tiled=True),
        lax.all_gather(down_weight, ("blk", "head"), axis=0, tiled=True),
    )
    down_gradient = jnp.einsum(
        "btf,btd->fd", hidden, out_cotangent, preferred_element_type=jnp.float32
    )
    hidden_gradient = jnp.einsum(
        "btd,fd->btf", out_cotangent, down_matrix, preferred_element_type=jnp.float32
    )
    gate_gradient, up_gradient = swish_back(hidden_gradient)
    gate_gradient = gate_gradient.astype(jnp.bfloat16)
    up_gradient = up_gradient.astype(jnp.bfloat16)
    gate_matrix_gradient = jnp.einsum(
        "btd,btf->df", normed_two, gate_gradient, preferred_element_type=jnp.float32
    )
    up_matrix_gradient = jnp.einsum(
        "btd,btf->df", normed_two, up_gradient, preferred_element_type=jnp.float32
    )
    normed_two_gradient = jnp.einsum(
        "btf,df->btd", gate_gradient, gate_matrix, preferred_element_type=jnp.float32
    ) + jnp.einsum("btf,df->btd", up_gradient, up_matrix, preferred_element_type=jnp.float32)
    resid_part, gain_two_gradient = norm_two_back(normed_two_gradient)
    resid_gradient = out_cotangent.astype(jnp.float32) + resid_part
    feedforward_sums = (
        lax.psum_scatter(gain_two_gradient, ("blk", "head"), scatter_dimension=0, tiled=True),
        lax.psum_scatter(gate_matrix_gradient, ("blk", "head"), scatter_dimension=0, tiled=True),
        lax.psum_scatter(up_matrix_gradient, ("blk", "head"), scatter_dimension=0, tiled=True),
        lax.psum_scatter(down_gradient, ("blk", "head"), scatter_dimension=0, tiled=True),
    )
    gain_again, query_matrix, key_matrix, value_matrix, query_again, key_again, output_matrix = (
        lax.all_gather(attention_norm, ("blk", "head"), axis=0, tiled=True),
        lax.all_gather(query_weight, ("blk", "head"), axis=0, tiled=True),
        lax.all_gather(key_projection, ("blk", "head"), axis=0, tiled=True),
        lax.all_gather(value_projection, ("blk", "head"), axis=0, tiled=True),
        lax.all_gather(query_norm, ("blk", "head"), axis=0, tiled=True),
        lax.all_gather(key_norm, ("blk", "head"), axis=0, tiled=True),
        lax.all_gather(output_weight, ("blk", "head"), axis=0, tiled=True),
    )
    branch_gradient = resid_gradient.astype(jnp.bfloat16)
    output_matrix_gradient = jnp.einsum(
        "bte,btd->ed", attended_tokens, branch_gradient, preferred_element_type=jnp.float32
    )
    attended_gradient = (
        jnp.einsum(
            "btd,ed->bte", branch_gradient, output_matrix, preferred_element_type=jnp.float32
        )
        .astype(jnp.bfloat16)
        .reshape(sequence_total, local_rows, QUERY_HEADS, HEAD_SIZE)
    )
    attended_grad_group = lax.all_to_all(
        attended_gradient, "head", split_axis=2, concat_axis=1, tiled=True
    ).reshape(sequence_total, group_rows, heads_shared, heads_per_group, HEAD_SIZE)
    delta = jnp.sum(
        jnp.transpose(attended_grad_group.astype(jnp.float32), (0, 2, 3, 1, 4)) * attended_five,
        axis=-1,
    )

    def block_grads(sums_in, key_current, value_current, key_pos):
        key_sum, value_sum, query_sum = sums_in
        scores = (
            jnp.einsum(
                "bqkgd,bckd->bkgqc", query_five, key_current, preferred_element_type=jnp.float32
            )
            * score_scale
        )
        allowed = key_pos[:, None, None, None, :] <= group_pos[:, None, None, :, None]
        weights = jnp.where(allowed, jnp.exp(scores - log_total[..., None]), 0.0)
        probs = weights.astype(jnp.bfloat16)
        value_sum = value_sum + jnp.einsum(
            "bkgqc,bqkgd->bckd", probs, attended_grad_group, preferred_element_type=jnp.float32
        )
        probs_gradient = jnp.einsum(
            "bqkgd,bckd->bkgqc",
            attended_grad_group,
            value_current,
            preferred_element_type=jnp.float32,
        )
        scores_gradient = (weights * (probs_gradient - delta[..., None])).astype(jnp.bfloat16)
        query_sum = (
            query_sum
            + jnp.einsum(
                "bkgqc,bckd->bqkgd",
                scores_gradient,
                key_current,
                preferred_element_type=jnp.float32,
            )
            * score_scale
        )
        key_sum = (
            key_sum
            + jnp.einsum(
                "bkgqc,bqkgd->bckd", scores_gradient, query_five, preferred_element_type=jnp.float32
            )
            * score_scale
        )
        return (key_sum, value_sum, query_sum)

    def pass_step(step_index, carry):
        key_current, value_current, key_sum, value_sum, query_sum = carry
        anchor = (span_index - step_index) % span_count
        key_pos = token_positions(stretch_order, anchor * group_rows, group_rows, stretch_rows)
        key_sum, value_sum, query_sum = block_grads(
            (key_sum, value_sum, query_sum), key_current, value_current, key_pos
        )
        key_current, value_current = passed_along((key_current, value_current), "blk", 1)
        key_sum, value_sum = (
            passed_along(key_sum.astype(jnp.bfloat16), "blk", 1).astype(key_sum.dtype),
            passed_along(value_sum.astype(jnp.bfloat16), "blk", 1).astype(value_sum.dtype),
        )
        return (key_current, value_current, key_sum, value_sum, query_sum)

    kv_zeros = jnp.zeros((sequence_total, group_rows, heads_shared, HEAD_SIZE), jnp.float32)
    query_zeros = jnp.zeros(
        (sequence_total, group_rows, heads_shared, heads_per_group, HEAD_SIZE), jnp.float32
    )
    final_state = lax.fori_loop(
        0, span_count, pass_step, (key_group, value_group, kv_zeros, kv_zeros, query_zeros)
    )
    key_grad_group = final_state[2].astype(jnp.bfloat16)
    value_grad_group = final_state[3].astype(jnp.bfloat16)
    query_grad_group = (
        final_state[4]
        .astype(jnp.bfloat16)
        .reshape(sequence_total, group_rows, heads_shared * heads_per_group, HEAD_SIZE)
    )
    query_grad_tokens, key_grad_tokens, value_gradient_tokens = (
        lax.all_to_all(query_grad_group, "head", split_axis=1, concat_axis=2, tiled=True),
        lax.all_to_all(key_grad_group, "head", split_axis=1, concat_axis=2, tiled=True),
        lax.all_to_all(value_grad_group, "head", split_axis=1, concat_axis=2, tiled=True),
    )
    query_raw_gradient, key_unnormed_gradient, query_gain_gradient, key_gain_gradient = heads_back(
        (query_grad_tokens.astype(jnp.float32), key_grad_tokens.astype(jnp.float32))
    )
    query_raw_gradient = query_raw_gradient.astype(jnp.bfloat16).reshape(
        sequence_total, local_rows, QUERY_HEADS * HEAD_SIZE
    )
    key_unnormed_gradient = key_unnormed_gradient.astype(jnp.bfloat16).reshape(
        sequence_total, local_rows, KEY_VALUE_HEADS * HEAD_SIZE
    )
    value_unnormed_gradient = value_gradient_tokens.reshape(
        sequence_total, local_rows, KEY_VALUE_HEADS * HEAD_SIZE
    )
    query_matrix_gradient = jnp.einsum(
        "btd,bte->de", first_normed, query_raw_gradient, preferred_element_type=jnp.float32
    )
    key_matrix_gradient = jnp.einsum(
        "btd,bte->de", first_normed, key_unnormed_gradient, preferred_element_type=jnp.float32
    )
    value_matrix_gradient = jnp.einsum(
        "btd,bte->de", first_normed, value_unnormed_gradient, preferred_element_type=jnp.float32
    )
    normed_one_gradient = jnp.einsum(
        "bte,de->btd", query_raw_gradient, query_matrix, preferred_element_type=jnp.float32
    )
    normed_one_gradient = normed_one_gradient + jnp.einsum(
        "bte,de->btd", key_unnormed_gradient, key_matrix, preferred_element_type=jnp.float32
    )
    normed_one_gradient = normed_one_gradient + jnp.einsum(
        "bte,de->btd", value_unnormed_gradient, value_matrix, preferred_element_type=jnp.float32
    )
    token_part, gain_one_gradient = norm_one_back(normed_one_gradient)
    tokens_gradient = (resid_gradient + token_part).astype(jnp.bfloat16)
    attention_sums = (
        lax.psum_scatter(gain_one_gradient, ("blk", "head"), scatter_dimension=0, tiled=True),
        lax.psum_scatter(query_matrix_gradient, ("blk", "head"), scatter_dimension=0, tiled=True),
        lax.psum_scatter(key_matrix_gradient, ("blk", "head"), scatter_dimension=0, tiled=True),
        lax.psum_scatter(value_matrix_gradient, ("blk", "head"), scatter_dimension=0, tiled=True),
        lax.psum_scatter(query_gain_gradient, ("blk", "head"), scatter_dimension=0, tiled=True),
        lax.psum_scatter(key_gain_gradient, ("blk", "head"), scatter_dimension=0, tiled=True),
        lax.psum_scatter(output_matrix_gradient, ("blk", "head"), scatter_dimension=0, tiled=True),
    )
    return (
        layer_out,
        tokens_gradient,
        attention_sums[0],
        attention_sums[1],
        attention_sums[2],
        attention_sums[3],
        attention_sums[4],
        attention_sums[5],
        attention_sums[6],
        feedforward_sums[0],
        feedforward_sums[1],
        feedforward_sums[2],
        feedforward_sums[3],
    )


LOG2E = math.log2(math.e)
STRIP = 128
CHUNK = 512
ALONG = (((1,), (1,)), ((), ()))
DOWN = (((0,), (0,)), ((), ()))


def two_heads(block):
    return jnp.concatenate([block[:, :HEAD_SIZE], block[:, HEAD_SIZE:]], axis=0)


def side_by_side(rows):
    half = rows.shape[0] // 2
    return jnp.concatenate([rows[:half], rows[half:]], axis=1)


CHEAP = pl.CostEstimate(flops=1, bytes_accessed=1, transcendentals=0)
LONG = pl.CostEstimate(flops=3 * 10**10, bytes_accessed=1 << 25, transcendentals=0)


def sort_strips(order_ref, kv_refs, keys, values):
    per = kv_refs[0].shape[0] // STRIP
    for j, ref in enumerate(kv_refs):
        for i in range(per):
            target = pl.multiple_of(order_ref[j * per + i] * STRIP, STRIP)
            here = slice(i * STRIP, (i + 1) * STRIP)
            keys[pl.ds(target, STRIP), :] = ref[here, :HEAD_SIZE]
            values[pl.ds(target, STRIP), :HEAD_SIZE] = ref[here, HEAD_SIZE:]


def attend_kernel(place_ref, order_ref, q_ref, *refs):
    kv_refs, (out_ref, lse_ref, keys, values) = refs[:4], refs[4:]
    step = pl.program_id(0)

    @pl.when(step == 0)
    def _():
        values[:, HEAD_SIZE:] = jnp.ones((values.shape[0], HEAD_SIZE), jnp.bfloat16)
        sort_strips(order_ref, kv_refs, keys, values)

    place = place_ref[step]
    queries = two_heads(q_ref[...])
    last = place // (CHUNK // STRIP)

    def part(index, total, masked):
        first = pl.multiple_of(index * CHUNK, CHUNK)
        scores = lax.dot_general(
            queries, keys[pl.ds(first, CHUNK), :], ALONG, preferred_element_type=jnp.float32
        )
        weights = jnp.exp2(scores)
        if masked:
            row = lax.broadcasted_iota(jnp.int32, scores.shape, 0) % STRIP
            column = lax.broadcasted_iota(jnp.int32, scores.shape, 1)
            weights = jnp.where(column - row <= place * STRIP - first, weights, 0.0)
        return total + jnp.dot(
            weights.astype(jnp.bfloat16),
            values[pl.ds(first, CHUNK), :],
            preferred_element_type=jnp.float32,
        )

    total = jnp.zeros((2 * STRIP, 2 * HEAD_SIZE), jnp.float32)
    total = lax.fori_loop(0, last, lambda index, t: part(index, t, False), total)
    total = part(last, total, True)
    norm = total[:, HEAD_SIZE:]
    out_ref[...] = side_by_side(total[:, :HEAD_SIZE] / norm).astype(jnp.bfloat16)
    lse_ref[0] = jnp.transpose(jnp.log2(norm))[:8]


def attend(place, order, queries, kv):
    rows, width = queries.shape
    steps = rows // STRIP
    total = sum(part.shape[0] for part in kv)
    strip = pl.BlockSpec((STRIP, width), lambda i, *_: (i, 0))
    return pl.pallas_call(
        attend_kernel,
        grid_spec=pltpu.PrefetchScalarGridSpec(
            num_scalar_prefetch=2,
            grid=(steps,),
            in_specs=[strip] + [pl.BlockSpec(part.shape, lambda i, *_: (0, 0)) for part in kv],
            out_specs=[strip, pl.BlockSpec((1, 8, 2 * STRIP), lambda i, *_: (i, 0, 0))],
            scratch_shapes=[
                pltpu.VMEM((total, HEAD_SIZE), jnp.bfloat16),
                pltpu.VMEM((total, 2 * HEAD_SIZE), jnp.bfloat16),
            ],
        ),
        out_shape=[
            jax.ShapeDtypeStruct((rows, width), jnp.bfloat16),
            jax.ShapeDtypeStruct((steps, 8, 2 * STRIP), jnp.float32),
        ],
        cost_estimate=LONG,
        name="attend",
    )(place, order, queries, *kv)


def attend_back_kernel(place_ref, order_ref, q_ref, out_ref, lse_ref, *refs, groups):
    grad_refs, kv_refs = refs[:groups], refs[groups : groups + 4]
    dq_ref, own_ref, far_ref, sent_ref = refs[groups + 4 : groups + 8]
    keys, values, key_sums, value_sums, grads_all = refs[groups + 8 :]
    step = pl.program_id(0)

    @pl.when(step == 0)
    def _():
        key_sums[...] = jnp.zeros_like(key_sums)
        value_sums[...] = jnp.zeros_like(value_sums)
        sort_strips(order_ref, kv_refs, keys, values)
        first = 0
        for ref in grad_refs:
            grads_all[first : first + ref.shape[0], :] = ref[...]
            first += ref.shape[0]

    place = place_ref[step]
    queries = two_heads(q_ref[...])
    grads = two_heads(grads_all[pl.ds(pl.multiple_of(step * STRIP, STRIP), STRIP), :])
    product = grads.astype(jnp.float32) * two_heads(out_ref[...]).astype(jnp.float32)
    delta = jnp.sum(jnp.transpose(product), axis=0, keepdims=True)
    lse = lse_ref[0, :1]
    last = place // (CHUNK // STRIP)

    def part(index, total, masked):
        first = pl.multiple_of(index * CHUNK, CHUNK)
        here = pl.ds(first, CHUNK)
        key_rows = keys[here, :]
        scores = lax.dot_general(key_rows, queries, ALONG, preferred_element_type=jnp.float32)
        weights = jnp.exp2(scores - lse)
        if masked:
            row = lax.broadcasted_iota(jnp.int32, scores.shape, 0)
            column = lax.broadcasted_iota(jnp.int32, scores.shape, 1) % STRIP
            weights = jnp.where(row - column <= place * STRIP - first, weights, 0.0)
        slopes = lax.dot_general(
            values[here, :], grads, ALONG, preferred_element_type=jnp.float32
        )
        score_grads = (weights * (slopes - delta)).astype(jnp.bfloat16)
        value_sums[here, :] += jnp.dot(
            weights.astype(jnp.bfloat16), grads, preferred_element_type=jnp.float32
        )
        key_sums[here, :] += jnp.dot(score_grads, queries, preferred_element_type=jnp.float32)
        return total + lax.dot_general(
            score_grads, key_rows, DOWN, preferred_element_type=jnp.float32
        )

    total = jnp.zeros((2 * STRIP, HEAD_SIZE), jnp.float32)
    total = lax.fori_loop(0, last, lambda index, t: part(index, t, False), total)
    total = part(last, total, True)
    dq_ref[...] = side_by_side(total * (1.0 / math.sqrt(HEAD_SIZE))).astype(jnp.bfloat16)

    @pl.when(step == pl.num_programs(0) - 1)
    def _():
        per = own_ref.shape[0] // STRIP
        for j in range(4):
            target = (own_ref, far_ref, sent_ref, sent_ref)[j]
            base = per if j == 3 else 0
            for i in range(per):
                source = pl.multiple_of(order_ref[j * per + i] * STRIP, STRIP)
                here = slice((base + i) * STRIP, (base + i + 1) * STRIP)
                target[here, :HEAD_SIZE] = (
                    key_sums[pl.ds(source, STRIP), :] * (1.0 / LOG2E)
                ).astype(jnp.bfloat16)
                target[here, HEAD_SIZE:] = value_sums[pl.ds(source, STRIP), :].astype(
                    jnp.bfloat16
                )


def attend_back(place, order, queries, grads, attended, lse, kv):
    rows, width = queries.shape
    steps = rows // STRIP
    total = sum(part.shape[0] for part in kv)
    strip = pl.BlockSpec((STRIP, width), lambda i, *_: (i, 0))

    def whole(shape):
        return pl.BlockSpec(shape, lambda i, *_: (0, 0))

    outs = [kv[0].shape, kv[0].shape, (2 * kv[0].shape[0], kv[0].shape[1])]
    return pl.pallas_call(
        lambda *refs: attend_back_kernel(*refs, groups=len(grads)),
        grid_spec=pltpu.PrefetchScalarGridSpec(
            num_scalar_prefetch=2,
            grid=(steps,),
            in_specs=[strip, strip, pl.BlockSpec((1, 8, 2 * STRIP), lambda i, *_: (i, 0, 0))]
            + [whole(part.shape) for part in (*grads, *kv)],
            out_specs=[strip] + [whole(shape) for shape in outs],
            scratch_shapes=[
                pltpu.VMEM((total, HEAD_SIZE), jnp.bfloat16),
                pltpu.VMEM((total, HEAD_SIZE), jnp.bfloat16),
                pltpu.VMEM((total, HEAD_SIZE), jnp.float32),
                pltpu.VMEM((total, HEAD_SIZE), jnp.float32),
                pltpu.VMEM((rows, width), jnp.bfloat16),
            ],
        ),
        out_shape=[jax.ShapeDtypeStruct((rows, width), jnp.bfloat16)]
        + [jax.ShapeDtypeStruct(shape, jnp.bfloat16) for shape in outs],
        cost_estimate=LONG,
        name="attend_back",
    )(place, order, queries, attended, lse, *grads, *kv)


def matmul(left, right, dims=(((1,), (0,)), ((), ()))):
    return lax.dot_general(left, right, dims, preferred_element_type=jnp.float32)


RING = (0, 2, 4, 6, 7, 5, 3, 1)
STRIPS = (0, 1, 7, 2, 6, 3, 5, 4)
GROUPS = ((0, 3), (3, 5), (5, 7), (7, 8))


def hop(value, by):
    count = len(RING)
    return lax.ppermute(value, "blk", [(RING[i], RING[(i + by) % count]) for i in range(count)])


def cross(value, by):
    return lax.ppermute(value, "head", [(i, i ^ by) for i in range(4)])


def add(left, right):
    return (left.astype(jnp.float32) + right.astype(jnp.float32)).astype(left.dtype)


class Gather:
    def __init__(self, own):
        self.got, self.step = {0: own}, 0
        self.state = (own, own)

    def go(self):
        self.step += 1
        left, right = self.state
        if self.step < 4:
            self.state = hop(left, -1), hop(right, 1)
            self.got[self.step], self.got[8 - self.step] = self.state
        else:
            half = left.shape[0] // 2
            self.got[4] = jnp.concatenate([hop(left[:half], -1), hop(right[half:], 1)], axis=0)
            self.state = (self.got[4],)

    def strips(self):
        return [self.got[s] for s in STRIPS]

    def group(self, index):
        first, last = GROUPS[index]
        return jnp.concatenate([self.got[s] for s in STRIPS[first:last]], axis=0)


class Scatter:
    def __init__(self, part):
        self.part, self.step = part, 0
        self.half = part[4].shape[0] // 2
        self.state = (part[4][: self.half], part[4][self.half :])

    def go(self):
        self.step += 1
        half, part = self.half, self.part
        up, down = hop(self.state[0], 1), hop(self.state[1], -1)
        if self.step == 1:
            up = jnp.concatenate([add(part[3][:half], up), part[3][half:]], axis=0)
            down = jnp.concatenate([part[5][:half], add(part[5][half:], down)], axis=0)
        elif self.step < 4:
            up, down = add(part[4 - self.step], up), add(part[4 + self.step], down)
        self.state = up, down

    def total(self):
        up, down = self.state
        wide = jnp.float32
        return self.part[0].astype(wide) + up.astype(wide) + down.astype(wide)


class Swap:
    def __init__(self, pieces, rows):
        cut = 4 * rows + rows // 2
        self.rows, self.step = rows, 0
        self.taken = [(pieces, 0, rows, 0, 0)]
        self.state = (pieces[rows:cut], pieces[cut:])

    def go(self, late=False):
        self.step += 1
        rows, step = self.rows, self.step
        right, left = hop(self.state[0], 1), hop(self.state[1], -1)
        if step < 4:
            self.taken.append((right, 0, rows, 8 - step, 0))
            self.taken.append((left, left.shape[0] - rows, rows, step, 0))
            self.state = right, left
            if not late:
                self.trim()
        else:
            self.taken.append((right, 0, rows // 2, 4, 0))
            self.taken.append((left, 0, rows // 2, 4, rows // 2))
            self.state = right, left

    def trim(self):
        self.state = self.state[0][self.rows :], self.state[1][: -self.rows]

    def operands(self):
        return [item[0] for item in self.taken]

    def specs(self):
        vmem = pl.BlockSpec(memory_space=pltpu.VMEM)
        own = pl.BlockSpec((self.rows, self.taken[0][0].shape[1]), lambda i: (0, 0))
        return [own] + [vmem] * (len(self.taken) - 1)

    def result(self):
        rows, taken = self.rows, [item[1:] for item in self.taken]

        def stack_kernel(*refs):
            for ref, (first, count, spot, top) in zip(refs[:-1], taken):
                at = spot * rows + top
                refs[-1][at : at + count, :] = ref[first : first + count, :]

        return pl.pallas_call(
            stack_kernel,
            grid=(1,),
            in_specs=self.specs(),
            out_specs=pl.BlockSpec(memory_space=pltpu.VMEM),
            out_shape=jax.ShapeDtypeStruct((8 * rows, self.taken[0][0].shape[1]), jnp.bfloat16),
            cost_estimate=CHEAP,
            name="stack",
        )(*self.operands())


def hold(rings, *extra):
    states, extra = lax.optimization_barrier(([ring.state for ring in rings], extra))
    for ring, state in zip(rings, states):
        ring.state = state
    return extra[0] if len(extra) == 1 else extra


def scatter_cross(own, far, sent):
    moved = cross(sent, 1)
    half = own.shape[0]
    return add(own, moved[:half]), add(far, moved[half:])


def columns(at, width):
    return pl.ds(pl.multiple_of(at * width, width), width)


def slice_kernel(at_ref, *refs, pad):
    weights, out_ref = refs[:-1], refs[-1]
    if pad:
        weights, pad_ref = weights[:-1], weights[-1]
    rows = weights[0].shape[0]
    each = rows + pad
    for s in range(8):
        first = 0
        for ref in weights:
            width = ref.shape[1] // 8
            out_ref[s * each : s * each + rows, first : first + width] = ref[
                :, columns(at_ref[s], width)
            ]
            first += width
        if pad:
            out_ref[s * each + rows : (s + 1) * each, :] = pad_ref[...]


def slice_pieces(at, *weights, pad=None):
    rows = weights[0].shape[0]
    cols = sum(w.shape[1] for w in weights) // 8
    extra = 0 if pad is None else pad.shape[0]
    operands = weights if pad is None else (*weights, pad)
    vmem = pl.BlockSpec(memory_space=pltpu.VMEM)
    return pl.pallas_call(
        lambda *refs: slice_kernel(*refs, pad=extra),
        in_specs=[pl.BlockSpec(memory_space=pltpu.SMEM)] + [vmem] * len(operands),
        out_specs=vmem,
        out_shape=jax.ShapeDtypeStruct((8 * (rows + extra), cols), jnp.bfloat16),
        cost_estimate=CHEAP,
        name="slice_pieces",
    )(at, *operands)


def assemble_kernel(at_ref, *refs):
    own = at_ref[8]
    for j, piece in enumerate(refs[:4]):
        refs[4][0, own ^ j] = piece[...]


def assemble(at, pieces, rows):
    count = at.shape[0] - 1
    total, cols = pieces[0].shape
    return pl.pallas_call(
        assemble_kernel,
        grid_spec=pltpu.PrefetchScalarGridSpec(
            num_scalar_prefetch=1,
            grid=(count,),
            in_specs=[pl.BlockSpec((rows, cols), lambda i, at: (i, 0))] * 4,
            out_specs=pl.BlockSpec((1, 4, rows, cols), lambda i, at: (at[i], 0, 0, 0)),
        ),
        out_shape=jax.ShapeDtypeStruct((count, 4, rows, cols), jnp.bfloat16),
        cost_estimate=CHEAP,
        name="assemble",
    )(at, *pieces).reshape(4 * total, cols)


def spun(rows, cosine, sine):
    return rows * cosine + pltpu.roll(rows, HEAD_SIZE // 2, 1) * sine


def project_kernel(at_ref, *refs, strips):
    token_refs, refs = refs[:strips], refs[strips:]
    pieces, refs = refs[:4], refs[4:]
    cos_ref, sin_ref, normed_ref, raw_ref, q_ref, kv_ref, matrix_ref, gains_ref = refs
    each = pieces[0].shape[0] // 8
    rows = matrix_ref.shape[0] // 32
    own = at_ref[8]
    gains = jnp.zeros(gains_ref.shape, jnp.float32)
    for s in range(8):
        for j in range(4):
            first = pl.multiple_of((at_ref[s] * 4 + (own ^ j)) * rows, rows)
            matrix_ref[pl.ds(first, rows), :] = pieces[j][s * each : s * each + rows, :]
            gains += pieces[j][s * each + rows : (s + 1) * each, :].astype(jnp.float32)
    gains_ref[...] = gains
    width = gains.shape[1]
    first = 0
    for ref in token_refs:
        block = ref[...].astype(jnp.float32)
        block = block * inverse_rms(block)
        here = slice(first, first + ref.shape[0])
        for i in range(block.shape[1] // width):
            cols = slice(i * width, (i + 1) * width)
            normed_ref[here, cols] = (block[:, cols] * gains[i : i + 1]).astype(jnp.bfloat16)
        first += ref.shape[0]
    query_gain, key_gain = gains[8:9, :HEAD_SIZE], gains[8:9, HEAD_SIZE : 2 * HEAD_SIZE]
    query_cols = q_ref.shape[1]
    step = 256
    for first in range(0, q_ref.shape[0], step):
        here = slice(first, first + step)
        raw = jnp.dot(normed_ref[here, :], matrix_ref[...], preferred_element_type=jnp.float32)
        raw_ref[here, :] = raw
        cosine, sine = cos_ref[here, :], sin_ref[here, :]
        for col in range(0, query_cols + HEAD_SIZE, HEAD_SIZE):
            part = raw[:, col : col + HEAD_SIZE]
            if col < query_cols:
                part = spun(part * inverse_rms(part) * query_gain, cosine, sine)
                part = part * (LOG2E / math.sqrt(HEAD_SIZE))
                q_ref[here, col : col + HEAD_SIZE] = part.astype(jnp.bfloat16)
            else:
                part = spun(part * inverse_rms(part) * key_gain, cosine, sine)
                kv_ref[here, :HEAD_SIZE] = part.astype(jnp.bfloat16)
        kv_ref[here, HEAD_SIZE:] = raw[:, query_cols + HEAD_SIZE :].astype(jnp.bfloat16)


def project(at, strips, pieces, cosine, sine, query_cols, pad):
    rows = sum(strip.shape[0] for strip in strips)
    width = strips[0].shape[1]
    cols = pieces[0].shape[1]
    vmem = pl.BlockSpec(memory_space=pltpu.VMEM)
    operands = (*strips, *pieces, cosine, sine)
    narrow, wide = jnp.bfloat16, jnp.float32
    return pl.pallas_call(
        lambda *refs: project_kernel(*refs, strips=len(strips)),
        in_specs=[pl.BlockSpec(memory_space=pltpu.SMEM)] + [vmem] * len(operands),
        out_specs=[vmem] * 6,
        out_shape=[
            jax.ShapeDtypeStruct((rows, width), narrow),
            jax.ShapeDtypeStruct((rows, cols), wide),
            jax.ShapeDtypeStruct((rows, query_cols), narrow),
            jax.ShapeDtypeStruct((rows, 2 * HEAD_SIZE), narrow),
            jax.ShapeDtypeStruct((width, cols), narrow),
            jax.ShapeDtypeStruct((pad, cols), wide),
        ],
        cost_estimate=LONG,
        name="project",
    )(at, *operands)


def project_back_kernel(
    dq_ref, dkv_ref, raw_ref, head_gain_ref, cos_ref, sin_ref, matrix_ref,
    grad_ref, part_ref, gain_ref,
):
    query_cols = dq_ref.shape[1]
    step = 256
    gain_ref[...] = jnp.zeros_like(gain_ref)
    for first in range(0, dq_ref.shape[0], step):
        here = slice(first, first + step)
        cosine, sine = cos_ref[here, :], sin_ref[here, :]
        for col in range(0, query_cols + HEAD_SIZE, HEAD_SIZE):
            cols = slice(col, col + HEAD_SIZE)
            which = 0 if col < query_cols else 1
            grads = dkv_ref[here, :HEAD_SIZE] if which else dq_ref[here, cols]
            raw = raw_ref[here, cols]
            rho = inverse_rms(raw)
            unit = raw * rho
            turned = spun(grads.astype(jnp.float32), cosine, -sine)
            gain_ref[which : which + 1, :] += jnp.sum(turned * unit, axis=0, keepdims=True)
            scaled = turned * head_gain_ref[which : which + 1]
            back = rho * (scaled - unit * jnp.mean(unit * scaled, axis=-1, keepdims=True))
            grad_ref[here, cols] = back.astype(jnp.bfloat16)
        grad_ref[here, query_cols + HEAD_SIZE :] = dkv_ref[here, HEAD_SIZE:]
        part_ref[here, :] = lax.dot_general(
            grad_ref[here, :], matrix_ref[...], ALONG, preferred_element_type=jnp.float32
        ).astype(jnp.bfloat16)


def project_back(query_grads, kv_grads, raw, head_gains, cosine, sine, matrix):
    rows, cols = raw.shape
    vmem = pl.BlockSpec(memory_space=pltpu.VMEM)
    return pl.pallas_call(
        project_back_kernel,
        in_specs=[vmem] * 7,
        out_specs=[vmem] * 3,
        out_shape=[
            jax.ShapeDtypeStruct((rows, cols), jnp.bfloat16),
            jax.ShapeDtypeStruct((rows, matrix.shape[0]), jnp.bfloat16),
            jax.ShapeDtypeStruct((8, HEAD_SIZE), jnp.float32),
        ],
        cost_estimate=LONG,
        name="project_back",
    )(query_grads, kv_grads, raw, head_gains, cosine, sine, matrix)


def dots(lefts, rights, dims):
    return sum(
        lax.dot_general(left[...], right[...], dims, preferred_element_type=jnp.float32)
        for left, right in zip(lefts, rights)
    )


def weight_grads_kernel(at_ref, *refs, groups, rows):
    own_ref, far_ref, sent_ref, held = refs[-4:]
    own = at_ref[8]
    sums = dots(refs[:groups], refs[groups : 2 * groups], DOWN)
    held[...] = sums.astype(jnp.bfloat16).reshape(held.shape)
    own_ref[:rows, :] = held[own]
    far_ref[:rows, :] = held[own ^ 2]
    sent_ref[0, :rows] = held[own ^ 1]
    sent_ref[1, :rows] = held[own ^ 3]
    if own_ref.shape[0] > rows:
        pad = refs[2 * groups][...]
        own_ref[rows:, :] = pad
        far_ref[rows:, :] = pad
        sent_ref[0, rows:] = pad
        sent_ref[1, rows:] = pad


def weight_grads(at, lefts, rights, rows, pad=None):
    count = at.shape[0] - 1
    cols = rights[0].shape[1]
    pads = [] if pad is None else [pad]
    each = rows + sum(p.shape[0] for p in pads)
    part = pl.BlockSpec((each, cols), lambda i, at: (i, 0))
    shape = jax.ShapeDtypeStruct((count * each, cols), jnp.bfloat16)
    own, far, sent = pl.pallas_call(
        lambda *refs: weight_grads_kernel(*refs, groups=len(lefts), rows=rows),
        grid_spec=pltpu.PrefetchScalarGridSpec(
            num_scalar_prefetch=1,
            grid=(count,),
            in_specs=[
                pl.BlockSpec((left.shape[0], 4 * rows), lambda i, at: (0, at[i]))
                for left in lefts
            ]
            + [pl.BlockSpec(right.shape, lambda i, at: (0, 0)) for right in (*rights, *pads)],
            out_specs=[part, part, pl.BlockSpec((2, each, cols), lambda i, at: (0, i, 0))],
            scratch_shapes=[pltpu.VMEM((4, rows, cols), jnp.bfloat16)],
        ),
        out_shape=[
            shape, shape, jax.ShapeDtypeStruct((2, count * each, cols), jnp.bfloat16),
        ],
        cost_estimate=CHEAP,
        name="weight_grads",
    )(at, *lefts, *rights, *pads)
    return own, far, sent.reshape(2 * count * each, cols)


def row_grads_kernel(*refs, lefts):
    left_refs, right_refs, (out_ref, held) = refs[:lefts], refs[lefts:-2], refs[-2:]

    @pl.when(pl.program_id(0) == 0)
    def _():
        first = 0
        for ref in right_refs:
            held[first : first + ref.shape[0], :] = ref[...]
            first += ref.shape[0]

    sums, first = 0.0, 0
    for ref in left_refs:
        sums += lax.dot_general(
            ref[...],
            held[first : first + ref.shape[0], :],
            DOWN,
            preferred_element_type=jnp.float32,
        )
        first += ref.shape[0]
    out_ref[...] = sums.astype(jnp.bfloat16)


def row_grads(lefts, rights, block=256):
    out_rows, cols = lefts[0].shape[1], rights[0].shape[1]
    total = sum(left.shape[0] for left in lefts)
    return pl.pallas_call(
        lambda *refs: row_grads_kernel(*refs, lefts=len(lefts)),
        grid=(out_rows // block,),
        in_specs=[pl.BlockSpec((left.shape[0], block), lambda i: (0, i)) for left in lefts]
        + [pl.BlockSpec(right.shape, lambda i: (0, 0)) for right in rights],
        out_specs=pl.BlockSpec((block, cols), lambda i: (i, 0)),
        out_shape=jax.ShapeDtypeStruct((out_rows, cols), jnp.bfloat16),
        scratch_shapes=[pltpu.VMEM((total, cols), jnp.bfloat16)],
        cost_estimate=CHEAP,
        name="row_grads",
    )(*lefts, *rights)


def hidden_grads_kernel(*refs, strips):
    matrix_ref, outs, held = refs[strips], refs[strips + 1 : -1], refs[-1]

    @pl.when(pl.program_id(0) == 0)
    def _():
        first = 0
        for ref in refs[:strips]:
            held[first : first + ref.shape[0], :] = ref[...]
            first += ref.shape[0]

    first = 0
    for out in outs:
        out[...] = lax.dot_general(
            held[first : first + out.shape[0], :],
            matrix_ref[...],
            ALONG,
            preferred_element_type=jnp.float32,
        )
        first += out.shape[0]


def hidden_grads_of(strips, matrix, block=256):
    rows = [(last - first) * strips[0].shape[0] for first, last in GROUPS]
    cols = matrix.shape[0]
    return pl.pallas_call(
        lambda *refs: hidden_grads_kernel(*refs, strips=len(strips)),
        grid=(cols // block,),
        in_specs=[pl.BlockSpec(strip.shape, lambda i: (0, 0)) for strip in strips]
        + [pl.BlockSpec((block, matrix.shape[1]), lambda i: (i, 0))],
        out_specs=[pl.BlockSpec((n, block), lambda i: (0, i)) for n in rows],
        out_shape=[jax.ShapeDtypeStruct((n, cols), jnp.float32) for n in rows],
        scratch_shapes=[pltpu.VMEM((sum(rows), matrix.shape[1]), jnp.bfloat16)],
        cost_estimate=CHEAP,
        name="hidden_grads",
    )(*strips, matrix)


def lane_sums(block):
    return sum(block[:, i : i + 128] for i in range(0, block.shape[1], 128))


def widen(at, swap, *weights):
    rows, taken, count = weights[0].shape[0], [item[1:] for item in swap.taken], len(weights)
    pad = swap.rows - rows

    def widen_kernel(at_ref, *refs):
        piece_refs, refs = refs[: len(taken)], refs[len(taken) :]
        grads, sums_ref = refs[count : 2 * count], refs[2 * count]
        for ref in refs[2 * count :]:
            ref[...] = jnp.zeros_like(ref)
        for ref, (start, size, spot, top) in zip(piece_refs, taken):
            used = min(size, rows - top)
            here = slice(top, top + used)
            first = 0
            for weight, grad in zip(refs[:count], grads):
                width = weight.shape[1] // 8
                there = columns(at_ref[spot], width)
                block = ref[start : start + used, first : first + width].astype(jnp.float32)
                grad[here, there] = block
                sums_ref[here, :] += lane_sums(block * weight[here, there].astype(jnp.float32))
                first += width
            if used < size:
                refs[-1][...] += ref[start + used : start + size, :].astype(jnp.float32)

    vmem = pl.BlockSpec(memory_space=pltpu.VMEM)
    shapes = [w.shape for w in weights] + [(rows, 128)]
    if pad:
        shapes.append((pad, swap.taken[0][0].shape[1]))
    return pl.pallas_call(
        widen_kernel,
        grid=(1,),
        in_specs=[pl.BlockSpec(memory_space=pltpu.SMEM), *swap.specs()] + [vmem] * count,
        out_specs=[vmem] * len(shapes),
        out_shape=[jax.ShapeDtypeStruct(shape, jnp.float32) for shape in shapes],
        cost_estimate=LONG,
        name="widen",
    )(at, *swap.operands(), *weights)


def grouped(strips):
    return [
        jnp.concatenate(strips[a:b], axis=0) if b - a > 1 else strips[a] for a, b in GROUPS
    ]


def split_groups(groups, rows):
    return [
        group[i * rows : (i + 1) * rows]
        for group in groups
        for i in range(group.shape[0] // rows)
    ]


def gather_head(rows):
    return lax.all_gather(rows, "head", axis=0, tiled=True)


def scatter_head(rows):
    return lax.psum_scatter(rows, "head", scatter_dimension=0, tiled=True)


def inverse_rms(rows):
    return lax.rsqrt(jnp.mean(rows * rows, axis=-1, keepdims=True) + EPS)


def per_device(
    tokens,
    attention_norm,
    query_weight,
    key_projection,
    value_projection,
    query_norm,
    key_norm,
    output_weight,
    feedforward_norm,
    gate_weight,
    up_weight,
    down_weight,
    stretch_order,
    out_cotangent,
):
    blk_count = lax.axis_size("blk")
    head_count = lax.axis_size("head")
    head_index = lax.axis_index("head")
    blk_index = lax.axis_index("blk")
    narrow, wide = jnp.bfloat16, jnp.float32
    tokens, out_cotangent = tokens[0], out_cotangent[0]
    local_rows, model_width = tokens.shape
    group_rows = local_rows * blk_count
    weight_rows = query_weight.shape[0]
    ff_local = gate_weight.shape[1] // blk_count
    query_cols = QUERY_HEADS // blk_count * HEAD_SIZE
    attn_cols = query_cols + 2 * HEAD_SIZE
    device_count = blk_count * head_count
    strip_count = blk_count * head_count
    halves = strip_count // stretch_order.shape[1]
    ring_place = jnp.where(blk_index % 2 == 0, blk_index // 2, 7 - blk_index // 2)

    spot = (ring_place + jnp.arange(blk_count, dtype=jnp.int32)) % blk_count
    at = jnp.where(spot < 4, 2 * spot, 15 - 2 * spot).astype(jnp.int32)
    at_own = jnp.concatenate([at, head_index[None].astype(jnp.int32)])
    ring_spot = (ring_place + jnp.asarray(STRIPS, jnp.int32)) % blk_count
    strip_blk = jnp.where(ring_spot < 4, 2 * ring_spot, 15 - 2 * ring_spot)
    strip_head = head_index ^ jnp.asarray((0, 2, 1, 3), jnp.int32)
    strip = (strip_blk[None, :] * head_count + strip_head[:, None]).reshape(strip_count)
    slots = jnp.arange(stretch_order.shape[1], dtype=jnp.int32)
    held = jnp.sum(
        jnp.where((strip // halves)[:, None] == slots[None, :], stretch_order, 0), axis=1
    )
    strip_place = held * halves + strip % halves
    order = strip_place.astype(jnp.int32)
    place = strip_place[:blk_count].astype(jnp.int32)
    positions = (
        place[:, None] * local_rows + jnp.arange(local_rows, dtype=jnp.int32)[None, :]
    ).reshape(group_rows)
    phases = angles(positions, HEAD_SIZE)[:, 0, :]
    cosine, sine = jnp.cos(phases), jnp.sin(phases)
    cosine = jnp.concatenate([cosine, cosine], axis=1)
    sine = jnp.concatenate([-sine, sine], axis=1)

    small = query_norm.shape[0]
    number = blk_index * head_count + head_index
    pad = 16

    def placed(share):
        return jnp.where(
            jnp.arange(device_count, dtype=jnp.int32)[:, None] == number, share[None, :], 0
        ).reshape(-1)

    gains = jnp.concatenate(
        [placed(attention_norm), placed(feedforward_norm), placed(query_norm), placed(key_norm)]
    ).astype(narrow)
    gains = jnp.pad(gains, (0, pad * attn_cols - gains.shape[0])).reshape(pad, attn_cols)
    down_matrix = gather_head(down_weight)
    output_rows = gather_head(output_weight)

    attn_swap = Swap(
        slice_pieces(at, query_weight, key_projection, value_projection, pad=gains),
        weight_rows + pad,
    )
    token_ring = Gather(tokens)
    ff_slices = slice_pieces(at, gate_weight, up_weight)
    token_ring.go()
    attn_swap.go()
    ff_slices, cosine, sine = hold((attn_swap,), ff_slices, cosine, sine)
    attn_swap.go()
    hold((attn_swap,))
    attn_swap.go()
    hold((attn_swap,))
    attn_swap.go()
    own = hold((token_ring,), attn_swap.result())
    near, far = cross(own, 1), cross(own, 2)
    token_ring.go()
    ff_swap, cotangent_ring = Swap(ff_slices, weight_rows), Gather(out_cotangent)
    hold((token_ring, ff_swap, cotangent_ring))
    token_ring.go()
    own, near, far = hold((token_ring,), own, near, far)
    both = cross(far, 1)
    token_ring.go()
    own, near, far, both = hold((token_ring, ff_swap, cotangent_ring), own, near, far, both)
    ff_swap.go()
    cotangent_ring.go()

    first_normed, attn_raw, query_rows, own, attn_matrix, gains = project(
        at_own, token_ring.strips(), (own, near, far, both), cosine, sine, query_cols, pad
    )
    gain_one = gains[:4].reshape(1, model_width)
    gain_two = gains[4:8].reshape(1, model_width)
    head_gains = jnp.pad(gains[8, : 2 * HEAD_SIZE].reshape(2, HEAD_SIZE), ((0, 6), (0, 0)))
    near, far = cross(own, 1), cross(own, 2)
    own, near, far = hold((ff_swap, cotangent_ring), own, near, far)
    both = cross(far, 1)
    kv = hold((ff_swap, cotangent_ring), own, far, near, both)
    ff_swap.go(late=True)
    cotangent_ring.go()
    attended, lse = attend(place, order, query_rows, kv)

    def by_groups(rows):
        return [rows[a * local_rows : b * local_rows] for a, b in GROUPS]

    def by_strips(groups):
        return dict(zip(STRIPS, split_groups(groups, local_rows)))

    attended = hold((cotangent_ring, ff_swap), attended)
    branch_parts = [matmul(rows, output_rows).astype(narrow) for rows in by_groups(attended)]
    branch_ring = Scatter(by_strips(branch_parts))
    branch_ring.go()
    ff_swap.trim()
    ff_swap.go()
    hold((branch_ring, ff_swap))
    branch_ring.go()
    ff_swap.go()
    cotangent_ring.go()
    ff_own = hold((branch_ring, cotangent_ring), ff_swap.result())
    ff_near, ff_far = cross(ff_own, 1), cross(ff_own, 2)
    branch_ring.go()
    cotangent_ring.go()
    cotangent_strips, down_matrix = hold(
        (branch_ring, cotangent_ring), cotangent_ring.strips(), down_matrix
    )
    branch_ring.go()
    hidden_grads = hidden_grads_of(cotangent_strips, down_matrix)
    hidden_grads, ff_near, ff_far = hold((branch_ring,), hidden_grads, ff_near, ff_far)
    ff_both = cross(ff_far, 1)
    tokens_wide = tokens.astype(wide)
    resid = tokens_wide + branch_ring.total()
    rho_two = inverse_rms(resid)
    unit_two = resid * rho_two

    second_ring = Gather((unit_two * gain_two).astype(narrow))
    second_groups, hidden_groups, ff_gradient_groups = [], [], []

    def feed_forward(index):
        rows = second_ring.group(index)
        ff_raw = matmul(rows, ff_matrix)
        gate, up_proj = ff_raw[:, :ff_local], ff_raw[:, ff_local:]
        sigma = jax.nn.sigmoid(gate)
        swish = gate * sigma
        hidden_gradient = hidden_grads[index]
        gate_gradient = hidden_gradient * up_proj * (sigma * (1.0 + gate * (1.0 - sigma)))
        hidden = (swish * up_proj).astype(narrow)
        gradient = jnp.concatenate([gate_gradient, hidden_gradient * swish], 1).astype(narrow)
        if index < 3:
            rows, hidden, gradient = hold((second_ring,), rows, hidden, gradient)
        second_groups.append(rows)
        hidden_groups.append(hidden)
        ff_gradient_groups.append(gradient)

    second_ring.go()
    ff_matrix = assemble(at_own, (ff_own, ff_near, ff_far, ff_both), weight_rows)
    ff_matrix = hold((second_ring,), ff_matrix)
    for index in range(3):
        second_ring.go()
        feed_forward(index)
    feed_forward(3)

    def back(index):
        return matmul(ff_gradient_groups[index], ff_matrix, ALONG).astype(narrow)

    def split(group):
        return [group[i : i + local_rows] for i in range(0, group.shape[0], local_rows)]

    parts = {4: back(3)}
    resid_ring = Scatter(parts)
    parts[3], parts[5] = split(hold((), back(2)))
    parts[2], parts[6] = split(hold((), back(1)))
    resid_ring.go()
    _, _, hidden_groups, cotangent_strips = hold(
        (resid_ring,), parts[2], parts[6], hidden_groups, cotangent_strips
    )
    resid_ring.go()
    down_gradient = row_grads(hidden_groups, cotangent_strips)
    back_zero, down_gradient, second_groups, ff_gradient_groups = hold(
        (resid_ring,), back(0), down_gradient, second_groups, ff_gradient_groups
    )
    down_gradient = scatter_head(down_gradient)
    parts[0], parts[1], parts[7] = split(back_zero)
    resid_ring.go()
    ff_own, ff_far, ff_sent = hold(
        (resid_ring,), *weight_grads(at_own, second_groups, ff_gradient_groups, weight_rows)
    )
    resid_ring.go()
    ff_own, ff_far = scatter_cross(ff_own, ff_far, ff_sent)
    ff_own, ff_far, hidden_groups = hold((resid_ring,), ff_own, ff_far, hidden_groups)
    ff_far = cross(ff_far, 2)
    scaled = gain_two * resid_ring.total()
    resid_gradient = out_cotangent.astype(wide) + rho_two * (
        scaled - unit_two * jnp.mean(unit_two * scaled, axis=-1, keepdims=True)
    )

    grad_ring = Gather(resid_gradient.astype(narrow))
    grad_groups, attended_grads = [], []

    def attention_back(index):
        rows = grad_ring.group(index)
        grads = matmul(rows, output_rows, ALONG).astype(narrow)
        if index < 3:
            rows, grads = hold((grad_ring,), rows, grads)
        grad_groups.append(rows)
        attended_grads.append(grads)

    grad_ring.go()
    out_parts = [matmul(rows, down_matrix).astype(narrow) for rows in hidden_groups]
    out_parts = hold((grad_ring,), *out_parts)
    out_ring = Scatter(by_strips(out_parts))
    grad_ring.go()
    hold((grad_ring,))
    grad_ring.go()
    attention_back(0)
    hold((out_ring, grad_ring))
    out_ring.go()
    grad_ring.go()
    attention_back(1)
    attention_back(2)
    ff_swap = Swap(add(ff_own, ff_far), weight_rows)
    hold((grad_ring, ff_swap, out_ring))
    out_ring.go()
    ff_swap.go(late=True)
    attention_back(3)
    query_grads, kv_own, kv_far, kv_sent = attend_back(
        place, order, query_rows, attended_grads, attended, lse, kv
    )
    query_grads, kv_own, kv_far, kv_sent, grad_groups, attended = hold(
        (out_ring, ff_swap), query_grads, kv_own, kv_far, kv_sent, grad_groups, attended
    )
    out_ring.go()
    ff_swap.trim()
    kv_own, kv_far = scatter_cross(kv_own, kv_far, kv_sent)
    output_weight_gradient = row_grads([attended], grad_groups)
    kv_own, kv_far, output_weight_gradient = hold(
        (out_ring, ff_swap), kv_own, kv_far, output_weight_gradient
    )
    ff_swap.go()
    kv_grads = hold((ff_swap,), add(kv_own, cross(kv_far, 2)))
    ff_swap.go()
    attn_gradient, first_parts, gain_sums = project_back(
        query_grads, kv_grads, attn_raw, head_gains, cosine, sine, attn_matrix
    )
    gain_sums = jnp.pad(
        gain_sums[:2].reshape(1, 2 * HEAD_SIZE).astype(narrow),
        ((0, pad - 1), (0, attn_cols - 2 * HEAD_SIZE)),
    )
    attn_gradient, first_parts, gain_sums, output_weight_gradient = hold(
        (ff_swap, out_ring), attn_gradient, first_parts, gain_sums, output_weight_gradient
    )
    token_ring = Scatter(by_strips(by_groups(first_parts)))
    token_ring.go()
    ff_swap.go()
    out_ring.go()
    attn_own, attn_far, attn_sent = weight_grads(
        at_own, [first_normed], [attn_gradient], weight_rows, gain_sums
    )
    attn_own, attn_far, attn_sent = hold(
        (token_ring, ff_swap, out_ring), attn_own, attn_far, attn_sent
    )
    token_ring.go()
    attn_own, attn_far = scatter_cross(attn_own, attn_far, attn_sent)
    attn_far = cross(attn_far, 2)
    layer_out = (resid + out_ring.total()).astype(narrow)
    gate_weight_gradient, up_weight_gradient, ff_sums = widen(at, ff_swap, gate_weight, up_weight)
    attn_swap = Swap(add(attn_own, attn_far), weight_rows + pad)
    gate_weight_gradient, up_weight_gradient, ff_sums, output_weight_gradient, layer_out = hold(
        (token_ring, attn_swap),
        gate_weight_gradient, up_weight_gradient, ff_sums, output_weight_gradient, layer_out,
    )
    output_weight_gradient = scatter_head(output_weight_gradient)
    attn_swap.go()
    token_ring.go()
    feedforward_norm_gradient = jnp.sum(ff_sums, axis=1) / feedforward_norm.astype(wide)
    feedforward_norm_gradient, down_gradient = hold(
        (token_ring, attn_swap), feedforward_norm_gradient, down_gradient.astype(wide)
    )
    attn_swap.go()
    token_ring.go()
    output_weight_gradient = hold(
        (token_ring, attn_swap), output_weight_gradient.astype(wide)
    )
    attn_swap.go()
    hold((attn_swap,))
    attn_swap.go()
    query_weight_gradient, key_weight_gradient, value_weight_gradient, norm_sums, gain_sums = widen(
        at, attn_swap, query_weight, key_projection, value_projection
    )
    attention_norm_gradient = jnp.sum(norm_sums, axis=1) / attention_norm.astype(wide)
    gain_sums = gain_sums[0, : 2 * HEAD_SIZE].reshape(2, HEAD_SIZE)
    gain_sums = lax.dynamic_slice_in_dim(gain_sums, number * small, small, 1)
    rho_one = inverse_rms(tokens_wide)
    unit_one = tokens_wide * rho_one
    scaled = gain_one * token_ring.total()
    tokens_gradient = resid_gradient + rho_one * (
        scaled - unit_one * jnp.mean(unit_one * scaled, axis=-1, keepdims=True)
    )
    return (
        layer_out[None],
        tokens_gradient.astype(narrow)[None],
        attention_norm_gradient,
        query_weight_gradient,
        key_weight_gradient,
        value_weight_gradient,
        gain_sums[0],
        gain_sums[1],
        output_weight_gradient,
        feedforward_norm_gradient,
        gate_weight_gradient,
        up_weight_gradient,
        down_gradient,
    )


def solution(mesh):
    placed = (
        P(None, ("blk", "head"), None),
        P(("blk", "head")),
        P(("blk", "head"), None),
        P(("blk", "head"), None),
        P(("blk", "head"), None),
        P(("blk", "head")),
        P(("blk", "head")),
        P(("blk", "head"), None),
        P(("blk", "head")),
        P(("blk", "head"), None),
        P(("blk", "head"), None),
        P(("blk", "head"), None),
        P(),
        P(None, ("blk", "head"), None),
    )
    fits = mesh.shape["blk"] == KEY_VALUE_HEADS and mesh.shape["head"] == 4
    return jax.shard_map(
        per_device if fits else per_device_by_tokens,
        mesh=mesh,
        in_specs=placed,
        out_specs=(
            P(None, ("blk", "head"), None),
            P(None, ("blk", "head"), None),
            P(("blk", "head")),
            P(("blk", "head"), None),
            P(("blk", "head"), None),
            P(("blk", "head"), None),
            P(("blk", "head")),
            P(("blk", "head")),
            P(("blk", "head"), None),
            P(("blk", "head")),
            P(("blk", "head"), None),
            P(("blk", "head"), None),
            P(("blk", "head"), None),
        ),
        check_vma=False,
    )
```

```python
import math

import jax
import jax.numpy as jnp
from jax import lax
from jax.experimental import pallas as pl
from jax.experimental.pallas import tpu as pltpu
from jax.sharding import PartitionSpec as P

QUERY_HEADS = 16
KEY_VALUE_HEADS = 8
HEAD_SIZE = 128


EPS = 1e-06
NEG = -1e30
ROPE_BASE = 1000000.0


def passed_along(value, axis, by):
    count = lax.axis_size(axis)
    return lax.ppermute(value, axis, [(i, (i + by) % count) for i in range(count)])


def norm_rows(inputs, norm_gain):
    return inputs * lax.rsqrt(jnp.mean(inputs * inputs, axis=-1, keepdims=True) + EPS) * norm_gain


def rotary(inputs, phases):
    half_width = inputs.shape[-1] // 2
    cosine = jnp.cos(phases)
    sine_term = jnp.sin(phases)
    first_half = inputs[..., :half_width]
    second_half = inputs[..., half_width:]
    return jnp.concatenate(
        [
            first_half * cosine - second_half * sine_term,
            second_half * cosine + first_half * sine_term,
        ],
        axis=-1,
    )


def angles(positions, head_width):
    half_width = head_width // 2
    frequency = jnp.exp(
        jnp.arange(half_width, dtype=jnp.float32) * (-2.0 * math.log(ROPE_BASE) / head_width)
    )
    return positions.astype(jnp.float32)[..., None, None] * frequency


def token_positions(stretch_order, first_row, row_count, stretch_rows):
    row_index = first_row + jnp.arange(row_count, dtype=jnp.int32)
    slot_index = row_index // stretch_rows
    matches = slot_index[:, None] == jnp.arange(stretch_order.shape[1], dtype=jnp.int32)[None, :]
    picked = jnp.sum(jnp.where(matches[None], stretch_order[:, None, :], 0), axis=-1)
    return picked * stretch_rows + row_index % stretch_rows


def per_device_by_tokens(
    tokens,
    attention_norm,
    query_weight,
    key_projection,
    value_projection,
    query_norm,
    key_norm,
    output_weight,
    feedforward_norm,
    gate_weight,
    up_weight,
    down_weight,
    stretch_order,
    out_cotangent,
):
    count_of_heads = lax.axis_size("head")
    span_count = lax.axis_size("blk")
    span_index = lax.axis_index("blk")
    head_index = lax.axis_index("head")
    sequence_total = tokens.shape[0]
    local_rows = tokens.shape[1]
    group_rows = local_rows * count_of_heads
    stretch_rows = group_rows // 2
    heads_shared = KEY_VALUE_HEADS // count_of_heads
    heads_per_group = QUERY_HEADS // KEY_VALUE_HEADS
    score_scale = 1.0 / math.sqrt(HEAD_SIZE)
    gain_one, query_matrix, key_matrix, value_matrix, query_gain, key_gain, output_matrix = (
        lax.all_gather(attention_norm, ("blk", "head"), axis=0, tiled=True),
        lax.all_gather(query_weight, ("blk", "head"), axis=0, tiled=True),
        lax.all_gather(key_projection, ("blk", "head"), axis=0, tiled=True),
        lax.all_gather(value_projection, ("blk", "head"), axis=0, tiled=True),
        lax.all_gather(query_norm, ("blk", "head"), axis=0, tiled=True),
        lax.all_gather(key_norm, ("blk", "head"), axis=0, tiled=True),
        lax.all_gather(output_weight, ("blk", "head"), axis=0, tiled=True),
    )
    gain_two, gate_matrix, up_matrix, down_matrix = (
        lax.all_gather(feedforward_norm, ("blk", "head"), axis=0, tiled=True),
        lax.all_gather(gate_weight, ("blk", "head"), axis=0, tiled=True),
        lax.all_gather(up_weight, ("blk", "head"), axis=0, tiled=True),
        lax.all_gather(down_weight, ("blk", "head"), axis=0, tiled=True),
    )
    gain_one = gain_one.astype(jnp.float32)
    gain_two = gain_two.astype(jnp.float32)
    query_gain = query_gain.astype(jnp.float32)
    key_gain = key_gain.astype(jnp.float32)
    own_first = (span_index * count_of_heads + head_index) * local_rows
    own_pos = token_positions(stretch_order, own_first, local_rows, stretch_rows)
    group_pos = token_positions(stretch_order, span_index * group_rows, group_rows, stretch_rows)
    phases = angles(own_pos, HEAD_SIZE)
    tokens_wide = tokens.astype(jnp.float32)
    first_normed, norm_one_back = jax.vjp(norm_rows, tokens_wide, gain_one)
    first_normed = first_normed.astype(jnp.bfloat16)
    query_raw = jnp.einsum(
        "btd,de->bte", first_normed, query_matrix, preferred_element_type=jnp.float32
    ).reshape(sequence_total, local_rows, QUERY_HEADS, HEAD_SIZE)
    key_unnormed = jnp.einsum(
        "btd,de->bte", first_normed, key_matrix, preferred_element_type=jnp.float32
    ).reshape(sequence_total, local_rows, KEY_VALUE_HEADS, HEAD_SIZE)
    value_tokens = (
        jnp.einsum("btd,de->bte", first_normed, value_matrix, preferred_element_type=jnp.float32)
        .astype(jnp.bfloat16)
        .reshape(sequence_total, local_rows, KEY_VALUE_HEADS, HEAD_SIZE)
    )

    def heads_local(query_in, key_in, query_scale, key_scale):
        return (
            rotary(norm_rows(query_in, query_scale), phases),
            rotary(norm_rows(key_in, key_scale), phases),
        )

    (query_tokens, key_tokens), heads_back = jax.vjp(
        heads_local, query_raw, key_unnormed, query_gain, key_gain
    )
    query_tokens = query_tokens.astype(jnp.bfloat16)
    key_tokens = key_tokens.astype(jnp.bfloat16)
    query_group, key_group, value_group = (
        lax.all_to_all(query_tokens, "head", split_axis=2, concat_axis=1, tiled=True),
        lax.all_to_all(key_tokens, "head", split_axis=2, concat_axis=1, tiled=True),
        lax.all_to_all(value_tokens, "head", split_axis=2, concat_axis=1, tiled=True),
    )
    query_five = query_group.reshape(
        sequence_total, group_rows, heads_shared, heads_per_group, HEAD_SIZE
    )

    def block_update(carry, key_block, value_block, key_pos):
        run_max, run_sum, run_total = carry
        scores = (
            jnp.einsum(
                "bqkgd,bckd->bkgqc", query_five, key_block, preferred_element_type=jnp.float32
            )
            * score_scale
        )
        allowed = key_pos[:, None, None, None, :] <= group_pos[:, None, None, :, None]
        scores = jnp.where(allowed, scores, NEG)
        new_max = jnp.maximum(run_max, jnp.max(scores, axis=-1))
        exponent = jnp.where(allowed, jnp.exp(scores - new_max[..., None]), 0.0)
        factor = jnp.exp(run_max - new_max)
        new_sum = run_sum * factor + jnp.sum(exponent, axis=-1)
        new_total = run_total * factor[..., None] + jnp.einsum(
            "bkgqc,bckd->bkgqd",
            exponent.astype(jnp.bfloat16),
            value_block,
            preferred_element_type=jnp.float32,
        )
        return (new_max, new_sum, new_total)

    def fold_update(carry, key_block, value_block, key_pos):
        result = block_update(carry, key_block, value_block, key_pos)
        return result

    stat_shape = (sequence_total, heads_shared, heads_per_group, group_rows)
    start_state = (
        jnp.full(stat_shape, NEG, jnp.float32),
        jnp.zeros(stat_shape, jnp.float32),
        jnp.zeros(stat_shape + (HEAD_SIZE,), jnp.float32),
    )
    key_piece = lax.all_gather(key_group, "blk", axis=1, tiled=True)
    value_piece = lax.all_gather(value_group, "blk", axis=1, tiled=True)
    piece_rows = key_piece.shape[1]
    block_len = math.gcd(group_rows, piece_rows)

    def inner(block_number, carry_in):
        offset = block_number * block_len
        key_block = lax.dynamic_slice_in_dim(key_piece, offset, block_len, 1)
        value_block = lax.dynamic_slice_in_dim(value_piece, offset, block_len, 1)
        key_pos = token_positions(stretch_order, offset, block_len, stretch_rows)
        return fold_update(carry_in, key_block, value_block, key_pos)

    run_max, run_sum, run_total = lax.fori_loop(0, piece_rows // block_len, inner, start_state)
    log_total = run_max + jnp.log(run_sum)
    attended_five = run_total / run_sum[..., None]
    attended_group = (
        jnp.transpose(attended_five, (0, 3, 1, 2, 4))
        .reshape(sequence_total, group_rows, heads_shared * heads_per_group, HEAD_SIZE)
        .astype(jnp.bfloat16)
    )
    attended_tokens = lax.all_to_all(
        attended_group, "head", split_axis=1, concat_axis=2, tiled=True
    ).reshape(sequence_total, local_rows, QUERY_HEADS * HEAD_SIZE)
    branch = jnp.einsum(
        "bte,ed->btd", attended_tokens, output_matrix, preferred_element_type=jnp.float32
    )
    resid = tokens_wide + branch
    normed_two, norm_two_back = jax.vjp(norm_rows, resid, gain_two)
    normed_two = normed_two.astype(jnp.bfloat16)
    gate = jnp.einsum("btd,df->btf", normed_two, gate_matrix, preferred_element_type=jnp.float32)
    up_proj = jnp.einsum("btd,df->btf", normed_two, up_matrix, preferred_element_type=jnp.float32)

    def swish_product(gate_in, up_in):
        return jax.nn.silu(gate_in) * up_in

    hidden, swish_back = jax.vjp(swish_product, gate, up_proj)
    hidden = hidden.astype(jnp.bfloat16)
    layer_out = (
        resid + jnp.einsum("btf,fd->btd", hidden, down_matrix, preferred_element_type=jnp.float32)
    ).astype(jnp.bfloat16)
    gain_again, gate_matrix, up_matrix, down_matrix = (
        lax.all_gather(feedforward_norm, ("blk", "head"), axis=0, tiled=True),
        lax.all_gather(gate_weight, ("blk", "head"), axis=0, tiled=True),
        lax.all_gather(up_weight, ("blk", "head"), axis=0, tiled=True),
        lax.all_gather(down_weight, ("blk", "head"), axis=0, tiled=True),
    )
    down_gradient = jnp.einsum(
        "btf,btd->fd", hidden, out_cotangent, preferred_element_type=jnp.float32
    )
    hidden_gradient = jnp.einsum(
        "btd,fd->btf", out_cotangent, down_matrix, preferred_element_type=jnp.float32
    )
    gate_gradient, up_gradient = swish_back(hidden_gradient)
    gate_gradient = gate_gradient.astype(jnp.bfloat16)
    up_gradient = up_gradient.astype(jnp.bfloat16)
    gate_matrix_gradient = jnp.einsum(
        "btd,btf->df", normed_two, gate_gradient, preferred_element_type=jnp.float32
    )
    up_matrix_gradient = jnp.einsum(
        "btd,btf->df", normed_two, up_gradient, preferred_element_type=jnp.float32
    )
    normed_two_gradient = jnp.einsum(
        "btf,df->btd", gate_gradient, gate_matrix, preferred_element_type=jnp.float32
    ) + jnp.einsum("btf,df->btd", up_gradient, up_matrix, preferred_element_type=jnp.float32)
    resid_part, gain_two_gradient = norm_two_back(normed_two_gradient)
    resid_gradient = out_cotangent.astype(jnp.float32) + resid_part
    feedforward_sums = (
        lax.psum_scatter(gain_two_gradient, ("blk", "head"), scatter_dimension=0, tiled=True),
        lax.psum_scatter(gate_matrix_gradient, ("blk", "head"), scatter_dimension=0, tiled=True),
        lax.psum_scatter(up_matrix_gradient, ("blk", "head"), scatter_dimension=0, tiled=True),
        lax.psum_scatter(down_gradient, ("blk", "head"), scatter_dimension=0, tiled=True),
    )
    gain_again, query_matrix, key_matrix, value_matrix, query_again, key_again, output_matrix = (
        lax.all_gather(attention_norm, ("blk", "head"), axis=0, tiled=True),
        lax.all_gather(query_weight, ("blk", "head"), axis=0, tiled=True),
        lax.all_gather(key_projection, ("blk", "head"), axis=0, tiled=True),
        lax.all_gather(value_projection, ("blk", "head"), axis=0, tiled=True),
        lax.all_gather(query_norm, ("blk", "head"), axis=0, tiled=True),
        lax.all_gather(key_norm, ("blk", "head"), axis=0, tiled=True),
        lax.all_gather(output_weight, ("blk", "head"), axis=0, tiled=True),
    )
    branch_gradient = resid_gradient.astype(jnp.bfloat16)
    output_matrix_gradient = jnp.einsum(
        "bte,btd->ed", attended_tokens, branch_gradient, preferred_element_type=jnp.float32
    )
    attended_gradient = (
        jnp.einsum(
            "btd,ed->bte", branch_gradient, output_matrix, preferred_element_type=jnp.float32
        )
        .astype(jnp.bfloat16)
        .reshape(sequence_total, local_rows, QUERY_HEADS, HEAD_SIZE)
    )
    attended_grad_group = lax.all_to_all(
        attended_gradient, "head", split_axis=2, concat_axis=1, tiled=True
    ).reshape(sequence_total, group_rows, heads_shared, heads_per_group, HEAD_SIZE)
    delta = jnp.sum(
        jnp.transpose(attended_grad_group.astype(jnp.float32), (0, 2, 3, 1, 4)) * attended_five,
        axis=-1,
    )

    def block_grads(sums_in, key_current, value_current, key_pos):
        key_sum, value_sum, query_sum = sums_in
        scores = (
            jnp.einsum(
                "bqkgd,bckd->bkgqc", query_five, key_current, preferred_element_type=jnp.float32
            )
            * score_scale
        )
        allowed = key_pos[:, None, None, None, :] <= group_pos[:, None, None, :, None]
        weights = jnp.where(allowed, jnp.exp(scores - log_total[..., None]), 0.0)
        probs = weights.astype(jnp.bfloat16)
        value_sum = value_sum + jnp.einsum(
            "bkgqc,bqkgd->bckd", probs, attended_grad_group, preferred_element_type=jnp.float32
        )
        probs_gradient = jnp.einsum(
            "bqkgd,bckd->bkgqc",
            attended_grad_group,
            value_current,
            preferred_element_type=jnp.float32,
        )
        scores_gradient = (weights * (probs_gradient - delta[..., None])).astype(jnp.bfloat16)
        query_sum = (
            query_sum
            + jnp.einsum(
                "bkgqc,bckd->bqkgd",
                scores_gradient,
                key_current,
                preferred_element_type=jnp.float32,
            )
            * score_scale
        )
        key_sum = (
            key_sum
            + jnp.einsum(
                "bkgqc,bqkgd->bckd", scores_gradient, query_five, preferred_element_type=jnp.float32
            )
            * score_scale
        )
        return (key_sum, value_sum, query_sum)

    def pass_step(step_index, carry):
        key_current, value_current, key_sum, value_sum, query_sum = carry
        anchor = (span_index - step_index) % span_count
        key_pos = token_positions(stretch_order, anchor * group_rows, group_rows, stretch_rows)
        key_sum, value_sum, query_sum = block_grads(
            (key_sum, value_sum, query_sum), key_current, value_current, key_pos
        )
        key_current, value_current = passed_along((key_current, value_current), "blk", 1)
        key_sum, value_sum = (
            passed_along(key_sum.astype(jnp.bfloat16), "blk", 1).astype(key_sum.dtype),
            passed_along(value_sum.astype(jnp.bfloat16), "blk", 1).astype(value_sum.dtype),
        )
        return (key_current, value_current, key_sum, value_sum, query_sum)

    kv_zeros = jnp.zeros((sequence_total, group_rows, heads_shared, HEAD_SIZE), jnp.float32)
    query_zeros = jnp.zeros(
        (sequence_total, group_rows, heads_shared, heads_per_group, HEAD_SIZE), jnp.float32
    )
    final_state = lax.fori_loop(
        0, span_count, pass_step, (key_group, value_group, kv_zeros, kv_zeros, query_zeros)
    )
    key_grad_group = final_state[2].astype(jnp.bfloat16)
    value_grad_group = final_state[3].astype(jnp.bfloat16)
    query_grad_group = (
        final_state[4]
        .astype(jnp.bfloat16)
        .reshape(sequence_total, group_rows, heads_shared * heads_per_group, HEAD_SIZE)
    )
    query_grad_tokens, key_grad_tokens, value_gradient_tokens = (
        lax.all_to_all(query_grad_group, "head", split_axis=1, concat_axis=2, tiled=True),
        lax.all_to_all(key_grad_group, "head", split_axis=1, concat_axis=2, tiled=True),
        lax.all_to_all(value_grad_group, "head", split_axis=1, concat_axis=2, tiled=True),
    )
    query_raw_gradient, key_unnormed_gradient, query_gain_gradient, key_gain_gradient = heads_back(
        (query_grad_tokens.astype(jnp.float32), key_grad_tokens.astype(jnp.float32))
    )
    query_raw_gradient = query_raw_gradient.astype(jnp.bfloat16).reshape(
        sequence_total, local_rows, QUERY_HEADS * HEAD_SIZE
    )
    key_unnormed_gradient = key_unnormed_gradient.astype(jnp.bfloat16).reshape(
        sequence_total, local_rows, KEY_VALUE_HEADS * HEAD_SIZE
    )
    value_unnormed_gradient = value_gradient_tokens.reshape(
        sequence_total, local_rows, KEY_VALUE_HEADS * HEAD_SIZE
    )
    query_matrix_gradient = jnp.einsum(
        "btd,bte->de", first_normed, query_raw_gradient, preferred_element_type=jnp.float32
    )
    key_matrix_gradient = jnp.einsum(
        "btd,bte->de", first_normed, key_unnormed_gradient, preferred_element_type=jnp.float32
    )
    value_matrix_gradient = jnp.einsum(
        "btd,bte->de", first_normed, value_unnormed_gradient, preferred_element_type=jnp.float32
    )
    normed_one_gradient = jnp.einsum(
        "bte,de->btd", query_raw_gradient, query_matrix, preferred_element_type=jnp.float32
    )
    normed_one_gradient = normed_one_gradient + jnp.einsum(
        "bte,de->btd", key_unnormed_gradient, key_matrix, preferred_element_type=jnp.float32
    )
    normed_one_gradient = normed_one_gradient + jnp.einsum(
        "bte,de->btd", value_unnormed_gradient, value_matrix, preferred_element_type=jnp.float32
    )
    token_part, gain_one_gradient = norm_one_back(normed_one_gradient)
    tokens_gradient = (resid_gradient + token_part).astype(jnp.bfloat16)
    attention_sums = (
        lax.psum_scatter(gain_one_gradient, ("blk", "head"), scatter_dimension=0, tiled=True),
        lax.psum_scatter(query_matrix_gradient, ("blk", "head"), scatter_dimension=0, tiled=True),
        lax.psum_scatter(key_matrix_gradient, ("blk", "head"), scatter_dimension=0, tiled=True),
        lax.psum_scatter(value_matrix_gradient, ("blk", "head"), scatter_dimension=0, tiled=True),
        lax.psum_scatter(query_gain_gradient, ("blk", "head"), scatter_dimension=0, tiled=True),
        lax.psum_scatter(key_gain_gradient, ("blk", "head"), scatter_dimension=0, tiled=True),
        lax.psum_scatter(output_matrix_gradient, ("blk", "head"), scatter_dimension=0, tiled=True),
    )
    return (
        layer_out,
        tokens_gradient,
        attention_sums[0],
        attention_sums[1],
        attention_sums[2],
        attention_sums[3],
        attention_sums[4],
        attention_sums[5],
        attention_sums[6],
        feedforward_sums[0],
        feedforward_sums[1],
        feedforward_sums[2],
        feedforward_sums[3],
    )


LOG2E = math.log2(math.e)
STRIP = 128
CHUNK = 512
ALONG = (((1,), (1,)), ((), ()))
DOWN = (((0,), (0,)), ((), ()))


def two_heads(block):
    return jnp.concatenate([block[:, :HEAD_SIZE], block[:, HEAD_SIZE:]], axis=0)


def side_by_side(rows):
    half = rows.shape[0] // 2
    return jnp.concatenate([rows[:half], rows[half:]], axis=1)


CHEAP = pl.CostEstimate(flops=1, bytes_accessed=1, transcendentals=0)
LONG = pl.CostEstimate(flops=3 * 10**10, bytes_accessed=1 << 25, transcendentals=0)


def sort_strips(order_ref, kv_refs, keys, values):
    per = kv_refs[0].shape[0] // STRIP
    for j, ref in enumerate(kv_refs):
        for i in range(per):
            target = pl.multiple_of(order_ref[j * per + i] * STRIP, STRIP)
            here = slice(i * STRIP, (i + 1) * STRIP)
            keys[pl.ds(target, STRIP), :] = ref[here, :HEAD_SIZE]
            values[pl.ds(target, STRIP), :HEAD_SIZE] = ref[here, HEAD_SIZE:]


def attend_kernel(place_ref, order_ref, q_ref, *refs):
    kv_refs, (out_ref, lse_ref, keys, values) = refs[:4], refs[4:]
    step = pl.program_id(0)

    @pl.when(step == 0)
    def _():
        values[:, HEAD_SIZE:] = jnp.ones((values.shape[0], HEAD_SIZE), jnp.bfloat16)
        sort_strips(order_ref, kv_refs, keys, values)

    place = place_ref[step]
    queries = two_heads(q_ref[...])
    last = place // (CHUNK // STRIP)

    def part(index, total, masked):
        first = pl.multiple_of(index * CHUNK, CHUNK)
        scores = lax.dot_general(
            queries, keys[pl.ds(first, CHUNK), :], ALONG, preferred_element_type=jnp.float32
        )
        weights = jnp.exp2(scores)
        if masked:
            row = lax.broadcasted_iota(jnp.int32, scores.shape, 0) % STRIP
            column = lax.broadcasted_iota(jnp.int32, scores.shape, 1)
            weights = jnp.where(column - row <= place * STRIP - first, weights, 0.0)
        return total + jnp.dot(
            weights.astype(jnp.bfloat16),
            values[pl.ds(first, CHUNK), :],
            preferred_element_type=jnp.float32,
        )

    total = jnp.zeros((2 * STRIP, 2 * HEAD_SIZE), jnp.float32)
    total = lax.fori_loop(0, last, lambda index, t: part(index, t, False), total)
    total = part(last, total, True)
    norm = total[:, HEAD_SIZE:]
    out_ref[...] = side_by_side(total[:, :HEAD_SIZE] / norm).astype(jnp.bfloat16)
    lse_ref[0] = jnp.transpose(jnp.log2(norm))[:8]


def attend(place, order, queries, kv):
    rows, width = queries.shape
    steps = rows // STRIP
    total = sum(part.shape[0] for part in kv)
    strip = pl.BlockSpec((STRIP, width), lambda i, *_: (i, 0))
    return pl.pallas_call(
        attend_kernel,
        grid_spec=pltpu.PrefetchScalarGridSpec(
            num_scalar_prefetch=2,
            grid=(steps,),
            in_specs=[strip] + [pl.BlockSpec(part.shape, lambda i, *_: (0, 0)) for part in kv],
            out_specs=[strip, pl.BlockSpec((1, 8, 2 * STRIP), lambda i, *_: (i, 0, 0))],
            scratch_shapes=[
                pltpu.VMEM((total, HEAD_SIZE), jnp.bfloat16),
                pltpu.VMEM((total, 2 * HEAD_SIZE), jnp.bfloat16),
            ],
        ),
        out_shape=[
            jax.ShapeDtypeStruct((rows, width), jnp.bfloat16),
            jax.ShapeDtypeStruct((steps, 8, 2 * STRIP), jnp.float32),
        ],
        cost_estimate=LONG,
        name="attend",
    )(place, order, queries, *kv)


def attend_back_kernel(place_ref, order_ref, q_ref, out_ref, lse_ref, *refs, groups):
    grad_refs, kv_refs = refs[:groups], refs[groups : groups + 4]
    dq_ref, own_ref, far_ref, sent_ref = refs[groups + 4 : groups + 8]
    keys, values, key_sums, value_sums, grads_all = refs[groups + 8 :]
    step = pl.program_id(0)

    @pl.when(step == 0)
    def _():
        key_sums[...] = jnp.zeros_like(key_sums)
        value_sums[...] = jnp.zeros_like(value_sums)
        sort_strips(order_ref, kv_refs, keys, values)
        first = 0
        for ref in grad_refs:
            grads_all[first : first + ref.shape[0], :] = ref[...]
            first += ref.shape[0]

    place = place_ref[step]
    queries = two_heads(q_ref[...])
    grads = two_heads(grads_all[pl.ds(pl.multiple_of(step * STRIP, STRIP), STRIP), :])
    product = grads.astype(jnp.float32) * two_heads(out_ref[...]).astype(jnp.float32)
    delta = jnp.sum(jnp.transpose(product), axis=0, keepdims=True)
    lse = lse_ref[0, :1]
    last = place // (CHUNK // STRIP)

    def part(index, total, masked):
        first = pl.multiple_of(index * CHUNK, CHUNK)
        here = pl.ds(first, CHUNK)
        key_rows = keys[here, :]
        scores = lax.dot_general(key_rows, queries, ALONG, preferred_element_type=jnp.float32)
        weights = jnp.exp2(scores - lse)
        if masked:
            row = lax.broadcasted_iota(jnp.int32, scores.shape, 0)
            column = lax.broadcasted_iota(jnp.int32, scores.shape, 1) % STRIP
            weights = jnp.where(row - column <= place * STRIP - first, weights, 0.0)
        slopes = lax.dot_general(
            values[here, :], grads, ALONG, preferred_element_type=jnp.float32
        )
        score_grads = (weights * (slopes - delta)).astype(jnp.bfloat16)
        value_sums[here, :] += jnp.dot(
            weights.astype(jnp.bfloat16), grads, preferred_element_type=jnp.float32
        )
        key_sums[here, :] += jnp.dot(score_grads, queries, preferred_element_type=jnp.float32)
        return total + lax.dot_general(
            score_grads, key_rows, DOWN, preferred_element_type=jnp.float32
        )

    total = jnp.zeros((2 * STRIP, HEAD_SIZE), jnp.float32)
    total = lax.fori_loop(0, last, lambda index, t: part(index, t, False), total)
    total = part(last, total, True)
    dq_ref[...] = side_by_side(total * (1.0 / math.sqrt(HEAD_SIZE))).astype(jnp.bfloat16)

    @pl.when(step == pl.num_programs(0) - 1)
    def _():
        per = own_ref.shape[0] // STRIP
        for j in range(4):
            target = (own_ref, far_ref, sent_ref, sent_ref)[j]
            base = per if j == 3 else 0
            for i in range(per):
                source = pl.multiple_of(order_ref[j * per + i] * STRIP, STRIP)
                here = slice((base + i) * STRIP, (base + i + 1) * STRIP)
                target[here, :HEAD_SIZE] = (
                    key_sums[pl.ds(source, STRIP), :] * (1.0 / LOG2E)
                ).astype(jnp.bfloat16)
                target[here, HEAD_SIZE:] = value_sums[pl.ds(source, STRIP), :].astype(
                    jnp.bfloat16
                )


def attend_back(place, order, queries, grads, attended, lse, kv):
    rows, width = queries.shape
    steps = rows // STRIP
    total = sum(part.shape[0] for part in kv)
    strip = pl.BlockSpec((STRIP, width), lambda i, *_: (i, 0))

    def whole(shape):
        return pl.BlockSpec(shape, lambda i, *_: (0, 0))

    outs = [kv[0].shape, kv[0].shape, (2 * kv[0].shape[0], kv[0].shape[1])]
    return pl.pallas_call(
        lambda *refs: attend_back_kernel(*refs, groups=len(grads)),
        grid_spec=pltpu.PrefetchScalarGridSpec(
            num_scalar_prefetch=2,
            grid=(steps,),
            in_specs=[strip, strip, pl.BlockSpec((1, 8, 2 * STRIP), lambda i, *_: (i, 0, 0))]
            + [whole(part.shape) for part in (*grads, *kv)],
            out_specs=[strip] + [whole(shape) for shape in outs],
            scratch_shapes=[
                pltpu.VMEM((total, HEAD_SIZE), jnp.bfloat16),
                pltpu.VMEM((total, HEAD_SIZE), jnp.bfloat16),
                pltpu.VMEM((total, HEAD_SIZE), jnp.float32),
                pltpu.VMEM((total, HEAD_SIZE), jnp.float32),
                pltpu.VMEM((rows, width), jnp.bfloat16),
            ],
        ),
        out_shape=[jax.ShapeDtypeStruct((rows, width), jnp.bfloat16)]
        + [jax.ShapeDtypeStruct(shape, jnp.bfloat16) for shape in outs],
        cost_estimate=LONG,
        name="attend_back",
    )(place, order, queries, attended, lse, *grads, *kv)


def matmul(left, right, dims=(((1,), (0,)), ((), ()))):
    return lax.dot_general(left, right, dims, preferred_element_type=jnp.float32)


RING = (0, 2, 4, 6, 7, 5, 3, 1)
STRIPS = (0, 1, 7, 2, 6, 3, 5, 4)
GROUPS = ((0, 3), (3, 5), (5, 7), (7, 8))


def hop(value, by):
    count = len(RING)
    return lax.ppermute(value, "blk", [(RING[i], RING[(i + by) % count]) for i in range(count)])


def cross(value, by):
    return lax.ppermute(value, "head", [(i, i ^ by) for i in range(4)])


def add(left, right):
    return (left.astype(jnp.float32) + right.astype(jnp.float32)).astype(left.dtype)


class Gather:
    def __init__(self, own):
        self.got, self.step = {0: own}, 0
        self.state = (own, own)

    def go(self):
        self.step += 1
        left, right = self.state
        if self.step < 4:
            self.state = hop(left, -1), hop(right, 1)
            self.got[self.step], self.got[8 - self.step] = self.state
        else:
            half = left.shape[0] // 2
            self.state = hop(left[:half], -1), hop(right[half:], 1)

    def strips(self):
        return [self.got[s] for s in STRIPS[:-1]] + list(self.state)

    def group(self, index):
        first, last = GROUPS[index]
        if index == 3:
            return jnp.concatenate(self.state, axis=0)
        return jnp.concatenate([self.got[s] for s in STRIPS[first:last]], axis=0)


class Scatter:
    def __init__(self, part):
        self.part, self.step = part, 0
        self.half = part[4].shape[0] // 2
        self.state = (part[4][: self.half], part[4][self.half :])

    def go(self):
        self.step += 1
        half, part = self.half, self.part
        up, down = hop(self.state[0], 1), hop(self.state[1], -1)
        if self.step == 1:
            up = jnp.concatenate([add(part[3][:half], up), part[3][half:]], axis=0)
            down = jnp.concatenate([part[5][:half], add(part[5][half:], down)], axis=0)
        elif self.step < 4:
            up, down = add(part[4 - self.step], up), add(part[4 + self.step], down)
        self.state = up, down

    def total(self):
        up, down = self.state
        wide = jnp.float32
        return self.part[0].astype(wide) + up.astype(wide) + down.astype(wide)


class Swap:
    def __init__(self, pieces, rows):
        self.rows, self.step = rows, 0
        self.taken = [(pieces, 0, rows, 0, 0)]
        self.across = pieces[4 * rows : 5 * rows]
        self.state = (pieces[rows : 4 * rows], pieces[5 * rows :])

    def go(self, late=False):
        self.step += 1
        rows, step = self.rows, self.step
        right, left = hop(self.state[0], 1), hop(self.state[1], -1)
        self.taken.append((right, 0, rows, 8 - step, 0))
        self.taken.append((left, left.shape[0] - rows, rows, step, 0))
        self.state = right, left
        if step == 1:
            self.taken.append((hop(self.across, 4), 0, rows, 4, 0))
        if step < 3 and not late:
            self.trim()

    def trim(self):
        self.state = self.state[0][self.rows :], self.state[1][: -self.rows]

    def operands(self):
        return [item[0] for item in self.taken]

    def specs(self):
        vmem = pl.BlockSpec(memory_space=pltpu.VMEM)
        own = pl.BlockSpec((self.rows, self.taken[0][0].shape[1]), lambda i: (0, 0))
        return [own] + [vmem] * (len(self.taken) - 1)

    def result(self):
        rows, taken = self.rows, [item[1:] for item in self.taken]

        def stack_kernel(*refs):
            for ref, (first, count, spot, top) in zip(refs[:-1], taken):
                at = spot * rows + top
                refs[-1][at : at + count, :] = ref[first : first + count, :]

        return pl.pallas_call(
            stack_kernel,
            grid=(1,),
            in_specs=self.specs(),
            out_specs=pl.BlockSpec(memory_space=pltpu.VMEM),
            out_shape=jax.ShapeDtypeStruct((8 * rows, self.taken[0][0].shape[1]), jnp.bfloat16),
            cost_estimate=CHEAP,
            name="stack",
        )(*self.operands())


def hold(rings, *extra):
    states, extra = lax.optimization_barrier(([ring.state for ring in rings], extra))
    for ring, state in zip(rings, states):
        ring.state = state
    return extra[0] if len(extra) == 1 else extra


def scatter_cross(own, far, sent):
    moved = cross(sent, 1)
    half = own.shape[0]
    return add(own, moved[:half]), add(far, moved[half:])


def columns(at, width):
    return pl.ds(pl.multiple_of(at * width, width), width)


def slice_kernel(at_ref, *refs, pad):
    weights, out_ref = refs[:-1], refs[-1]
    if pad:
        weights, pad_ref = weights[:-1], weights[-1]
    rows = weights[0].shape[0]
    each = rows + pad
    for s in range(8):
        first = 0
        for ref in weights:
            width = ref.shape[1] // 8
            out_ref[s * each : s * each + rows, first : first + width] = ref[
                :, columns(at_ref[s], width)
            ]
            first += width
        if pad:
            out_ref[s * each + rows : (s + 1) * each, :] = pad_ref[...]


def slice_pieces(at, *weights, pad=None):
    rows = weights[0].shape[0]
    cols = sum(w.shape[1] for w in weights) // 8
    extra = 0 if pad is None else pad.shape[0]
    operands = weights if pad is None else (*weights, pad)
    vmem = pl.BlockSpec(memory_space=pltpu.VMEM)
    return pl.pallas_call(
        lambda *refs: slice_kernel(*refs, pad=extra),
        in_specs=[pl.BlockSpec(memory_space=pltpu.SMEM)] + [vmem] * len(operands),
        out_specs=vmem,
        out_shape=jax.ShapeDtypeStruct((8 * (rows + extra), cols), jnp.bfloat16),
        cost_estimate=CHEAP,
        name="slice_pieces",
    )(at, *operands)


def assemble_kernel(at_ref, *refs):
    own = at_ref[8]
    for j, piece in enumerate(refs[:4]):
        refs[4][0, own ^ j] = piece[...]


def assemble(at, pieces, rows):
    count = at.shape[0] - 1
    total, cols = pieces[0].shape
    return pl.pallas_call(
        assemble_kernel,
        grid_spec=pltpu.PrefetchScalarGridSpec(
            num_scalar_prefetch=1,
            grid=(count,),
            in_specs=[pl.BlockSpec((rows, cols), lambda i, at: (i, 0))] * 4,
            out_specs=pl.BlockSpec((1, 4, rows, cols), lambda i, at: (at[i], 0, 0, 0)),
        ),
        out_shape=jax.ShapeDtypeStruct((count, 4, rows, cols), jnp.bfloat16),
        cost_estimate=CHEAP,
        name="assemble",
    )(at, *pieces).reshape(4 * total, cols)


def spun(rows, cosine, sine):
    return rows * cosine + pltpu.roll(rows, HEAD_SIZE // 2, 1) * sine


def project_kernel(at_ref, *refs, strips):
    token_refs, refs = refs[:strips], refs[strips:]
    pieces, refs = refs[:4], refs[4:]
    cos_ref, sin_ref, normed_ref, raw_ref, q_ref, kv_ref, matrix_ref, gains_ref = refs
    each = pieces[0].shape[0] // 8
    rows = matrix_ref.shape[0] // 32
    own = at_ref[8]
    gains = jnp.zeros(gains_ref.shape, jnp.float32)
    for s in range(8):
        for j in range(4):
            first = pl.multiple_of((at_ref[s] * 4 + (own ^ j)) * rows, rows)
            matrix_ref[pl.ds(first, rows), :] = pieces[j][s * each : s * each + rows, :]
            gains += pieces[j][s * each + rows : (s + 1) * each, :].astype(jnp.float32)
    gains_ref[...] = gains
    width = gains.shape[1]
    first = 0
    for ref in token_refs:
        block = ref[...].astype(jnp.float32)
        block = block * inverse_rms(block)
        here = slice(first, first + ref.shape[0])
        for i in range(block.shape[1] // width):
            cols = slice(i * width, (i + 1) * width)
            normed_ref[here, cols] = (block[:, cols] * gains[i : i + 1]).astype(jnp.bfloat16)
        first += ref.shape[0]
    query_gain, key_gain = gains[8:9, :HEAD_SIZE], gains[8:9, HEAD_SIZE : 2 * HEAD_SIZE]
    query_cols = q_ref.shape[1]
    step = 256
    for first in range(0, q_ref.shape[0], step):
        here = slice(first, first + step)
        raw = jnp.dot(normed_ref[here, :], matrix_ref[...], preferred_element_type=jnp.float32)
        raw_ref[here, :] = raw
        cosine, sine = cos_ref[here, :], sin_ref[here, :]
        for col in range(0, query_cols + HEAD_SIZE, HEAD_SIZE):
            part = raw[:, col : col + HEAD_SIZE]
            if col < query_cols:
                part = spun(part * inverse_rms(part) * query_gain, cosine, sine)
                part = part * (LOG2E / math.sqrt(HEAD_SIZE))
                q_ref[here, col : col + HEAD_SIZE] = part.astype(jnp.bfloat16)
            else:
                part = spun(part * inverse_rms(part) * key_gain, cosine, sine)
                kv_ref[here, :HEAD_SIZE] = part.astype(jnp.bfloat16)
        kv_ref[here, HEAD_SIZE:] = raw[:, query_cols + HEAD_SIZE :].astype(jnp.bfloat16)


def project(at, strips, pieces, cosine, sine, query_cols, pad):
    rows = sum(strip.shape[0] for strip in strips)
    width = strips[0].shape[1]
    cols = pieces[0].shape[1]
    vmem = pl.BlockSpec(memory_space=pltpu.VMEM)
    operands = (*strips, *pieces, cosine, sine)
    narrow, wide = jnp.bfloat16, jnp.float32
    return pl.pallas_call(
        lambda *refs: project_kernel(*refs, strips=len(strips)),
        in_specs=[pl.BlockSpec(memory_space=pltpu.SMEM)] + [vmem] * len(operands),
        out_specs=[vmem] * 6,
        out_shape=[
            jax.ShapeDtypeStruct((rows, width), narrow),
            jax.ShapeDtypeStruct((rows, cols), wide),
            jax.ShapeDtypeStruct((rows, query_cols), narrow),
            jax.ShapeDtypeStruct((rows, 2 * HEAD_SIZE), narrow),
            jax.ShapeDtypeStruct((width, cols), narrow),
            jax.ShapeDtypeStruct((pad, cols), wide),
        ],
        cost_estimate=LONG,
        name="project",
    )(at, *operands)


def project_back_kernel(
    dq_ref, dkv_ref, raw_ref, head_gain_ref, cos_ref, sin_ref, matrix_ref,
    grad_ref, part_ref, gain_ref,
):
    query_cols = dq_ref.shape[1]
    step = 256
    gain_ref[...] = jnp.zeros_like(gain_ref)
    for first in range(0, dq_ref.shape[0], step):
        here = slice(first, first + step)
        cosine, sine = cos_ref[here, :], sin_ref[here, :]
        for col in range(0, query_cols + HEAD_SIZE, HEAD_SIZE):
            cols = slice(col, col + HEAD_SIZE)
            which = 0 if col < query_cols else 1
            grads = dkv_ref[here, :HEAD_SIZE] if which else dq_ref[here, cols]
            raw = raw_ref[here, cols]
            rho = inverse_rms(raw)
            unit = raw * rho
            turned = spun(grads.astype(jnp.float32), cosine, -sine)
            gain_ref[which : which + 1, :] += jnp.sum(turned * unit, axis=0, keepdims=True)
            scaled = turned * head_gain_ref[which : which + 1]
            back = rho * (scaled - unit * jnp.mean(unit * scaled, axis=-1, keepdims=True))
            grad_ref[here, cols] = back.astype(jnp.bfloat16)
        grad_ref[here, query_cols + HEAD_SIZE :] = dkv_ref[here, HEAD_SIZE:]
        part_ref[here, :] = lax.dot_general(
            grad_ref[here, :], matrix_ref[...], ALONG, preferred_element_type=jnp.float32
        ).astype(jnp.bfloat16)


def project_back(query_grads, kv_grads, raw, head_gains, cosine, sine, matrix):
    rows, cols = raw.shape
    vmem = pl.BlockSpec(memory_space=pltpu.VMEM)
    return pl.pallas_call(
        project_back_kernel,
        in_specs=[vmem] * 7,
        out_specs=[vmem] * 3,
        out_shape=[
            jax.ShapeDtypeStruct((rows, cols), jnp.bfloat16),
            jax.ShapeDtypeStruct((rows, matrix.shape[0]), jnp.bfloat16),
            jax.ShapeDtypeStruct((8, HEAD_SIZE), jnp.float32),
        ],
        cost_estimate=LONG,
        name="project_back",
    )(query_grads, kv_grads, raw, head_gains, cosine, sine, matrix)


def dots(lefts, rights, dims):
    return sum(
        lax.dot_general(left[...], right[...], dims, preferred_element_type=jnp.float32)
        for left, right in zip(lefts, rights)
    )


def weight_grads_kernel(at_ref, *refs, groups, rows):
    own_ref, far_ref, sent_ref, held = refs[-4:]
    own = at_ref[8]
    sums = dots(refs[:groups], refs[groups : 2 * groups], DOWN)
    held[...] = sums.astype(jnp.bfloat16).reshape(held.shape)
    own_ref[:rows, :] = held[own]
    far_ref[:rows, :] = held[own ^ 2]
    sent_ref[0, :rows] = held[own ^ 1]
    sent_ref[1, :rows] = held[own ^ 3]
    if own_ref.shape[0] > rows:
        pad = refs[2 * groups][...]
        own_ref[rows:, :] = pad
        far_ref[rows:, :] = pad
        sent_ref[0, rows:] = pad
        sent_ref[1, rows:] = pad


def weight_grads(at, lefts, rights, rows, pad=None):
    count = at.shape[0] - 1
    cols = rights[0].shape[1]
    pads = [] if pad is None else [pad]
    each = rows + sum(p.shape[0] for p in pads)
    part = pl.BlockSpec((each, cols), lambda i, at: (i, 0))
    shape = jax.ShapeDtypeStruct((count * each, cols), jnp.bfloat16)
    own, far, sent = pl.pallas_call(
        lambda *refs: weight_grads_kernel(*refs, groups=len(lefts), rows=rows),
        grid_spec=pltpu.PrefetchScalarGridSpec(
            num_scalar_prefetch=1,
            grid=(count,),
            in_specs=[
                pl.BlockSpec((left.shape[0], 4 * rows), lambda i, at: (0, at[i]))
                for left in lefts
            ]
            + [pl.BlockSpec(right.shape, lambda i, at: (0, 0)) for right in (*rights, *pads)],
            out_specs=[part, part, pl.BlockSpec((2, each, cols), lambda i, at: (0, i, 0))],
            scratch_shapes=[pltpu.VMEM((4, rows, cols), jnp.bfloat16)],
        ),
        out_shape=[
            shape, shape, jax.ShapeDtypeStruct((2, count * each, cols), jnp.bfloat16),
        ],
        cost_estimate=CHEAP,
        name="weight_grads",
    )(at, *lefts, *rights, *pads)
    return own, far, sent.reshape(2 * count * each, cols)


def row_grads_kernel(*refs, lefts):
    left_refs, right_refs, (out_ref, held) = refs[:lefts], refs[lefts:-2], refs[-2:]

    @pl.when(pl.program_id(0) == 0)
    def _():
        first = 0
        for ref in right_refs:
            held[first : first + ref.shape[0], :] = ref[...]
            first += ref.shape[0]

    sums, first = 0.0, 0
    for ref in left_refs:
        sums += lax.dot_general(
            ref[...],
            held[first : first + ref.shape[0], :],
            DOWN,
            preferred_element_type=jnp.float32,
        )
        first += ref.shape[0]
    out_ref[...] = sums.astype(jnp.bfloat16)


def row_grads(lefts, rights, block=256):
    out_rows, cols = lefts[0].shape[1], rights[0].shape[1]
    total = sum(left.shape[0] for left in lefts)
    return pl.pallas_call(
        lambda *refs: row_grads_kernel(*refs, lefts=len(lefts)),
        grid=(out_rows // block,),
        in_specs=[pl.BlockSpec((left.shape[0], block), lambda i: (0, i)) for left in lefts]
        + [pl.BlockSpec(right.shape, lambda i: (0, 0)) for right in rights],
        out_specs=pl.BlockSpec((block, cols), lambda i: (i, 0)),
        out_shape=jax.ShapeDtypeStruct((out_rows, cols), jnp.bfloat16),
        scratch_shapes=[pltpu.VMEM((total, cols), jnp.bfloat16)],
        cost_estimate=CHEAP,
        name="row_grads",
    )(*lefts, *rights)


def hidden_grads_kernel(*refs, strips):
    matrix_ref, outs, held = refs[strips], refs[strips + 1 : -1], refs[-1]

    @pl.when(pl.program_id(0) == 0)
    def _():
        first = 0
        for ref in refs[:strips]:
            held[first : first + ref.shape[0], :] = ref[...]
            first += ref.shape[0]

    first = 0
    for out in outs:
        out[...] = lax.dot_general(
            held[first : first + out.shape[0], :],
            matrix_ref[...],
            ALONG,
            preferred_element_type=jnp.float32,
        )
        first += out.shape[0]


def hidden_grads_of(strips, matrix, block=256):
    rows = [(last - first) * strips[0].shape[0] for first, last in GROUPS]
    cols = matrix.shape[0]
    return pl.pallas_call(
        lambda *refs: hidden_grads_kernel(*refs, strips=len(strips)),
        grid=(cols // block,),
        in_specs=[pl.BlockSpec(strip.shape, lambda i: (0, 0)) for strip in strips]
        + [pl.BlockSpec((block, matrix.shape[1]), lambda i: (i, 0))],
        out_specs=[pl.BlockSpec((n, block), lambda i: (0, i)) for n in rows],
        out_shape=[jax.ShapeDtypeStruct((n, cols), jnp.float32) for n in rows],
        scratch_shapes=[pltpu.VMEM((sum(rows), matrix.shape[1]), jnp.bfloat16)],
        cost_estimate=CHEAP,
        name="hidden_grads",
    )(*strips, matrix)


def lane_sums(block):
    return sum(block[:, i : i + 128] for i in range(0, block.shape[1], 128))


def widen(at, swap, *weights):
    rows, taken, count = weights[0].shape[0], [item[1:] for item in swap.taken], len(weights)
    pad = swap.rows - rows

    def widen_kernel(at_ref, *refs):
        piece_refs, refs = refs[: len(taken)], refs[len(taken) :]
        grads, sums_ref = refs[count : 2 * count], refs[2 * count]
        for ref in refs[2 * count :]:
            ref[...] = jnp.zeros_like(ref)
        for ref, (start, size, spot, top) in zip(piece_refs, taken):
            used = min(size, rows - top)
            here = slice(top, top + used)
            first = 0
            for weight, grad in zip(refs[:count], grads):
                width = weight.shape[1] // 8
                there = columns(at_ref[spot], width)
                block = ref[start : start + used, first : first + width].astype(jnp.float32)
                grad[here, there] = block
                sums_ref[here, :] += lane_sums(block * weight[here, there].astype(jnp.float32))
                first += width
            if used < size:
                refs[-1][...] += ref[start + used : start + size, :].astype(jnp.float32)

    vmem = pl.BlockSpec(memory_space=pltpu.VMEM)
    shapes = [w.shape for w in weights] + [(rows, 128)]
    if pad:
        shapes.append((pad, swap.taken[0][0].shape[1]))
    return pl.pallas_call(
        widen_kernel,
        grid=(1,),
        in_specs=[pl.BlockSpec(memory_space=pltpu.SMEM), *swap.specs()] + [vmem] * count,
        out_specs=[vmem] * len(shapes),
        out_shape=[jax.ShapeDtypeStruct(shape, jnp.float32) for shape in shapes],
        cost_estimate=LONG,
        name="widen",
    )(at, *swap.operands(), *weights)


def grouped(strips):
    return [
        jnp.concatenate(strips[a:b], axis=0) if b - a > 1 else strips[a] for a, b in GROUPS
    ]


def split_groups(groups, rows):
    return [
        group[i * rows : (i + 1) * rows]
        for group in groups
        for i in range(group.shape[0] // rows)
    ]


def gather_head(rows):
    return lax.all_gather(rows, "head", axis=0, tiled=True)


def scatter_head(rows):
    return lax.psum_scatter(rows, "head", scatter_dimension=0, tiled=True)


def inverse_rms(rows):
    return lax.rsqrt(jnp.mean(rows * rows, axis=-1, keepdims=True) + EPS)


def per_device(
    tokens,
    attention_norm,
    query_weight,
    key_projection,
    value_projection,
    query_norm,
    key_norm,
    output_weight,
    feedforward_norm,
    gate_weight,
    up_weight,
    down_weight,
    stretch_order,
    out_cotangent,
):
    blk_count = lax.axis_size("blk")
    head_count = lax.axis_size("head")
    head_index = lax.axis_index("head")
    blk_index = lax.axis_index("blk")
    narrow, wide = jnp.bfloat16, jnp.float32
    tokens, out_cotangent = tokens[0], out_cotangent[0]
    local_rows, model_width = tokens.shape
    group_rows = local_rows * blk_count
    weight_rows = query_weight.shape[0]
    ff_local = gate_weight.shape[1] // blk_count
    query_cols = QUERY_HEADS // blk_count * HEAD_SIZE
    attn_cols = query_cols + 2 * HEAD_SIZE
    device_count = blk_count * head_count
    strip_count = blk_count * head_count
    halves = strip_count // stretch_order.shape[1]
    ring_place = jnp.where(blk_index % 2 == 0, blk_index // 2, 7 - blk_index // 2)

    spot = (ring_place + jnp.arange(blk_count, dtype=jnp.int32)) % blk_count
    at = jnp.where(spot < 4, 2 * spot, 15 - 2 * spot).astype(jnp.int32)
    at_own = jnp.concatenate([at, head_index[None].astype(jnp.int32)])
    ring_spot = (ring_place + jnp.asarray(STRIPS, jnp.int32)) % blk_count
    strip_blk = jnp.where(ring_spot < 4, 2 * ring_spot, 15 - 2 * ring_spot)
    strip_head = head_index ^ jnp.asarray((0, 2, 1, 3), jnp.int32)
    strip = (strip_blk[None, :] * head_count + strip_head[:, None]).reshape(strip_count)
    slots = jnp.arange(stretch_order.shape[1], dtype=jnp.int32)
    held = jnp.sum(
        jnp.where((strip // halves)[:, None] == slots[None, :], stretch_order, 0), axis=1
    )
    strip_place = held * halves + strip % halves
    order = strip_place.astype(jnp.int32)
    place = strip_place[:blk_count].astype(jnp.int32)
    positions = (
        place[:, None] * local_rows + jnp.arange(local_rows, dtype=jnp.int32)[None, :]
    ).reshape(group_rows)
    phases = angles(positions, HEAD_SIZE)[:, 0, :]
    cosine, sine = jnp.cos(phases), jnp.sin(phases)
    cosine = jnp.concatenate([cosine, cosine], axis=1)
    sine = jnp.concatenate([-sine, sine], axis=1)

    small = query_norm.shape[0]
    number = blk_index * head_count + head_index
    pad = 16

    def placed(share):
        return jnp.where(
            jnp.arange(device_count, dtype=jnp.int32)[:, None] == number, share[None, :], 0
        ).reshape(-1)

    gains = jnp.concatenate(
        [placed(attention_norm), placed(feedforward_norm), placed(query_norm), placed(key_norm)]
    ).astype(narrow)
    gains = jnp.pad(gains, (0, pad * attn_cols - gains.shape[0])).reshape(pad, attn_cols)
    down_matrix = gather_head(down_weight)
    output_rows = gather_head(output_weight)

    attn_swap = Swap(
        slice_pieces(at, query_weight, key_projection, value_projection, pad=gains),
        weight_rows + pad,
    )
    token_ring = Gather(tokens)
    ff_slices = slice_pieces(at, gate_weight, up_weight)
    token_ring.go()
    attn_swap.go()
    ff_slices, cosine, sine = hold((attn_swap,), ff_slices, cosine, sine)
    attn_swap.go()
    hold((attn_swap,))
    attn_swap.go()
    own = hold((token_ring,), attn_swap.result())
    near, far = cross(own, 1), cross(own, 2)
    token_ring.go()
    ff_swap, cotangent_ring = Swap(ff_slices, weight_rows), Gather(out_cotangent)
    hold((token_ring, ff_swap, cotangent_ring))
    token_ring.go()
    own, near, far = hold((token_ring,), own, near, far)
    both = cross(far, 1)
    token_ring.go()
    own, near, far, both = hold((token_ring, ff_swap, cotangent_ring), own, near, far, both)
    ff_swap.go()
    cotangent_ring.go()

    first_normed, attn_raw, query_rows, own, attn_matrix, gains = project(
        at_own, token_ring.strips(), (own, near, far, both), cosine, sine, query_cols, pad
    )
    gain_one = gains[:4].reshape(1, model_width)
    gain_two = gains[4:8].reshape(1, model_width)
    head_gains = jnp.pad(gains[8, : 2 * HEAD_SIZE].reshape(2, HEAD_SIZE), ((0, 6), (0, 0)))
    near, far = cross(own, 1), cross(own, 2)
    own, near, far = hold((ff_swap, cotangent_ring), own, near, far)
    both = cross(far, 1)
    kv = hold((ff_swap, cotangent_ring), own, far, near, both)
    ff_swap.go(late=True)
    cotangent_ring.go()
    attended, lse = attend(place, order, query_rows, kv)

    def by_groups(rows):
        return [rows[a * local_rows : b * local_rows] for a, b in GROUPS]

    def by_strips(groups):
        return dict(zip(STRIPS, split_groups(groups, local_rows)))

    attended = hold((cotangent_ring, ff_swap), attended)
    branch_parts = [matmul(rows, output_rows).astype(narrow) for rows in by_groups(attended)]
    branch_ring = Scatter(by_strips(branch_parts))
    branch_ring.go()
    ff_swap.trim()
    ff_swap.go()
    ff_own = hold((branch_ring,), ff_swap.result())
    ff_near, ff_far = cross(ff_own, 1), cross(ff_own, 2)
    branch_ring.go()
    cotangent_ring.go()
    hold((branch_ring, cotangent_ring))
    branch_ring.go()
    cotangent_ring.go()
    ff_near, ff_far, down_matrix = hold(
        (branch_ring, cotangent_ring), ff_near, ff_far, down_matrix
    )
    cotangent_strips = hold((), cotangent_ring.strips())
    branch_ring.go()
    hidden_grads = hidden_grads_of(cotangent_strips, down_matrix)
    ff_both = cross(ff_far, 1)
    hidden_grads, ff_both = hold((branch_ring,), hidden_grads, ff_both)
    tokens_wide = tokens.astype(wide)
    resid = tokens_wide + branch_ring.total()
    rho_two = inverse_rms(resid)
    unit_two = resid * rho_two

    second_ring = Gather((unit_two * gain_two).astype(narrow))
    second_groups, hidden_groups, ff_gradient_groups = [], [], []

    def feed_forward(index):
        rows = second_ring.group(index)
        ff_raw = matmul(rows, ff_matrix)
        gate, up_proj = ff_raw[:, :ff_local], ff_raw[:, ff_local:]
        sigma = jax.nn.sigmoid(gate)
        swish = gate * sigma
        hidden_gradient = hidden_grads[index]
        gate_gradient = hidden_gradient * up_proj * (sigma * (1.0 + gate * (1.0 - sigma)))
        hidden = (swish * up_proj).astype(narrow)
        gradient = jnp.concatenate([gate_gradient, hidden_gradient * swish], 1).astype(narrow)
        if index < 3:
            rows, hidden, gradient = hold((second_ring,), rows, hidden, gradient)
        second_groups.append(rows)
        hidden_groups.append(hidden)
        ff_gradient_groups.append(gradient)

    second_ring.go()
    ff_matrix = assemble(at_own, (ff_own, ff_near, ff_far, ff_both), weight_rows)
    ff_matrix = hold((second_ring,), ff_matrix)
    for index in range(3):
        second_ring.go()
        feed_forward(index)
    feed_forward(3)

    def back(index):
        return matmul(ff_gradient_groups[index], ff_matrix, ALONG).astype(narrow)

    def split(group):
        return [group[i : i + local_rows] for i in range(0, group.shape[0], local_rows)]

    parts = {4: back(3)}
    resid_ring = Scatter(parts)
    parts[3], parts[5] = split(hold((), back(2)))
    parts[2], parts[6] = split(hold((), back(1)))
    resid_ring.go()
    _, _, hidden_groups, cotangent_strips = hold(
        (resid_ring,), parts[2], parts[6], hidden_groups, cotangent_strips
    )
    resid_ring.go()
    down_gradient = row_grads(hidden_groups, cotangent_strips)
    back_zero, down_gradient, second_groups, ff_gradient_groups = hold(
        (resid_ring,), back(0), down_gradient, second_groups, ff_gradient_groups
    )
    down_gradient = scatter_head(down_gradient)
    parts[0], parts[1], parts[7] = split(back_zero)
    resid_ring.go()
    ff_own, ff_far, ff_sent = hold(
        (resid_ring,), *weight_grads(at_own, second_groups, ff_gradient_groups, weight_rows)
    )
    resid_ring.go()
    ff_own, ff_far = scatter_cross(ff_own, ff_far, ff_sent)
    ff_own, ff_far, hidden_groups = hold((resid_ring,), ff_own, ff_far, hidden_groups)
    ff_far = cross(ff_far, 2)
    scaled = gain_two * resid_ring.total()
    resid_gradient = out_cotangent.astype(wide) + rho_two * (
        scaled - unit_two * jnp.mean(unit_two * scaled, axis=-1, keepdims=True)
    )

    grad_ring = Gather(resid_gradient.astype(narrow))
    grad_groups, attended_grads = [], []

    def attention_back(index):
        rows = grad_ring.group(index)
        grads = matmul(rows, output_rows, ALONG).astype(narrow)
        if index < 3:
            rows, grads = hold((grad_ring,), rows, grads)
        grad_groups.append(rows)
        attended_grads.append(grads)

    grad_ring.go()
    out_parts = [matmul(rows, down_matrix).astype(narrow) for rows in hidden_groups]
    out_parts = hold((grad_ring,), *out_parts)
    out_ring = Scatter(by_strips(out_parts))
    grad_ring.go()
    hold((grad_ring,))
    grad_ring.go()
    attention_back(0)
    hold((out_ring, grad_ring))
    out_ring.go()
    grad_ring.go()
    attention_back(1)
    attention_back(2)
    ff_swap = Swap(add(ff_own, ff_far), weight_rows)
    hold((grad_ring, ff_swap, out_ring))
    out_ring.go()
    ff_swap.go(late=True)
    attention_back(3)
    query_grads, kv_own, kv_far, kv_sent = attend_back(
        place, order, query_rows, attended_grads, attended, lse, kv
    )
    query_grads, kv_own, kv_far, kv_sent, grad_groups, attended = hold(
        (out_ring, ff_swap), query_grads, kv_own, kv_far, kv_sent, grad_groups, attended
    )
    out_ring.go()
    ff_swap.trim()
    kv_own, kv_far = scatter_cross(kv_own, kv_far, kv_sent)
    output_weight_gradient = row_grads([attended], grad_groups)
    kv_own, kv_far, output_weight_gradient = hold(
        (out_ring, ff_swap), kv_own, kv_far, output_weight_gradient
    )
    ff_swap.go()
    kv_grads = hold((ff_swap,), add(kv_own, cross(kv_far, 2)))
    ff_swap.go()
    attn_gradient, first_parts, gain_sums = project_back(
        query_grads, kv_grads, attn_raw, head_gains, cosine, sine, attn_matrix
    )
    gain_sums = jnp.pad(
        gain_sums[:2].reshape(1, 2 * HEAD_SIZE).astype(narrow),
        ((0, pad - 1), (0, attn_cols - 2 * HEAD_SIZE)),
    )
    attn_gradient, first_parts, gain_sums, output_weight_gradient = hold(
        (ff_swap, out_ring), attn_gradient, first_parts, gain_sums, output_weight_gradient
    )
    token_ring = Scatter(by_strips(by_groups(first_parts)))
    token_ring.go()
    out_ring.go()
    attn_own, attn_far, attn_sent = weight_grads(
        at_own, [first_normed], [attn_gradient], weight_rows, gain_sums
    )
    attn_own, attn_far, attn_sent = hold(
        (token_ring, out_ring), attn_own, attn_far, attn_sent
    )
    token_ring.go()
    attn_own, attn_far = scatter_cross(attn_own, attn_far, attn_sent)
    attn_far = cross(attn_far, 2)
    layer_out = (resid + out_ring.total()).astype(narrow)
    gate_weight_gradient, up_weight_gradient, ff_sums = widen(at, ff_swap, gate_weight, up_weight)
    attn_swap = Swap(add(attn_own, attn_far), weight_rows + pad)
    gate_weight_gradient, up_weight_gradient, ff_sums, output_weight_gradient, layer_out = hold(
        (token_ring, attn_swap),
        gate_weight_gradient, up_weight_gradient, ff_sums, output_weight_gradient, layer_out,
    )
    output_weight_gradient = scatter_head(output_weight_gradient)
    attn_swap.go()
    token_ring.go()
    feedforward_norm_gradient = jnp.sum(ff_sums, axis=1) / feedforward_norm.astype(wide)
    feedforward_norm_gradient, down_gradient = hold(
        (token_ring, attn_swap), feedforward_norm_gradient, down_gradient.astype(wide)
    )
    attn_swap.go()
    token_ring.go()
    output_weight_gradient = hold(
        (token_ring, attn_swap), output_weight_gradient.astype(wide)
    )
    attn_swap.go()
    query_weight_gradient, key_weight_gradient, value_weight_gradient, norm_sums, gain_sums = widen(
        at, attn_swap, query_weight, key_projection, value_projection
    )
    attention_norm_gradient = jnp.sum(norm_sums, axis=1) / attention_norm.astype(wide)
    gain_sums = gain_sums[0, : 2 * HEAD_SIZE].reshape(2, HEAD_SIZE)
    gain_sums = lax.dynamic_slice_in_dim(gain_sums, number * small, small, 1)
    rho_one = inverse_rms(tokens_wide)
    unit_one = tokens_wide * rho_one
    scaled = gain_one * token_ring.total()
    tokens_gradient = resid_gradient + rho_one * (
        scaled - unit_one * jnp.mean(unit_one * scaled, axis=-1, keepdims=True)
    )
    return (
        layer_out[None],
        tokens_gradient.astype(narrow)[None],
        attention_norm_gradient,
        query_weight_gradient,
        key_weight_gradient,
        value_weight_gradient,
        gain_sums[0],
        gain_sums[1],
        output_weight_gradient,
        feedforward_norm_gradient,
        gate_weight_gradient,
        up_weight_gradient,
        down_gradient,
    )


def solution(mesh):
    placed = (
        P(None, ("blk", "head"), None),
        P(("blk", "head")),
        P(("blk", "head"), None),
        P(("blk", "head"), None),
        P(("blk", "head"), None),
        P(("blk", "head")),
        P(("blk", "head")),
        P(("blk", "head"), None),
        P(("blk", "head")),
        P(("blk", "head"), None),
        P(("blk", "head"), None),
        P(("blk", "head"), None),
        P(),
        P(None, ("blk", "head"), None),
    )
    fits = mesh.shape["blk"] == KEY_VALUE_HEADS and mesh.shape["head"] == 4
    return jax.shard_map(
        per_device if fits else per_device_by_tokens,
        mesh=mesh,
        in_specs=placed,
        out_specs=(
            P(None, ("blk", "head"), None),
            P(None, ("blk", "head"), None),
            P(("blk", "head")),
            P(("blk", "head"), None),
            P(("blk", "head"), None),
            P(("blk", "head"), None),
            P(("blk", "head")),
            P(("blk", "head")),
            P(("blk", "head"), None),
            P(("blk", "head")),
            P(("blk", "head"), None),
            P(("blk", "head"), None),
            P(("blk", "head"), None),
        ),
        check_vma=False,
    )
```

```python
import math

import jax
import jax.numpy as jnp
from jax import lax
from jax.experimental import pallas as pl
from jax.experimental.pallas import tpu as pltpu
from jax.sharding import PartitionSpec as P

QUERY_HEADS = 16
KEY_VALUE_HEADS = 8
HEAD_SIZE = 128


EPS = 1e-06
NEG = -1e30
ROPE_BASE = 1000000.0


def passed_along(value, axis, by):
    count = lax.axis_size(axis)
    return lax.ppermute(value, axis, [(i, (i + by) % count) for i in range(count)])


def norm_rows(inputs, norm_gain):
    return inputs * lax.rsqrt(jnp.mean(inputs * inputs, axis=-1, keepdims=True) + EPS) * norm_gain


def rotary(inputs, phases):
    half_width = inputs.shape[-1] // 2
    cosine = jnp.cos(phases)
    sine_term = jnp.sin(phases)
    first_half = inputs[..., :half_width]
    second_half = inputs[..., half_width:]
    return jnp.concatenate(
        [
            first_half * cosine - second_half * sine_term,
            second_half * cosine + first_half * sine_term,
        ],
        axis=-1,
    )


def angles(positions, head_width):
    half_width = head_width // 2
    frequency = jnp.exp(
        jnp.arange(half_width, dtype=jnp.float32) * (-2.0 * math.log(ROPE_BASE) / head_width)
    )
    return positions.astype(jnp.float32)[..., None, None] * frequency


def token_positions(stretch_order, first_row, row_count, stretch_rows):
    row_index = first_row + jnp.arange(row_count, dtype=jnp.int32)
    slot_index = row_index // stretch_rows
    matches = slot_index[:, None] == jnp.arange(stretch_order.shape[1], dtype=jnp.int32)[None, :]
    picked = jnp.sum(jnp.where(matches[None], stretch_order[:, None, :], 0), axis=-1)
    return picked * stretch_rows + row_index % stretch_rows


def per_device_by_tokens(
    tokens,
    attention_norm,
    query_weight,
    key_projection,
    value_projection,
    query_norm,
    key_norm,
    output_weight,
    feedforward_norm,
    gate_weight,
    up_weight,
    down_weight,
    stretch_order,
    out_cotangent,
):
    count_of_heads = lax.axis_size("head")
    span_count = lax.axis_size("blk")
    span_index = lax.axis_index("blk")
    head_index = lax.axis_index("head")
    sequence_total = tokens.shape[0]
    local_rows = tokens.shape[1]
    group_rows = local_rows * count_of_heads
    stretch_rows = group_rows // 2
    heads_shared = KEY_VALUE_HEADS // count_of_heads
    heads_per_group = QUERY_HEADS // KEY_VALUE_HEADS
    score_scale = 1.0 / math.sqrt(HEAD_SIZE)
    gain_one, query_matrix, key_matrix, value_matrix, query_gain, key_gain, output_matrix = (
        lax.all_gather(attention_norm, ("blk", "head"), axis=0, tiled=True),
        lax.all_gather(query_weight, ("blk", "head"), axis=0, tiled=True),
        lax.all_gather(key_projection, ("blk", "head"), axis=0, tiled=True),
        lax.all_gather(value_projection, ("blk", "head"), axis=0, tiled=True),
        lax.all_gather(query_norm, ("blk", "head"), axis=0, tiled=True),
        lax.all_gather(key_norm, ("blk", "head"), axis=0, tiled=True),
        lax.all_gather(output_weight, ("blk", "head"), axis=0, tiled=True),
    )
    gain_two, gate_matrix, up_matrix, down_matrix = (
        lax.all_gather(feedforward_norm, ("blk", "head"), axis=0, tiled=True),
        lax.all_gather(gate_weight, ("blk", "head"), axis=0, tiled=True),
        lax.all_gather(up_weight, ("blk", "head"), axis=0, tiled=True),
        lax.all_gather(down_weight, ("blk", "head"), axis=0, tiled=True),
    )
    gain_one = gain_one.astype(jnp.float32)
    gain_two = gain_two.astype(jnp.float32)
    query_gain = query_gain.astype(jnp.float32)
    key_gain = key_gain.astype(jnp.float32)
    own_first = (span_index * count_of_heads + head_index) * local_rows
    own_pos = token_positions(stretch_order, own_first, local_rows, stretch_rows)
    group_pos = token_positions(stretch_order, span_index * group_rows, group_rows, stretch_rows)
    phases = angles(own_pos, HEAD_SIZE)
    tokens_wide = tokens.astype(jnp.float32)
    first_normed, norm_one_back = jax.vjp(norm_rows, tokens_wide, gain_one)
    first_normed = first_normed.astype(jnp.bfloat16)
    query_raw = jnp.einsum(
        "btd,de->bte", first_normed, query_matrix, preferred_element_type=jnp.float32
    ).reshape(sequence_total, local_rows, QUERY_HEADS, HEAD_SIZE)
    key_unnormed = jnp.einsum(
        "btd,de->bte", first_normed, key_matrix, preferred_element_type=jnp.float32
    ).reshape(sequence_total, local_rows, KEY_VALUE_HEADS, HEAD_SIZE)
    value_tokens = (
        jnp.einsum("btd,de->bte", first_normed, value_matrix, preferred_element_type=jnp.float32)
        .astype(jnp.bfloat16)
        .reshape(sequence_total, local_rows, KEY_VALUE_HEADS, HEAD_SIZE)
    )

    def heads_local(query_in, key_in, query_scale, key_scale):
        return (
            rotary(norm_rows(query_in, query_scale), phases),
            rotary(norm_rows(key_in, key_scale), phases),
        )

    (query_tokens, key_tokens), heads_back = jax.vjp(
        heads_local, query_raw, key_unnormed, query_gain, key_gain
    )
    query_tokens = query_tokens.astype(jnp.bfloat16)
    key_tokens = key_tokens.astype(jnp.bfloat16)
    query_group, key_group, value_group = (
        lax.all_to_all(query_tokens, "head", split_axis=2, concat_axis=1, tiled=True),
        lax.all_to_all(key_tokens, "head", split_axis=2, concat_axis=1, tiled=True),
        lax.all_to_all(value_tokens, "head", split_axis=2, concat_axis=1, tiled=True),
    )
    query_five = query_group.reshape(
        sequence_total, group_rows, heads_shared, heads_per_group, HEAD_SIZE
    )

    def block_update(carry, key_block, value_block, key_pos):
        run_max, run_sum, run_total = carry
        scores = (
            jnp.einsum(
                "bqkgd,bckd->bkgqc", query_five, key_block, preferred_element_type=jnp.float32
            )
            * score_scale
        )
        allowed = key_pos[:, None, None, None, :] <= group_pos[:, None, None, :, None]
        scores = jnp.where(allowed, scores, NEG)
        new_max = jnp.maximum(run_max, jnp.max(scores, axis=-1))
        exponent = jnp.where(allowed, jnp.exp(scores - new_max[..., None]), 0.0)
        factor = jnp.exp(run_max - new_max)
        new_sum = run_sum * factor + jnp.sum(exponent, axis=-1)
        new_total = run_total * factor[..., None] + jnp.einsum(
            "bkgqc,bckd->bkgqd",
            exponent.astype(jnp.bfloat16),
            value_block,
            preferred_element_type=jnp.float32,
        )
        return (new_max, new_sum, new_total)

    def fold_update(carry, key_block, value_block, key_pos):
        result = block_update(carry, key_block, value_block, key_pos)
        return result

    stat_shape = (sequence_total, heads_shared, heads_per_group, group_rows)
    start_state = (
        jnp.full(stat_shape, NEG, jnp.float32),
        jnp.zeros(stat_shape, jnp.float32),
        jnp.zeros(stat_shape + (HEAD_SIZE,), jnp.float32),
    )
    key_piece = lax.all_gather(key_group, "blk", axis=1, tiled=True)
    value_piece = lax.all_gather(value_group, "blk", axis=1, tiled=True)
    piece_rows = key_piece.shape[1]
    block_len = math.gcd(group_rows, piece_rows)

    def inner(block_number, carry_in):
        offset = block_number * block_len
        key_block = lax.dynamic_slice_in_dim(key_piece, offset, block_len, 1)
        value_block = lax.dynamic_slice_in_dim(value_piece, offset, block_len, 1)
        key_pos = token_positions(stretch_order, offset, block_len, stretch_rows)
        return fold_update(carry_in, key_block, value_block, key_pos)

    run_max, run_sum, run_total = lax.fori_loop(0, piece_rows // block_len, inner, start_state)
    log_total = run_max + jnp.log(run_sum)
    attended_five = run_total / run_sum[..., None]
    attended_group = (
        jnp.transpose(attended_five, (0, 3, 1, 2, 4))
        .reshape(sequence_total, group_rows, heads_shared * heads_per_group, HEAD_SIZE)
        .astype(jnp.bfloat16)
    )
    attended_tokens = lax.all_to_all(
        attended_group, "head", split_axis=1, concat_axis=2, tiled=True
    ).reshape(sequence_total, local_rows, QUERY_HEADS * HEAD_SIZE)
    branch = jnp.einsum(
        "bte,ed->btd", attended_tokens, output_matrix, preferred_element_type=jnp.float32
    )
    resid = tokens_wide + branch
    normed_two, norm_two_back = jax.vjp(norm_rows, resid, gain_two)
    normed_two = normed_two.astype(jnp.bfloat16)
    gate = jnp.einsum("btd,df->btf", normed_two, gate_matrix, preferred_element_type=jnp.float32)
    up_proj = jnp.einsum("btd,df->btf", normed_two, up_matrix, preferred_element_type=jnp.float32)

    def swish_product(gate_in, up_in):
        return jax.nn.silu(gate_in) * up_in

    hidden, swish_back = jax.vjp(swish_product, gate, up_proj)
    hidden = hidden.astype(jnp.bfloat16)
    layer_out = (
        resid + jnp.einsum("btf,fd->btd", hidden, down_matrix, preferred_element_type=jnp.float32)
    ).astype(jnp.bfloat16)
    gain_again, gate_matrix, up_matrix, down_matrix = (
        lax.all_gather(feedforward_norm, ("blk", "head"), axis=0, tiled=True),
        lax.all_gather(gate_weight, ("blk", "head"), axis=0, tiled=True),
        lax.all_gather(up_weight, ("blk", "head"), axis=0, tiled=True),
        lax.all_gather(down_weight, ("blk", "head"), axis=0, tiled=True),
    )
    down_gradient = jnp.einsum(
        "btf,btd->fd", hidden, out_cotangent, preferred_element_type=jnp.float32
    )
    hidden_gradient = jnp.einsum(
        "btd,fd->btf", out_cotangent, down_matrix, preferred_element_type=jnp.float32
    )
    gate_gradient, up_gradient = swish_back(hidden_gradient)
    gate_gradient = gate_gradient.astype(jnp.bfloat16)
    up_gradient = up_gradient.astype(jnp.bfloat16)
    gate_matrix_gradient = jnp.einsum(
        "btd,btf->df", normed_two, gate_gradient, preferred_element_type=jnp.float32
    )
    up_matrix_gradient = jnp.einsum(
        "btd,btf->df", normed_two, up_gradient, preferred_element_type=jnp.float32
    )
    normed_two_gradient = jnp.einsum(
        "btf,df->btd", gate_gradient, gate_matrix, preferred_element_type=jnp.float32
    ) + jnp.einsum("btf,df->btd", up_gradient, up_matrix, preferred_element_type=jnp.float32)
    resid_part, gain_two_gradient = norm_two_back(normed_two_gradient)
    resid_gradient = out_cotangent.astype(jnp.float32) + resid_part
    feedforward_sums = (
        lax.psum_scatter(gain_two_gradient, ("blk", "head"), scatter_dimension=0, tiled=True),
        lax.psum_scatter(gate_matrix_gradient, ("blk", "head"), scatter_dimension=0, tiled=True),
        lax.psum_scatter(up_matrix_gradient, ("blk", "head"), scatter_dimension=0, tiled=True),
        lax.psum_scatter(down_gradient, ("blk", "head"), scatter_dimension=0, tiled=True),
    )
    gain_again, query_matrix, key_matrix, value_matrix, query_again, key_again, output_matrix = (
        lax.all_gather(attention_norm, ("blk", "head"), axis=0, tiled=True),
        lax.all_gather(query_weight, ("blk", "head"), axis=0, tiled=True),
        lax.all_gather(key_projection, ("blk", "head"), axis=0, tiled=True),
        lax.all_gather(value_projection, ("blk", "head"), axis=0, tiled=True),
        lax.all_gather(query_norm, ("blk", "head"), axis=0, tiled=True),
        lax.all_gather(key_norm, ("blk", "head"), axis=0, tiled=True),
        lax.all_gather(output_weight, ("blk", "head"), axis=0, tiled=True),
    )
    branch_gradient = resid_gradient.astype(jnp.bfloat16)
    output_matrix_gradient = jnp.einsum(
        "bte,btd->ed", attended_tokens, branch_gradient, preferred_element_type=jnp.float32
    )
    attended_gradient = (
        jnp.einsum(
            "btd,ed->bte", branch_gradient, output_matrix, preferred_element_type=jnp.float32
        )
        .astype(jnp.bfloat16)
        .reshape(sequence_total, local_rows, QUERY_HEADS, HEAD_SIZE)
    )
    attended_grad_group = lax.all_to_all(
        attended_gradient, "head", split_axis=2, concat_axis=1, tiled=True
    ).reshape(sequence_total, group_rows, heads_shared, heads_per_group, HEAD_SIZE)
    delta = jnp.sum(
        jnp.transpose(attended_grad_group.astype(jnp.float32), (0, 2, 3, 1, 4)) * attended_five,
        axis=-1,
    )

    def block_grads(sums_in, key_current, value_current, key_pos):
        key_sum, value_sum, query_sum = sums_in
        scores = (
            jnp.einsum(
                "bqkgd,bckd->bkgqc", query_five, key_current, preferred_element_type=jnp.float32
            )
            * score_scale
        )
        allowed = key_pos[:, None, None, None, :] <= group_pos[:, None, None, :, None]
        weights = jnp.where(allowed, jnp.exp(scores - log_total[..., None]), 0.0)
        probs = weights.astype(jnp.bfloat16)
        value_sum = value_sum + jnp.einsum(
            "bkgqc,bqkgd->bckd", probs, attended_grad_group, preferred_element_type=jnp.float32
        )
        probs_gradient = jnp.einsum(
            "bqkgd,bckd->bkgqc",
            attended_grad_group,
            value_current,
            preferred_element_type=jnp.float32,
        )
        scores_gradient = (weights * (probs_gradient - delta[..., None])).astype(jnp.bfloat16)
        query_sum = (
            query_sum
            + jnp.einsum(
                "bkgqc,bckd->bqkgd",
                scores_gradient,
                key_current,
                preferred_element_type=jnp.float32,
            )
            * score_scale
        )
        key_sum = (
            key_sum
            + jnp.einsum(
                "bkgqc,bqkgd->bckd", scores_gradient, query_five, preferred_element_type=jnp.float32
            )
            * score_scale
        )
        return (key_sum, value_sum, query_sum)

    def pass_step(step_index, carry):
        key_current, value_current, key_sum, value_sum, query_sum = carry
        anchor = (span_index - step_index) % span_count
        key_pos = token_positions(stretch_order, anchor * group_rows, group_rows, stretch_rows)
        key_sum, value_sum, query_sum = block_grads(
            (key_sum, value_sum, query_sum), key_current, value_current, key_pos
        )
        key_current, value_current = passed_along((key_current, value_current), "blk", 1)
        key_sum, value_sum = (
            passed_along(key_sum.astype(jnp.bfloat16), "blk", 1).astype(key_sum.dtype),
            passed_along(value_sum.astype(jnp.bfloat16), "blk", 1).astype(value_sum.dtype),
        )
        return (key_current, value_current, key_sum, value_sum, query_sum)

    kv_zeros = jnp.zeros((sequence_total, group_rows, heads_shared, HEAD_SIZE), jnp.float32)
    query_zeros = jnp.zeros(
        (sequence_total, group_rows, heads_shared, heads_per_group, HEAD_SIZE), jnp.float32
    )
    final_state = lax.fori_loop(
        0, span_count, pass_step, (key_group, value_group, kv_zeros, kv_zeros, query_zeros)
    )
    key_grad_group = final_state[2].astype(jnp.bfloat16)
    value_grad_group = final_state[3].astype(jnp.bfloat16)
    query_grad_group = (
        final_state[4]
        .astype(jnp.bfloat16)
        .reshape(sequence_total, group_rows, heads_shared * heads_per_group, HEAD_SIZE)
    )
    query_grad_tokens, key_grad_tokens, value_gradient_tokens = (
        lax.all_to_all(query_grad_group, "head", split_axis=1, concat_axis=2, tiled=True),
        lax.all_to_all(key_grad_group, "head", split_axis=1, concat_axis=2, tiled=True),
        lax.all_to_all(value_grad_group, "head", split_axis=1, concat_axis=2, tiled=True),
    )
    query_raw_gradient, key_unnormed_gradient, query_gain_gradient, key_gain_gradient = heads_back(
        (query_grad_tokens.astype(jnp.float32), key_grad_tokens.astype(jnp.float32))
    )
    query_raw_gradient = query_raw_gradient.astype(jnp.bfloat16).reshape(
        sequence_total, local_rows, QUERY_HEADS * HEAD_SIZE
    )
    key_unnormed_gradient = key_unnormed_gradient.astype(jnp.bfloat16).reshape(
        sequence_total, local_rows, KEY_VALUE_HEADS * HEAD_SIZE
    )
    value_unnormed_gradient = value_gradient_tokens.reshape(
        sequence_total, local_rows, KEY_VALUE_HEADS * HEAD_SIZE
    )
    query_matrix_gradient = jnp.einsum(
        "btd,bte->de", first_normed, query_raw_gradient, preferred_element_type=jnp.float32
    )
    key_matrix_gradient = jnp.einsum(
        "btd,bte->de", first_normed, key_unnormed_gradient, preferred_element_type=jnp.float32
    )
    value_matrix_gradient = jnp.einsum(
        "btd,bte->de", first_normed, value_unnormed_gradient, preferred_element_type=jnp.float32
    )
    normed_one_gradient = jnp.einsum(
        "bte,de->btd", query_raw_gradient, query_matrix, preferred_element_type=jnp.float32
    )
    normed_one_gradient = normed_one_gradient + jnp.einsum(
        "bte,de->btd", key_unnormed_gradient, key_matrix, preferred_element_type=jnp.float32
    )
    normed_one_gradient = normed_one_gradient + jnp.einsum(
        "bte,de->btd", value_unnormed_gradient, value_matrix, preferred_element_type=jnp.float32
    )
    token_part, gain_one_gradient = norm_one_back(normed_one_gradient)
    tokens_gradient = (resid_gradient + token_part).astype(jnp.bfloat16)
    attention_sums = (
        lax.psum_scatter(gain_one_gradient, ("blk", "head"), scatter_dimension=0, tiled=True),
        lax.psum_scatter(query_matrix_gradient, ("blk", "head"), scatter_dimension=0, tiled=True),
        lax.psum_scatter(key_matrix_gradient, ("blk", "head"), scatter_dimension=0, tiled=True),
        lax.psum_scatter(value_matrix_gradient, ("blk", "head"), scatter_dimension=0, tiled=True),
        lax.psum_scatter(query_gain_gradient, ("blk", "head"), scatter_dimension=0, tiled=True),
        lax.psum_scatter(key_gain_gradient, ("blk", "head"), scatter_dimension=0, tiled=True),
        lax.psum_scatter(output_matrix_gradient, ("blk", "head"), scatter_dimension=0, tiled=True),
    )
    return (
        layer_out,
        tokens_gradient,
        attention_sums[0],
        attention_sums[1],
        attention_sums[2],
        attention_sums[3],
        attention_sums[4],
        attention_sums[5],
        attention_sums[6],
        feedforward_sums[0],
        feedforward_sums[1],
        feedforward_sums[2],
        feedforward_sums[3],
    )


LOG2E = math.log2(math.e)
STRIP = 128
CHUNK = 512
ALONG = (((1,), (1,)), ((), ()))
DOWN = (((0,), (0,)), ((), ()))


def two_heads(block):
    return jnp.concatenate([block[:, :HEAD_SIZE], block[:, HEAD_SIZE:]], axis=0)


def side_by_side(rows):
    half = rows.shape[0] // 2
    return jnp.concatenate([rows[:half], rows[half:]], axis=1)


CHEAP = pl.CostEstimate(flops=1, bytes_accessed=1, transcendentals=0)
LONG = pl.CostEstimate(flops=3 * 10**10, bytes_accessed=1 << 25, transcendentals=0)


def sort_strips(order_ref, kv_refs, keys, values):
    per = kv_refs[0].shape[0] // STRIP
    for j, ref in enumerate(kv_refs):
        for i in range(per):
            target = pl.multiple_of(order_ref[j * per + i] * STRIP, STRIP)
            here = slice(i * STRIP, (i + 1) * STRIP)
            keys[pl.ds(target, STRIP), :] = ref[here, :HEAD_SIZE]
            values[pl.ds(target, STRIP), :HEAD_SIZE] = ref[here, HEAD_SIZE:]


def attend_kernel(place_ref, order_ref, q_ref, *refs):
    kv_refs, (out_ref, lse_ref, keys, values) = refs[:4], refs[4:]
    step = pl.program_id(0)

    @pl.when(step == 0)
    def _():
        values[:, HEAD_SIZE:] = jnp.ones((values.shape[0], HEAD_SIZE), jnp.bfloat16)
        sort_strips(order_ref, kv_refs, keys, values)

    place = place_ref[step]
    queries = two_heads(q_ref[...])
    last = place // (CHUNK // STRIP)

    def part(index, total, masked):
        first = pl.multiple_of(index * CHUNK, CHUNK)
        scores = lax.dot_general(
            queries, keys[pl.ds(first, CHUNK), :], ALONG, preferred_element_type=jnp.float32
        )
        weights = jnp.exp2(scores)
        if masked:
            row = lax.broadcasted_iota(jnp.int32, scores.shape, 0) % STRIP
            column = lax.broadcasted_iota(jnp.int32, scores.shape, 1)
            weights = jnp.where(column - row <= place * STRIP - first, weights, 0.0)
        return total + jnp.dot(
            weights.astype(jnp.bfloat16),
            values[pl.ds(first, CHUNK), :],
            preferred_element_type=jnp.float32,
        )

    total = jnp.zeros((2 * STRIP, 2 * HEAD_SIZE), jnp.float32)
    total = lax.fori_loop(0, last, lambda index, t: part(index, t, False), total)
    total = part(last, total, True)
    norm = total[:, HEAD_SIZE:]
    out_ref[...] = side_by_side(total[:, :HEAD_SIZE] / norm).astype(jnp.bfloat16)
    lse_ref[0] = jnp.transpose(jnp.log2(norm))[:8]


def attend(place, order, queries, kv):
    rows, width = queries.shape
    steps = rows // STRIP
    total = sum(part.shape[0] for part in kv)
    strip = pl.BlockSpec((STRIP, width), lambda i, *_: (i, 0))
    return pl.pallas_call(
        attend_kernel,
        grid_spec=pltpu.PrefetchScalarGridSpec(
            num_scalar_prefetch=2,
            grid=(steps,),
            in_specs=[strip] + [pl.BlockSpec(part.shape, lambda i, *_: (0, 0)) for part in kv],
            out_specs=[strip, pl.BlockSpec((1, 8, 2 * STRIP), lambda i, *_: (i, 0, 0))],
            scratch_shapes=[
                pltpu.VMEM((total, HEAD_SIZE), jnp.bfloat16),
                pltpu.VMEM((total, 2 * HEAD_SIZE), jnp.bfloat16),
            ],
        ),
        out_shape=[
            jax.ShapeDtypeStruct((rows, width), jnp.bfloat16),
            jax.ShapeDtypeStruct((steps, 8, 2 * STRIP), jnp.float32),
        ],
        cost_estimate=LONG,
        name="attend",
    )(place, order, queries, *kv)


def attend_back_kernel(place_ref, order_ref, q_ref, out_ref, lse_ref, *refs, groups):
    grad_refs, kv_refs = refs[:groups], refs[groups : groups + 4]
    dq_ref, own_ref, far_ref, sent_ref = refs[groups + 4 : groups + 8]
    keys, values, key_sums, value_sums, grads_all = refs[groups + 8 :]
    step = pl.program_id(0)

    @pl.when(step == 0)
    def _():
        key_sums[...] = jnp.zeros_like(key_sums)
        value_sums[...] = jnp.zeros_like(value_sums)
        sort_strips(order_ref, kv_refs, keys, values)
        first = 0
        for ref in grad_refs:
            grads_all[first : first + ref.shape[0], :] = ref[...]
            first += ref.shape[0]

    place = place_ref[step]
    queries = two_heads(q_ref[...])
    grads = two_heads(grads_all[pl.ds(pl.multiple_of(step * STRIP, STRIP), STRIP), :])
    product = grads.astype(jnp.float32) * two_heads(out_ref[...]).astype(jnp.float32)
    delta = jnp.sum(jnp.transpose(product), axis=0, keepdims=True)
    lse = lse_ref[0, :1]
    last = place // (CHUNK // STRIP)

    def part(index, total, masked):
        first = pl.multiple_of(index * CHUNK, CHUNK)
        here = pl.ds(first, CHUNK)
        key_rows = keys[here, :]
        scores = lax.dot_general(key_rows, queries, ALONG, preferred_element_type=jnp.float32)
        weights = jnp.exp2(scores - lse)
        if masked:
            row = lax.broadcasted_iota(jnp.int32, scores.shape, 0)
            column = lax.broadcasted_iota(jnp.int32, scores.shape, 1) % STRIP
            weights = jnp.where(row - column <= place * STRIP - first, weights, 0.0)
        slopes = lax.dot_general(
            values[here, :], grads, ALONG, preferred_element_type=jnp.float32
        )
        score_grads = (weights * (slopes - delta)).astype(jnp.bfloat16)
        value_sums[here, :] += jnp.dot(
            weights.astype(jnp.bfloat16), grads, preferred_element_type=jnp.float32
        )
        key_sums[here, :] += jnp.dot(score_grads, queries, preferred_element_type=jnp.float32)
        return total + lax.dot_general(
            score_grads, key_rows, DOWN, preferred_element_type=jnp.float32
        )

    total = jnp.zeros((2 * STRIP, HEAD_SIZE), jnp.float32)
    total = lax.fori_loop(0, last, lambda index, t: part(index, t, False), total)
    total = part(last, total, True)
    dq_ref[...] = side_by_side(total * (1.0 / math.sqrt(HEAD_SIZE))).astype(jnp.bfloat16)

    @pl.when(step == pl.num_programs(0) - 1)
    def _():
        per = own_ref.shape[0] // STRIP
        for j in range(4):
            target = (own_ref, far_ref, sent_ref, sent_ref)[j]
            base = per if j == 3 else 0
            for i in range(per):
                source = pl.multiple_of(order_ref[j * per + i] * STRIP, STRIP)
                here = slice((base + i) * STRIP, (base + i + 1) * STRIP)
                target[here, :HEAD_SIZE] = (
                    key_sums[pl.ds(source, STRIP), :] * (1.0 / LOG2E)
                ).astype(jnp.bfloat16)
                target[here, HEAD_SIZE:] = value_sums[pl.ds(source, STRIP), :].astype(
                    jnp.bfloat16
                )


def attend_back(place, order, queries, grads, attended, lse, kv):
    rows, width = queries.shape
    steps = rows // STRIP
    total = sum(part.shape[0] for part in kv)
    strip = pl.BlockSpec((STRIP, width), lambda i, *_: (i, 0))

    def whole(shape):
        return pl.BlockSpec(shape, lambda i, *_: (0, 0))

    outs = [kv[0].shape, kv[0].shape, (2 * kv[0].shape[0], kv[0].shape[1])]
    return pl.pallas_call(
        lambda *refs: attend_back_kernel(*refs, groups=len(grads)),
        grid_spec=pltpu.PrefetchScalarGridSpec(
            num_scalar_prefetch=2,
            grid=(steps,),
            in_specs=[strip, strip, pl.BlockSpec((1, 8, 2 * STRIP), lambda i, *_: (i, 0, 0))]
            + [whole(part.shape) for part in (*grads, *kv)],
            out_specs=[strip] + [whole(shape) for shape in outs],
            scratch_shapes=[
                pltpu.VMEM((total, HEAD_SIZE), jnp.bfloat16),
                pltpu.VMEM((total, HEAD_SIZE), jnp.bfloat16),
                pltpu.VMEM((total, HEAD_SIZE), jnp.float32),
                pltpu.VMEM((total, HEAD_SIZE), jnp.float32),
                pltpu.VMEM((rows, width), jnp.bfloat16),
            ],
        ),
        out_shape=[jax.ShapeDtypeStruct((rows, width), jnp.bfloat16)]
        + [jax.ShapeDtypeStruct(shape, jnp.bfloat16) for shape in outs],
        cost_estimate=LONG,
        name="attend_back",
    )(place, order, queries, attended, lse, *grads, *kv)


def matmul(left, right, dims=(((1,), (0,)), ((), ()))):
    return lax.dot_general(left, right, dims, preferred_element_type=jnp.float32)


RING = (0, 2, 4, 6, 7, 5, 3, 1)
STRIPS = (0, 1, 7, 2, 6, 3, 5, 4)
GROUPS = ((0, 3), (3, 5), (5, 7), (7, 8))


def hop(value, by):
    count = len(RING)
    return lax.ppermute(value, "blk", [(RING[i], RING[(i + by) % count]) for i in range(count)])


def cross(value, by):
    return lax.ppermute(value, "head", [(i, i ^ by) for i in range(4)])


def add(left, right):
    return (left.astype(jnp.float32) + right.astype(jnp.float32)).astype(left.dtype)


class Gather:
    def __init__(self, own):
        self.got, self.step = {0: own}, 0
        self.state = (own, own)

    def go(self):
        self.step += 1
        left, right = self.state
        if self.step < 4:
            self.state = hop(left, -1), hop(right, 1)
            self.got[self.step], self.got[8 - self.step] = self.state
        else:
            half = left.shape[0] // 2
            self.state = hop(left[:half], -1), hop(right[half:], 1)

    def strips(self):
        return [self.got[s] for s in STRIPS[:-1]] + list(self.state)

    def group(self, index):
        first, last = GROUPS[index]
        if index == 3:
            return jnp.concatenate(self.state, axis=0)
        return jnp.concatenate([self.got[s] for s in STRIPS[first:last]], axis=0)


class Scatter:
    def __init__(self, part):
        self.part, self.step = part, 0
        self.half = part[4].shape[0] // 2
        self.state = (part[4][: self.half], part[4][self.half :])

    def go(self):
        self.step += 1
        half, part = self.half, self.part
        up, down = hop(self.state[0], 1), hop(self.state[1], -1)
        if self.step == 1:
            up = jnp.concatenate([add(part[3][:half], up), part[3][half:]], axis=0)
            down = jnp.concatenate([part[5][:half], add(part[5][half:], down)], axis=0)
        elif self.step < 4:
            up, down = add(part[4 - self.step], up), add(part[4 + self.step], down)
        self.state = up, down

    def total(self):
        up, down = self.state
        wide = jnp.float32
        return self.part[0].astype(wide) + up.astype(wide) + down.astype(wide)


class Swap:
    def __init__(self, pieces, rows):
        self.rows, self.step = rows, 0
        self.taken = [(pieces, 0, rows, 0, 0)]
        self.across = pieces[4 * rows : 5 * rows]
        self.state = (pieces[rows : 4 * rows], pieces[5 * rows :])

    def go(self, late=False):
        self.step += 1
        rows, step = self.rows, self.step
        right, left = hop(self.state[0], 1), hop(self.state[1], -1)
        self.taken.append((right, 0, rows, 8 - step, 0))
        self.taken.append((left, left.shape[0] - rows, rows, step, 0))
        self.state = right, left
        if step == 1 and not late:
            self.opposite(hop(self.across, 4))
        if step < 3 and not late:
            self.trim()

    def opposite(self, piece):
        self.taken.append((piece, 0, self.rows, 4, 0))

    def trim(self):
        self.state = self.state[0][self.rows :], self.state[1][: -self.rows]

    def operands(self):
        return [item[0] for item in self.taken]

    def specs(self):
        vmem = pl.BlockSpec(memory_space=pltpu.VMEM)
        own = pl.BlockSpec((self.rows, self.taken[0][0].shape[1]), lambda i: (0, 0))
        return [own] + [vmem] * (len(self.taken) - 1)

    def result(self):
        rows, taken = self.rows, [item[1:] for item in self.taken]

        def stack_kernel(*refs):
            for ref, (first, count, spot, top) in zip(refs[:-1], taken):
                at = spot * rows + top
                refs[-1][at : at + count, :] = ref[first : first + count, :]

        return pl.pallas_call(
            stack_kernel,
            grid=(1,),
            in_specs=self.specs(),
            out_specs=pl.BlockSpec(memory_space=pltpu.VMEM),
            out_shape=jax.ShapeDtypeStruct((8 * rows, self.taken[0][0].shape[1]), jnp.bfloat16),
            cost_estimate=CHEAP,
            name="stack",
        )(*self.operands())


def hold(rings, *extra):
    states, extra = lax.optimization_barrier(([ring.state for ring in rings], extra))
    for ring, state in zip(rings, states):
        ring.state = state
    return extra[0] if len(extra) == 1 else extra


def scatter_cross(own, far, sent):
    moved = cross(sent, 1)
    half = own.shape[0]
    return add(own, moved[:half]), add(far, moved[half:])


def columns(at, width):
    return pl.ds(pl.multiple_of(at * width, width), width)


def slice_kernel(at_ref, *refs, pad):
    weights, out_ref = refs[:-1], refs[-1]
    if pad:
        weights, pad_ref = weights[:-1], weights[-1]
    rows = weights[0].shape[0]
    each = rows + pad
    for s in range(8):
        first = 0
        for ref in weights:
            width = ref.shape[1] // 8
            out_ref[s * each : s * each + rows, first : first + width] = ref[
                :, columns(at_ref[s], width)
            ]
            first += width
        if pad:
            out_ref[s * each + rows : (s + 1) * each, :] = pad_ref[...]


def slice_pieces(at, *weights, pad=None):
    rows = weights[0].shape[0]
    cols = sum(w.shape[1] for w in weights) // 8
    extra = 0 if pad is None else pad.shape[0]
    operands = weights if pad is None else (*weights, pad)
    vmem = pl.BlockSpec(memory_space=pltpu.VMEM)
    return pl.pallas_call(
        lambda *refs: slice_kernel(*refs, pad=extra),
        in_specs=[pl.BlockSpec(memory_space=pltpu.SMEM)] + [vmem] * len(operands),
        out_specs=vmem,
        out_shape=jax.ShapeDtypeStruct((8 * (rows + extra), cols), jnp.bfloat16),
        cost_estimate=CHEAP,
        name="slice_pieces",
    )(at, *operands)


def assemble_kernel(at_ref, *refs):
    own = at_ref[8]
    for j, piece in enumerate(refs[:4]):
        refs[4][0, own ^ j] = piece[...]


def assemble(at, pieces, rows):
    count = at.shape[0] - 1
    total, cols = pieces[0].shape
    return pl.pallas_call(
        assemble_kernel,
        grid_spec=pltpu.PrefetchScalarGridSpec(
            num_scalar_prefetch=1,
            grid=(count,),
            in_specs=[pl.BlockSpec((rows, cols), lambda i, at: (i, 0))] * 4,
            out_specs=pl.BlockSpec((1, 4, rows, cols), lambda i, at: (at[i], 0, 0, 0)),
        ),
        out_shape=jax.ShapeDtypeStruct((count, 4, rows, cols), jnp.bfloat16),
        cost_estimate=CHEAP,
        name="assemble",
    )(at, *pieces).reshape(4 * total, cols)


def spun(rows, cosine, sine):
    return rows * cosine + pltpu.roll(rows, HEAD_SIZE // 2, 1) * sine


def project_kernel(at_ref, *refs, strips):
    token_refs, refs = refs[:strips], refs[strips:]
    pieces, refs = refs[:4], refs[4:]
    cos_ref, sin_ref, normed_ref, raw_ref, q_ref, kv_ref, matrix_ref, gains_ref = refs
    each = pieces[0].shape[0] // 8
    rows = matrix_ref.shape[0] // 32
    own = at_ref[8]
    gains = jnp.zeros(gains_ref.shape, jnp.float32)
    for s in range(8):
        for j in range(4):
            first = pl.multiple_of((at_ref[s] * 4 + (own ^ j)) * rows, rows)
            matrix_ref[pl.ds(first, rows), :] = pieces[j][s * each : s * each + rows, :]
            gains += pieces[j][s * each + rows : (s + 1) * each, :].astype(jnp.float32)
    gains_ref[...] = gains
    width = gains.shape[1]
    first = 0
    for ref in token_refs:
        block = ref[...].astype(jnp.float32)
        block = block * inverse_rms(block)
        here = slice(first, first + ref.shape[0])
        for i in range(block.shape[1] // width):
            cols = slice(i * width, (i + 1) * width)
            normed_ref[here, cols] = (block[:, cols] * gains[i : i + 1]).astype(jnp.bfloat16)
        first += ref.shape[0]
    query_gain, key_gain = gains[8:9, :HEAD_SIZE], gains[8:9, HEAD_SIZE : 2 * HEAD_SIZE]
    query_cols = q_ref.shape[1]
    step = 256
    for first in range(0, q_ref.shape[0], step):
        here = slice(first, first + step)
        raw = jnp.dot(normed_ref[here, :], matrix_ref[...], preferred_element_type=jnp.float32)
        raw_ref[here, :] = raw
        cosine, sine = cos_ref[here, :], sin_ref[here, :]
        for col in range(0, query_cols + HEAD_SIZE, HEAD_SIZE):
            part = raw[:, col : col + HEAD_SIZE]
            if col < query_cols:
                part = spun(part * inverse_rms(part) * query_gain, cosine, sine)
                part = part * (LOG2E / math.sqrt(HEAD_SIZE))
                q_ref[here, col : col + HEAD_SIZE] = part.astype(jnp.bfloat16)
            else:
                part = spun(part * inverse_rms(part) * key_gain, cosine, sine)
                kv_ref[here, :HEAD_SIZE] = part.astype(jnp.bfloat16)
        kv_ref[here, HEAD_SIZE:] = raw[:, query_cols + HEAD_SIZE :].astype(jnp.bfloat16)


def project(at, strips, pieces, cosine, sine, query_cols, pad):
    rows = sum(strip.shape[0] for strip in strips)
    width = strips[0].shape[1]
    cols = pieces[0].shape[1]
    vmem = pl.BlockSpec(memory_space=pltpu.VMEM)
    operands = (*strips, *pieces, cosine, sine)
    narrow, wide = jnp.bfloat16, jnp.float32
    return pl.pallas_call(
        lambda *refs: project_kernel(*refs, strips=len(strips)),
        in_specs=[pl.BlockSpec(memory_space=pltpu.SMEM)] + [vmem] * len(operands),
        out_specs=[vmem] * 6,
        out_shape=[
            jax.ShapeDtypeStruct((rows, width), narrow),
            jax.ShapeDtypeStruct((rows, cols), wide),
            jax.ShapeDtypeStruct((rows, query_cols), narrow),
            jax.ShapeDtypeStruct((rows, 2 * HEAD_SIZE), narrow),
            jax.ShapeDtypeStruct((width, cols), narrow),
            jax.ShapeDtypeStruct((pad, cols), wide),
        ],
        cost_estimate=LONG,
        name="project",
    )(at, *operands)


def project_back_kernel(
    dq_ref, dkv_ref, raw_ref, head_gain_ref, cos_ref, sin_ref, matrix_ref,
    grad_ref, part_ref, gain_ref,
):
    query_cols = dq_ref.shape[1]
    step = 256
    gain_ref[...] = jnp.zeros_like(gain_ref)
    for first in range(0, dq_ref.shape[0], step):
        here = slice(first, first + step)
        cosine, sine = cos_ref[here, :], sin_ref[here, :]
        for col in range(0, query_cols + HEAD_SIZE, HEAD_SIZE):
            cols = slice(col, col + HEAD_SIZE)
            which = 0 if col < query_cols else 1
            grads = dkv_ref[here, :HEAD_SIZE] if which else dq_ref[here, cols]
            raw = raw_ref[here, cols]
            rho = inverse_rms(raw)
            unit = raw * rho
            turned = spun(grads.astype(jnp.float32), cosine, -sine)
            gain_ref[which : which + 1, :] += jnp.sum(turned * unit, axis=0, keepdims=True)
            scaled = turned * head_gain_ref[which : which + 1]
            back = rho * (scaled - unit * jnp.mean(unit * scaled, axis=-1, keepdims=True))
            grad_ref[here, cols] = back.astype(jnp.bfloat16)
        grad_ref[here, query_cols + HEAD_SIZE :] = dkv_ref[here, HEAD_SIZE:]
        part_ref[here, :] = lax.dot_general(
            grad_ref[here, :], matrix_ref[...], ALONG, preferred_element_type=jnp.float32
        ).astype(jnp.bfloat16)


def project_back(query_grads, kv_grads, raw, head_gains, cosine, sine, matrix):
    rows, cols = raw.shape
    vmem = pl.BlockSpec(memory_space=pltpu.VMEM)
    return pl.pallas_call(
        project_back_kernel,
        in_specs=[vmem] * 7,
        out_specs=[vmem] * 3,
        out_shape=[
            jax.ShapeDtypeStruct((rows, cols), jnp.bfloat16),
            jax.ShapeDtypeStruct((rows, matrix.shape[0]), jnp.bfloat16),
            jax.ShapeDtypeStruct((8, HEAD_SIZE), jnp.float32),
        ],
        cost_estimate=LONG,
        name="project_back",
    )(query_grads, kv_grads, raw, head_gains, cosine, sine, matrix)


def dots(lefts, rights, dims):
    return sum(
        lax.dot_general(left[...], right[...], dims, preferred_element_type=jnp.float32)
        for left, right in zip(lefts, rights)
    )


def weight_grads_kernel(at_ref, *refs, groups, rows):
    own_ref, far_ref, sent_ref, held = refs[-4:]
    own = at_ref[8]
    sums = dots(refs[:groups], refs[groups : 2 * groups], DOWN)
    held[...] = sums.astype(jnp.bfloat16).reshape(held.shape)
    own_ref[:rows, :] = held[own]
    far_ref[:rows, :] = held[own ^ 2]
    sent_ref[0, :rows] = held[own ^ 1]
    sent_ref[1, :rows] = held[own ^ 3]
    if own_ref.shape[0] > rows:
        pad = refs[2 * groups][...]
        own_ref[rows:, :] = pad
        far_ref[rows:, :] = pad
        sent_ref[0, rows:] = pad
        sent_ref[1, rows:] = pad


def weight_grads(at, lefts, rights, rows, pad=None):
    count = at.shape[0] - 1
    cols = rights[0].shape[1]
    pads = [] if pad is None else [pad]
    each = rows + sum(p.shape[0] for p in pads)
    part = pl.BlockSpec((each, cols), lambda i, at: (i, 0))
    shape = jax.ShapeDtypeStruct((count * each, cols), jnp.bfloat16)
    own, far, sent = pl.pallas_call(
        lambda *refs: weight_grads_kernel(*refs, groups=len(lefts), rows=rows),
        grid_spec=pltpu.PrefetchScalarGridSpec(
            num_scalar_prefetch=1,
            grid=(count,),
            in_specs=[
                pl.BlockSpec((left.shape[0], 4 * rows), lambda i, at: (0, at[i]))
                for left in lefts
            ]
            + [pl.BlockSpec(right.shape, lambda i, at: (0, 0)) for right in (*rights, *pads)],
            out_specs=[part, part, pl.BlockSpec((2, each, cols), lambda i, at: (0, i, 0))],
            scratch_shapes=[pltpu.VMEM((4, rows, cols), jnp.bfloat16)],
        ),
        out_shape=[
            shape, shape, jax.ShapeDtypeStruct((2, count * each, cols), jnp.bfloat16),
        ],
        cost_estimate=CHEAP,
        name="weight_grads",
    )(at, *lefts, *rights, *pads)
    return own, far, sent.reshape(2 * count * each, cols)


def row_grads_kernel(*refs, lefts):
    left_refs, right_refs, (out_ref, held) = refs[:lefts], refs[lefts:-2], refs[-2:]

    @pl.when(pl.program_id(0) == 0)
    def _():
        first = 0
        for ref in right_refs:
            held[first : first + ref.shape[0], :] = ref[...]
            first += ref.shape[0]

    sums, first = 0.0, 0
    for ref in left_refs:
        sums += lax.dot_general(
            ref[...],
            held[first : first + ref.shape[0], :],
            DOWN,
            preferred_element_type=jnp.float32,
        )
        first += ref.shape[0]
    out_ref[...] = sums.astype(jnp.bfloat16)


def row_grads(lefts, rights, block=256):
    out_rows, cols = lefts[0].shape[1], rights[0].shape[1]
    total = sum(left.shape[0] for left in lefts)
    return pl.pallas_call(
        lambda *refs: row_grads_kernel(*refs, lefts=len(lefts)),
        grid=(out_rows // block,),
        in_specs=[pl.BlockSpec((left.shape[0], block), lambda i: (0, i)) for left in lefts]
        + [pl.BlockSpec(right.shape, lambda i: (0, 0)) for right in rights],
        out_specs=pl.BlockSpec((block, cols), lambda i: (i, 0)),
        out_shape=jax.ShapeDtypeStruct((out_rows, cols), jnp.bfloat16),
        scratch_shapes=[pltpu.VMEM((total, cols), jnp.bfloat16)],
        cost_estimate=CHEAP,
        name="row_grads",
    )(*lefts, *rights)


def hidden_grads_kernel(*refs, strips):
    matrix_ref, outs, held = refs[strips], refs[strips + 1 : -1], refs[-1]

    @pl.when(pl.program_id(0) == 0)
    def _():
        first = 0
        for ref in refs[:strips]:
            held[first : first + ref.shape[0], :] = ref[...]
            first += ref.shape[0]

    first = 0
    for out in outs:
        out[...] = lax.dot_general(
            held[first : first + out.shape[0], :],
            matrix_ref[...],
            ALONG,
            preferred_element_type=jnp.float32,
        )
        first += out.shape[0]


def hidden_grads_of(strips, matrix, block=256):
    rows = [(last - first) * strips[0].shape[0] for first, last in GROUPS]
    cols = matrix.shape[0]
    return pl.pallas_call(
        lambda *refs: hidden_grads_kernel(*refs, strips=len(strips)),
        grid=(cols // block,),
        in_specs=[pl.BlockSpec(strip.shape, lambda i: (0, 0)) for strip in strips]
        + [pl.BlockSpec((block, matrix.shape[1]), lambda i: (i, 0))],
        out_specs=[pl.BlockSpec((n, block), lambda i: (0, i)) for n in rows],
        out_shape=[jax.ShapeDtypeStruct((n, cols), jnp.float32) for n in rows],
        scratch_shapes=[pltpu.VMEM((sum(rows), matrix.shape[1]), jnp.bfloat16)],
        cost_estimate=CHEAP,
        name="hidden_grads",
    )(*strips, matrix)


def lane_sums(block):
    return sum(block[:, i : i + 128] for i in range(0, block.shape[1], 128))


def widen(at, swap, *weights):
    rows, taken, count = weights[0].shape[0], [item[1:] for item in swap.taken], len(weights)
    pad = swap.rows - rows

    def widen_kernel(at_ref, *refs):
        piece_refs, refs = refs[: len(taken)], refs[len(taken) :]
        grads, sums_ref = refs[count : 2 * count], refs[2 * count]
        for ref in refs[2 * count :]:
            ref[...] = jnp.zeros_like(ref)
        for ref, (start, size, spot, top) in zip(piece_refs, taken):
            used = min(size, rows - top)
            here = slice(top, top + used)
            first = 0
            for weight, grad in zip(refs[:count], grads):
                width = weight.shape[1] // 8
                there = columns(at_ref[spot], width)
                block = ref[start : start + used, first : first + width].astype(jnp.float32)
                grad[here, there] = block
                sums_ref[here, :] += lane_sums(block * weight[here, there].astype(jnp.float32))
                first += width
            if used < size:
                refs[-1][...] += ref[start + used : start + size, :].astype(jnp.float32)

    vmem = pl.BlockSpec(memory_space=pltpu.VMEM)
    shapes = [w.shape for w in weights] + [(rows, 128)]
    if pad:
        shapes.append((pad, swap.taken[0][0].shape[1]))
    return pl.pallas_call(
        widen_kernel,
        grid=(1,),
        in_specs=[pl.BlockSpec(memory_space=pltpu.SMEM), *swap.specs()] + [vmem] * count,
        out_specs=[vmem] * len(shapes),
        out_shape=[jax.ShapeDtypeStruct(shape, jnp.float32) for shape in shapes],
        cost_estimate=LONG,
        name="widen",
    )(at, *swap.operands(), *weights)


def grouped(strips):
    return [
        jnp.concatenate(strips[a:b], axis=0) if b - a > 1 else strips[a] for a, b in GROUPS
    ]


def split_groups(groups, rows):
    return [
        group[i * rows : (i + 1) * rows]
        for group in groups
        for i in range(group.shape[0] // rows)
    ]


def gather_head(rows):
    return lax.all_gather(rows, "head", axis=0, tiled=True)


def scatter_head(rows):
    return lax.psum_scatter(rows, "head", scatter_dimension=0, tiled=True)


def inverse_rms(rows):
    return lax.rsqrt(jnp.mean(rows * rows, axis=-1, keepdims=True) + EPS)


def per_device(
    tokens,
    attention_norm,
    query_weight,
    key_projection,
    value_projection,
    query_norm,
    key_norm,
    output_weight,
    feedforward_norm,
    gate_weight,
    up_weight,
    down_weight,
    stretch_order,
    out_cotangent,
):
    blk_count = lax.axis_size("blk")
    head_count = lax.axis_size("head")
    head_index = lax.axis_index("head")
    blk_index = lax.axis_index("blk")
    narrow, wide = jnp.bfloat16, jnp.float32
    tokens, out_cotangent = tokens[0], out_cotangent[0]
    local_rows, model_width = tokens.shape
    group_rows = local_rows * blk_count
    weight_rows = query_weight.shape[0]
    ff_local = gate_weight.shape[1] // blk_count
    query_cols = QUERY_HEADS // blk_count * HEAD_SIZE
    attn_cols = query_cols + 2 * HEAD_SIZE
    device_count = blk_count * head_count
    strip_count = blk_count * head_count
    halves = strip_count // stretch_order.shape[1]
    ring_place = jnp.where(blk_index % 2 == 0, blk_index // 2, 7 - blk_index // 2)

    spot = (ring_place + jnp.arange(blk_count, dtype=jnp.int32)) % blk_count
    at = jnp.where(spot < 4, 2 * spot, 15 - 2 * spot).astype(jnp.int32)
    at_own = jnp.concatenate([at, head_index[None].astype(jnp.int32)])
    ring_spot = (ring_place + jnp.asarray(STRIPS, jnp.int32)) % blk_count
    strip_blk = jnp.where(ring_spot < 4, 2 * ring_spot, 15 - 2 * ring_spot)
    strip_head = head_index ^ jnp.asarray((0, 2, 1, 3), jnp.int32)
    strip = (strip_blk[None, :] * head_count + strip_head[:, None]).reshape(strip_count)
    slots = jnp.arange(stretch_order.shape[1], dtype=jnp.int32)
    held = jnp.sum(
        jnp.where((strip // halves)[:, None] == slots[None, :], stretch_order, 0), axis=1
    )
    strip_place = held * halves + strip % halves
    order = strip_place.astype(jnp.int32)
    place = strip_place[:blk_count].astype(jnp.int32)
    positions = (
        place[:, None] * local_rows + jnp.arange(local_rows, dtype=jnp.int32)[None, :]
    ).reshape(group_rows)
    phases = angles(positions, HEAD_SIZE)[:, 0, :]
    cosine, sine = jnp.cos(phases), jnp.sin(phases)
    cosine = jnp.concatenate([cosine, cosine], axis=1)
    sine = jnp.concatenate([-sine, sine], axis=1)

    small = query_norm.shape[0]
    number = blk_index * head_count + head_index
    pad = 16

    def placed(share):
        return jnp.where(
            jnp.arange(device_count, dtype=jnp.int32)[:, None] == number, share[None, :], 0
        ).reshape(-1)

    gains = jnp.concatenate(
        [placed(attention_norm), placed(feedforward_norm), placed(query_norm), placed(key_norm)]
    ).astype(narrow)
    gains = jnp.pad(gains, (0, pad * attn_cols - gains.shape[0])).reshape(pad, attn_cols)
    down_matrix = gather_head(down_weight)
    output_rows = gather_head(output_weight)

    attn_swap = Swap(
        slice_pieces(at, query_weight, key_projection, value_projection, pad=gains),
        weight_rows + pad,
    )
    token_ring = Gather(tokens)
    ff_slices = slice_pieces(at, gate_weight, up_weight)
    token_ring.go()
    attn_swap.go()
    ff_slices, cosine, sine = hold((attn_swap,), ff_slices, cosine, sine)
    attn_swap.go()
    hold((attn_swap,))
    attn_swap.go()
    own = hold((token_ring,), attn_swap.result())
    near, far = cross(own, 1), cross(own, 2)
    token_ring.go()
    ff_swap, cotangent_ring = Swap(ff_slices, weight_rows), Gather(out_cotangent)
    hold((token_ring, ff_swap, cotangent_ring))
    token_ring.go()
    own, near, far = hold((token_ring,), own, near, far)
    both = cross(far, 1)
    token_ring.go()
    own, near, far, both = hold((token_ring, ff_swap, cotangent_ring), own, near, far, both)
    ff_swap.go()
    cotangent_ring.go()

    first_normed, attn_raw, query_rows, own, attn_matrix, gains = project(
        at_own, token_ring.strips(), (own, near, far, both), cosine, sine, query_cols, pad
    )
    gain_one = gains[:4].reshape(1, model_width)
    gain_two = gains[4:8].reshape(1, model_width)
    head_gains = jnp.pad(gains[8, : 2 * HEAD_SIZE].reshape(2, HEAD_SIZE), ((0, 6), (0, 0)))
    near, far = cross(own, 1), cross(own, 2)
    own, near, far = hold((ff_swap, cotangent_ring), own, near, far)
    both = cross(far, 1)
    kv = hold((ff_swap, cotangent_ring), own, far, near, both)
    ff_swap.go(late=True)
    cotangent_ring.go()
    attended, lse = attend(place, order, query_rows, kv)

    def by_groups(rows):
        return [rows[a * local_rows : b * local_rows] for a, b in GROUPS]

    def by_strips(groups):
        return dict(zip(STRIPS, split_groups(groups, local_rows)))

    attended = hold((cotangent_ring, ff_swap), attended)
    branch_parts = [matmul(rows, output_rows).astype(narrow) for rows in by_groups(attended)]
    branch_ring = Scatter(by_strips(branch_parts))
    branch_ring.go()
    ff_swap.trim()
    ff_swap.go()
    ff_own = hold((branch_ring,), ff_swap.result())
    ff_near, ff_far = cross(ff_own, 1), cross(ff_own, 2)
    branch_ring.go()
    cotangent_ring.go()
    hold((branch_ring, cotangent_ring))
    branch_ring.go()
    cotangent_ring.go()
    ff_near, ff_far, down_matrix = hold(
        (branch_ring, cotangent_ring), ff_near, ff_far, down_matrix
    )
    cotangent_strips = hold((), cotangent_ring.strips())
    branch_ring.go()
    hidden_grads = hidden_grads_of(cotangent_strips, down_matrix)
    ff_both = cross(ff_far, 1)
    hidden_grads, ff_both = hold((branch_ring,), hidden_grads, ff_both)
    tokens_wide = tokens.astype(wide)
    resid = tokens_wide + branch_ring.total()
    rho_two = inverse_rms(resid)
    unit_two = resid * rho_two

    second_ring = Gather((unit_two * gain_two).astype(narrow))
    second_groups, hidden_groups, ff_gradient_groups = [], [], []

    def feed_forward(index):
        rows = second_ring.group(index)
        ff_raw = matmul(rows, ff_matrix)
        gate, up_proj = ff_raw[:, :ff_local], ff_raw[:, ff_local:]
        sigma = jax.nn.sigmoid(gate)
        swish = gate * sigma
        hidden_gradient = hidden_grads[index]
        gate_gradient = hidden_gradient * up_proj * (sigma * (1.0 + gate * (1.0 - sigma)))
        hidden = (swish * up_proj).astype(narrow)
        gradient = jnp.concatenate([gate_gradient, hidden_gradient * swish], 1).astype(narrow)
        if index < 3:
            rows, hidden, gradient = hold((second_ring,), rows, hidden, gradient)
        second_groups.append(rows)
        hidden_groups.append(hidden)
        ff_gradient_groups.append(gradient)

    second_ring.go()
    ff_matrix = assemble(at_own, (ff_own, ff_near, ff_far, ff_both), weight_rows)
    ff_matrix = hold((second_ring,), ff_matrix)
    for index in range(3):
        second_ring.go()
        feed_forward(index)
    feed_forward(3)

    def back(index):
        return matmul(ff_gradient_groups[index], ff_matrix, ALONG).astype(narrow)

    def split(group):
        return [group[i : i + local_rows] for i in range(0, group.shape[0], local_rows)]

    parts = {4: back(3)}
    resid_ring = Scatter(parts)
    parts[3], parts[5] = split(hold((), back(2)))
    parts[2], parts[6] = split(hold((), back(1)))
    resid_ring.go()
    _, _, hidden_groups, cotangent_strips = hold(
        (resid_ring,), parts[2], parts[6], hidden_groups, cotangent_strips
    )
    resid_ring.go()
    down_gradient = row_grads(hidden_groups, cotangent_strips)
    back_zero, down_gradient, second_groups, ff_gradient_groups = hold(
        (resid_ring,), back(0), down_gradient, second_groups, ff_gradient_groups
    )
    down_gradient = scatter_head(down_gradient)
    parts[0], parts[1], parts[7] = split(back_zero)
    resid_ring.go()
    ff_own, ff_far, ff_sent = hold(
        (resid_ring,), *weight_grads(at_own, second_groups, ff_gradient_groups, weight_rows)
    )
    resid_ring.go()
    ff_own, ff_far = scatter_cross(ff_own, ff_far, ff_sent)
    ff_own, ff_far, hidden_groups = hold((resid_ring,), ff_own, ff_far, hidden_groups)
    ff_far = cross(ff_far, 2)
    scaled = gain_two * resid_ring.total()
    resid_gradient = out_cotangent.astype(wide) + rho_two * (
        scaled - unit_two * jnp.mean(unit_two * scaled, axis=-1, keepdims=True)
    )

    grad_ring = Gather(resid_gradient.astype(narrow))
    grad_groups, attended_grads = [], []

    def attention_back(index):
        rows = grad_ring.group(index)
        grads = matmul(rows, output_rows, ALONG).astype(narrow)
        if index < 3:
            rows, grads = hold((grad_ring,), rows, grads)
        grad_groups.append(rows)
        attended_grads.append(grads)

    grad_ring.go()
    out_parts = [matmul(rows, down_matrix).astype(narrow) for rows in hidden_groups]
    out_parts = hold((grad_ring,), *out_parts)
    out_ring = Scatter(by_strips(out_parts))
    grad_ring.go()
    hold((grad_ring,))
    grad_ring.go()
    attention_back(0)
    hold((out_ring, grad_ring))
    out_ring.go()
    grad_ring.go()
    attention_back(1)
    attention_back(2)
    ff_swap = Swap(add(ff_own, ff_far), weight_rows)
    hold((grad_ring, ff_swap, out_ring))
    out_ring.go()
    ff_swap.go(late=True)
    attention_back(3)
    query_grads, kv_own, kv_far, kv_sent = attend_back(
        place, order, query_rows, attended_grads, attended, lse, kv
    )
    query_grads, kv_own, kv_far, kv_sent, grad_groups, attended, down_gradient = hold(
        (out_ring, ff_swap),
        query_grads, kv_own, kv_far, kv_sent, grad_groups, attended, down_gradient,
    )
    out_ring.go()
    ff_swap.trim()
    kv_own, kv_far = scatter_cross(kv_own, kv_far, kv_sent)
    output_weight_gradient = row_grads([attended], grad_groups)
    kv_own, kv_far, output_weight_gradient = hold(
        (out_ring, ff_swap), kv_own, kv_far, output_weight_gradient
    )
    ff_swap.go()
    kv_grads, ff_opposite = hold(
        (ff_swap,), add(kv_own, cross(kv_far, 2)), hop(ff_swap.across, 4)
    )
    ff_swap.opposite(ff_opposite)
    ff_swap.go()
    attn_gradient, first_parts, gain_sums = project_back(
        query_grads, kv_grads, attn_raw, head_gains, cosine, sine, attn_matrix
    )
    gain_sums = jnp.pad(
        gain_sums[:2].reshape(1, 2 * HEAD_SIZE).astype(narrow),
        ((0, pad - 1), (0, attn_cols - 2 * HEAD_SIZE)),
    )
    attn_gradient, first_parts, gain_sums, output_weight_gradient = hold(
        (ff_swap, out_ring), attn_gradient, first_parts, gain_sums, output_weight_gradient
    )
    token_ring = Scatter(by_strips(by_groups(first_parts)))
    token_ring.go()
    out_ring.go()
    attn_own, attn_far, attn_sent = weight_grads(
        at_own, [first_normed], [attn_gradient], weight_rows, gain_sums
    )
    attn_own, attn_far, attn_sent = hold(
        (token_ring, out_ring), attn_own, attn_far, attn_sent
    )
    token_ring.go()
    attn_own, attn_far = scatter_cross(attn_own, attn_far, attn_sent)
    attn_far = cross(attn_far, 2)
    layer_out = (resid + out_ring.total()).astype(narrow)
    attn_swap = Swap(add(attn_own, attn_far), weight_rows + pad)
    output_weight_gradient, layer_out, gate_weight, up_weight = hold(
        (token_ring, attn_swap), output_weight_gradient, layer_out, gate_weight, up_weight
    )
    output_weight_gradient = scatter_head(output_weight_gradient)
    attn_swap.go()
    token_ring.go()
    gate_weight_gradient, up_weight_gradient, ff_sums = widen(at, ff_swap, gate_weight, up_weight)
    gate_weight_gradient, up_weight_gradient, ff_sums = hold(
        (token_ring, attn_swap), gate_weight_gradient, up_weight_gradient, ff_sums
    )
    feedforward_norm_gradient = jnp.sum(ff_sums, axis=1) / feedforward_norm.astype(wide)
    down_gradient = down_gradient.astype(wide)
    attn_swap.go()
    token_ring.go()
    output_weight_gradient, down_gradient, feedforward_norm_gradient = hold(
        (token_ring, attn_swap),
        output_weight_gradient.astype(wide), down_gradient, feedforward_norm_gradient,
    )
    attn_swap.go()
    query_weight_gradient, key_weight_gradient, value_weight_gradient, norm_sums, gain_sums = widen(
        at, attn_swap, query_weight, key_projection, value_projection
    )
    attention_norm_gradient = jnp.sum(norm_sums, axis=1) / attention_norm.astype(wide)
    gain_sums = gain_sums[0, : 2 * HEAD_SIZE].reshape(2, HEAD_SIZE)
    gain_sums = lax.dynamic_slice_in_dim(gain_sums, number * small, small, 1)
    rho_one = inverse_rms(tokens_wide)
    unit_one = tokens_wide * rho_one
    scaled = gain_one * token_ring.total()
    tokens_gradient = resid_gradient + rho_one * (
        scaled - unit_one * jnp.mean(unit_one * scaled, axis=-1, keepdims=True)
    )
    return (
        layer_out[None],
        tokens_gradient.astype(narrow)[None],
        attention_norm_gradient,
        query_weight_gradient,
        key_weight_gradient,
        value_weight_gradient,
        gain_sums[0],
        gain_sums[1],
        output_weight_gradient,
        feedforward_norm_gradient,
        gate_weight_gradient,
        up_weight_gradient,
        down_gradient,
    )


def solution(mesh):
    placed = (
        P(None, ("blk", "head"), None),
        P(("blk", "head")),
        P(("blk", "head"), None),
        P(("blk", "head"), None),
        P(("blk", "head"), None),
        P(("blk", "head")),
        P(("blk", "head")),
        P(("blk", "head"), None),
        P(("blk", "head")),
        P(("blk", "head"), None),
        P(("blk", "head"), None),
        P(("blk", "head"), None),
        P(),
        P(None, ("blk", "head"), None),
    )
    fits = mesh.shape["blk"] == KEY_VALUE_HEADS and mesh.shape["head"] == 4
    return jax.shard_map(
        per_device if fits else per_device_by_tokens,
        mesh=mesh,
        in_specs=placed,
        out_specs=(
            P(None, ("blk", "head"), None),
            P(None, ("blk", "head"), None),
            P(("blk", "head")),
            P(("blk", "head"), None),
            P(("blk", "head"), None),
            P(("blk", "head"), None),
            P(("blk", "head")),
            P(("blk", "head")),
            P(("blk", "head"), None),
            P(("blk", "head")),
            P(("blk", "head"), None),
            P(("blk", "head"), None),
            P(("blk", "head"), None),
        ),
        check_vma=False,
    )
```

```python
import math

import jax
import jax.numpy as jnp
from jax import lax
from jax.experimental import pallas as pl
from jax.experimental.pallas import tpu as pltpu
from jax.sharding import PartitionSpec as P

QUERY_HEADS = 16
KEY_VALUE_HEADS = 8
HEAD_SIZE = 128


EPS = 1e-06
NEG = -1e30
ROPE_BASE = 1000000.0


def passed_along(value, axis, by):
    count = lax.axis_size(axis)
    return lax.ppermute(value, axis, [(i, (i + by) % count) for i in range(count)])


def norm_rows(inputs, norm_gain):
    return inputs * lax.rsqrt(jnp.mean(inputs * inputs, axis=-1, keepdims=True) + EPS) * norm_gain


def rotary(inputs, phases):
    half_width = inputs.shape[-1] // 2
    cosine = jnp.cos(phases)
    sine_term = jnp.sin(phases)
    first_half = inputs[..., :half_width]
    second_half = inputs[..., half_width:]
    return jnp.concatenate(
        [
            first_half * cosine - second_half * sine_term,
            second_half * cosine + first_half * sine_term,
        ],
        axis=-1,
    )


def angles(positions, head_width):
    half_width = head_width // 2
    frequency = jnp.exp(
        jnp.arange(half_width, dtype=jnp.float32) * (-2.0 * math.log(ROPE_BASE) / head_width)
    )
    return positions.astype(jnp.float32)[..., None, None] * frequency


def token_positions(stretch_order, first_row, row_count, stretch_rows):
    row_index = first_row + jnp.arange(row_count, dtype=jnp.int32)
    slot_index = row_index // stretch_rows
    matches = slot_index[:, None] == jnp.arange(stretch_order.shape[1], dtype=jnp.int32)[None, :]
    picked = jnp.sum(jnp.where(matches[None], stretch_order[:, None, :], 0), axis=-1)
    return picked * stretch_rows + row_index % stretch_rows


def per_device_by_tokens(
    tokens,
    attention_norm,
    query_weight,
    key_projection,
    value_projection,
    query_norm,
    key_norm,
    output_weight,
    feedforward_norm,
    gate_weight,
    up_weight,
    down_weight,
    stretch_order,
    out_cotangent,
):
    count_of_heads = lax.axis_size("head")
    span_count = lax.axis_size("blk")
    span_index = lax.axis_index("blk")
    head_index = lax.axis_index("head")
    sequence_total = tokens.shape[0]
    local_rows = tokens.shape[1]
    group_rows = local_rows * count_of_heads
    stretch_rows = group_rows // 2
    heads_shared = KEY_VALUE_HEADS // count_of_heads
    heads_per_group = QUERY_HEADS // KEY_VALUE_HEADS
    score_scale = 1.0 / math.sqrt(HEAD_SIZE)
    gain_one, query_matrix, key_matrix, value_matrix, query_gain, key_gain, output_matrix = (
        lax.all_gather(attention_norm, ("blk", "head"), axis=0, tiled=True),
        lax.all_gather(query_weight, ("blk", "head"), axis=0, tiled=True),
        lax.all_gather(key_projection, ("blk", "head"), axis=0, tiled=True),
        lax.all_gather(value_projection, ("blk", "head"), axis=0, tiled=True),
        lax.all_gather(query_norm, ("blk", "head"), axis=0, tiled=True),
        lax.all_gather(key_norm, ("blk", "head"), axis=0, tiled=True),
        lax.all_gather(output_weight, ("blk", "head"), axis=0, tiled=True),
    )
    gain_two, gate_matrix, up_matrix, down_matrix = (
        lax.all_gather(feedforward_norm, ("blk", "head"), axis=0, tiled=True),
        lax.all_gather(gate_weight, ("blk", "head"), axis=0, tiled=True),
        lax.all_gather(up_weight, ("blk", "head"), axis=0, tiled=True),
        lax.all_gather(down_weight, ("blk", "head"), axis=0, tiled=True),
    )
    gain_one = gain_one.astype(jnp.float32)
    gain_two = gain_two.astype(jnp.float32)
    query_gain = query_gain.astype(jnp.float32)
    key_gain = key_gain.astype(jnp.float32)
    own_first = (span_index * count_of_heads + head_index) * local_rows
    own_pos = token_positions(stretch_order, own_first, local_rows, stretch_rows)
    group_pos = token_positions(stretch_order, span_index * group_rows, group_rows, stretch_rows)
    phases = angles(own_pos, HEAD_SIZE)
    tokens_wide = tokens.astype(jnp.float32)
    first_normed, norm_one_back = jax.vjp(norm_rows, tokens_wide, gain_one)
    first_normed = first_normed.astype(jnp.bfloat16)
    query_raw = jnp.einsum(
        "btd,de->bte", first_normed, query_matrix, preferred_element_type=jnp.float32
    ).reshape(sequence_total, local_rows, QUERY_HEADS, HEAD_SIZE)
    key_unnormed = jnp.einsum(
        "btd,de->bte", first_normed, key_matrix, preferred_element_type=jnp.float32
    ).reshape(sequence_total, local_rows, KEY_VALUE_HEADS, HEAD_SIZE)
    value_tokens = (
        jnp.einsum("btd,de->bte", first_normed, value_matrix, preferred_element_type=jnp.float32)
        .astype(jnp.bfloat16)
        .reshape(sequence_total, local_rows, KEY_VALUE_HEADS, HEAD_SIZE)
    )

    def heads_local(query_in, key_in, query_scale, key_scale):
        return (
            rotary(norm_rows(query_in, query_scale), phases),
            rotary(norm_rows(key_in, key_scale), phases),
        )

    (query_tokens, key_tokens), heads_back = jax.vjp(
        heads_local, query_raw, key_unnormed, query_gain, key_gain
    )
    query_tokens = query_tokens.astype(jnp.bfloat16)
    key_tokens = key_tokens.astype(jnp.bfloat16)
    query_group, key_group, value_group = (
        lax.all_to_all(query_tokens, "head", split_axis=2, concat_axis=1, tiled=True),
        lax.all_to_all(key_tokens, "head", split_axis=2, concat_axis=1, tiled=True),
        lax.all_to_all(value_tokens, "head", split_axis=2, concat_axis=1, tiled=True),
    )
    query_five = query_group.reshape(
        sequence_total, group_rows, heads_shared, heads_per_group, HEAD_SIZE
    )

    def block_update(carry, key_block, value_block, key_pos):
        run_max, run_sum, run_total = carry
        scores = (
            jnp.einsum(
                "bqkgd,bckd->bkgqc", query_five, key_block, preferred_element_type=jnp.float32
            )
            * score_scale
        )
        allowed = key_pos[:, None, None, None, :] <= group_pos[:, None, None, :, None]
        scores = jnp.where(allowed, scores, NEG)
        new_max = jnp.maximum(run_max, jnp.max(scores, axis=-1))
        exponent = jnp.where(allowed, jnp.exp(scores - new_max[..., None]), 0.0)
        factor = jnp.exp(run_max - new_max)
        new_sum = run_sum * factor + jnp.sum(exponent, axis=-1)
        new_total = run_total * factor[..., None] + jnp.einsum(
            "bkgqc,bckd->bkgqd",
            exponent.astype(jnp.bfloat16),
            value_block,
            preferred_element_type=jnp.float32,
        )
        return (new_max, new_sum, new_total)

    def fold_update(carry, key_block, value_block, key_pos):
        result = block_update(carry, key_block, value_block, key_pos)
        return result

    stat_shape = (sequence_total, heads_shared, heads_per_group, group_rows)
    start_state = (
        jnp.full(stat_shape, NEG, jnp.float32),
        jnp.zeros(stat_shape, jnp.float32),
        jnp.zeros(stat_shape + (HEAD_SIZE,), jnp.float32),
    )
    key_piece = lax.all_gather(key_group, "blk", axis=1, tiled=True)
    value_piece = lax.all_gather(value_group, "blk", axis=1, tiled=True)
    piece_rows = key_piece.shape[1]
    block_len = math.gcd(group_rows, piece_rows)

    def inner(block_number, carry_in):
        offset = block_number * block_len
        key_block = lax.dynamic_slice_in_dim(key_piece, offset, block_len, 1)
        value_block = lax.dynamic_slice_in_dim(value_piece, offset, block_len, 1)
        key_pos = token_positions(stretch_order, offset, block_len, stretch_rows)
        return fold_update(carry_in, key_block, value_block, key_pos)

    run_max, run_sum, run_total = lax.fori_loop(0, piece_rows // block_len, inner, start_state)
    log_total = run_max + jnp.log(run_sum)
    attended_five = run_total / run_sum[..., None]
    attended_group = (
        jnp.transpose(attended_five, (0, 3, 1, 2, 4))
        .reshape(sequence_total, group_rows, heads_shared * heads_per_group, HEAD_SIZE)
        .astype(jnp.bfloat16)
    )
    attended_tokens = lax.all_to_all(
        attended_group, "head", split_axis=1, concat_axis=2, tiled=True
    ).reshape(sequence_total, local_rows, QUERY_HEADS * HEAD_SIZE)
    branch = jnp.einsum(
        "bte,ed->btd", attended_tokens, output_matrix, preferred_element_type=jnp.float32
    )
    resid = tokens_wide + branch
    normed_two, norm_two_back = jax.vjp(norm_rows, resid, gain_two)
    normed_two = normed_two.astype(jnp.bfloat16)
    gate = jnp.einsum("btd,df->btf", normed_two, gate_matrix, preferred_element_type=jnp.float32)
    up_proj = jnp.einsum("btd,df->btf", normed_two, up_matrix, preferred_element_type=jnp.float32)

    def swish_product(gate_in, up_in):
        return jax.nn.silu(gate_in) * up_in

    hidden, swish_back = jax.vjp(swish_product, gate, up_proj)
    hidden = hidden.astype(jnp.bfloat16)
    layer_out = (
        resid + jnp.einsum("btf,fd->btd", hidden, down_matrix, preferred_element_type=jnp.float32)
    ).astype(jnp.bfloat16)
    gain_again, gate_matrix, up_matrix, down_matrix = (
        lax.all_gather(feedforward_norm, ("blk", "head"), axis=0, tiled=True),
        lax.all_gather(gate_weight, ("blk", "head"), axis=0, tiled=True),
        lax.all_gather(up_weight, ("blk", "head"), axis=0, tiled=True),
        lax.all_gather(down_weight, ("blk", "head"), axis=0, tiled=True),
    )
    down_gradient = jnp.einsum(
        "btf,btd->fd", hidden, out_cotangent, preferred_element_type=jnp.float32
    )
    hidden_gradient = jnp.einsum(
        "btd,fd->btf", out_cotangent, down_matrix, preferred_element_type=jnp.float32
    )
    gate_gradient, up_gradient = swish_back(hidden_gradient)
    gate_gradient = gate_gradient.astype(jnp.bfloat16)
    up_gradient = up_gradient.astype(jnp.bfloat16)
    gate_matrix_gradient = jnp.einsum(
        "btd,btf->df", normed_two, gate_gradient, preferred_element_type=jnp.float32
    )
    up_matrix_gradient = jnp.einsum(
        "btd,btf->df", normed_two, up_gradient, preferred_element_type=jnp.float32
    )
    normed_two_gradient = jnp.einsum(
        "btf,df->btd", gate_gradient, gate_matrix, preferred_element_type=jnp.float32
    ) + jnp.einsum("btf,df->btd", up_gradient, up_matrix, preferred_element_type=jnp.float32)
    resid_part, gain_two_gradient = norm_two_back(normed_two_gradient)
    resid_gradient = out_cotangent.astype(jnp.float32) + resid_part
    feedforward_sums = (
        lax.psum_scatter(gain_two_gradient, ("blk", "head"), scatter_dimension=0, tiled=True),
        lax.psum_scatter(gate_matrix_gradient, ("blk", "head"), scatter_dimension=0, tiled=True),
        lax.psum_scatter(up_matrix_gradient, ("blk", "head"), scatter_dimension=0, tiled=True),
        lax.psum_scatter(down_gradient, ("blk", "head"), scatter_dimension=0, tiled=True),
    )
    gain_again, query_matrix, key_matrix, value_matrix, query_again, key_again, output_matrix = (
        lax.all_gather(attention_norm, ("blk", "head"), axis=0, tiled=True),
        lax.all_gather(query_weight, ("blk", "head"), axis=0, tiled=True),
        lax.all_gather(key_projection, ("blk", "head"), axis=0, tiled=True),
        lax.all_gather(value_projection, ("blk", "head"), axis=0, tiled=True),
        lax.all_gather(query_norm, ("blk", "head"), axis=0, tiled=True),
        lax.all_gather(key_norm, ("blk", "head"), axis=0, tiled=True),
        lax.all_gather(output_weight, ("blk", "head"), axis=0, tiled=True),
    )
    branch_gradient = resid_gradient.astype(jnp.bfloat16)
    output_matrix_gradient = jnp.einsum(
        "bte,btd->ed", attended_tokens, branch_gradient, preferred_element_type=jnp.float32
    )
    attended_gradient = (
        jnp.einsum(
            "btd,ed->bte", branch_gradient, output_matrix, preferred_element_type=jnp.float32
        )
        .astype(jnp.bfloat16)
        .reshape(sequence_total, local_rows, QUERY_HEADS, HEAD_SIZE)
    )
    attended_grad_group = lax.all_to_all(
        attended_gradient, "head", split_axis=2, concat_axis=1, tiled=True
    ).reshape(sequence_total, group_rows, heads_shared, heads_per_group, HEAD_SIZE)
    delta = jnp.sum(
        jnp.transpose(attended_grad_group.astype(jnp.float32), (0, 2, 3, 1, 4)) * attended_five,
        axis=-1,
    )

    def block_grads(sums_in, key_current, value_current, key_pos):
        key_sum, value_sum, query_sum = sums_in
        scores = (
            jnp.einsum(
                "bqkgd,bckd->bkgqc", query_five, key_current, preferred_element_type=jnp.float32
            )
            * score_scale
        )
        allowed = key_pos[:, None, None, None, :] <= group_pos[:, None, None, :, None]
        weights = jnp.where(allowed, jnp.exp(scores - log_total[..., None]), 0.0)
        probs = weights.astype(jnp.bfloat16)
        value_sum = value_sum + jnp.einsum(
            "bkgqc,bqkgd->bckd", probs, attended_grad_group, preferred_element_type=jnp.float32
        )
        probs_gradient = jnp.einsum(
            "bqkgd,bckd->bkgqc",
            attended_grad_group,
            value_current,
            preferred_element_type=jnp.float32,
        )
        scores_gradient = (weights * (probs_gradient - delta[..., None])).astype(jnp.bfloat16)
        query_sum = (
            query_sum
            + jnp.einsum(
                "bkgqc,bckd->bqkgd",
                scores_gradient,
                key_current,
                preferred_element_type=jnp.float32,
            )
            * score_scale
        )
        key_sum = (
            key_sum
            + jnp.einsum(
                "bkgqc,bqkgd->bckd", scores_gradient, query_five, preferred_element_type=jnp.float32
            )
            * score_scale
        )
        return (key_sum, value_sum, query_sum)

    def pass_step(step_index, carry):
        key_current, value_current, key_sum, value_sum, query_sum = carry
        anchor = (span_index - step_index) % span_count
        key_pos = token_positions(stretch_order, anchor * group_rows, group_rows, stretch_rows)
        key_sum, value_sum, query_sum = block_grads(
            (key_sum, value_sum, query_sum), key_current, value_current, key_pos
        )
        key_current, value_current = passed_along((key_current, value_current), "blk", 1)
        key_sum, value_sum = (
            passed_along(key_sum.astype(jnp.bfloat16), "blk", 1).astype(key_sum.dtype),
            passed_along(value_sum.astype(jnp.bfloat16), "blk", 1).astype(value_sum.dtype),
        )
        return (key_current, value_current, key_sum, value_sum, query_sum)

    kv_zeros = jnp.zeros((sequence_total, group_rows, heads_shared, HEAD_SIZE), jnp.float32)
    query_zeros = jnp.zeros(
        (sequence_total, group_rows, heads_shared, heads_per_group, HEAD_SIZE), jnp.float32
    )
    final_state = lax.fori_loop(
        0, span_count, pass_step, (key_group, value_group, kv_zeros, kv_zeros, query_zeros)
    )
    key_grad_group = final_state[2].astype(jnp.bfloat16)
    value_grad_group = final_state[3].astype(jnp.bfloat16)
    query_grad_group = (
        final_state[4]
        .astype(jnp.bfloat16)
        .reshape(sequence_total, group_rows, heads_shared * heads_per_group, HEAD_SIZE)
    )
    query_grad_tokens, key_grad_tokens, value_gradient_tokens = (
        lax.all_to_all(query_grad_group, "head", split_axis=1, concat_axis=2, tiled=True),
        lax.all_to_all(key_grad_group, "head", split_axis=1, concat_axis=2, tiled=True),
        lax.all_to_all(value_grad_group, "head", split_axis=1, concat_axis=2, tiled=True),
    )
    query_raw_gradient, key_unnormed_gradient, query_gain_gradient, key_gain_gradient = heads_back(
        (query_grad_tokens.astype(jnp.float32), key_grad_tokens.astype(jnp.float32))
    )
    query_raw_gradient = query_raw_gradient.astype(jnp.bfloat16).reshape(
        sequence_total, local_rows, QUERY_HEADS * HEAD_SIZE
    )
    key_unnormed_gradient = key_unnormed_gradient.astype(jnp.bfloat16).reshape(
        sequence_total, local_rows, KEY_VALUE_HEADS * HEAD_SIZE
    )
    value_unnormed_gradient = value_gradient_tokens.reshape(
        sequence_total, local_rows, KEY_VALUE_HEADS * HEAD_SIZE
    )
    query_matrix_gradient = jnp.einsum(
        "btd,bte->de", first_normed, query_raw_gradient, preferred_element_type=jnp.float32
    )
    key_matrix_gradient = jnp.einsum(
        "btd,bte->de", first_normed, key_unnormed_gradient, preferred_element_type=jnp.float32
    )
    value_matrix_gradient = jnp.einsum(
        "btd,bte->de", first_normed, value_unnormed_gradient, preferred_element_type=jnp.float32
    )
    normed_one_gradient = jnp.einsum(
        "bte,de->btd", query_raw_gradient, query_matrix, preferred_element_type=jnp.float32
    )
    normed_one_gradient = normed_one_gradient + jnp.einsum(
        "bte,de->btd", key_unnormed_gradient, key_matrix, preferred_element_type=jnp.float32
    )
    normed_one_gradient = normed_one_gradient + jnp.einsum(
        "bte,de->btd", value_unnormed_gradient, value_matrix, preferred_element_type=jnp.float32
    )
    token_part, gain_one_gradient = norm_one_back(normed_one_gradient)
    tokens_gradient = (resid_gradient + token_part).astype(jnp.bfloat16)
    attention_sums = (
        lax.psum_scatter(gain_one_gradient, ("blk", "head"), scatter_dimension=0, tiled=True),
        lax.psum_scatter(query_matrix_gradient, ("blk", "head"), scatter_dimension=0, tiled=True),
        lax.psum_scatter(key_matrix_gradient, ("blk", "head"), scatter_dimension=0, tiled=True),
        lax.psum_scatter(value_matrix_gradient, ("blk", "head"), scatter_dimension=0, tiled=True),
        lax.psum_scatter(query_gain_gradient, ("blk", "head"), scatter_dimension=0, tiled=True),
        lax.psum_scatter(key_gain_gradient, ("blk", "head"), scatter_dimension=0, tiled=True),
        lax.psum_scatter(output_matrix_gradient, ("blk", "head"), scatter_dimension=0, tiled=True),
    )
    return (
        layer_out,
        tokens_gradient,
        attention_sums[0],
        attention_sums[1],
        attention_sums[2],
        attention_sums[3],
        attention_sums[4],
        attention_sums[5],
        attention_sums[6],
        feedforward_sums[0],
        feedforward_sums[1],
        feedforward_sums[2],
        feedforward_sums[3],
    )


LOG2E = math.log2(math.e)
STRIP = 128
CHUNK = 512
ALONG = (((1,), (1,)), ((), ()))
DOWN = (((0,), (0,)), ((), ()))


def two_heads(block):
    return jnp.concatenate([block[:, :HEAD_SIZE], block[:, HEAD_SIZE:]], axis=0)


def side_by_side(rows):
    half = rows.shape[0] // 2
    return jnp.concatenate([rows[:half], rows[half:]], axis=1)


CHEAP = pl.CostEstimate(flops=1, bytes_accessed=1, transcendentals=0)
LONG = pl.CostEstimate(flops=3 * 10**10, bytes_accessed=1 << 25, transcendentals=0)


def sort_strips(order_ref, kv_refs, keys, values):
    per = kv_refs[0].shape[0] // STRIP
    for j, ref in enumerate(kv_refs):
        for i in range(per):
            target = pl.multiple_of(order_ref[j * per + i] * STRIP, STRIP)
            here = slice(i * STRIP, (i + 1) * STRIP)
            keys[pl.ds(target, STRIP), :] = ref[here, :HEAD_SIZE]
            values[pl.ds(target, STRIP), :HEAD_SIZE] = ref[here, HEAD_SIZE:]


def attend_kernel(place_ref, order_ref, q_ref, *refs):
    kv_refs, (out_ref, lse_ref, keys, values) = refs[:4], refs[4:]
    step = pl.program_id(0)

    @pl.when(step == 0)
    def _():
        values[:, HEAD_SIZE:] = jnp.ones((values.shape[0], HEAD_SIZE), jnp.bfloat16)
        sort_strips(order_ref, kv_refs, keys, values)

    place = place_ref[step]
    queries = two_heads(q_ref[...])
    last = place // (CHUNK // STRIP)

    def part(index, total, masked):
        first = pl.multiple_of(index * CHUNK, CHUNK)
        scores = lax.dot_general(
            queries, keys[pl.ds(first, CHUNK), :], ALONG, preferred_element_type=jnp.float32
        )
        weights = jnp.exp2(scores)
        if masked:
            row = lax.broadcasted_iota(jnp.int32, scores.shape, 0) % STRIP
            column = lax.broadcasted_iota(jnp.int32, scores.shape, 1)
            weights = jnp.where(column - row <= place * STRIP - first, weights, 0.0)
        return total + jnp.dot(
            weights.astype(jnp.bfloat16),
            values[pl.ds(first, CHUNK), :],
            preferred_element_type=jnp.float32,
        )

    total = jnp.zeros((2 * STRIP, 2 * HEAD_SIZE), jnp.float32)
    total = lax.fori_loop(0, last, lambda index, t: part(index, t, False), total)
    total = part(last, total, True)
    norm = total[:, HEAD_SIZE:]
    out_ref[...] = side_by_side(total[:, :HEAD_SIZE] / norm).astype(jnp.bfloat16)
    lse_ref[0] = jnp.transpose(jnp.log2(norm))[:8]


def attend(place, order, queries, kv):
    rows, width = queries.shape
    steps = rows // STRIP
    total = sum(part.shape[0] for part in kv)
    strip = pl.BlockSpec((STRIP, width), lambda i, *_: (i, 0))
    return pl.pallas_call(
        attend_kernel,
        grid_spec=pltpu.PrefetchScalarGridSpec(
            num_scalar_prefetch=2,
            grid=(steps,),
            in_specs=[strip] + [pl.BlockSpec(part.shape, lambda i, *_: (0, 0)) for part in kv],
            out_specs=[strip, pl.BlockSpec((1, 8, 2 * STRIP), lambda i, *_: (i, 0, 0))],
            scratch_shapes=[
                pltpu.VMEM((total, HEAD_SIZE), jnp.bfloat16),
                pltpu.VMEM((total, 2 * HEAD_SIZE), jnp.bfloat16),
            ],
        ),
        out_shape=[
            jax.ShapeDtypeStruct((rows, width), jnp.bfloat16),
            jax.ShapeDtypeStruct((steps, 8, 2 * STRIP), jnp.float32),
        ],
        cost_estimate=LONG,
        name="attend",
    )(place, order, queries, *kv)


def attend_back_kernel(place_ref, order_ref, q_ref, out_ref, lse_ref, *refs, groups):
    grad_refs, kv_refs = refs[:groups], refs[groups : groups + 4]
    dq_ref, own_ref, far_ref, sent_ref = refs[groups + 4 : groups + 8]
    keys, values, key_sums, value_sums, grads_all = refs[groups + 8 :]
    step = pl.program_id(0)

    @pl.when(step == 0)
    def _():
        key_sums[...] = jnp.zeros_like(key_sums)
        value_sums[...] = jnp.zeros_like(value_sums)
        sort_strips(order_ref, kv_refs, keys, values)
        first = 0
        for ref in grad_refs:
            grads_all[first : first + ref.shape[0], :] = ref[...]
            first += ref.shape[0]

    place = place_ref[step]
    queries = two_heads(q_ref[...])
    grads = two_heads(grads_all[pl.ds(pl.multiple_of(step * STRIP, STRIP), STRIP), :])
    product = grads.astype(jnp.float32) * two_heads(out_ref[...]).astype(jnp.float32)
    delta = jnp.sum(jnp.transpose(product), axis=0, keepdims=True)
    lse = lse_ref[0, :1]
    last = place // (CHUNK // STRIP)

    def part(index, total, masked):
        first = pl.multiple_of(index * CHUNK, CHUNK)
        here = pl.ds(first, CHUNK)
        key_rows = keys[here, :]
        scores = lax.dot_general(key_rows, queries, ALONG, preferred_element_type=jnp.float32)
        weights = jnp.exp2(scores - lse)
        if masked:
            row = lax.broadcasted_iota(jnp.int32, scores.shape, 0)
            column = lax.broadcasted_iota(jnp.int32, scores.shape, 1) % STRIP
            weights = jnp.where(row - column <= place * STRIP - first, weights, 0.0)
        slopes = lax.dot_general(
            values[here, :], grads, ALONG, preferred_element_type=jnp.float32
        )
        score_grads = (weights * (slopes - delta)).astype(jnp.bfloat16)
        value_sums[here, :] += jnp.dot(
            weights.astype(jnp.bfloat16), grads, preferred_element_type=jnp.float32
        )
        key_sums[here, :] += jnp.dot(score_grads, queries, preferred_element_type=jnp.float32)
        return total + lax.dot_general(
            score_grads, key_rows, DOWN, preferred_element_type=jnp.float32
        )

    total = jnp.zeros((2 * STRIP, HEAD_SIZE), jnp.float32)
    total = lax.fori_loop(0, last, lambda index, t: part(index, t, False), total)
    total = part(last, total, True)
    dq_ref[...] = side_by_side(total * (1.0 / math.sqrt(HEAD_SIZE))).astype(jnp.bfloat16)

    @pl.when(step == pl.num_programs(0) - 1)
    def _():
        per = own_ref.shape[0] // STRIP
        for j in range(4):
            target = (own_ref, far_ref, sent_ref, sent_ref)[j]
            base = per if j == 3 else 0
            for i in range(per):
                source = pl.multiple_of(order_ref[j * per + i] * STRIP, STRIP)
                here = slice((base + i) * STRIP, (base + i + 1) * STRIP)
                target[here, :HEAD_SIZE] = (
                    key_sums[pl.ds(source, STRIP), :] * (1.0 / LOG2E)
                ).astype(jnp.bfloat16)
                target[here, HEAD_SIZE:] = value_sums[pl.ds(source, STRIP), :].astype(
                    jnp.bfloat16
                )


def attend_back(place, order, queries, grads, attended, lse, kv):
    rows, width = queries.shape
    steps = rows // STRIP
    total = sum(part.shape[0] for part in kv)
    strip = pl.BlockSpec((STRIP, width), lambda i, *_: (i, 0))

    def whole(shape):
        return pl.BlockSpec(shape, lambda i, *_: (0, 0))

    outs = [kv[0].shape, kv[0].shape, (2 * kv[0].shape[0], kv[0].shape[1])]
    return pl.pallas_call(
        lambda *refs: attend_back_kernel(*refs, groups=len(grads)),
        grid_spec=pltpu.PrefetchScalarGridSpec(
            num_scalar_prefetch=2,
            grid=(steps,),
            in_specs=[strip, strip, pl.BlockSpec((1, 8, 2 * STRIP), lambda i, *_: (i, 0, 0))]
            + [whole(part.shape) for part in (*grads, *kv)],
            out_specs=[strip] + [whole(shape) for shape in outs],
            scratch_shapes=[
                pltpu.VMEM((total, HEAD_SIZE), jnp.bfloat16),
                pltpu.VMEM((total, HEAD_SIZE), jnp.bfloat16),
                pltpu.VMEM((total, HEAD_SIZE), jnp.float32),
                pltpu.VMEM((total, HEAD_SIZE), jnp.float32),
                pltpu.VMEM((rows, width), jnp.bfloat16),
            ],
        ),
        out_shape=[jax.ShapeDtypeStruct((rows, width), jnp.bfloat16)]
        + [jax.ShapeDtypeStruct(shape, jnp.bfloat16) for shape in outs],
        cost_estimate=LONG,
        name="attend_back",
    )(place, order, queries, attended, lse, *grads, *kv)


def matmul(left, right, dims=(((1,), (0,)), ((), ()))):
    return lax.dot_general(left, right, dims, preferred_element_type=jnp.float32)


RING = (0, 2, 4, 6, 7, 5, 3, 1)
STRIPS = (0, 1, 7, 2, 6, 3, 5, 4)
GROUPS = ((0, 3), (3, 5), (5, 7), (7, 8))


def hop(value, by):
    count = len(RING)
    return lax.ppermute(value, "blk", [(RING[i], RING[(i + by) % count]) for i in range(count)])


def cross(value, by):
    return lax.ppermute(value, "head", [(i, i ^ by) for i in range(4)])


def add(left, right):
    return (left.astype(jnp.float32) + right.astype(jnp.float32)).astype(left.dtype)


class Gather:
    def __init__(self, own):
        self.got, self.step = {0: own}, 0
        self.state = (own, own)

    def go(self):
        self.step += 1
        left, right = self.state
        if self.step < 4:
            self.state = hop(left, -1), hop(right, 1)
            self.got[self.step], self.got[8 - self.step] = self.state
        else:
            half = left.shape[0] // 2
            self.state = hop(left[:half], -1), hop(right[half:], 1)

    def strips(self):
        return [self.got[s] for s in STRIPS[:-1]] + list(self.state)

    def group(self, index):
        first, last = GROUPS[index]
        if index == 3:
            return jnp.concatenate(self.state, axis=0)
        return jnp.concatenate([self.got[s] for s in STRIPS[first:last]], axis=0)


class Scatter:
    def __init__(self, part):
        self.part, self.step = part, 0
        self.half = part[4].shape[0] // 2
        self.state = (part[4][: self.half], part[4][self.half :])

    def go(self):
        self.step += 1
        half, part = self.half, self.part
        up, down = hop(self.state[0], 1), hop(self.state[1], -1)
        if self.step == 1:
            up = jnp.concatenate([add(part[3][:half], up), part[3][half:]], axis=0)
            down = jnp.concatenate([part[5][:half], add(part[5][half:], down)], axis=0)
        elif self.step < 4:
            up, down = add(part[4 - self.step], up), add(part[4 + self.step], down)
        self.state = up, down

    def total(self):
        up, down = self.state
        wide = jnp.float32
        return self.part[0].astype(wide) + up.astype(wide) + down.astype(wide)


class Swap:
    def __init__(self, pieces, rows):
        self.rows, self.step = rows, 0
        self.taken = [(pieces, 0, rows, 0, 0)]
        self.across = pieces[4 * rows : 5 * rows]
        self.state = (pieces[rows : 4 * rows], pieces[5 * rows :])

    def go(self, late=False):
        self.step += 1
        rows, step = self.rows, self.step
        right, left = hop(self.state[0], 1), hop(self.state[1], -1)
        self.taken.append((right, 0, rows, 8 - step, 0))
        self.taken.append((left, left.shape[0] - rows, rows, step, 0))
        self.state = right, left
        if step == 1 and not late:
            self.opposite(hop(self.across, 4))
        if step < 3 and not late:
            self.trim()

    def opposite(self, piece):
        self.taken.append((piece, 0, self.rows, 4, 0))

    def trim(self):
        self.state = self.state[0][self.rows :], self.state[1][: -self.rows]

    def operands(self):
        return [item[0] for item in self.taken]

    def specs(self):
        vmem = pl.BlockSpec(memory_space=pltpu.VMEM)
        own = pl.BlockSpec((self.rows, self.taken[0][0].shape[1]), lambda i: (0, 0))
        return [own] + [vmem] * (len(self.taken) - 1)

    def result(self):
        rows, taken = self.rows, [item[1:] for item in self.taken]

        def stack_kernel(*refs):
            for ref, (first, count, spot, top) in zip(refs[:-1], taken):
                at = spot * rows + top
                refs[-1][at : at + count, :] = ref[first : first + count, :]

        return pl.pallas_call(
            stack_kernel,
            grid=(1,),
            in_specs=self.specs(),
            out_specs=pl.BlockSpec(memory_space=pltpu.VMEM),
            out_shape=jax.ShapeDtypeStruct((8 * rows, self.taken[0][0].shape[1]), jnp.bfloat16),
            cost_estimate=CHEAP,
            name="stack",
        )(*self.operands())


def hold(rings, *extra):
    states, extra = lax.optimization_barrier(([ring.state for ring in rings], extra))
    for ring, state in zip(rings, states):
        ring.state = state
    return extra[0] if len(extra) == 1 else extra


def scatter_cross(own, far, sent):
    moved = cross(sent, 1)
    half = own.shape[0]
    return add(own, moved[:half]), add(far, moved[half:])


def columns(at, width):
    return pl.ds(pl.multiple_of(at * width, width), width)


def slice_kernel(at_ref, *refs, pad):
    weights, out_ref = refs[:-1], refs[-1]
    if pad:
        weights, pad_ref = weights[:-1], weights[-1]
    rows = weights[0].shape[0]
    each = rows + pad
    for s in range(8):
        first = 0
        for ref in weights:
            width = ref.shape[1] // 8
            out_ref[s * each : s * each + rows, first : first + width] = ref[
                :, columns(at_ref[s], width)
            ]
            first += width
        if pad:
            out_ref[s * each + rows : (s + 1) * each, :] = pad_ref[...]


def slice_pieces(at, *weights, pad=None):
    rows = weights[0].shape[0]
    cols = sum(w.shape[1] for w in weights) // 8
    extra = 0 if pad is None else pad.shape[0]
    operands = weights if pad is None else (*weights, pad)
    vmem = pl.BlockSpec(memory_space=pltpu.VMEM)
    return pl.pallas_call(
        lambda *refs: slice_kernel(*refs, pad=extra),
        in_specs=[pl.BlockSpec(memory_space=pltpu.SMEM)] + [vmem] * len(operands),
        out_specs=vmem,
        out_shape=jax.ShapeDtypeStruct((8 * (rows + extra), cols), jnp.bfloat16),
        cost_estimate=CHEAP,
        name="slice_pieces",
    )(at, *operands)


def assemble_kernel(at_ref, *refs):
    own = at_ref[8]
    for j, piece in enumerate(refs[:4]):
        refs[4][0, own ^ j] = piece[...]


def assemble(at, pieces, rows):
    count = at.shape[0] - 1
    total, cols = pieces[0].shape
    return pl.pallas_call(
        assemble_kernel,
        grid_spec=pltpu.PrefetchScalarGridSpec(
            num_scalar_prefetch=1,
            grid=(count,),
            in_specs=[pl.BlockSpec((rows, cols), lambda i, at: (i, 0))] * 4,
            out_specs=pl.BlockSpec((1, 4, rows, cols), lambda i, at: (at[i], 0, 0, 0)),
        ),
        out_shape=jax.ShapeDtypeStruct((count, 4, rows, cols), jnp.bfloat16),
        cost_estimate=CHEAP,
        name="assemble",
    )(at, *pieces).reshape(4 * total, cols)


def spun(rows, cosine, sine):
    return rows * cosine + pltpu.roll(rows, HEAD_SIZE // 2, 1) * sine


def project_kernel(at_ref, *refs, strips):
    token_refs, refs = refs[:strips], refs[strips:]
    pieces, refs = refs[:4], refs[4:]
    cos_ref, sin_ref, normed_ref, raw_ref, q_ref, kv_ref, matrix_ref, gains_ref = refs
    each = pieces[0].shape[0] // 8
    rows = matrix_ref.shape[0] // 32
    own = at_ref[8]
    gains = jnp.zeros(gains_ref.shape, jnp.float32)
    for s in range(8):
        for j in range(4):
            first = pl.multiple_of((at_ref[s] * 4 + (own ^ j)) * rows, rows)
            matrix_ref[pl.ds(first, rows), :] = pieces[j][s * each : s * each + rows, :]
            gains += pieces[j][s * each + rows : (s + 1) * each, :].astype(jnp.float32)
    gains_ref[...] = gains
    width = gains.shape[1]
    first = 0
    for ref in token_refs:
        block = ref[...].astype(jnp.float32)
        block = block * inverse_rms(block)
        here = slice(first, first + ref.shape[0])
        for i in range(block.shape[1] // width):
            cols = slice(i * width, (i + 1) * width)
            normed_ref[here, cols] = (block[:, cols] * gains[i : i + 1]).astype(jnp.bfloat16)
        first += ref.shape[0]
    query_gain, key_gain = gains[8:9, :HEAD_SIZE], gains[8:9, HEAD_SIZE : 2 * HEAD_SIZE]
    query_cols = q_ref.shape[1]
    step = 256
    for first in range(0, q_ref.shape[0], step):
        here = slice(first, first + step)
        raw = jnp.dot(normed_ref[here, :], matrix_ref[...], preferred_element_type=jnp.float32)
        raw_ref[here, :] = raw
        cosine, sine = cos_ref[here, :], sin_ref[here, :]
        for col in range(0, query_cols + HEAD_SIZE, HEAD_SIZE):
            part = raw[:, col : col + HEAD_SIZE]
            if col < query_cols:
                part = spun(part * inverse_rms(part) * query_gain, cosine, sine)
                part = part * (LOG2E / math.sqrt(HEAD_SIZE))
                q_ref[here, col : col + HEAD_SIZE] = part.astype(jnp.bfloat16)
            else:
                part = spun(part * inverse_rms(part) * key_gain, cosine, sine)
                kv_ref[here, :HEAD_SIZE] = part.astype(jnp.bfloat16)
        kv_ref[here, HEAD_SIZE:] = raw[:, query_cols + HEAD_SIZE :].astype(jnp.bfloat16)


def project(at, strips, pieces, cosine, sine, query_cols, pad):
    rows = sum(strip.shape[0] for strip in strips)
    width = strips[0].shape[1]
    cols = pieces[0].shape[1]
    vmem = pl.BlockSpec(memory_space=pltpu.VMEM)
    operands = (*strips, *pieces, cosine, sine)
    narrow, wide = jnp.bfloat16, jnp.float32
    return pl.pallas_call(
        lambda *refs: project_kernel(*refs, strips=len(strips)),
        in_specs=[pl.BlockSpec(memory_space=pltpu.SMEM)] + [vmem] * len(operands),
        out_specs=[vmem] * 6,
        out_shape=[
            jax.ShapeDtypeStruct((rows, width), narrow),
            jax.ShapeDtypeStruct((rows, cols), wide),
            jax.ShapeDtypeStruct((rows, query_cols), narrow),
            jax.ShapeDtypeStruct((rows, 2 * HEAD_SIZE), narrow),
            jax.ShapeDtypeStruct((width, cols), narrow),
            jax.ShapeDtypeStruct((pad, cols), wide),
        ],
        cost_estimate=LONG,
        name="project",
    )(at, *operands)


def project_back_kernel(
    dq_ref, dkv_ref, raw_ref, head_gain_ref, cos_ref, sin_ref, matrix_ref,
    grad_ref, part_ref, gain_ref,
):
    query_cols = dq_ref.shape[1]
    step = 256
    gain_ref[...] = jnp.zeros_like(gain_ref)
    for first in range(0, dq_ref.shape[0], step):
        here = slice(first, first + step)
        cosine, sine = cos_ref[here, :], sin_ref[here, :]
        for col in range(0, query_cols + HEAD_SIZE, HEAD_SIZE):
            cols = slice(col, col + HEAD_SIZE)
            which = 0 if col < query_cols else 1
            grads = dkv_ref[here, :HEAD_SIZE] if which else dq_ref[here, cols]
            raw = raw_ref[here, cols]
            rho = inverse_rms(raw)
            unit = raw * rho
            turned = spun(grads.astype(jnp.float32), cosine, -sine)
            gain_ref[which : which + 1, :] += jnp.sum(turned * unit, axis=0, keepdims=True)
            scaled = turned * head_gain_ref[which : which + 1]
            back = rho * (scaled - unit * jnp.mean(unit * scaled, axis=-1, keepdims=True))
            grad_ref[here, cols] = back.astype(jnp.bfloat16)
        grad_ref[here, query_cols + HEAD_SIZE :] = dkv_ref[here, HEAD_SIZE:]
        part_ref[here, :] = lax.dot_general(
            grad_ref[here, :], matrix_ref[...], ALONG, preferred_element_type=jnp.float32
        ).astype(jnp.bfloat16)


def project_back(query_grads, kv_grads, raw, head_gains, cosine, sine, matrix):
    rows, cols = raw.shape
    vmem = pl.BlockSpec(memory_space=pltpu.VMEM)
    return pl.pallas_call(
        project_back_kernel,
        in_specs=[vmem] * 7,
        out_specs=[vmem] * 3,
        out_shape=[
            jax.ShapeDtypeStruct((rows, cols), jnp.bfloat16),
            jax.ShapeDtypeStruct((rows, matrix.shape[0]), jnp.bfloat16),
            jax.ShapeDtypeStruct((8, HEAD_SIZE), jnp.float32),
        ],
        cost_estimate=LONG,
        name="project_back",
    )(query_grads, kv_grads, raw, head_gains, cosine, sine, matrix)


def dots(lefts, rights, dims):
    return sum(
        lax.dot_general(left[...], right[...], dims, preferred_element_type=jnp.float32)
        for left, right in zip(lefts, rights)
    )


def weight_grads_kernel(at_ref, *refs, groups, rows):
    own_ref, far_ref, sent_ref, held = refs[-4:]
    own = at_ref[8]
    sums = dots(refs[:groups], refs[groups : 2 * groups], DOWN)
    held[...] = sums.astype(jnp.bfloat16).reshape(held.shape)
    own_ref[:rows, :] = held[own]
    far_ref[:rows, :] = held[own ^ 2]
    sent_ref[0, :rows] = held[own ^ 1]
    sent_ref[1, :rows] = held[own ^ 3]
    if own_ref.shape[0] > rows:
        pad = refs[2 * groups][...]
        own_ref[rows:, :] = pad
        far_ref[rows:, :] = pad
        sent_ref[0, rows:] = pad
        sent_ref[1, rows:] = pad


def weight_grads(at, lefts, rights, rows, pad=None):
    count = at.shape[0] - 1
    cols = rights[0].shape[1]
    pads = [] if pad is None else [pad]
    each = rows + sum(p.shape[0] for p in pads)
    part = pl.BlockSpec((each, cols), lambda i, at: (i, 0))
    shape = jax.ShapeDtypeStruct((count * each, cols), jnp.bfloat16)
    own, far, sent = pl.pallas_call(
        lambda *refs: weight_grads_kernel(*refs, groups=len(lefts), rows=rows),
        grid_spec=pltpu.PrefetchScalarGridSpec(
            num_scalar_prefetch=1,
            grid=(count,),
            in_specs=[
                pl.BlockSpec((left.shape[0], 4 * rows), lambda i, at: (0, at[i]))
                for left in lefts
            ]
            + [pl.BlockSpec(right.shape, lambda i, at: (0, 0)) for right in (*rights, *pads)],
            out_specs=[part, part, pl.BlockSpec((2, each, cols), lambda i, at: (0, i, 0))],
            scratch_shapes=[pltpu.VMEM((4, rows, cols), jnp.bfloat16)],
        ),
        out_shape=[
            shape, shape, jax.ShapeDtypeStruct((2, count * each, cols), jnp.bfloat16),
        ],
        cost_estimate=CHEAP,
        name="weight_grads",
    )(at, *lefts, *rights, *pads)
    return own, far, sent.reshape(2 * count * each, cols)


def row_grads_kernel(*refs, lefts):
    left_refs, right_refs, (out_ref, held) = refs[:lefts], refs[lefts:-2], refs[-2:]

    @pl.when(pl.program_id(0) == 0)
    def _():
        first = 0
        for ref in right_refs:
            held[first : first + ref.shape[0], :] = ref[...]
            first += ref.shape[0]

    sums, first = 0.0, 0
    for ref in left_refs:
        sums += lax.dot_general(
            ref[...],
            held[first : first + ref.shape[0], :],
            DOWN,
            preferred_element_type=jnp.float32,
        )
        first += ref.shape[0]
    out_ref[...] = sums.astype(jnp.bfloat16)


def row_grads(lefts, rights, block=256):
    out_rows, cols = lefts[0].shape[1], rights[0].shape[1]
    total = sum(left.shape[0] for left in lefts)
    return pl.pallas_call(
        lambda *refs: row_grads_kernel(*refs, lefts=len(lefts)),
        grid=(out_rows // block,),
        in_specs=[pl.BlockSpec((left.shape[0], block), lambda i: (0, i)) for left in lefts]
        + [pl.BlockSpec(right.shape, lambda i: (0, 0)) for right in rights],
        out_specs=pl.BlockSpec((block, cols), lambda i: (i, 0)),
        out_shape=jax.ShapeDtypeStruct((out_rows, cols), jnp.bfloat16),
        scratch_shapes=[pltpu.VMEM((total, cols), jnp.bfloat16)],
        cost_estimate=CHEAP,
        name="row_grads",
    )(*lefts, *rights)


def hidden_grads_kernel(*refs, strips):
    matrix_ref, outs, held = refs[strips], refs[strips + 1 : -1], refs[-1]

    @pl.when(pl.program_id(0) == 0)
    def _():
        first = 0
        for ref in refs[:strips]:
            held[first : first + ref.shape[0], :] = ref[...]
            first += ref.shape[0]

    first = 0
    for out in outs:
        out[...] = lax.dot_general(
            held[first : first + out.shape[0], :],
            matrix_ref[...],
            ALONG,
            preferred_element_type=jnp.float32,
        )
        first += out.shape[0]


def hidden_grads_of(strips, matrix, block=256):
    rows = [(last - first) * strips[0].shape[0] for first, last in GROUPS]
    cols = matrix.shape[0]
    return pl.pallas_call(
        lambda *refs: hidden_grads_kernel(*refs, strips=len(strips)),
        grid=(cols // block,),
        in_specs=[pl.BlockSpec(strip.shape, lambda i: (0, 0)) for strip in strips]
        + [pl.BlockSpec((block, matrix.shape[1]), lambda i: (i, 0))],
        out_specs=[pl.BlockSpec((n, block), lambda i: (0, i)) for n in rows],
        out_shape=[jax.ShapeDtypeStruct((n, cols), jnp.float32) for n in rows],
        scratch_shapes=[pltpu.VMEM((sum(rows), matrix.shape[1]), jnp.bfloat16)],
        cost_estimate=CHEAP,
        name="hidden_grads",
    )(*strips, matrix)


def lane_sums(block):
    return sum(block[:, i : i + 128] for i in range(0, block.shape[1], 128))


def widen(at, swap, *weights):
    rows, taken, count = weights[0].shape[0], [item[1:] for item in swap.taken], len(weights)
    pad = swap.rows - rows

    def widen_kernel(at_ref, *refs):
        piece_refs, refs = refs[: len(taken)], refs[len(taken) :]
        grads, sums_ref = refs[count : 2 * count], refs[2 * count]
        for ref in refs[2 * count :]:
            ref[...] = jnp.zeros_like(ref)
        for ref, (start, size, spot, top) in zip(piece_refs, taken):
            used = min(size, rows - top)
            here = slice(top, top + used)
            first = 0
            for weight, grad in zip(refs[:count], grads):
                width = weight.shape[1] // 8
                there = columns(at_ref[spot], width)
                block = ref[start : start + used, first : first + width].astype(jnp.float32)
                grad[here, there] = block
                sums_ref[here, :] += lane_sums(block * weight[here, there].astype(jnp.float32))
                first += width
            if used < size:
                refs[-1][...] += ref[start + used : start + size, :].astype(jnp.float32)

    vmem = pl.BlockSpec(memory_space=pltpu.VMEM)
    shapes = [w.shape for w in weights] + [(rows, 128)]
    if pad:
        shapes.append((pad, swap.taken[0][0].shape[1]))
    return pl.pallas_call(
        widen_kernel,
        grid=(1,),
        in_specs=[pl.BlockSpec(memory_space=pltpu.SMEM), *swap.specs()] + [vmem] * count,
        out_specs=[vmem] * len(shapes),
        out_shape=[jax.ShapeDtypeStruct(shape, jnp.float32) for shape in shapes],
        cost_estimate=LONG,
        name="widen",
    )(at, *swap.operands(), *weights)


def grouped(strips):
    return [
        jnp.concatenate(strips[a:b], axis=0) if b - a > 1 else strips[a] for a, b in GROUPS
    ]


def split_groups(groups, rows):
    return [
        group[i * rows : (i + 1) * rows]
        for group in groups
        for i in range(group.shape[0] // rows)
    ]


def gather_head(rows):
    return lax.all_gather(rows, "head", axis=0, tiled=True)


def scatter_head(rows):
    return lax.psum_scatter(rows, "head", scatter_dimension=0, tiled=True)


def inverse_rms(rows):
    return lax.rsqrt(jnp.mean(rows * rows, axis=-1, keepdims=True) + EPS)


def per_device(
    tokens,
    attention_norm,
    query_weight,
    key_projection,
    value_projection,
    query_norm,
    key_norm,
    output_weight,
    feedforward_norm,
    gate_weight,
    up_weight,
    down_weight,
    stretch_order,
    out_cotangent,
):
    blk_count = lax.axis_size("blk")
    head_count = lax.axis_size("head")
    head_index = lax.axis_index("head")
    blk_index = lax.axis_index("blk")
    narrow, wide = jnp.bfloat16, jnp.float32
    tokens, out_cotangent = tokens[0], out_cotangent[0]
    local_rows, model_width = tokens.shape
    group_rows = local_rows * blk_count
    weight_rows = query_weight.shape[0]
    ff_local = gate_weight.shape[1] // blk_count
    query_cols = QUERY_HEADS // blk_count * HEAD_SIZE
    attn_cols = query_cols + 2 * HEAD_SIZE
    device_count = blk_count * head_count
    strip_count = blk_count * head_count
    halves = strip_count // stretch_order.shape[1]
    ring_place = jnp.where(blk_index % 2 == 0, blk_index // 2, 7 - blk_index // 2)

    spot = (ring_place + jnp.arange(blk_count, dtype=jnp.int32)) % blk_count
    at = jnp.where(spot < 4, 2 * spot, 15 - 2 * spot).astype(jnp.int32)
    at_own = jnp.concatenate([at, head_index[None].astype(jnp.int32)])
    ring_spot = (ring_place + jnp.asarray(STRIPS, jnp.int32)) % blk_count
    strip_blk = jnp.where(ring_spot < 4, 2 * ring_spot, 15 - 2 * ring_spot)
    strip_head = head_index ^ jnp.asarray((0, 2, 1, 3), jnp.int32)
    strip = (strip_blk[None, :] * head_count + strip_head[:, None]).reshape(strip_count)
    slots = jnp.arange(stretch_order.shape[1], dtype=jnp.int32)
    held = jnp.sum(
        jnp.where((strip // halves)[:, None] == slots[None, :], stretch_order, 0), axis=1
    )
    strip_place = held * halves + strip % halves
    order = strip_place.astype(jnp.int32)
    place = strip_place[:blk_count].astype(jnp.int32)
    positions = (
        place[:, None] * local_rows + jnp.arange(local_rows, dtype=jnp.int32)[None, :]
    ).reshape(group_rows)
    phases = angles(positions, HEAD_SIZE)[:, 0, :]
    cosine, sine = jnp.cos(phases), jnp.sin(phases)
    cosine = jnp.concatenate([cosine, cosine], axis=1)
    sine = jnp.concatenate([-sine, sine], axis=1)

    small = query_norm.shape[0]
    number = blk_index * head_count + head_index
    pad = 16

    def placed(share):
        return jnp.where(
            jnp.arange(device_count, dtype=jnp.int32)[:, None] == number, share[None, :], 0
        ).reshape(-1)

    gains = jnp.concatenate(
        [placed(attention_norm), placed(feedforward_norm), placed(query_norm), placed(key_norm)]
    ).astype(narrow)
    gains = jnp.pad(gains, (0, pad * attn_cols - gains.shape[0])).reshape(pad, attn_cols)
    down_matrix = gather_head(down_weight)
    output_rows = gather_head(output_weight)

    attn_swap = Swap(
        slice_pieces(at, query_weight, key_projection, value_projection, pad=gains),
        weight_rows + pad,
    )
    token_ring = Gather(tokens)
    ff_slices = slice_pieces(at, gate_weight, up_weight)
    token_ring.go()
    attn_swap.go()
    ff_slices, cosine, sine = hold((attn_swap,), ff_slices, cosine, sine)
    attn_swap.go()
    hold((attn_swap,))
    attn_swap.go()
    own = hold((token_ring,), attn_swap.result())
    near, far = cross(own, 1), cross(own, 2)
    token_ring.go()
    ff_swap, cotangent_ring = Swap(ff_slices, weight_rows), Gather(out_cotangent)
    hold((token_ring, ff_swap, cotangent_ring))
    token_ring.go()
    own, near, far = hold((token_ring,), own, near, far)
    both = cross(far, 1)
    token_ring.go()
    own, near, far, both = hold((token_ring, ff_swap, cotangent_ring), own, near, far, both)
    ff_swap.go()
    cotangent_ring.go()

    first_normed, attn_raw, query_rows, own, attn_matrix, gains = project(
        at_own, token_ring.strips(), (own, near, far, both), cosine, sine, query_cols, pad
    )
    gain_one = gains[:4].reshape(1, model_width)
    gain_two = gains[4:8].reshape(1, model_width)
    head_gains = jnp.pad(gains[8, : 2 * HEAD_SIZE].reshape(2, HEAD_SIZE), ((0, 6), (0, 0)))
    near, far = cross(own, 1), cross(own, 2)
    own, near, far = hold((ff_swap, cotangent_ring), own, near, far)
    both = cross(far, 1)
    kv = hold((ff_swap, cotangent_ring), own, far, near, both)
    ff_swap.go(late=True)
    cotangent_ring.go()
    attended, lse = attend(place, order, query_rows, kv)

    def by_groups(rows):
        return [rows[a * local_rows : b * local_rows] for a, b in GROUPS]

    def by_strips(groups):
        return dict(zip(STRIPS, split_groups(groups, local_rows)))

    attended = hold((cotangent_ring, ff_swap), attended)
    branch_parts = [matmul(rows, output_rows).astype(narrow) for rows in by_groups(attended)]
    branch_ring = Scatter(by_strips(branch_parts))
    branch_ring.go()
    ff_swap.trim()
    ff_swap.go()
    ff_own = hold((branch_ring,), ff_swap.result())
    ff_near, ff_far = cross(ff_own, 1), cross(ff_own, 2)
    branch_ring.go()
    cotangent_ring.go()
    hold((branch_ring, cotangent_ring))
    branch_ring.go()
    cotangent_ring.go()
    ff_near, ff_far, down_matrix = hold(
        (branch_ring, cotangent_ring), ff_near, ff_far, down_matrix
    )
    cotangent_strips = hold((), cotangent_ring.strips())
    branch_ring.go()
    hidden_grads = hidden_grads_of(cotangent_strips, down_matrix)
    ff_both = cross(ff_far, 1)
    hidden_grads, ff_both = hold((branch_ring,), hidden_grads, ff_both)
    tokens_wide = tokens.astype(wide)
    resid = tokens_wide + branch_ring.total()
    rho_two = inverse_rms(resid)
    unit_two = resid * rho_two

    second_ring = Gather((unit_two * gain_two).astype(narrow))
    second_groups, hidden_groups, ff_gradient_groups = [], [], []

    def feed_forward(index):
        rows = second_ring.group(index)
        ff_raw = matmul(rows, ff_matrix)
        gate, up_proj = ff_raw[:, :ff_local], ff_raw[:, ff_local:]
        sigma = jax.nn.sigmoid(gate)
        swish = gate * sigma
        hidden_gradient = hidden_grads[index]
        gate_gradient = hidden_gradient * up_proj * (sigma * (1.0 + gate * (1.0 - sigma)))
        hidden = (swish * up_proj).astype(narrow)
        gradient = jnp.concatenate([gate_gradient, hidden_gradient * swish], 1).astype(narrow)
        if index < 3:
            rows, hidden, gradient = hold((second_ring,), rows, hidden, gradient)
        second_groups.append(rows)
        hidden_groups.append(hidden)
        ff_gradient_groups.append(gradient)

    second_ring.go()
    ff_matrix = assemble(at_own, (ff_own, ff_near, ff_far, ff_both), weight_rows)
    ff_matrix = hold((second_ring,), ff_matrix)
    for index in range(3):
        second_ring.go()
        feed_forward(index)
    feed_forward(3)

    def back(index):
        return matmul(ff_gradient_groups[index], ff_matrix, ALONG).astype(narrow)

    def split(group):
        return [group[i : i + local_rows] for i in range(0, group.shape[0], local_rows)]

    parts = {4: back(3)}
    resid_ring = Scatter(parts)
    parts[3], parts[5] = split(hold((), back(2)))
    parts[2], parts[6] = split(hold((), back(1)))
    resid_ring.go()
    hold((resid_ring,), parts[2], parts[6])
    resid_ring.go()
    back_zero, second_groups, ff_gradient_groups = hold(
        (resid_ring,), back(0), second_groups, ff_gradient_groups
    )
    parts[0], parts[1], parts[7] = split(back_zero)
    resid_ring.go()
    ff_own, ff_far, ff_sent = hold(
        (resid_ring,), *weight_grads(at_own, second_groups, ff_gradient_groups, weight_rows)
    )
    resid_ring.go()
    ff_own, ff_far = scatter_cross(ff_own, ff_far, ff_sent)
    ff_own, ff_far, hidden_groups = hold((resid_ring,), ff_own, ff_far, hidden_groups)
    ff_far = cross(ff_far, 2)
    scaled = gain_two * resid_ring.total()
    resid_gradient = out_cotangent.astype(wide) + rho_two * (
        scaled - unit_two * jnp.mean(unit_two * scaled, axis=-1, keepdims=True)
    )

    grad_ring = Gather(resid_gradient.astype(narrow))
    grad_groups, attended_grads = [], []

    def attention_back(index):
        rows = grad_ring.group(index)
        grads = matmul(rows, output_rows, ALONG).astype(narrow)
        if index < 3:
            rows, grads = hold((grad_ring,), rows, grads)
        grad_groups.append(rows)
        attended_grads.append(grads)

    grad_ring.go()
    out_parts = [matmul(rows, down_matrix).astype(narrow) for rows in hidden_groups]
    out_parts = hold((grad_ring,), *out_parts)
    out_ring = Scatter(by_strips(out_parts))
    grad_ring.go()
    hidden_groups, cotangent_strips = hold((grad_ring,), hidden_groups, cotangent_strips)
    grad_ring.go()
    attention_back(0)
    down_gradient = hold((out_ring, grad_ring), row_grads(hidden_groups, cotangent_strips))
    down_gradient = scatter_head(down_gradient)
    out_ring.go()
    grad_ring.go()
    attention_back(1)
    attention_back(2)
    ff_swap = Swap(add(ff_own, ff_far), weight_rows)
    hold((grad_ring, ff_swap, out_ring))
    out_ring.go()
    ff_swap.go(late=True)
    attention_back(3)
    query_grads, kv_own, kv_far, kv_sent = attend_back(
        place, order, query_rows, attended_grads, attended, lse, kv
    )
    query_grads, kv_own, kv_far, kv_sent, grad_groups, attended = hold(
        (out_ring, ff_swap), query_grads, kv_own, kv_far, kv_sent, grad_groups, attended
    )
    out_ring.go()
    ff_swap.trim()
    kv_own, kv_far = scatter_cross(kv_own, kv_far, kv_sent)
    output_weight_gradient = row_grads([attended], grad_groups)
    kv_own, kv_far, output_weight_gradient, down_gradient = hold(
        (out_ring, ff_swap), kv_own, kv_far, output_weight_gradient, down_gradient
    )
    ff_swap.go()
    kv_grads, ff_opposite = hold(
        (ff_swap,), add(kv_own, cross(kv_far, 2)), hop(ff_swap.across, 4)
    )
    ff_swap.opposite(ff_opposite)
    ff_swap.go()
    attn_gradient, first_parts, gain_sums = project_back(
        query_grads, kv_grads, attn_raw, head_gains, cosine, sine, attn_matrix
    )
    gain_sums = jnp.pad(
        gain_sums[:2].reshape(1, 2 * HEAD_SIZE).astype(narrow),
        ((0, pad - 1), (0, attn_cols - 2 * HEAD_SIZE)),
    )
    attn_gradient, first_parts, gain_sums, output_weight_gradient = hold(
        (ff_swap, out_ring), attn_gradient, first_parts, gain_sums, output_weight_gradient
    )
    token_ring = Scatter(by_strips(by_groups(first_parts)))
    token_ring.go()
    out_ring.go()
    attn_own, attn_far, attn_sent = weight_grads(
        at_own, [first_normed], [attn_gradient], weight_rows, gain_sums
    )
    attn_own, attn_far, attn_sent = hold(
        (token_ring, out_ring), attn_own, attn_far, attn_sent
    )
    token_ring.go()
    attn_own, attn_far = scatter_cross(attn_own, attn_far, attn_sent)
    attn_far = cross(attn_far, 2)
    layer_out = (resid + out_ring.total()).astype(narrow)
    attn_swap = Swap(add(attn_own, attn_far), weight_rows + pad)
    output_weight_gradient, layer_out, gate_weight, up_weight = hold(
        (token_ring, attn_swap), output_weight_gradient, layer_out, gate_weight, up_weight
    )
    output_weight_gradient = scatter_head(output_weight_gradient)
    attn_swap.go()
    token_ring.go()
    gate_weight_gradient, up_weight_gradient, ff_sums = widen(at, ff_swap, gate_weight, up_weight)
    gate_weight_gradient, up_weight_gradient, ff_sums = hold(
        (token_ring, attn_swap), gate_weight_gradient, up_weight_gradient, ff_sums
    )
    feedforward_norm_gradient = jnp.sum(ff_sums, axis=1) / feedforward_norm.astype(wide)
    down_gradient = down_gradient.astype(wide)
    attn_swap.go()
    token_ring.go()
    output_weight_gradient, down_gradient, feedforward_norm_gradient = hold(
        (token_ring, attn_swap),
        output_weight_gradient.astype(wide), down_gradient, feedforward_norm_gradient,
    )
    attn_swap.go()
    query_weight_gradient, key_weight_gradient, value_weight_gradient, norm_sums, gain_sums = widen(
        at, attn_swap, query_weight, key_projection, value_projection
    )
    attention_norm_gradient = jnp.sum(norm_sums, axis=1) / attention_norm.astype(wide)
    gain_sums = gain_sums[0, : 2 * HEAD_SIZE].reshape(2, HEAD_SIZE)
    gain_sums = lax.dynamic_slice_in_dim(gain_sums, number * small, small, 1)
    rho_one = inverse_rms(tokens_wide)
    unit_one = tokens_wide * rho_one
    scaled = gain_one * token_ring.total()
    tokens_gradient = resid_gradient + rho_one * (
        scaled - unit_one * jnp.mean(unit_one * scaled, axis=-1, keepdims=True)
    )
    return (
        layer_out[None],
        tokens_gradient.astype(narrow)[None],
        attention_norm_gradient,
        query_weight_gradient,
        key_weight_gradient,
        value_weight_gradient,
        gain_sums[0],
        gain_sums[1],
        output_weight_gradient,
        feedforward_norm_gradient,
        gate_weight_gradient,
        up_weight_gradient,
        down_gradient,
    )


def solution(mesh):
    placed = (
        P(None, ("blk", "head"), None),
        P(("blk", "head")),
        P(("blk", "head"), None),
        P(("blk", "head"), None),
        P(("blk", "head"), None),
        P(("blk", "head")),
        P(("blk", "head")),
        P(("blk", "head"), None),
        P(("blk", "head")),
        P(("blk", "head"), None),
        P(("blk", "head"), None),
        P(("blk", "head"), None),
        P(),
        P(None, ("blk", "head"), None),
    )
    fits = mesh.shape["blk"] == KEY_VALUE_HEADS and mesh.shape["head"] == 4
    return jax.shard_map(
        per_device if fits else per_device_by_tokens,
        mesh=mesh,
        in_specs=placed,
        out_specs=(
            P(None, ("blk", "head"), None),
            P(None, ("blk", "head"), None),
            P(("blk", "head")),
            P(("blk", "head"), None),
            P(("blk", "head"), None),
            P(("blk", "head"), None),
            P(("blk", "head")),
            P(("blk", "head")),
            P(("blk", "head"), None),
            P(("blk", "head")),
            P(("blk", "head"), None),
            P(("blk", "head"), None),
            P(("blk", "head"), None),
        ),
        check_vma=False,
    )
```
